32 devices in a mesh: dp: 8 (over y, x, core), fsdp: 4 (over z).
Axes of the slice: x: 2, y: 2, z: 4, core: 2. Of those that a mesh axis runs over, the one named last changes fastest.
Arguments:
- patches: bfloat16 [2, 2048, 1152], P(None, ('dp', 'fsdp')), may hold values from -6 to 6
- cotangent: bfloat16 [2, 2048, 1152], P(None, ('dp', 'fsdp')), may hold values from -6 to 6
- conditioning: float32 [2, 8, 1152], replicated, may hold values from -6 to 6
- frame_of_slot: int32 [2, 2048], P(None, ('dp', 'fsdp')), may hold values from 0 to 127, as said below
- clip_of_slot: int32 [2, 2048], P(None, ('dp', 'fsdp')), may hold values from 0 to 7, as said below
- w_ada: bfloat16 [1152, 6912], P('dp', 'fsdp'), may hold values from -0.1875 to 0.1875
- b_ada: bfloat16 [6912], P('fsdp'), may hold values from -3 to 3
- w_qkv: bfloat16 [1152, 3456], P('dp', 'fsdp'), may hold values from -0.1875 to 0.1875
- b_qv: bfloat16 [2304], P('fsdp'), may hold values from -2 to 2
- w_proj: bfloat16 [1152, 1152], P('dp', 'fsdp'), may hold values from -1 to 1
- b_proj: bfloat16 [1152], P('fsdp'), may hold values from -2 to 2
- w_fc1: bfloat16 [1152, 4608], P('dp', 'fsdp'), may hold values from -0.1875 to 0.1875
- b_fc1: bfloat16 [4608], P('fsdp'), may hold values from -3 to 3
- w_fc2: bfloat16 [4608, 1152], P('dp', 'fsdp'), may hold values from -0.09375 to 0.09375
- b_fc2: bfloat16 [1152], P('fsdp'), may hold values from -2 to 2
Outputs:
- output: bfloat16 [2, 2048, 1152], P(None, ('dp', 'fsdp'))
- input_grad: bfloat16 [2, 2048, 1152], P(None, ('dp', 'fsdp'))
- cond_grad: float32 [2, 8, 1152], P(None, None, 'fsdp')
- grad_w_ada: float32 [1152, 6912], P('dp', 'fsdp')
- grad_b_ada: float32 [6912], P('fsdp')
- grad_w_qkv: float32 [1152, 3456], P('dp', 'fsdp')
- grad_b_qv: float32 [2304], P('fsdp')
- grad_w_proj: float32 [1152, 1152], P('dp', 'fsdp')
- grad_b_proj: float32 [1152], P('fsdp')
- grad_w_fc1: float32 [1152, 4608], P('dp', 'fsdp')
- grad_b_fc1: float32 [4608], P('fsdp')
- grad_w_fc2: float32 [4608, 1152], P('dp', 'fsdp')
- grad_b_fc2: float32 [1152], P('fsdp')
The draws below stay inside these ranges and needn't reach their ends.
Inputs may be any that keep to these rules, and one draw needn't show every extreme that they name: `frame_of_slot`: in each micro-batch, each aligned block of 64 slots holds either one frame of 64 patches or four frames of 16 patches one after another; no frame number appears in two blocks. `clip_of_slot`: all slots of one frame name the same clip.
All inputs are finite; a program needn't handle non-finite values.
Results may differ from the reference program's by a relative error of at most 0.018.
Values may be sent and summed in bfloat16 or wider, within the bound.
A program may use at most 256 MiB of HBM per device.

```python
import math
import jax
import jax.numpy as jnp
from jax import lax

D = 1152
HEADS = 16
HEAD_DIM = 72
FF = 4608
L_SHORT = 16
TOK_DEV = 64
CLIPS = 8
MB = 2
TOKENS = 2048
N_DP = 8
N_FSDP = 4


def frame_table(key):
    device_count = TOKENS // TOK_DEV
    frame_kinds = jax.random.randint(jax.random.fold_in(key, 11), (MB, device_count), 0, 2)
    places = jnp.arange(TOK_DEV, dtype=jnp.int32) // L_SHORT
    owners = jnp.arange(device_count, dtype=jnp.int32)
    single_place = 3 * (owners % 2)
    local_place = jnp.where(frame_kinds[:, :, None] == 1, single_place[None, :, None], places[None, None, :])
    frames = 4 * owners[None, :, None] + local_place
    return frames.reshape(MB, TOKENS).astype(jnp.int32)


def draw_frame_of_slot(key, part):
    return frame_table(key)


def draw_clip_of_slot(key, part):
    frames = frame_table(key)
    device_count = TOKENS // TOK_DEV
    clip_table = jax.random.randint(jax.random.fold_in(key, 23), (MB, 4 * device_count), 0, CLIPS)
    return jnp.take_along_axis(clip_table, frames, axis=1).astype(jnp.int32)


def raised(drawn, own_key, source, target, parts, factor):
    def block_of(dim):
        return (jnp.arange(drawn.shape[dim]) // (drawn.shape[dim] // parts)).reshape((-1,) + (1,) * (drawn.ndim - 1 - dim))

    near = jax.random.permutation(own_key, parts)[block_of(target)]
    second = (block_of(target) + parts // 2) % parts
    return jnp.where((block_of(source) == near) | (block_of(source) == second), factor * drawn, drawn)


def block_scale(own_key, shape, cuts, smallest, top_value):
    def one(axis_at, parts):
        heights = jax.random.uniform(jax.random.fold_in(jax.random.fold_in(own_key, 6), axis_at), (parts,), jnp.float32, smallest / len(cuts), top_value / len(cuts))
        return jnp.repeat(jnp.exp(heights), shape[axis_at] // parts).reshape((-1,) + (1,) * (len(shape) - axis_at - 1))

    gain = one(*cuts[0])
    for cut in cuts[1:]:
        gain = gain * one(*cut)
    return gain


def bell_draw(own_key, shape, scale, most, pieces=(), held_as=jnp.bfloat16):
    drawn = jax.random.normal(own_key, shape, jnp.float32) * scale
    if len(pieces) > 0:
        drawn = block_scale(own_key, shape, pieces, -0.22, 0.18) * drawn
    return jnp.clip(drawn, min=-most, max=most).astype(held_as)


def gaussian_with(key, shape, width, most, cuts, heavy, kind=jnp.bfloat16):
    array = width * jax.random.normal(key, shape, jnp.float32)
    if cuts:
        array = array * block_scale(key, shape, cuts, -0.22, 0.18)
    return jnp.clip(raised(array, jax.random.fold_in(key, 3), *heavy), -most, most).astype(kind)


def setup_inputs(seed: int = 0) -> dict:
    key_list = jax.random.split(jax.random.key(seed), 16)
    patches = bell_draw(key_list[0], (MB, TOKENS, D), 1.0, 6.0, ((1, 32),))
    cotangent = gaussian_with(key_list[1], (MB, TOKENS, D), 1.0, 6.0, ((1, 32),), (1, 2, 32, 2.75))
    conditioning = bell_draw(key_list[2], (MB, CLIPS, D), 1.0, 6.0, (), jnp.float32)
    frame_of_slot = draw_frame_of_slot(jax.random.fold_in(key_list[15], 71), 0)
    clip_of_slot = draw_clip_of_slot(jax.random.fold_in(key_list[15], 71), 0)
    w_ada = bell_draw(key_list[5], (D, 6 * D), D ** -0.5, 0.1875, ((0, 8), (1, 4)))
    b_ada = bell_draw(key_list[6], (6 * D,), 0.5, 3.0, ((0, 4),))
    w_qkv = bell_draw(key_list[7], (D, 3 * D), D ** -0.5, 0.1875, ((0, 8), (1, 4)))
    b_qv = bell_draw(key_list[8], (2 * D,), 0.3, 2.0, ((0, 4),))
    w_proj = bell_draw(key_list[9], (D, D), (D // 32) ** -0.5, 1.0, ((0, 8), (1, 4)))
    b_proj = bell_draw(key_list[10], (D,), 0.3, 2.0, ((0, 4),))
    w_fc1 = bell_draw(key_list[11], (D, FF), D ** -0.5, 0.1875, ((0, 8), (1, 4)))
    b_fc1 = bell_draw(key_list[12], (FF,), 0.5, 3.0, ((0, 4),))
    w_fc2 = bell_draw(key_list[13], (FF, D), FF ** -0.5, 0.09375, ((0, 8), (1, 4)))
    b_fc2 = bell_draw(key_list[14], (D,), 0.3, 2.0, ((0, 4),))
    return dict(patches=patches, cotangent=cotangent, conditioning=conditioning, frame_of_slot=frame_of_slot, clip_of_slot=clip_of_slot, w_ada=w_ada, b_ada=b_ada, w_qkv=w_qkv, b_qv=b_qv, w_proj=w_proj, b_proj=b_proj, w_fc1=w_fc1, b_fc1=b_fc1, w_fc2=w_fc2, b_fc2=b_fc2)


EPS = 1e-06
GELU_C = math.sqrt(2.0 / math.pi)
PRECISE = lax.Precision.HIGHEST
NEG_FILL = -1e+30

@jax.custom_vjp
def low(v):
    return lax.optimization_barrier(v.astype(jnp.bfloat16)).astype(jnp.float32)

@jax.custom_vjp
def low_back(v):
    return v

def low_keep(v):
    return (low(v), None)

def low_pass(kept, grad):
    return (grad,)

def back_keep(v):
    return (v, None)

def back_low(kept, grad):
    return (low(grad),)
low.defvjp(low_keep, low_pass)
low_back.defvjp(back_keep, back_low)

def layer_norm(values):
    centre = values - lax.optimization_barrier(jnp.mean(values, axis=-1, keepdims=True))
    return centre * lax.rsqrt(lax.optimization_barrier(jnp.mean(centre * centre, axis=-1, keepdims=True)) + EPS)

def gelu_tanh(hidden):
    return 0.5 * hidden * (1.0 + jnp.tanh(GELU_C * (hidden + 0.044715 * hidden * hidden * hidden)))

def block_step(params, modulation, inputs_now):
    w_qkv, b_qv, w_proj, b_proj, w_fc1, b_fc1, w_fc2, b_fc2 = params
    patch_rows, frame_ids, clip_ids = inputs_now
    group_count, length_now = frame_ids.shape
    token_mod = jnp.take(modulation, clip_ids, axis=0)
    shift_one, scale_one, gate_one, shift_two, scale_two, gate_two = jnp.split(token_mod, 6, axis=-1)
    a_in = low(layer_norm(patch_rows) * (1.0 + scale_one) + shift_one)
    qkv_bias = jnp.concatenate([b_qv[:D], jnp.zeros((D,), b_qv.dtype), b_qv[D:]])
    qkv = low(low_back(jnp.matmul(a_in, w_qkv, precision=PRECISE) + qkv_bias))
    queries = qkv[..., :D].reshape(group_count, length_now, HEADS, HEAD_DIM)
    key_rows = qkv[..., D:2 * D].reshape(group_count, length_now, HEADS, HEAD_DIM)
    value_rows = qkv[..., 2 * D:].reshape(group_count, length_now, HEADS, HEAD_DIM)
    scores = jnp.einsum('gqhd,gkhd->ghqk', queries, key_rows, precision=PRECISE) * HEAD_DIM ** (-0.5)
    scores = low_back(scores)
    same_frame = (frame_ids[:, :, None] == frame_ids[:, None, :])[:, None, :, :]
    scores = jnp.where(same_frame, scores, NEG_FILL)
    exp_scores = jnp.exp(scores - lax.optimization_barrier(jnp.max(scores, axis=-1, keepdims=True)))
    shares = exp_scores / lax.optimization_barrier(jnp.sum(exp_scores, axis=-1, keepdims=True))
    mixed = jnp.einsum('ghqk,gkhd->gqhd', low(shares), value_rows, precision=PRECISE)
    mixed = low(low_back(mixed.reshape(group_count, length_now, D)))
    attn_out = low_back(jnp.matmul(mixed, w_proj, precision=PRECISE) + b_proj)
    after_attn = patch_rows + gate_one * attn_out
    m_in = low(layer_norm(after_attn) * (1.0 + scale_two) + shift_two)
    hidden = low_back(jnp.matmul(m_in, w_fc1, precision=PRECISE) + b_fc1)
    act_low = low(gelu_tanh(hidden))
    branch = low_back(jnp.matmul(act_low, w_fc2, precision=PRECISE) + b_fc2)
    return after_attn + gate_two * branch

def forward(patch_float, cond_float, frame_of_slot, clip_of_slot, weights):
    w_ada, b_ada = (weights[0], weights[1])
    rest_params = weights[2:]
    device_count = N_DP * N_FSDP
    group_size = math.gcd(device_count, max(1, 4096 // TOK_DEV))
    group_total = device_count // group_size
    checked_step = jax.checkpoint(block_step)
    results = []
    for micro_index in range(MB):
        silu_cond = low(jax.nn.silu(cond_float[micro_index]))
        modulation = jnp.matmul(silu_cond, w_ada, precision=PRECISE) + b_ada
        inputs_all = (patch_float[micro_index].reshape(group_total, group_size, TOK_DEV, D), frame_of_slot[micro_index].reshape(group_total, group_size, TOK_DEV), clip_of_slot[micro_index].reshape(group_total, group_size, TOK_DEV))

        def scan_step(carried, inputs_now):
            return (carried, checked_step(rest_params, modulation, inputs_now))
        carried, block_out = lax.scan(scan_step, None, inputs_all)
        results.append(block_out.reshape(TOKENS, D))
    return jnp.stack(results)

def reference(patches, cotangent, conditioning, frame_of_slot, clip_of_slot, w_ada, b_ada, w_qkv, b_qv, w_proj, b_proj, w_fc1, b_fc1, w_fc2, b_fc2):
    weights = (w_ada, b_ada, w_qkv, b_qv, w_proj, b_proj, w_fc1, b_fc1, w_fc2, b_fc2)
    weights = tuple((item.astype(jnp.float32) for item in weights))

    def run_block(patch_float, cond_float, *weight_float):
        return forward(patch_float, cond_float, frame_of_slot, clip_of_slot, weight_float)
    output, pull_back = jax.vjp(run_block, patches.astype(jnp.float32), conditioning.astype(jnp.float32), *weights)
    grads = pull_back(cotangent.astype(jnp.float32))
    return (output.astype(jnp.bfloat16), grads[0].astype(jnp.bfloat16), grads[1], grads[2], grads[3], grads[4], grads[5], grads[6], grads[7], grads[8], grads[9], grads[10], grads[11])
```

```python
import functools
import math

import jax
import jax.numpy as jnp
from jax import lax
from jax.experimental import pallas as pl
from jax.experimental.pallas import tpu as pltpu
from jax.sharding import PartitionSpec as P

HEAD_DIM = 72
EPS = 1e-06
GELU_C = math.sqrt(2.0 / math.pi)
PRECISE = lax.Precision.HIGHEST
NEG_FILL = -1e30
MESH_ID = pl.DeviceIdType.MESH
F32 = jnp.float32
BF16 = jnp.bfloat16


def xor_of(index, step, size):
    result, bit = 0, 1
    while bit < size:
        mine = (index // bit) % 2
        result = result + ((mine + (step // bit) % 2) % 2) * bit
        bit *= 2
    return result


class Place:
    def __init__(self, n_chip, n_plane):
        self.n = {"core": 2, "chip": n_chip, "plane": n_plane, "dp": 2 * n_chip}
        self.dp = lax.axis_index("dp")
        self.f = lax.axis_index("fsdp")
        self.c = self.dp // 2
        self.k = self.dp % 2

    def index(self, axis):
        return {"core": self.k, "chip": self.c, "plane": self.f, "dp": self.dp}[axis]

    def peer(self, axis, step):
        other = xor_of(self.index(axis), step, self.n[axis])
        if axis == "core":
            return other, (self.c * 2 + other, self.f)
        if axis == "chip":
            return other, (other * 2 + self.k, self.f)
        if axis == "plane":
            return other, (self.dp, other)
        return other, (other, self.f)


def greet(place, axes):
    barrier = pltpu.get_barrier_semaphore()
    count = 0
    for axis in axes:
        for step in range(1, place.n[axis]):
            pl.semaphore_signal(
                barrier, inc=1, device_id=place.peer(axis, step)[1], device_id_type=MESH_ID
            )
            count += 1
    pl.semaphore_wait(barrier, count)


class Wires:
    def __init__(self, send, recv, local):
        self.send, self.recv, self.local = send, recv, local
        self.remote_count = 0
        self.local_count = 0

    def far(self, src, dst, device):
        at = self.remote_count
        self.remote_count += 1
        copy = pltpu.make_async_remote_copy(
            src_ref=src,
            dst_ref=dst,
            send_sem=self.send.at[at],
            recv_sem=self.recv.at[at],
            device_id=device,
            device_id_type=MESH_ID,
        )
        copy.start()
        return copy

    def near(self, src, dst):
        at = self.local_count
        self.local_count += 1
        copy = pltpu.make_async_copy(src, dst, self.local.at[at])
        copy.start()
        return copy


def wait_all(copies):
    for copy in copies:
        copy.wait()


ANYWHERE = pl.BlockSpec(memory_space=pl.ANY)
ON_CHIP = pl.BlockSpec(memory_space=pltpu.VMEM)


def exchange(name, collective_id, sizes, items):
    n_chip, n_plane = sizes
    n_of = {"core": 2, "chip": n_chip, "plane": n_plane, "dp": 2 * n_chip}
    axes = sorted({item[0] for item in items})
    outs = []
    n_far = 0
    for axis, kind, array in items:
        n_far += n_of[axis] - 1
        shape = array.shape if kind == "a2a" else (n_of[axis],) + array.shape
        outs.append(jax.ShapeDtypeStruct(shape, array.dtype))

    def kernel(*refs):
        ins = refs[: len(items)]
        results = refs[len(items) : 2 * len(items)]
        place = Place(n_chip, n_plane)
        wires = Wires(*refs[2 * len(items) :])
        greet(place, axes)
        copies = []
        for (axis, kind, _), src, dst in zip(items, ins, results):
            mine = place.index(axis)
            for step in range(1, n_of[axis]):
                other, device = place.peer(axis, step)
                piece = src if kind == "ag" else src.at[other]
                copies.append(wires.far(piece, dst.at[mine], device))
        for (axis, kind, _), src, dst in zip(items, ins, results):
            mine = place.index(axis)
            copies.append(wires.near(src if kind == "ag" else src.at[mine], dst.at[mine]))
        wait_all(copies)

    return pl.pallas_call(
        kernel,
        out_shape=tuple(outs),
        in_specs=[ANYWHERE] * len(items),
        out_specs=tuple([ANYWHERE] * len(items)),
        scratch_shapes=[
            pltpu.SemaphoreType.DMA((n_far,)),
            pltpu.SemaphoreType.DMA((n_far,)),
            pltpu.SemaphoreType.DMA((len(items),)),
        ],
        compiler_params=pltpu.CompilerParams(collective_id=collective_id, has_side_effects=True),
        name=name,
    )(*[item[2] for item in items])


def start_kernel(dims, x, cot, ids, bias, mod, wq, w1, wp, w2):
    nc, nf = dims["nc"], dims["nf"]
    per_q, per_1 = dims["per_q"], dims["per_1"]
    chip_q, chip_1 = dims["chip_q"], dims["chip_1"]
    part_q = nc * chip_q
    rows, half = mod.shape[1], mod.shape[2]
    n_far = 5 * (nf - 1) + 3 * (nc - 1) + 4 * (nc - 1) + 4 + 1 + (nc - 1) + (nf - 1) + 1
    outs = (
        jax.ShapeDtypeStruct((nc,) + x.shape, x.dtype),
        jax.ShapeDtypeStruct((nc,) + cot.shape, cot.dtype),
        jax.ShapeDtypeStruct((nc,) + ids.shape, ids.dtype),
        jax.ShapeDtypeStruct((nf,) + bias.shape, bias.dtype),
        jax.ShapeDtypeStruct((nf, 2, rows, half), F32),
        jax.ShapeDtypeStruct((3, nc, 2, chip_q) + wq.shape[1:], BF16),
        jax.ShapeDtypeStruct((chip_1, nc, 2) + w1.shape[1:], BF16),
        jax.ShapeDtypeStruct((2, nf) + wp.shape, BF16),
        jax.ShapeDtypeStruct((2, nf) + w2.shape, BF16),
        jax.ShapeDtypeStruct((nf * per_q,) + wq.shape[1:], BF16),
        jax.ShapeDtypeStruct((nf * per_1,) + w1.shape[1:], BF16),
    )

    def kernel(
        x_in, c_in, i_in, b_in, m_in, q_in, f1_in, p_in, f2_in,
        x_all, c_all, i_all, b_all, m_all, q_chip, f1_chip, p_chip, f2_chip, q_rows, f1_rows,
        m_core, m_sum, m_chip, send, recv, local,
    ):
        place = Place(nc, nf)
        wires = Wires(send, recv, local)
        c, k, f = place.c, place.k, place.f
        greet(place, ("core", "chip", "plane"))
        core_other, core_peer = place.peer("core", 1)
        chip_peers = [place.peer("chip", step) for step in range(1, nc)]
        plane_peers = [place.peer("plane", step) for step in range(1, nf)]

        m_first = wires.far(m_in.at[core_other], m_core, core_peer)
        q_got, f1_got, p_got, f2_got, small = [], [], [], [], []
        for _, peer in plane_peers:
            q_got.append(wires.far(q_in, q_rows.at[pl.ds(f * per_q, per_q)], peer))
            small.append(wires.far(b_in, b_all.at[f], peer))
        q_got.append(wires.near(q_in, q_rows.at[pl.ds(f * per_q, per_q)]))
        small.append(wires.near(b_in, b_all.at[f]))
        for _, peer in chip_peers:
            small.append(wires.far(i_in, i_all.at[c], peer))
            small.append(wires.far(x_in, x_all.at[c], peer))
        m_first.wait()
        m_sum[...] = m_in[k] + m_core[...]
        m_chip[c] = m_sum[...]
        m_second = [wires.far(m_sum, m_chip.at[c], peer) for _, peer in chip_peers]
        for _, peer in plane_peers:
            p_got.append(wires.far(p_in, p_chip.at[k, f], peer))
        for _, peer in plane_peers:
            f1_got.append(wires.far(f1_in, f1_rows.at[pl.ds(f * per_1, per_1)], peer))
        for _, peer in plane_peers:
            f2_got.append(wires.far(f2_in, f2_chip.at[k, f], peer))
        p_got.append(wires.near(p_in, p_chip.at[k, f]))
        f1_got.append(wires.near(f1_in, f1_rows.at[pl.ds(f * per_1, per_1)]))
        f2_got.append(wires.near(f2_in, f2_chip.at[k, f]))
        small.append(wires.near(i_in, i_all.at[c]))
        small.append(wires.near(x_in, x_all.at[c]))
        for _, peer in chip_peers:
            small.append(wires.far(c_in, c_all.at[c], peer))
        small.append(wires.near(c_in, c_all.at[c]))
        wait_all(m_second)
        total = m_chip[0]
        for other in range(1, nc):
            total = total + m_chip[other]
        m_all[f, k] = total
        wait_all([wires.far(m_all.at[f, k], m_all.at[f, k], peer) for _, peer in plane_peers])
        m_last = wires.far(m_all.at[:, k], m_all.at[:, k], core_peer)

        wait_all(q_got)
        q_moved = []
        for kind in range(3):
            for other, peer in chip_peers:
                q_moved.append(
                    wires.far(
                        q_rows.at[pl.ds(kind * part_q + other * chip_q, chip_q)],
                        q_chip.at[kind, c, k],
                        peer,
                    )
                )
            q_moved.append(
                wires.near(
                    q_rows.at[pl.ds(kind * part_q + c * chip_q, chip_q)], q_chip.at[kind, c, k]
                )
            )
        wait_all(p_got)
        last = [m_last, wires.far(p_chip.at[k], p_chip.at[k], core_peer)]
        wait_all(q_moved)
        last.append(wires.far(q_chip.at[:, :, k], q_chip.at[:, :, k], core_peer))
        wait_all(f1_got)
        f1_moved = []
        for other, peer in chip_peers:
            f1_moved.append(
                wires.far(f1_rows.at[pl.ds(other * chip_1, chip_1)], f1_chip.at[:, c, k], peer)
            )
        f1_moved.append(
            wires.near(f1_rows.at[pl.ds(c * chip_1, chip_1)], f1_chip.at[:, c, k])
        )
        wait_all(f2_got)
        last.append(wires.far(f2_chip.at[k], f2_chip.at[k], core_peer))
        wait_all(f1_moved)
        last.append(wires.far(f1_chip.at[:, :, k], f1_chip.at[:, :, k], core_peer))
        wait_all(small)
        wait_all(last)

    return pl.pallas_call(
        kernel,
        out_shape=outs,
        in_specs=[ANYWHERE] * 4 + [ON_CHIP] + [ANYWHERE] * 4,
        out_specs=tuple([ANYWHERE] * 4 + [ON_CHIP] + [ANYWHERE] * 6),
        scratch_shapes=[
            pltpu.VMEM((rows, half), F32),
            pltpu.VMEM((rows, half), F32),
            pltpu.VMEM((nc, rows, half), F32),
            pltpu.SemaphoreType.DMA((n_far,)),
            pltpu.SemaphoreType.DMA((n_far,)),
            pltpu.SemaphoreType.DMA((12,)),
        ],
        compiler_params=pltpu.CompilerParams(collective_id=0, has_side_effects=True),
        name="start",
    )(x, cot, ids, bias, mod, wq, w1, wp, w2)


def sum_small_kernel(dims, terms):
    nc, nf = dims["nc"], dims["nf"]
    _, _, rows, half = terms.shape
    n_far = (nf - 1) + 1 + (nc - 1) + 1

    def kernel(t_in, total, z_got, both, core_got, chip_got, send, recv, local):
        place = Place(nc, nf)
        wires = Wires(send, recv, local)
        c, k, f = place.c, place.k, place.f
        greet(place, ("core", "chip", "plane"))
        core_other, core_peer = place.peer("core", 1)
        copies = []
        for step in range(1, nf):
            other, peer = place.peer("plane", step)
            copies.append(wires.far(t_in.at[other], z_got.at[f], peer))
        z_got[f] = t_in[f]
        wait_all(copies)
        value = z_got[0]
        for other in range(1, nf):
            value = value + z_got[other]
        both[...] = value
        wires.far(both.at[core_other], core_got, core_peer).wait()
        chip_got[c] = both[k] + core_got[...]
        copies = []
        for step in range(1, nc):
            _, peer = place.peer("chip", step)
            copies.append(wires.far(chip_got.at[c], chip_got.at[c], peer))
        wait_all(copies)
        value = chip_got[0]
        for other in range(1, nc):
            value = value + chip_got[other]
        total[k] = value
        wires.far(total.at[k], total.at[k], core_peer).wait()

    return pl.pallas_call(
        kernel,
        out_shape=jax.ShapeDtypeStruct((2, rows, half), F32),
        in_specs=[ON_CHIP],
        out_specs=ON_CHIP,
        scratch_shapes=[
            pltpu.VMEM((nf, 2, rows, half), F32),
            pltpu.VMEM((2, rows, half), F32),
            pltpu.VMEM((rows, half), F32),
            pltpu.VMEM((nc, rows, half), F32),
            pltpu.SemaphoreType.DMA((n_far,)),
            pltpu.SemaphoreType.DMA((n_far,)),
            pltpu.SemaphoreType.DMA((1,)),
        ],
        compiler_params=pltpu.CompilerParams(collective_id=1, has_side_effects=True),
        name="sum_small",
    )(terms)


def cond_kernel(dims, part):
    nc, nf = dims["nc"], dims["nf"]
    nd = 2 * nc
    rows, width = part.shape
    n_far = (nf - 1) + (nd - 1)

    def kernel(p_in, out, got, send, recv, local):
        place = Place(nc, nf)
        wires = Wires(send, recv, local)
        greet(place, ("plane", "dp"))
        copies = []
        for step in range(1, nf):
            copies.append(wires.far(p_in, got.at[place.f], place.peer("plane", step)[1]))
        got[place.f] = p_in[...]
        wait_all(copies)
        value = got[0]
        for other in range(1, nf):
            value = value + got[other]
        out[place.dp] = value
        copies = []
        for step in range(1, nd):
            copies.append(
                wires.far(out.at[place.dp], out.at[place.dp], place.peer("dp", step)[1])
            )
        wait_all(copies)

    return pl.pallas_call(
        kernel,
        out_shape=jax.ShapeDtypeStruct((nd, rows, width), F32),
        in_specs=[ON_CHIP],
        out_specs=ON_CHIP,
        scratch_shapes=[
            pltpu.VMEM((nf, rows, width), F32),
            pltpu.SemaphoreType.DMA((n_far,)),
            pltpu.SemaphoreType.DMA((n_far,)),
            pltpu.SemaphoreType.DMA((1,)),
        ],
        compiler_params=pltpu.CompilerParams(collective_id=2, has_side_effects=True),
        name="cond_sum",
    )(part)


def dot(left, right):
    return jnp.dot(left, right, preferred_element_type=F32)


def dot_rt(left, right):
    return lax.dot_general(left, right, (((1,), (1,)), ((), ())), preferred_element_type=F32)


def dot_lt(left, right):
    return lax.dot_general(left, right, (((0,), (0,)), ((), ())), preferred_element_type=F32)


def precise(left, right, dims):
    return lax.dot_general(
        left, right, (dims, ((), ())), precision=PRECISE, preferred_element_type=F32
    )


def ln_parts(values):
    centre = values - jnp.mean(values, axis=-1, keepdims=True)
    scale = lax.rsqrt(jnp.mean(centre * centre, axis=-1, keepdims=True) + EPS)
    return centre * scale, scale


def ln_back(normal, scale, grad):
    return scale * (
        grad
        - jnp.mean(grad, axis=-1, keepdims=True)
        - normal * jnp.mean(grad * normal, axis=-1, keepdims=True)
    )


def gelu_both(h):
    square = h * h
    t = jnp.tanh(GELU_C * (h + 0.044715 * h * square))
    value = 0.5 * h * (1.0 + t)
    slope = 0.5 * (1.0 + t) + 0.5 * h * (1.0 - t * t) * GELU_C * (1.0 + 3 * 0.044715 * square)
    return value, slope


def per_device(
    n_dp, nf, patches, cotangent, conditioning, frame_of_slot, clip_of_slot,
    w_ada, b_ada, w_qkv, b_qv, w_proj, b_proj, w_fc1, b_fc1, w_fc2, b_fc2,
):
    nc = n_dp // 2
    sizes = (nc, nf)
    micro, block, width = patches.shape
    own = micro * block
    clips = conditioning.shape[1]
    rows_d = width // n_dp
    cols_f = width // nf
    ff = w_fc1.shape[1] * nf
    ff_d = ff // n_dp
    chip_w = width // nc
    piece_q = math.gcd(3 * width // nf, chip_w)
    piece_1 = math.gcd(ff // nf, ff_d)
    dims = dict(
        nc=nc,
        nf=nf,
        per_q=3 * width // nf // piece_q,
        per_1=ff // nf // piece_1,
        chip_q=chip_w // piece_q,
        chip_1=ff // nc // piece_1,
    )
    dp = lax.axis_index("dp")
    f = lax.axis_index("fsdp")
    c, k = dp // 2, dp % 2

    q_send = w_qkv.reshape(rows_d, dims["per_q"], piece_q).transpose(1, 0, 2)
    f1_send = w_fc1.reshape(rows_d, dims["per_1"], piece_1).transpose(1, 0, 2)
    f2_send = w_fc2.T
    cond = conditioning.reshape(micro * clips, width)
    silu_cond = jax.nn.silu(cond)
    silu_low = silu_cond.astype(BF16)
    ada_w = w_ada.shape[1]
    silu_part = lax.dynamic_slice_in_dim(silu_low, dp * rows_d, rows_d, 1)
    mod_part = dot(silu_part, w_ada) + jnp.where(dp == 0, b_ada.astype(F32), 0.0)[None]
    mod_send = mod_part.reshape(-1, 2, ada_w // 2).transpose(1, 0, 2)
    ids = jnp.stack([frame_of_slot.reshape(own), clip_of_slot.reshape(own)])
    ids = jnp.concatenate([ids, jnp.zeros((6, own), jnp.int32)])
    bias_send = jnp.concatenate([b_qv, b_proj, b_fc1, b_fc2]).astype(F32)[None]

    (x_all, c_all, ids_all, bias_all, mod_all, q_chip, f1_chip, p_chip, f2_chip, _, _) = start_kernel(
        dims, patches.reshape(own, width), cotangent.reshape(own, width), ids, bias_send, mod_send,
        q_send, f1_send, w_proj, f2_send,
    )
    group = nc * own
    modulation = mod_all.transpose(2, 0, 1, 3).reshape(micro * clips, 6 * width)
    q_parts = [
        q_chip[i].reshape(nc, 2, dims["chip_q"], rows_d, piece_q).transpose(0, 1, 3, 2, 4).reshape(width, chip_w)
        for i in range(3)
    ]
    w1 = f1_chip.transpose(1, 2, 3, 0, 4).reshape(width, ff // nc)
    wp = p_chip.transpose(0, 2, 1, 3).reshape(chip_w, width)
    w2t = f2_chip.reshape(2, width, ff_d).transpose(1, 0, 2).reshape(width, 2 * ff_d)
    cut = [0, 2 * cols_f, 3 * cols_f, 3 * cols_f + ff // nf, 4 * cols_f + ff // nf]
    b_parts = [bias_all[:, 0, a:b].reshape(-1) for a, b in zip(cut[:-1], cut[1:])]
    bq = lax.dynamic_slice_in_dim(b_parts[0], c * chip_w, chip_w, 0)
    bv = lax.dynamic_slice_in_dim(b_parts[0], width + c * chip_w, chip_w, 0)
    b1 = lax.dynamic_slice_in_dim(b_parts[2], c * (ff // nc), ff // nc, 0)

    def hot_of(clip_ids):
        count = clip_ids.shape[0]
        row = (jnp.arange(count, dtype=jnp.int32) // block) % micro * clips + clip_ids
        return (row[:, None] == jnp.arange(micro * clips, dtype=jnp.int32)[None]).astype(F32)

    hot_group = hot_of(ids_all[:, 1].reshape(group))
    hot_own = hot_of(clip_of_slot.reshape(own))
    mod_group = precise(hot_group, modulation, ((1,), (0,)))
    mod_own = precise(hot_own, modulation, ((1,), (0,)))
    shift1, scale1 = mod_group[:, :width], mod_group[:, width : 2 * width]
    gate1 = mod_own[:, 2 * width : 3 * width]
    shift2, scale2 = mod_own[:, 3 * width : 4 * width], mod_own[:, 4 * width : 5 * width]
    gate2_group, gate2 = mod_group[:, 5 * width :], mod_own[:, 5 * width :]

    x_group = x_all.reshape(group, width).astype(F32)
    norm1, rstd1 = ln_parts(x_group)
    a_in = (norm1 * (1.0 + scale1) + shift1).astype(BF16)
    zero = jnp.zeros_like(bq)
    q, kk, v = [
        (dot(a_in, w) + b[None]).astype(BF16) for w, b in zip(q_parts, (bq, zero, bv))
    ]
    heads = chip_w // HEAD_DIM
    blocks = group // block
    q4, k4, v4 = [t.reshape(blocks, block, heads, HEAD_DIM) for t in (q, kk, v)]
    frames = ids_all[:, 0].reshape(blocks, block)
    same = (frames[:, :, None] == frames[:, None, :])[:, None]
    scores = jnp.einsum("bqhd,bkhd->bhqk", q4, k4, preferred_element_type=F32) * HEAD_DIM ** (-0.5)
    scores = jnp.where(same, scores, NEG_FILL)
    top = jnp.max(scores, axis=-1, keepdims=True)
    raised = jnp.exp(scores - top)
    probs = raised / jnp.sum(raised, axis=-1, keepdims=True)
    probs_low = probs.astype(BF16)
    mixed = jnp.einsum("bhqk,bkhd->bqhd", probs_low, v4, preferred_element_type=F32)
    mixed = mixed.reshape(group, chip_w).astype(BF16)
    attn_part = dot(mixed, wp)
    (attn_got,) = exchange(
        "attn_sum", 3, sizes, [("chip", "a2a", attn_part.astype(BF16).reshape(nc, own, width))]
    )
    attn = jnp.sum(attn_got.astype(F32), axis=0) + b_parts[1][None]
    x_own = patches.reshape(own, width).astype(F32)
    after = x_own + gate1 * attn
    norm2, rstd2 = ln_parts(after)
    m_own = (norm2 * (1.0 + scale2) + shift2).astype(BF16)
    (m_all,) = exchange("m_gather", 4, sizes, [("chip", "ag", m_own)])
    m_in = m_all.reshape(group, width)

    hidden = dot(m_in, w1) + b1[None]
    act, slope = gelu_both(hidden)
    act = act.astype(BF16)
    branch_part = dot_rt(act, w2t)
    cot_group = c_all.reshape(group, width).astype(F32)
    d_branch = (gate2_group * cot_group).astype(BF16)
    grad_2t = dot_lt(d_branch, act)
    d_hidden = (dot(d_branch, w2t) * slope).astype(BF16)
    grad_1 = dot_lt(m_in, d_hidden)
    d_m_part = dot_rt(d_hidden, w1)
    branch_got, d_m_got = exchange(
        "ff_sum",
        5,
        sizes,
        [
            ("chip", "a2a", d_m_part.astype(BF16).reshape(nc, own, width)),
            ("chip", "a2a", branch_part.astype(BF16).reshape(nc, own, width)),
        ],
    )[::-1]
    branch = jnp.sum(branch_got.astype(F32), axis=0) + b_parts[3][None]
    output = (after + gate2 * branch).astype(BF16)
    d_m = jnp.sum(d_m_got.astype(F32), axis=0)
    cot_own = cotangent.reshape(own, width).astype(F32)
    d_after = cot_own + ln_back(norm2, rstd2, d_m * (1.0 + scale2))
    d_attn = (gate1 * d_after).astype(BF16)
    (d_attn_all,) = exchange("d_attn_gather", 6, sizes, [("chip", "ag", d_attn)])
    d_attn_group = d_attn_all.reshape(group, width)
    grad_p = dot_lt(mixed, d_attn_group)
    d_mix = dot_rt(d_attn_group, wp).astype(BF16).reshape(blocks, block, heads, HEAD_DIM)
    d_probs = jnp.einsum("bqhd,bkhd->bhqk", d_mix, v4, preferred_element_type=F32)
    d_scores = probs * (d_probs - jnp.sum(probs * d_probs, axis=-1, keepdims=True))
    d_scores = d_scores.astype(BF16)
    dq = jnp.einsum("bhqk,bkhd->bqhd", d_scores, k4, preferred_element_type=F32) * HEAD_DIM ** (-0.5)
    dk = jnp.einsum("bhqk,bqhd->bkhd", d_scores, q4, preferred_element_type=F32) * HEAD_DIM ** (-0.5)
    dv = jnp.einsum("bhqk,bqhd->bkhd", probs_low, d_mix, preferred_element_type=F32)
    dqkv = [t.reshape(group, chip_w).astype(BF16) for t in (dq, dk, dv)]
    d_a_part = sum(dot_rt(t, w) for t, w in zip(dqkv, q_parts))
    grad_q = jnp.stack([dot_lt(a_in, t) for t in dqkv])
    (d_a_got,) = exchange(
        "d_a_sum", 7, sizes, [("chip", "a2a", d_a_part.astype(BF16).reshape(nc, own, width))]
    )
    d_a = jnp.sum(d_a_got.astype(F32), axis=0)
    norm1_own, rstd1_own = ln_parts(x_own)
    scale1_own = mod_own[:, width : 2 * width]
    input_grad = (d_after + ln_back(norm1_own, rstd1_own, d_a * (1.0 + scale1_own))).astype(BF16)

    g_q = grad_q.reshape(3, nc, 2, rows_d, dims["chip_q"], piece_q).transpose(2, 1, 0, 4, 3, 5)
    g_1 = grad_1.reshape(nc, 2, rows_d, dims["chip_1"], piece_1).transpose(1, 0, 3, 2, 4)
    g_p = grad_p.reshape(2, rows_d, nf, cols_f).transpose(0, 2, 1, 3)
    g_2 = grad_2t.reshape(nf, cols_f, 2, ff_d).transpose(2, 0, 1, 3)
    got = exchange("grad_core", 8, sizes, [("core", "a2a", g.astype(BF16)) for g in (g_q, g_1, g_p, g_2)])
    s_q, s_1, s_p, s_2 = [jnp.sum(g.astype(F32), axis=0).astype(BF16) for g in got]
    r_q, r_1 = exchange("grad_chip", 9, sizes, [("chip", "a2a", s_q), ("chip", "a2a", s_1)])
    z_q = r_q.transpose(1, 0, 2, 3, 4).reshape(nf, dims["per_q"], rows_d, piece_q)
    z_1 = r_1.reshape(nf, dims["per_1"], rows_d, piece_1)
    got = exchange("grad_plane", 10, sizes, [("plane", "a2a", g) for g in (z_q, z_1, s_p, s_2)])
    o_q, o_1, o_p, o_2 = [jnp.sum(g.astype(F32), axis=0) for g in got]
    grad_w_qkv = o_q.transpose(1, 0, 2).reshape(rows_d, 3 * width // nf)
    grad_w_fc1 = o_1.transpose(1, 0, 2).reshape(rows_d, ff // nf)
    grad_w_fc2 = o_2.T

    d_token = jnp.concatenate(
        [d_a, d_a * norm1_own, d_after * attn, d_m, d_m * norm2, cot_own * branch], axis=1
    )
    d_mod = precise(hot_own, d_token, ((0,), (0,)))
    d_branch_own = (gate2 * cot_own).astype(BF16).astype(F32)

    def columns(value):
        return jnp.sum(value.astype(F32), axis=0)

    def spread(value, count):
        return lax.dynamic_update_slice_in_dim(
            jnp.zeros((count,), F32), value, c * value.shape[0], 0
        )

    g_bqv = jnp.concatenate([spread(columns(dqkv[0]), width), spread(columns(dqkv[2]), width)])
    g_b1 = spread(columns(d_hidden), ff)
    bias_terms = jnp.concatenate(
        [
            g_bqv.reshape(nf, -1),
            columns(d_attn).reshape(nf, -1),
            g_b1.reshape(nf, -1),
            columns(d_branch_own).reshape(nf, -1),
        ],
        axis=1,
    )
    n_bias = bias_terms.shape[1]
    bias_rows = -(-n_bias // ada_w)
    bias_terms = jnp.pad(bias_terms, ((0, 0), (0, bias_rows * ada_w - n_bias)))
    terms = jnp.concatenate(
        [d_mod.reshape(micro * clips, nf, ada_w).transpose(1, 0, 2), bias_terms.reshape(nf, bias_rows, ada_w)],
        axis=1,
    )
    pad_rows = -terms.shape[1] % 8
    terms = jnp.pad(terms, ((0, 0), (0, pad_rows), (0, 0)))
    terms = terms.reshape(nf, -1, 2, ada_w // 2).transpose(0, 2, 1, 3)
    total = sum_small_kernel(dims, terms).transpose(1, 0, 2).reshape(-1, ada_w)
    d_cols = total[: micro * clips]
    bias_sums = total[micro * clips : micro * clips + bias_rows].reshape(-1)[:n_bias]
    g_parts = [bias_sums[a:b] for a, b in zip(cut[:-1], cut[1:])]
    grad_w_ada = precise(silu_part.astype(F32), d_cols, ((0,), (0,)))
    grad_b_ada = jnp.sum(d_cols, axis=0)
    d_silu_part = precise(d_cols, w_ada.astype(F32), ((1,), (1,)))
    d_silu = cond_kernel(dims, d_silu_part).transpose(1, 0, 2).reshape(micro * clips, width)
    d_silu_own = lax.dynamic_slice_in_dim(d_silu, f * cols_f, cols_f, 1)
    cond_own = lax.dynamic_slice_in_dim(cond, f * cols_f, cols_f, 1)
    _, silu_back = jax.vjp(jax.nn.silu, cond_own)
    cond_grad = silu_back(d_silu_own)[0].reshape(micro, clips, cols_f)
    return (
        output.reshape(patches.shape),
        input_grad.reshape(patches.shape),
        cond_grad,
        grad_w_ada,
        grad_b_ada,
        grad_w_qkv,
        g_parts[0],
        o_p,
        g_parts[1],
        grad_w_fc1,
        g_parts[2],
        grad_w_fc2,
        g_parts[3],
    )


def solution(mesh):
    tokens = P(None, ("dp", "fsdp"), None)
    ids = P(None, ("dp", "fsdp"))
    both, cols = P("dp", "fsdp"), P("fsdp")
    in_specs = (tokens, tokens, P(), ids, ids) + (both, cols) * 5
    out_specs = (tokens, tokens, P(None, None, "fsdp")) + (both, cols) * 5
    return jax.shard_map(
        functools.partial(per_device, mesh.shape["dp"], mesh.shape["fsdp"]),
        mesh=mesh,
        in_specs=in_specs,
        out_specs=out_specs,
        check_vma=False,
    )
```

```python
import functools
import math
import types

import jax
import jax.numpy as jnp
from jax import lax
from jax.experimental import pallas as pl
from jax.experimental.pallas import tpu as pltpu
from jax.sharding import PartitionSpec as P

HEAD_DIM = 72
EPS = 1e-06
GELU_C = math.sqrt(2.0 / math.pi)
PRECISE = lax.Precision.HIGHEST
NEG_FILL = -1e30
SUB = 16
CORE, CHIP, PLANE, ALL = range(4)
GATHER, SPREAD = range(2)
MESH_ID = pl.DeviceIdType.MESH
F32 = jnp.float32
BF16 = jnp.bfloat16


def xor_of(index, step, size):
    result, bit = 0, 1
    while bit < size:
        mine = (index // bit) % 2
        result = result + ((mine + (step // bit) % 2) % 2) * bit
        bit *= 2
    return result


class Place:
    def __init__(self, n_chip, n_plane):
        self.n = {CORE: 2, CHIP: n_chip, PLANE: n_plane, ALL: 2 * n_chip}
        self.dp = lax.axis_index("dp")
        self.f = lax.axis_index("fsdp")
        self.c = self.dp // 2
        self.k = self.dp % 2

    def index(self, axis):
        return {CORE: self.k, CHIP: self.c, PLANE: self.f, ALL: self.dp}[axis]

    def peer(self, axis, step):
        other = xor_of(self.index(axis), step, self.n[axis])
        if axis == CORE:
            return other, (self.c * 2 + other, self.f)
        if axis == CHIP:
            return other, (other * 2 + self.k, self.f)
        if axis == PLANE:
            return other, (self.dp, other)
        return other, (other, self.f)


def greet(place, axes):
    barrier = pltpu.get_barrier_semaphore()
    count = 0
    for axis in axes:
        for step in range(1, place.n[axis]):
            pl.semaphore_signal(
                barrier, inc=1, device_id=place.peer(axis, step)[1], device_id_type=MESH_ID
            )
            count += 1
    pl.semaphore_wait(barrier, count)


class Wires:
    def __init__(self, send, recv, local):
        self.send, self.recv, self.local = send, recv, local
        self.remote_count = 0
        self.local_count = 0

    def far(self, src, dst, device):
        at = self.remote_count
        self.remote_count += 1
        copy = pltpu.make_async_remote_copy(
            src_ref=src,
            dst_ref=dst,
            send_sem=self.send.at[at],
            recv_sem=self.recv.at[at],
            device_id=device,
            device_id_type=MESH_ID,
        )
        copy.start()
        return copy

    def near(self, src, dst):
        at = self.local_count
        self.local_count += 1
        copy = pltpu.make_async_copy(src, dst, self.local.at[at])
        copy.start()
        return copy


def wait_all(copies):
    for copy in copies:
        copy.wait()


ANYWHERE = pl.BlockSpec(memory_space=pl.ANY)
ON_CHIP = pl.BlockSpec(memory_space=pltpu.VMEM)


def exchange(name, collective_id, sizes, items):
    n_chip, n_plane = sizes
    n_of = {CORE: 2, CHIP: n_chip, PLANE: n_plane, ALL: 2 * n_chip}
    axes = sorted({item[0] for item in items})
    outs = []
    n_far = 0
    for axis, kind, array in items:
        n_far += n_of[axis] - 1
        shape = array.shape if kind == SPREAD else (n_of[axis],) + array.shape
        outs.append(jax.ShapeDtypeStruct(shape, array.dtype))

    def kernel(*refs):
        ins = refs[: len(items)]
        results = refs[len(items) : 2 * len(items)]
        place = Place(n_chip, n_plane)
        wires = Wires(*refs[2 * len(items) :])
        greet(place, axes)
        copies = []
        for (axis, kind, _), src, dst in zip(items, ins, results):
            mine = place.index(axis)
            for step in range(1, n_of[axis]):
                other, device = place.peer(axis, step)
                piece = src if kind == GATHER else src.at[other]
                copies.append(wires.far(piece, dst.at[mine], device))
        for (axis, kind, _), src, dst in zip(items, ins, results):
            mine = place.index(axis)
            copies.append(wires.near(src if kind == GATHER else src.at[mine], dst.at[mine]))
        wait_all(copies)

    return pl.pallas_call(
        kernel,
        out_shape=tuple(outs),
        in_specs=[ANYWHERE] * len(items),
        out_specs=tuple([ANYWHERE] * len(items)),
        scratch_shapes=[
            pltpu.SemaphoreType.DMA((n_far,)),
            pltpu.SemaphoreType.DMA((n_far,)),
            pltpu.SemaphoreType.DMA((len(items),)),
        ],
        compiler_params=pltpu.CompilerParams(collective_id=collective_id, has_side_effects=True),
        name=name,
    )(*[item[2] for item in items])


def start_kernel(dims, x, cot, ids, bias, mod, wq, w1, wp, w2):
    nc, nf = dims.nc, dims.nf
    per_q, per_1 = dims.per_q, dims.per_1
    chip_q, chip_1 = dims.chip_q, dims.chip_1
    part_q = nc * chip_q
    rows, half = mod.shape[1], mod.shape[2]
    n_far = 5 * (nf - 1) + 3 * (nc - 1) + 4 * (nc - 1) + 4 + 1 + (nc - 1) + (nf - 1) + 1
    outs = (
        jax.ShapeDtypeStruct((nc,) + x.shape, x.dtype),
        jax.ShapeDtypeStruct((nc,) + cot.shape, cot.dtype),
        jax.ShapeDtypeStruct((nc,) + ids.shape, ids.dtype),
        jax.ShapeDtypeStruct((nf,) + bias.shape, bias.dtype),
        jax.ShapeDtypeStruct((nf, 2, rows, half), F32),
        jax.ShapeDtypeStruct((3, nc, 2, chip_q) + wq.shape[1:], BF16),
        jax.ShapeDtypeStruct((chip_1, nc, 2) + w1.shape[1:], BF16),
        jax.ShapeDtypeStruct((2, nf) + wp.shape, BF16),
        jax.ShapeDtypeStruct((2, nf) + w2.shape, BF16),
        jax.ShapeDtypeStruct((nf * per_q,) + wq.shape[1:], BF16),
        jax.ShapeDtypeStruct((nf * per_1,) + w1.shape[1:], BF16),
    )

    def kernel(
        x_in, c_in, i_in, b_in, m_in, q_in, f1_in, p_in, f2_in,
        x_all, c_all, i_all, b_all, m_all, q_chip, f1_chip, p_chip, f2_chip, q_rows, f1_rows,
        m_core, m_sum, m_chip, send, recv, local,
    ):
        place = Place(nc, nf)
        wires = Wires(send, recv, local)
        c, k, f = place.c, place.k, place.f
        greet(place, (CORE, CHIP, PLANE))
        core_other, core_peer = place.peer(CORE, 1)
        chip_peers = [place.peer(CHIP, step) for step in range(1, nc)]
        plane_peers = [place.peer(PLANE, step) for step in range(1, nf)]

        m_first = wires.far(m_in.at[core_other], m_core, core_peer)
        q_got, f1_got, p_got, f2_got, small = [], [], [], [], []
        for _, peer in plane_peers:
            q_got.append(wires.far(q_in, q_rows.at[pl.ds(f * per_q, per_q)], peer))
            small.append(wires.far(b_in, b_all.at[f], peer))
        q_got.append(wires.near(q_in, q_rows.at[pl.ds(f * per_q, per_q)]))
        small.append(wires.near(b_in, b_all.at[f]))
        for _, peer in chip_peers:
            small.append(wires.far(i_in, i_all.at[c], peer))
            small.append(wires.far(x_in, x_all.at[c], peer))
        m_first.wait()
        m_sum[...] = m_in[k] + m_core[...]
        m_chip[c] = m_sum[...]
        m_second = [wires.far(m_sum, m_chip.at[c], peer) for _, peer in chip_peers]
        for _, peer in plane_peers:
            p_got.append(wires.far(p_in, p_chip.at[k, f], peer))
        for _, peer in plane_peers:
            f1_got.append(wires.far(f1_in, f1_rows.at[pl.ds(f * per_1, per_1)], peer))
        for _, peer in plane_peers:
            f2_got.append(wires.far(f2_in, f2_chip.at[k, f], peer))
        p_got.append(wires.near(p_in, p_chip.at[k, f]))
        f1_got.append(wires.near(f1_in, f1_rows.at[pl.ds(f * per_1, per_1)]))
        f2_got.append(wires.near(f2_in, f2_chip.at[k, f]))
        small.append(wires.near(i_in, i_all.at[c]))
        small.append(wires.near(x_in, x_all.at[c]))
        for _, peer in chip_peers:
            small.append(wires.far(c_in, c_all.at[c], peer))
        small.append(wires.near(c_in, c_all.at[c]))
        wait_all(m_second)
        total = m_chip[0]
        for other in range(1, nc):
            total = total + m_chip[other]
        m_all[f, k] = total
        wait_all([wires.far(m_all.at[f, k], m_all.at[f, k], peer) for _, peer in plane_peers])
        m_last = wires.far(m_all.at[:, k], m_all.at[:, k], core_peer)

        wait_all(q_got)
        q_moved = []
        for kind in range(3):
            for other, peer in chip_peers:
                q_moved.append(
                    wires.far(
                        q_rows.at[pl.ds(kind * part_q + other * chip_q, chip_q)],
                        q_chip.at[kind, c, k],
                        peer,
                    )
                )
            q_moved.append(
                wires.near(
                    q_rows.at[pl.ds(kind * part_q + c * chip_q, chip_q)], q_chip.at[kind, c, k]
                )
            )
        wait_all(p_got)
        last = [m_last, wires.far(p_chip.at[k], p_chip.at[k], core_peer)]
        wait_all(q_moved)
        last.append(wires.far(q_chip.at[:, :, k], q_chip.at[:, :, k], core_peer))
        wait_all(f1_got)
        f1_moved = []
        for other, peer in chip_peers:
            f1_moved.append(
                wires.far(f1_rows.at[pl.ds(other * chip_1, chip_1)], f1_chip.at[:, c, k], peer)
            )
        f1_moved.append(
            wires.near(f1_rows.at[pl.ds(c * chip_1, chip_1)], f1_chip.at[:, c, k])
        )
        wait_all(f2_got)
        last.append(wires.far(f2_chip.at[k], f2_chip.at[k], core_peer))
        wait_all(f1_moved)
        last.append(wires.far(f1_chip.at[:, :, k], f1_chip.at[:, :, k], core_peer))
        wait_all(small)
        wait_all(last)

    return pl.pallas_call(
        kernel,
        out_shape=outs,
        in_specs=[ANYWHERE] * 4 + [ON_CHIP] + [ANYWHERE] * 4,
        out_specs=tuple([ANYWHERE] * 4 + [ON_CHIP] + [ANYWHERE] * 6),
        scratch_shapes=[
            pltpu.VMEM((rows, half), F32),
            pltpu.VMEM((rows, half), F32),
            pltpu.VMEM((nc, rows, half), F32),
            pltpu.SemaphoreType.DMA((n_far,)),
            pltpu.SemaphoreType.DMA((n_far,)),
            pltpu.SemaphoreType.DMA((12,)),
        ],
        compiler_params=pltpu.CompilerParams(collective_id=0, has_side_effects=True),
        name="start",
    )(x, cot, ids, bias, mod, wq, w1, wp, w2)


def sum_small_kernel(dims, terms):
    nc, nf = dims.nc, dims.nf
    _, _, rows, half = terms.shape
    n_far = (nf - 1) + 1 + (nc - 1) + 1

    def kernel(t_in, total, z_got, both, core_got, chip_got, send, recv, local):
        place = Place(nc, nf)
        wires = Wires(send, recv, local)
        c, k, f = place.c, place.k, place.f
        greet(place, (CORE, CHIP, PLANE))
        core_other, core_peer = place.peer(CORE, 1)
        copies = []
        for step in range(1, nf):
            other, peer = place.peer(PLANE, step)
            copies.append(wires.far(t_in.at[other], z_got.at[f], peer))
        z_got[f] = t_in[f]
        wait_all(copies)
        value = z_got[0]
        for other in range(1, nf):
            value = value + z_got[other]
        both[...] = value
        wires.far(both.at[core_other], core_got, core_peer).wait()
        chip_got[c] = both[k] + core_got[...]
        copies = []
        for step in range(1, nc):
            _, peer = place.peer(CHIP, step)
            copies.append(wires.far(chip_got.at[c], chip_got.at[c], peer))
        wait_all(copies)
        value = chip_got[0]
        for other in range(1, nc):
            value = value + chip_got[other]
        total[k] = value
        wires.far(total.at[k], total.at[k], core_peer).wait()

    return pl.pallas_call(
        kernel,
        out_shape=jax.ShapeDtypeStruct((2, rows, half), F32),
        in_specs=[ON_CHIP],
        out_specs=ON_CHIP,
        scratch_shapes=[
            pltpu.VMEM((nf, 2, rows, half), F32),
            pltpu.VMEM((2, rows, half), F32),
            pltpu.VMEM((rows, half), F32),
            pltpu.VMEM((nc, rows, half), F32),
            pltpu.SemaphoreType.DMA((n_far,)),
            pltpu.SemaphoreType.DMA((n_far,)),
            pltpu.SemaphoreType.DMA((1,)),
        ],
        compiler_params=pltpu.CompilerParams(collective_id=1, has_side_effects=True),
        name="sum_small",
    )(terms)


def cond_kernel(dims, part):
    nc, nf = dims.nc, dims.nf
    nd = 2 * nc
    rows, width = part.shape
    n_far = (nf - 1) + (nd - 1)

    def kernel(p_in, out, got, send, recv, local):
        place = Place(nc, nf)
        wires = Wires(send, recv, local)
        greet(place, (PLANE, ALL))
        copies = []
        for step in range(1, nf):
            copies.append(wires.far(p_in, got.at[place.f], place.peer(PLANE, step)[1]))
        got[place.f] = p_in[...]
        wait_all(copies)
        value = got[0]
        for other in range(1, nf):
            value = value + got[other]
        out[place.dp] = value
        copies = []
        for step in range(1, nd):
            copies.append(
                wires.far(out.at[place.dp], out.at[place.dp], place.peer(ALL, step)[1])
            )
        wait_all(copies)

    return pl.pallas_call(
        kernel,
        out_shape=jax.ShapeDtypeStruct((nd, rows, width), F32),
        in_specs=[ON_CHIP],
        out_specs=ON_CHIP,
        scratch_shapes=[
            pltpu.VMEM((nf, rows, width), F32),
            pltpu.SemaphoreType.DMA((n_far,)),
            pltpu.SemaphoreType.DMA((n_far,)),
            pltpu.SemaphoreType.DMA((1,)),
        ],
        compiler_params=pltpu.CompilerParams(collective_id=2, has_side_effects=True),
        name="cond_sum",
    )(part)


def dot(left, right):
    return jnp.dot(left, right, preferred_element_type=F32)


def dot_rt(left, right):
    return lax.dot_general(left, right, (((1,), (1,)), ((), ())), preferred_element_type=F32)


def dot_lt(left, right):
    return lax.dot_general(left, right, (((0,), (0,)), ((), ())), preferred_element_type=F32)


def precise(left, right, dims):
    return lax.dot_general(
        left, right, (dims, ((), ())), precision=PRECISE, preferred_element_type=F32
    )


def ln_parts(values):
    centre = values - jnp.mean(values, axis=-1, keepdims=True)
    scale = lax.rsqrt(jnp.mean(centre * centre, axis=-1, keepdims=True) + EPS)
    return centre * scale, scale


def ln_back(normal, scale, grad):
    return scale * (
        grad
        - jnp.mean(grad, axis=-1, keepdims=True)
        - normal * jnp.mean(grad * normal, axis=-1, keepdims=True)
    )


def gelu_both(h):
    square = h * h
    t = jnp.tanh(GELU_C * (h + 0.044715 * h * square))
    value = 0.5 * h * (1.0 + t)
    slope = 0.5 * (1.0 + t) + 0.5 * h * (1.0 - t * t) * GELU_C * (1.0 + 3 * 0.044715 * square)
    return value, slope


def block_kernel(dims, x, cot, mask, hot, bias, mod, wq, w1, wp, w2):
    nc, nf = dims.nc, dims.nf
    own, width = x.shape
    group = nc * own
    per_q, rows_d, chip_w = wq.shape
    per_1, _, ff_d = w1.shape
    cols_f = w2.shape[0]
    pad_p = wp.shape[1]
    step_p = dims.step_p
    heads = chip_w // HEAD_DIM
    n_rows = mod.shape[1]
    n_sub = own // SUB
    head_scale = HEAD_DIM ** (-0.5)

    outs = (
        jax.ShapeDtypeStruct((own, width), BF16),
        jax.ShapeDtypeStruct((own, width), BF16),
        jax.ShapeDtypeStruct((per_q, rows_d, chip_w), F32),
        jax.ShapeDtypeStruct((per_1, rows_d, ff_d), F32),
        jax.ShapeDtypeStruct((rows_d, pad_p), F32),
        jax.ShapeDtypeStruct((cols_f, ff_d), F32),
        jax.ShapeDtypeStruct((2, n_rows, width), F32),
        jax.ShapeDtypeStruct((nc, 8, width), F32),
    )
    tokens = (nc, own, width)
    n_sem = 160
    scratch = dict(
        xg=pltpu.VMEM(tokens, BF16),
        cg=pltpu.VMEM(tokens, BF16),
        maskg=pltpu.VMEM((nc, own, own), BF16),
        hotg=pltpu.VMEM((nc, n_sub, 128), F32),
        biasg=pltpu.VMEM((nf, 8, width), F32),
        m_core=pltpu.VMEM((n_rows, width), F32),
        m_chip=pltpu.VMEM((nc, n_rows, width), F32),
        m_win=pltpu.VMEM((nf, 2, n_rows, width), F32),
        tab=pltpu.VMEM((3, nc * n_sub, width), F32),
        own_tab=pltpu.VMEM((6, n_sub, width), F32),
        q_rows=pltpu.VMEM((nf * per_q, rows_d, chip_w), BF16),
        f1_rows=pltpu.VMEM((nf * per_1, rows_d, ff_d), BF16),
        w_q=pltpu.VMEM((3, nc, 2, rows_d, chip_w), BF16),
        w_1=pltpu.VMEM((2, nc, 2, rows_d, ff_d), BF16),
        p_got=pltpu.VMEM((2, nf, rows_d, pad_p), BF16),
        w_p=pltpu.VMEM((chip_w, width), BF16),
        w_2=pltpu.VMEM((2, nf, cols_f, ff_d), BF16),
        a_in=pltpu.VMEM(tokens, BF16),
        qkv=pltpu.VMEM((3, nc, own, chip_w), BF16),
        probs=pltpu.VMEM((nc * heads, own, own), F32),
        mixed=pltpu.VMEM((nc, own, chip_w), BF16),
        sum_s=pltpu.VMEM(tokens, BF16),
        sum_r=pltpu.VMEM(tokens, BF16),
        br_s=pltpu.VMEM(tokens, BF16),
        br_r=pltpu.VMEM(tokens, BF16),
        m_all=pltpu.VMEM(tokens, BF16),
        da_all=pltpu.VMEM(tokens, BF16),
        attn=pltpu.VMEM((own, width), F32),
        after=pltpu.VMEM((own, width), F32),
        d_after=pltpu.VMEM((own, width), F32),
        hid=pltpu.VMEM((2, own, ff_d), F32),
        slope=pltpu.VMEM((2, own, ff_d), F32),
        act=pltpu.VMEM((2, nc, own, ff_d), BF16),
        d_hid=pltpu.VMEM((2, nc, own, ff_d), BF16),
        dbr=pltpu.VMEM(tokens, BF16),
        d_qkv=pltpu.VMEM((3, nc, own, chip_w), BF16),
        g_2=pltpu.VMEM((2, nf, cols_f, ff_d), BF16),
        g_2r=pltpu.VMEM((nf, cols_f, ff_d), BF16),
        g_1=pltpu.VMEM((2, nc, 2, rows_d, ff_d), BF16),
        g_1r=pltpu.VMEM((2, nc, rows_d, ff_d), BF16),
        g_q=pltpu.VMEM((3, nc, 2, rows_d, chip_w), BF16),
        g_qr=pltpu.VMEM((3, nc, rows_d, chip_w), BF16),
        g_p=pltpu.VMEM((2, rows_d, width), BF16),
        g_pr=pltpu.VMEM((rows_d, width), BF16),
        z_q=pltpu.VMEM((nf, per_q, rows_d, chip_w), BF16),
        z_1=pltpu.VMEM((nf, per_1, rows_d, ff_d), BF16),
        z_p=pltpu.VMEM((nf, rows_d, pad_p), BF16),
        z_2=pltpu.VMEM((nf, cols_f, ff_d), BF16),
        sub=pltpu.VMEM((6, n_sub, width), F32),
        d_mod=pltpu.VMEM((6, n_rows, width), F32),
        d_bias=pltpu.VMEM((8, width), F32),
        dz=pltpu.VMEM((nf, 2, n_rows, width), F32),
        dzb=pltpu.VMEM((nf, 8, width), F32),
        d_both=pltpu.VMEM((2, n_rows, width), F32),
        d_bsum=pltpu.VMEM((8, width), F32),
        d_coreb=pltpu.VMEM((8, width), F32),
        send=pltpu.SemaphoreType.DMA((n_sem,)),
        recv=pltpu.SemaphoreType.DMA((n_sem,)),
        local=pltpu.SemaphoreType.DMA((32,)),
    )
    names = list(scratch)

    def kernel(
        x_in, c_in, mask_in, hot_in, bias_in, mod_in, q_in, f1_in, p_in, f2_in,
        out, x_grad, o_q, o_1, o_p, o_2, o_mod, o_bias, *rest,
    ):
        r = types.SimpleNamespace(**dict(zip(names, rest)))
        place = Place(nc, nf)
        wires = Wires(r.send, r.recv, r.local)
        c, k, f = place.c, place.k, place.f
        core_o, core_dev = place.peer(CORE, 1)
        chip_peers = [place.peer(CHIP, step) for step in range(1, nc)]
        plane_peers = [place.peer(PLANE, step) for step in range(1, nf)]

        def loop(count, body):
            def run(i, carry):
                body(i)
                return carry

            lax.fori_loop(0, count, run, 0)

        def sub_rows(g):
            return pl.ds(pl.multiple_of(g * SUB, SUB), SUB)

        def chip_send(src, dst, base, step):
            other, device = place.peer(CHIP, step)
            return pltpu.make_async_remote_copy(
                src_ref=src(other),
                dst_ref=dst.at[c],
                send_sem=r.send.at[base + step - 1],
                recv_sem=r.recv.at[base + step - 1],
                device_id=device,
                device_id_type=MESH_ID,
            )

        def reserve(count):
            base = wires.remote_count
            wires.remote_count += count
            return base

        greet(place, (CORE, CHIP, PLANE))

        w_q, q_rows = r.w_q, r.q_rows
        m_first = wires.far(mod_in.at[core_o], r.m_core, core_dev)
        q_far = [
            wires.far(q_in, q_rows.at[pl.ds(f * per_q, per_q)], peer) for _, peer in plane_peers
        ]
        first = []
        for _, peer in chip_peers:
            first.append(wires.far(hot_in, r.hotg.at[c], peer))
            first.append(wires.far(x_in, r.xg.at[c], peer))
            first.append(wires.far(mask_in, r.maskg.at[c], peer))
        for _, peer in plane_peers:
            first.append(wires.far(bias_in, r.biasg.at[f], peer))
        first.append(wires.near(hot_in, r.hotg.at[c]))
        first.append(wires.near(x_in, r.xg.at[c]))
        first.append(wires.near(mask_in, r.maskg.at[c]))
        first.append(wires.near(bias_in, r.biasg.at[f]))

        q_base = reserve(3 * nc)
        q_local = wires.local_count
        wires.local_count += 3

        def q_piece(plane, source, at, i):
            piece = per_q * plane + i
            kind, chip = piece // nc, piece % nc
            src = source.at[at]
            dst = w_q.at[kind, c, k]
            far = pltpu.make_async_remote_copy(
                src_ref=src,
                dst_ref=dst,
                send_sem=r.send.at[q_base + kind * nc + chip],
                recv_sem=r.recv.at[q_base + kind * nc + c],
                device_id=(chip * 2 + k, f),
                device_id_type=MESH_ID,
            )
            near = pltpu.make_async_copy(src, dst, r.local.at[q_local + kind])
            return chip, far, near

        def q_forward(plane, source, at_of):
            for i in range(per_q):
                chip, far, near = q_piece(plane, source, at_of(i), i)

                @pl.when(chip != c)
                def _():
                    far.start()

                @pl.when(chip == c)
                def _():
                    near.start()

        q_forward(f, q_in, lambda i: i)
        m_first.wait()
        m_chip = r.m_chip
        m_chip[c] = mod_in[k] + r.m_core[...]
        m_second = [wires.far(m_chip.at[c], m_chip.at[c], peer) for _, peer in chip_peers]
        q_forward_order = []
        for step, copy in enumerate(q_far, 1):
            copy.wait_recv()
            plane = xor_of(f, step, nf)
            q_forward(plane, q_rows, lambda i: per_q * plane + i)
            if step == 1:
                wait_all(m_second)
                total = m_chip[0]
                for other in range(1, nc):
                    total = total + m_chip[other]
                r.m_win[f, k] = total
                m_third = [
                    wires.far(r.m_win.at[f, k], r.m_win.at[f, k], peer)
                    for _, peer in plane_peers
                ]
        p_far = [wires.far(p_in, r.p_got.at[k, f], peer) for _, peer in plane_peers]
        f1_rows = r.f1_rows
        f1_far = [
            wires.far(f1_in, f1_rows.at[pl.ds(f * per_1, per_1)], peer) for _, peer in plane_peers
        ]
        f2_far = [wires.far(f2_in, r.w_2.at[k, f], peer) for _, peer in plane_peers]
        p_far.append(wires.near(p_in, r.p_got.at[k, f]))
        f1_far.append(wires.near(f1_in, f1_rows.at[pl.ds(f * per_1, per_1)]))
        f2_far.append(wires.near(f2_in, r.w_2.at[k, f]))
        wait_all(m_third)
        m_last = wires.far(r.m_win.at[:, k], r.m_win.at[:, k], core_dev)
        for copy in q_far:
            copy.wait_send()
        q_core = []
        for kind in range(3):
            for other, _ in chip_peers:
                pltpu.make_async_remote_copy(
                    src_ref=w_q.at[kind, other, k],
                    dst_ref=w_q.at[kind, other, k],
                    send_sem=r.send.at[q_base + kind * nc + other],
                    recv_sem=r.recv.at[q_base + kind * nc + other],
                    device_id=core_dev,
                    device_id_type=MESH_ID,
                ).wait()
            pltpu.make_async_copy(
                w_q.at[kind, c, k], w_q.at[kind, c, k], r.local.at[q_local + kind]
            ).wait()
            q_core.append(wires.far(w_q.at[kind, :, k], w_q.at[kind, :, k], core_dev))

        wait_all(first)
        m_last.wait()
        hot_rows = r.hotg[...].reshape(nc * n_sub, 128)[:, :n_rows]
        places = lax.broadcasted_iota(jnp.int32, (nc * n_sub, n_rows), 1).astype(F32)
        hot_of = jnp.where(hot_rows == places, 1.0, 0.0)
        own_hot = r.hotg[c][:, :n_rows]
        own_hot = jnp.where(
            own_hot == lax.broadcasted_iota(jnp.int32, (n_sub, n_rows), 1).astype(F32), 1.0, 0.0
        )
        starts = [6 * plane // nf for plane in range(nf)]
        for kind in range(6):
            value = None
            for plane in range(nf):
                if 0 <= kind - starts[plane] < 2:
                    term = r.m_win[plane, kind - starts[plane]]
                    value = term if value is None else value + term
            if kind in (0, 1, 5):
                r.tab[kind % 3] = jnp.dot(hot_of, value, precision=PRECISE, preferred_element_type=F32)
            r.own_tab[kind] = jnp.dot(own_hot, value, precision=PRECISE, preferred_element_type=F32)

        def tab_row(kind, blk, g):
            return r.tab[kind % 3, pl.ds(blk * n_sub + g, 1), :]

        def own_row(kind, g):
            return r.own_tab[kind, pl.ds(g, 1), :]

        def make_a(blk):
            def body(g):
                rows = sub_rows(g)
                normal, _ = ln_parts(r.xg[blk, rows, :].astype(F32))
                value = normal * (1.0 + tab_row(1, blk, g)) + tab_row(0, blk, g)
                r.a_in[blk, rows, :] = value.astype(BF16)

            loop(n_sub, body)

        loop(nc, make_a)
        c_far = [wires.far(c_in, r.cg.at[c], peer) for _, peer in chip_peers]
        c_far.append(wires.near(c_in, r.cg.at[c]))

        wait_all(p_far)
        p_core = wires.far(r.p_got.at[k], r.p_got.at[k], core_dev)
        wait_all(q_core)
        p_core.wait()
        blocks_p = width // 128
        for half in range(2):
            for j in range(blocks_p):
                value = None
                for plane in range(nf):
                    at = j * 128 - plane * step_p
                    if 0 <= at < pad_p:
                        term = r.p_got[half, plane, :, at : at + 128]
                        value = term if value is None else value + term
                r.w_p[half * rows_d : (half + 1) * rows_d, j * 128 : (j + 1) * 128] = value
        lane = lax.broadcasted_iota(jnp.int32, (1, chip_w), 1)
        head_of = [
            jnp.where((lane >= HEAD_DIM * h) & (lane < HEAD_DIM * (h + 1)), 1.0, 0.0).astype(BF16)
            for h in range(heads)
        ]

        def weight_q(kind):
            return w_q[kind].reshape(width, chip_w)

        b_row = pl.ds(2 + c % 2, 1)
        bias_q = r.biasg[c // 2, b_row, pl.ds(0, chip_w)]
        bias_v = r.biasg[nc // 2 + c // 2, b_row, pl.ds(0, chip_w)]
        sum_base = reserve(nc - 1)
        sum_s, sum_r = r.sum_s, r.sum_r

        def attend(i):
            step = (i + 1) % nc
            blk = xor_of(c, step, nc)
            a_now = r.a_in[blk]
            r.qkv[0, blk] = (dot(a_now, weight_q(0)) + bias_q).astype(BF16)
            r.qkv[1, blk] = dot(a_now, weight_q(1)).astype(BF16)
            r.qkv[2, blk] = (dot(a_now, weight_q(2)) + bias_v).astype(BF16)
            q_now, k_now, v_now = r.qkv[0, blk], r.qkv[1, blk], r.qkv[2, blk]
            same = r.maskg[blk].astype(F32) > 0.5
            mixed = jnp.zeros((own, chip_w), F32)
            for h in range(heads):
                scores = dot_rt(q_now * head_of[h], k_now) * head_scale
                scores = jnp.where(same, scores, NEG_FILL)
                raised = jnp.exp(scores - jnp.max(scores, axis=-1, keepdims=True))
                share = raised / jnp.sum(raised, axis=-1, keepdims=True)
                r.probs[blk * heads + h] = share
                mixed = mixed + dot(share.astype(BF16), v_now * head_of[h])
            mixed = mixed.astype(BF16)
            r.mixed[blk] = mixed
            part = dot(mixed, r.w_p[...]).astype(BF16)

            @pl.when(step != 0)
            def _():
                sum_s[blk] = part
                chip_send(lambda other: sum_s.at[other], sum_r, sum_base, step).start()

            @pl.when(step == 0)
            def _():
                sum_r[c] = part

        loop(nc, attend)

        wait_all(f1_far)
        f1_moved = [
            wires.far(f1_rows.at[pl.ds(other * per_1, per_1)], r.w_1.at[:, c, k], peer)
            for other, peer in chip_peers
        ]
        f1_moved.append(
            wires.near(f1_rows.at[pl.ds(c * per_1, per_1)], r.w_1.at[:, c, k])
        )

        for step in range(1, nc):
            chip_send(lambda other: sum_s.at[other], sum_r, sum_base, step).wait()
        bias_p = r.biasg[0, 0:1, :]
        bias_o = r.biasg[0, 1:2, :]
        for plane in range(1, nf):
            bias_p = bias_p + r.biasg[plane, 0:1, :]
            bias_o = bias_o + r.biasg[plane, 1:2, :]

        def after_attention(g):
            rows = sub_rows(g)
            value = sum_r[0, rows, :].astype(F32)
            for other in range(1, nc):
                value = value + sum_r[other, rows, :].astype(F32)
            value = value + bias_p
            r.attn[rows, :] = value
            after = r.xg[c, rows, :].astype(F32) + own_row(2, g) * value
            r.after[rows, :] = after
            normal, _ = ln_parts(after)
            r.m_all[c, rows, :] = (normal * (1.0 + own_row(4, g)) + own_row(3, g)).astype(BF16)

        loop(n_sub, after_attention)
        m_all = r.m_all
        m_base = reserve(nc - 1)
        for step in range(1, nc):
            chip_send(lambda other: m_all.at[c], m_all, m_base, step).start()

        wait_all(f1_moved)
        f1_core = wires.far(r.w_1.at[:, :, k], r.w_1.at[:, :, k], core_dev)
        wait_all(c_far)

        def make_dbr(blk):
            def body(g):
                rows = sub_rows(g)
                value = r.cg[blk, rows, :].astype(F32) * tab_row(5, blk, g)
                r.dbr[blk, rows, :] = value.astype(BF16)

            loop(n_sub, body)

        loop(nc, make_dbr)
        f1_core.wait()
        wait_all(f2_far)
        wires.far(r.w_2.at[k], r.w_2.at[k], core_dev).wait()

        def weight_1(h):
            return r.w_1[h].reshape(width, ff_d)

        def weight_2(h):
            return r.w_2[h].reshape(width, ff_d)

        dm_base = reserve(nc - 1)
        br_base = reserve(nc - 1)
        dm_s, dm_r, br_s, br_r = sum_s, sum_r, r.br_s, r.br_r

        def feed(step):
            blk = xor_of(c, step, nc)

            @pl.when(step != 0)
            def _():
                chip_send(lambda other: m_all.at[c], m_all, m_base, step).wait_recv()

            m_now = m_all[blk]
            for h in range(2):
                bias_1 = r.biasg[c, 4 + h : 5 + h, pl.ds(0, ff_d)]
                r.hid[h] = dot(m_now, weight_1(h)) + bias_1

            def gelu_rows(g):
                rows = sub_rows(g)
                for h in range(2):
                    value, slope = gelu_both(r.hid[h, rows, :])
                    r.act[h, blk, rows, :] = value.astype(BF16)
                    r.slope[h, rows, :] = slope

            loop(n_sub, gelu_rows)
            d_now = r.dbr[blk]
            for h in range(2):
                r.hid[h] = dot(d_now, weight_2(h))

            def back_rows(g):
                rows = sub_rows(g)
                for h in range(2):
                    value = r.hid[h, rows, :] * r.slope[h, rows, :]
                    r.d_hid[h, blk, rows, :] = value.astype(BF16)

            loop(n_sub, back_rows)
            part = dot_rt(r.d_hid[0, blk], weight_1(0)) + dot_rt(r.d_hid[1, blk], weight_1(1))
            part = part.astype(BF16)

            @pl.when(step != 0)
            def _():
                dm_s[blk] = part
                chip_send(lambda other: dm_s.at[other], dm_r, dm_base, step).start()

            @pl.when(step == 0)
            def _():
                dm_r[c] = part

            part2 = dot_rt(r.act[0, blk], weight_2(0)) + dot_rt(r.act[1, blk], weight_2(1))
            part2 = part2.astype(BF16)

            @pl.when(step != 0)
            def _():
                br_s[blk] = part2
                chip_send(lambda other: br_s.at[other], br_r, br_base, step).start()

            @pl.when(step == 0)
            def _():
                br_r[c] = part2

        loop(nc, feed)
        for step in range(1, nc):
            chip_send(lambda other: m_all.at[c], m_all, m_base, step).wait_send()

        dbr_all = r.dbr[...].reshape(group, width)

        def column_cuts(count):
            return [(at, min(at + 256, count)) for at in range(0, count, 256)]

        for lo, hi in column_cuts(ff_d):
            value = dot_lt(dbr_all, r.act[core_o, :, :, lo:hi].reshape(group, hi - lo))
            r.g_2[core_o, :, :, lo:hi] = value.astype(BF16).reshape(nf, cols_f, hi - lo)
        g2_core = wires.far(r.g_2.at[core_o], r.g_2r, core_dev)
        g2_core.wait()
        for lo, hi in column_cuts(ff_d):
            value = dot_lt(dbr_all, r.act[k, :, :, lo:hi].reshape(group, hi - lo))
            value = value.reshape(nf, cols_f, hi - lo) + r.g_2r[:, :, lo:hi].astype(F32)
            r.g_2[k, :, :, lo:hi] = value.astype(BF16)
        z2_far = [
            wires.far(r.g_2.at[k, other], r.z_2.at[f], peer) for other, peer in plane_peers
        ]

        for step in range(1, nc):
            chip_send(lambda other: dm_s.at[other], dm_r, dm_base, step).wait()
        da_all = r.da_all

        def back_norm2(g):
            rows = sub_rows(g)
            d_m = dm_r[0, rows, :].astype(F32)
            for other in range(1, nc):
                d_m = d_m + dm_r[other, rows, :].astype(F32)
            normal, scale = ln_parts(r.after[rows, :])
            cot_now = r.cg[c, rows, :].astype(F32)
            d_after = cot_now + ln_back(normal, scale, d_m * (1.0 + own_row(4, g)))
            r.d_after[rows, :] = d_after
            da_all[c, rows, :] = (own_row(2, g) * d_after).astype(BF16)
            at = pl.ds(g, 1)
            r.sub[3, at, :] = jnp.sum(d_m, axis=0, keepdims=True)
            r.sub[4, at, :] = jnp.sum(d_m * normal, axis=0, keepdims=True)
            r.sub[2, at, :] = jnp.sum(d_after * r.attn[rows, :], axis=0, keepdims=True)

        loop(n_sub, back_norm2)
        da_base = reserve(nc - 1)
        for step in range(1, nc):
            chip_send(lambda other: da_all.at[c], da_all, da_base, step).start()

        m_rows = m_all[...].reshape(group, width)
        for h in range(2):
            for lo, hi in column_cuts(ff_d):
                value = dot_lt(m_rows, r.d_hid[h, :, :, lo:hi].reshape(group, hi - lo))
                r.g_1[h, :, :, :, lo:hi] = value.astype(BF16).reshape(nc, 2, rows_d, hi - lo)
        g1_core = wires.far(r.g_1.at[:, :, core_o], r.g_1r, core_dev)

        for step in range(1, nc):
            chip_send(lambda other: br_s.at[other], br_r, br_base, step).wait()

        def finish_out(g):
            rows = sub_rows(g)
            branch = br_r[0, rows, :].astype(F32)
            for other in range(1, nc):
                branch = branch + br_r[other, rows, :].astype(F32)
            branch = branch + bias_o
            out[rows, :] = (r.after[rows, :] + own_row(5, g) * branch).astype(BF16)
            cot_now = r.cg[c, rows, :].astype(F32)
            r.sub[5, pl.ds(g, 1), :] = jnp.sum(cot_now * branch, axis=0, keepdims=True)

        loop(n_sub, finish_out)
        g1_core.wait()
        for h in range(2):
            for chip in range(nc):
                value = r.g_1[h, chip, k].astype(F32) + r.g_1r[h, chip].astype(F32)
                r.g_1[h, chip, k] = value.astype(BF16)
        f1_rows[pl.ds(per_1 * c, per_1)] = r.g_1[:, c, k]
        y1_far = [
            wires.far(r.g_1.at[:, other, k], f1_rows.at[pl.ds(per_1 * c, per_1)], peer)
            for other, peer in chip_peers
        ]

        back_base = reserve(nc - 1)

        def attend_back(step):
            blk = xor_of(c, step, nc)

            @pl.when(step != 0)
            def _():
                chip_send(lambda other: da_all.at[c], da_all, da_base, step).wait_recv()

            d_mix = dot_rt(da_all[blk], r.w_p[...]).astype(BF16)
            q_now, k_now, v_now = r.qkv[0, blk], r.qkv[1, blk], r.qkv[2, blk]
            d_q = jnp.zeros((own, chip_w), F32)
            d_k = jnp.zeros((own, chip_w), F32)
            d_v = jnp.zeros((own, chip_w), F32)
            for h in range(heads):
                d_mix_h = d_mix * head_of[h]
                share = r.probs[blk * heads + h]
                d_share = dot_rt(d_mix_h, v_now)
                d_score = share * (d_share - jnp.sum(share * d_share, axis=-1, keepdims=True))
                d_score = d_score.astype(BF16)
                d_q = d_q + dot(d_score, k_now * head_of[h])
                d_k = d_k + dot_lt(d_score, q_now * head_of[h])
                d_v = d_v + dot_lt(share.astype(BF16), d_mix_h)
            d_q = (d_q * head_scale).astype(BF16)
            d_k = (d_k * head_scale).astype(BF16)
            d_v = d_v.astype(BF16)
            r.d_qkv[0, blk] = d_q
            r.d_qkv[1, blk] = d_k
            r.d_qkv[2, blk] = d_v
            part = dot_rt(d_q, weight_q(0)) + dot_rt(d_k, weight_q(1)) + dot_rt(d_v, weight_q(2))
            part = part.astype(BF16)

            @pl.when(step != 0)
            def _():
                sum_s[blk] = part
                chip_send(lambda other: sum_s.at[other], sum_r, back_base, step).start()

            @pl.when(step == 0)
            def _():
                sum_r[c] = part

        loop(nc, attend_back)
        for step in range(1, nc):
            chip_send(lambda other: da_all.at[c], da_all, da_base, step).wait_send()

        wait_all(y1_far)
        z1_far = [
            wires.far(f1_rows.at[pl.ds(per_1 * other, per_1)], r.z_1.at[f], peer)
            for other, peer in plane_peers
        ]

        a_rows = r.a_in[...].reshape(group, width)
        q_core_back = []
        for kind in range(3):
            for lo, hi in column_cuts(chip_w):
                value = dot_lt(a_rows, r.d_qkv[kind, :, :, lo:hi].reshape(group, hi - lo))
                r.g_q[kind, :, :, :, lo:hi] = value.astype(BF16).reshape(nc, 2, rows_d, hi - lo)
            q_core_back.append(wires.far(r.g_q.at[kind, :, core_o], r.g_qr.at[kind], core_dev))
        da_rows = da_all[...].reshape(group, width)
        value = dot_lt(r.mixed[...].reshape(group, chip_w), da_rows).astype(BF16)
        r.g_p[...] = value.reshape(2, rows_d, width)
        p_core_back = wires.far(r.g_p.at[core_o], r.g_pr, core_dev)
        yq_far = []
        for kind in range(3):
            q_core_back[kind].wait()
            for chip in range(nc):
                value = r.g_q[kind, chip, k].astype(F32) + r.g_qr[kind, chip].astype(F32)
                r.g_q[kind, chip, k] = value.astype(BF16)
            q_rows[kind * nc + c] = r.g_q[kind, c, k]
            for other, peer in chip_peers:
                yq_far.append(
                    wires.far(r.g_q.at[kind, other, k], q_rows.at[kind * nc + c], peer)
                )
        p_core_back.wait()
        r.g_p[k] = (r.g_p[k].astype(F32) + r.g_pr[...].astype(F32)).astype(BF16)
        zp_far = [
            wires.far(
                r.g_p.at[k, :, pl.ds(pl.multiple_of(other * step_p, 128), pad_p)],
                r.z_p.at[f],
                peer,
            )
            for other, peer in plane_peers
        ]

        for step in range(1, nc):
            chip_send(lambda other: sum_s.at[other], sum_r, back_base, step).wait()

        def back_norm1(g):
            rows = sub_rows(g)
            d_a = sum_r[0, rows, :].astype(F32)
            for other in range(1, nc):
                d_a = d_a + sum_r[other, rows, :].astype(F32)
            normal, scale = ln_parts(r.xg[c, rows, :].astype(F32))
            value = r.d_after[rows, :] + ln_back(normal, scale, d_a * (1.0 + own_row(1, g)))
            x_grad[rows, :] = value.astype(BF16)
            at = pl.ds(g, 1)
            r.sub[0, at, :] = jnp.sum(d_a, axis=0, keepdims=True)
            r.sub[1, at, :] = jnp.sum(d_a * normal, axis=0, keepdims=True)

        loop(n_sub, back_norm1)
        for kind in range(6):
            r.d_mod[kind] = lax.dot_general(
                own_hot, r.sub[kind], (((0,), (0,)), ((), ())),
                precision=PRECISE, preferred_element_type=F32,
            )
        ones_own = jnp.ones((8, own), BF16)
        ones_all = jnp.ones((8, group), BF16)
        r.d_bias[...] = jnp.zeros((8, width), F32)
        r.d_bias[0:1, :] = dot(ones_own, da_all[c])[0:1]
        r.d_bias[1:2, :] = dot(ones_own, r.dbr[c])[0:1]
        for at, kind in ((2, 0), (3, 2)):
            sums = dot(ones_all, r.d_qkv[kind].reshape(group, chip_w))
            r.d_bias[at : at + 1, 0:chip_w] = sums[0:1]
        for h in range(2):
            sums = dot(ones_all, r.d_hid[h].reshape(group, ff_d))
            r.d_bias[4 + h : 5 + h, 0:ff_d] = sums[0:1]

        small = []
        for other, peer in plane_peers:
            small.append(
                wires.far(r.d_mod.at[pl.ds(6 * other // nf, 2)], r.dz.at[f], peer)
            )
            small.append(wires.far(r.d_bias, r.dzb.at[f], peer))
        wait_all(yq_far)
        zq_far = [
            wires.far(q_rows.at[pl.ds(per_q * other, per_q)], r.z_q.at[f], peer)
            for other, peer in plane_peers
        ]
        r.dz[f] = r.d_mod[pl.ds(6 * f // nf, 2)]
        r.dzb[f] = r.d_bias[...]
        wait_all(small)
        value, value_b = r.dz[0], r.dzb[0]
        for plane in range(1, nf):
            value = value + r.dz[plane]
            value_b = value_b + r.dzb[plane]
        r.d_both[...] = value
        r.d_bsum[...] = value_b
        small = [
            wires.far(r.d_both.at[core_o], r.m_core, core_dev),
            wires.far(r.d_bsum, r.d_coreb, core_dev),
        ]
        wait_all(small)
        m_chip[c] = r.d_both[k] + r.m_core[...]
        o_bias[c] = r.d_bsum[...] + r.d_coreb[...]
        small = []
        for _, peer in chip_peers:
            small.append(wires.far(m_chip.at[c], m_chip.at[c], peer))
            small.append(wires.far(o_bias.at[c], o_bias.at[c], peer))

        wait_all(z2_far)
        r.z_2[f] = r.g_2[k, f]
        total = r.z_2[0].astype(F32)
        for plane in range(1, nf):
            total = total + r.z_2[plane].astype(F32)
        o_2[...] = total
        wait_all(z1_far)
        r.z_1[f] = f1_rows[pl.ds(per_1 * f, per_1)]
        total = r.z_1[0].astype(F32)
        for plane in range(1, nf):
            total = total + r.z_1[plane].astype(F32)
        o_1[...] = total
        wait_all(small)
        value = m_chip[0]
        for chip in range(1, nc):
            value = value + m_chip[chip]
        o_mod[k] = value
        m_end = wires.far(o_mod.at[k], o_mod.at[k], core_dev)
        wait_all(zp_far)
        for plane in range(nf):

            @pl.when(f == plane)
            def _():
                r.z_p[plane] = r.g_p[k, :, plane * step_p : plane * step_p + pad_p]

        total = r.z_p[0].astype(F32)
        for plane in range(1, nf):
            total = total + r.z_p[plane].astype(F32)
        o_p[...] = total
        wait_all(zq_far)
        r.z_q[f] = q_rows[pl.ds(per_q * f, per_q)]
        total = r.z_q[0].astype(F32)
        for plane in range(1, nf):
            total = total + r.z_q[plane].astype(F32)
        o_q[...] = total
        m_end.wait()
        assert wires.remote_count <= n_sem and wires.local_count <= 32

    return pl.pallas_call(
        kernel,
        out_shape=outs,
        in_specs=[ANYWHERE] * 5 + [ON_CHIP] + [ANYWHERE] * 4,
        out_specs=tuple([ON_CHIP] * len(outs)),
        scratch_shapes=list(scratch.values()),
        compiler_params=pltpu.CompilerParams(
            collective_id=0, has_side_effects=True, vmem_limit_bytes=63 * 2**20
        ),
        name="block",
    )(x, cot, mask, hot, bias, mod, wq, w1, wp, w2)


def fits_block(n_dp, nf, width, ff, own, micro):
    nc = n_dp // 2
    return (
        nc == nf
        and nf == 4
        and width % (128 * nf) == 128
        and ff == 4 * width
        and (width // n_dp) % 16 == 0
        and (width // nc) % HEAD_DIM == 0
        and own % (2 * SUB) == 0
    )


def per_device(
    n_dp, nf, patches, cotangent, conditioning, frame_of_slot, clip_of_slot,
    w_ada, b_ada, w_qkv, b_qv, w_proj, b_proj, w_fc1, b_fc1, w_fc2, b_fc2,
):
    nc = n_dp // 2
    sizes = (nc, nf)
    micro, block, width = patches.shape
    own = micro * block
    clips = conditioning.shape[1]
    rows_d = width // n_dp
    cols_f = width // nf
    ff = w_fc1.shape[1] * nf
    ff_d = ff // n_dp
    chip_w = width // nc
    piece_q = math.gcd(3 * width // nf, chip_w)
    piece_1 = math.gcd(ff // nf, ff_d)
    dims = types.SimpleNamespace(
        nc=nc,
        nf=nf,
        per_q=3 * width // nf // piece_q,
        per_1=ff // nf // piece_1,
        chip_q=chip_w // piece_q,
        chip_1=ff // nc // piece_1,
    )
    dp = lax.axis_index("dp")
    f = lax.axis_index("fsdp")
    c, k = dp // 2, dp % 2

    q_send = w_qkv.reshape(rows_d, dims.per_q, piece_q).transpose(1, 0, 2)
    f1_send = w_fc1.reshape(rows_d, dims.per_1, piece_1).transpose(1, 0, 2)
    f2_send = w_fc2.T
    cond = conditioning.reshape(micro * clips, width)
    silu_cond = jax.nn.silu(cond)
    silu_low = silu_cond.astype(BF16)
    ada_w = w_ada.shape[1]
    silu_part = lax.dynamic_slice_in_dim(silu_low, dp * rows_d, rows_d, 1)
    mod_part = dot(silu_part, w_ada) + jnp.where(dp == 0, b_ada.astype(F32), 0.0)[None]
    mod_send = mod_part.reshape(-1, 2, ada_w // 2).transpose(1, 0, 2)
    cut = [0, 2 * cols_f, 3 * cols_f, 3 * cols_f + ff // nf, 4 * cols_f + ff // nf]
    cond_own = lax.dynamic_slice_in_dim(cond, f * cols_f, cols_f, 1)

    def ada_outputs(d_cols):
        grad_w_ada = precise(silu_part.astype(F32), d_cols, ((0,), (0,)))
        d_silu_part = precise(d_cols, w_ada.astype(F32), ((1,), (1,)))
        d_silu = cond_kernel(dims, d_silu_part).transpose(1, 0, 2).reshape(micro * clips, width)
        d_silu_own = lax.dynamic_slice_in_dim(d_silu, f * cols_f, cols_f, 1)
        _, silu_back = jax.vjp(jax.nn.silu, cond_own)
        cond_grad = silu_back(d_silu_own)[0].reshape(micro, clips, cols_f)
        return cond_grad, grad_w_ada, jnp.sum(d_cols, axis=0)

    if fits_block(n_dp, nf, width, ff, own, micro):
        n_rows = micro * clips
        window = f * ada_w - 6 * f // nf * width
        pad_p = width // nf // 128 * 128 + 128
        dims.step_p = (width - pad_p) // (nf - 1)
        shift_p = f * (cols_f - dims.step_p)

        def lanes(value, start):
            empty = jnp.zeros(value.shape[:-1] + (width,), F32)
            return lax.dynamic_update_slice_in_dim(empty, value.astype(F32), start, value.ndim - 1)

        mod_send = jnp.zeros((n_rows, 2 * width), F32)
        mod_send = lax.dynamic_update_slice_in_dim(mod_send, mod_part, window, 1)
        mod_send = mod_send.reshape(n_rows, 2, width).transpose(1, 0, 2)
        p_send = jnp.zeros((rows_d, pad_p), BF16)
        p_send = lax.dynamic_update_slice_in_dim(p_send, w_proj, shift_p, 1)
        bias_send = jnp.concatenate(
            [
                lanes(b_proj[None], f * cols_f),
                lanes(b_fc2[None], f * cols_f),
                lanes(b_qv.reshape(2, chip_w), 0),
                lanes(b_fc1.reshape(2, ff_d), 0),
                jnp.zeros((2, width), F32),
            ]
        )
        frames = frame_of_slot + jnp.arange(micro, dtype=jnp.int32)[:, None] * 65536
        frames = frames.reshape(own)
        mask = (frames[:, None] == frames[None, :]).astype(BF16)
        row = clip_of_slot + jnp.arange(micro, dtype=jnp.int32)[:, None] * clips
        row = row.reshape(own // SUB, SUB)[:, :1].astype(F32)
        hot = jnp.broadcast_to(row, (own // SUB, 128))
        output, input_grad, o_q, o_1, o_p, o_2, o_mod, o_bias = block_kernel(
            dims, patches.reshape(own, width), cotangent.reshape(own, width), mask, hot, bias_send,
            mod_send, q_send, f1_send, p_send, f2_send,
        )
        d_cols = o_mod.transpose(1, 0, 2).reshape(n_rows, 2 * width)
        d_cols = lax.dynamic_slice_in_dim(d_cols, window, ada_w, 1)
        cond_grad, grad_w_ada, grad_b_ada = ada_outputs(d_cols)
        own_bias = jnp.sum(o_bias[:, :2], axis=0)
        own_bias = lax.dynamic_slice_in_dim(own_bias, f * cols_f, cols_f, 1)
        qv = jnp.concatenate([o_bias[:, 2, :chip_w], o_bias[:, 3, :chip_w]])
        qv = lax.dynamic_slice_in_dim(qv, 2 * f, 2, 0).reshape(2 * chip_w)
        fc1 = lax.dynamic_index_in_dim(o_bias[:, 4:6, :ff_d], f, 0, False).reshape(2 * ff_d)
        return (
            output.reshape(patches.shape),
            input_grad.reshape(patches.shape),
            cond_grad,
            grad_w_ada,
            grad_b_ada,
            o_q.transpose(1, 0, 2).reshape(rows_d, 3 * width // nf),
            qv,
            lax.dynamic_slice_in_dim(o_p, shift_p, cols_f, 1),
            own_bias[0],
            o_1.transpose(1, 0, 2).reshape(rows_d, ff // nf),
            fc1,
            o_2.T,
            own_bias[1],
        )

    ids = jnp.stack([frame_of_slot.reshape(own), clip_of_slot.reshape(own)])
    ids = jnp.concatenate([ids, jnp.zeros((6, own), jnp.int32)])
    bias_send = jnp.concatenate([b_qv, b_proj, b_fc1, b_fc2]).astype(F32)[None]

    (x_all, c_all, ids_all, bias_all, mod_all, q_chip, f1_chip, p_chip, f2_chip, _, _) = start_kernel(
        dims, patches.reshape(own, width), cotangent.reshape(own, width), ids, bias_send, mod_send,
        q_send, f1_send, w_proj, f2_send,
    )
    group = nc * own
    modulation = mod_all.transpose(2, 0, 1, 3).reshape(micro * clips, 6 * width)
    q_parts = [
        q_chip[i].reshape(nc, 2, dims.chip_q, rows_d, piece_q).transpose(0, 1, 3, 2, 4).reshape(width, chip_w)
        for i in range(3)
    ]
    w1 = f1_chip.transpose(1, 2, 3, 0, 4).reshape(width, ff // nc)
    wp = p_chip.transpose(0, 2, 1, 3).reshape(chip_w, width)
    w2t = f2_chip.reshape(2, width, ff_d).transpose(1, 0, 2).reshape(width, 2 * ff_d)
    b_parts = [bias_all[:, 0, a:b].reshape(-1) for a, b in zip(cut[:-1], cut[1:])]
    bq = lax.dynamic_slice_in_dim(b_parts[0], c * chip_w, chip_w, 0)
    bv = lax.dynamic_slice_in_dim(b_parts[0], width + c * chip_w, chip_w, 0)
    b1 = lax.dynamic_slice_in_dim(b_parts[2], c * (ff // nc), ff // nc, 0)

    def hot_of(clip_ids):
        count = clip_ids.shape[0]
        row = (jnp.arange(count, dtype=jnp.int32) // block) % micro * clips + clip_ids
        return (row[:, None] == jnp.arange(micro * clips, dtype=jnp.int32)[None]).astype(F32)

    hot_group = hot_of(ids_all[:, 1].reshape(group))
    hot_own = hot_of(clip_of_slot.reshape(own))
    mod_group = precise(hot_group, modulation, ((1,), (0,)))
    mod_own = precise(hot_own, modulation, ((1,), (0,)))
    shift1, scale1 = mod_group[:, :width], mod_group[:, width : 2 * width]
    gate1 = mod_own[:, 2 * width : 3 * width]
    shift2, scale2 = mod_own[:, 3 * width : 4 * width], mod_own[:, 4 * width : 5 * width]
    gate2_group, gate2 = mod_group[:, 5 * width :], mod_own[:, 5 * width :]

    x_group = x_all.reshape(group, width).astype(F32)
    norm1, rstd1 = ln_parts(x_group)
    a_in = (norm1 * (1.0 + scale1) + shift1).astype(BF16)
    zero = jnp.zeros_like(bq)
    q, kk, v = [
        (dot(a_in, w) + b[None]).astype(BF16) for w, b in zip(q_parts, (bq, zero, bv))
    ]
    heads = chip_w // HEAD_DIM
    blocks = group // block
    q4, k4, v4 = [t.reshape(blocks, block, heads, HEAD_DIM) for t in (q, kk, v)]
    frames = ids_all[:, 0].reshape(blocks, block)
    same = (frames[:, :, None] == frames[:, None, :])[:, None]
    scores = jnp.einsum("bqhd,bkhd->bhqk", q4, k4, preferred_element_type=F32) * HEAD_DIM ** (-0.5)
    scores = jnp.where(same, scores, NEG_FILL)
    top = jnp.max(scores, axis=-1, keepdims=True)
    raised = jnp.exp(scores - top)
    probs = raised / jnp.sum(raised, axis=-1, keepdims=True)
    probs_low = probs.astype(BF16)
    mixed = jnp.einsum("bhqk,bkhd->bqhd", probs_low, v4, preferred_element_type=F32)
    mixed = mixed.reshape(group, chip_w).astype(BF16)
    attn_part = dot(mixed, wp)
    (attn_got,) = exchange(
        "attn_sum", 3, sizes, [(CHIP, SPREAD, attn_part.astype(BF16).reshape(nc, own, width))]
    )
    attn = jnp.sum(attn_got.astype(F32), axis=0) + b_parts[1][None]
    x_own = patches.reshape(own, width).astype(F32)
    after = x_own + gate1 * attn
    norm2, rstd2 = ln_parts(after)
    m_own = (norm2 * (1.0 + scale2) + shift2).astype(BF16)
    (m_all,) = exchange("m_gather", 4, sizes, [(CHIP, GATHER, m_own)])
    m_in = m_all.reshape(group, width)

    hidden = dot(m_in, w1) + b1[None]
    act, slope = gelu_both(hidden)
    act = act.astype(BF16)
    branch_part = dot_rt(act, w2t)
    cot_group = c_all.reshape(group, width).astype(F32)
    d_branch = (gate2_group * cot_group).astype(BF16)
    grad_2t = dot_lt(d_branch, act)
    d_hidden = (dot(d_branch, w2t) * slope).astype(BF16)
    grad_1 = dot_lt(m_in, d_hidden)
    d_m_part = dot_rt(d_hidden, w1)
    branch_got, d_m_got = exchange(
        "ff_sum",
        5,
        sizes,
        [
            (CHIP, SPREAD, d_m_part.astype(BF16).reshape(nc, own, width)),
            (CHIP, SPREAD, branch_part.astype(BF16).reshape(nc, own, width)),
        ],
    )[::-1]
    branch = jnp.sum(branch_got.astype(F32), axis=0) + b_parts[3][None]
    output = (after + gate2 * branch).astype(BF16)
    d_m = jnp.sum(d_m_got.astype(F32), axis=0)
    cot_own = cotangent.reshape(own, width).astype(F32)
    d_after = cot_own + ln_back(norm2, rstd2, d_m * (1.0 + scale2))
    d_attn = (gate1 * d_after).astype(BF16)
    (d_attn_all,) = exchange("d_attn_gather", 6, sizes, [(CHIP, GATHER, d_attn)])
    d_attn_group = d_attn_all.reshape(group, width)
    grad_p = dot_lt(mixed, d_attn_group)
    d_mix = dot_rt(d_attn_group, wp).astype(BF16).reshape(blocks, block, heads, HEAD_DIM)
    d_probs = jnp.einsum("bqhd,bkhd->bhqk", d_mix, v4, preferred_element_type=F32)
    d_scores = probs * (d_probs - jnp.sum(probs * d_probs, axis=-1, keepdims=True))
    d_scores = d_scores.astype(BF16)
    dq = jnp.einsum("bhqk,bkhd->bqhd", d_scores, k4, preferred_element_type=F32) * HEAD_DIM ** (-0.5)
    dk = jnp.einsum("bhqk,bqhd->bkhd", d_scores, q4, preferred_element_type=F32) * HEAD_DIM ** (-0.5)
    dv = jnp.einsum("bhqk,bqhd->bkhd", probs_low, d_mix, preferred_element_type=F32)
    dqkv = [t.reshape(group, chip_w).astype(BF16) for t in (dq, dk, dv)]
    d_a_part = sum(dot_rt(t, w) for t, w in zip(dqkv, q_parts))
    grad_q = jnp.stack([dot_lt(a_in, t) for t in dqkv])
    (d_a_got,) = exchange(
        "d_a_sum", 7, sizes, [(CHIP, SPREAD, d_a_part.astype(BF16).reshape(nc, own, width))]
    )
    d_a = jnp.sum(d_a_got.astype(F32), axis=0)
    norm1_own, rstd1_own = ln_parts(x_own)
    scale1_own = mod_own[:, width : 2 * width]
    input_grad = (d_after + ln_back(norm1_own, rstd1_own, d_a * (1.0 + scale1_own))).astype(BF16)

    g_q = grad_q.reshape(3, nc, 2, rows_d, dims.chip_q, piece_q).transpose(2, 1, 0, 4, 3, 5)
    g_1 = grad_1.reshape(nc, 2, rows_d, dims.chip_1, piece_1).transpose(1, 0, 3, 2, 4)
    g_p = grad_p.reshape(2, rows_d, nf, cols_f).transpose(0, 2, 1, 3)
    g_2 = grad_2t.reshape(nf, cols_f, 2, ff_d).transpose(2, 0, 1, 3)
    got = exchange("grad_core", 8, sizes, [(CORE, SPREAD, g.astype(BF16)) for g in (g_q, g_1, g_p, g_2)])
    s_q, s_1, s_p, s_2 = [jnp.sum(g.astype(F32), axis=0).astype(BF16) for g in got]
    r_q, r_1 = exchange("grad_chip", 9, sizes, [(CHIP, SPREAD, s_q), (CHIP, SPREAD, s_1)])
    z_q = r_q.transpose(1, 0, 2, 3, 4).reshape(nf, dims.per_q, rows_d, piece_q)
    z_1 = r_1.reshape(nf, dims.per_1, rows_d, piece_1)
    got = exchange("grad_plane", 10, sizes, [(PLANE, SPREAD, g) for g in (z_q, z_1, s_p, s_2)])
    o_q, o_1, o_p, o_2 = [jnp.sum(g.astype(F32), axis=0) for g in got]
    grad_w_qkv = o_q.transpose(1, 0, 2).reshape(rows_d, 3 * width // nf)
    grad_w_fc1 = o_1.transpose(1, 0, 2).reshape(rows_d, ff // nf)
    grad_w_fc2 = o_2.T

    d_token = jnp.concatenate(
        [d_a, d_a * norm1_own, d_after * attn, d_m, d_m * norm2, cot_own * branch], axis=1
    )
    d_mod = precise(hot_own, d_token, ((0,), (0,)))
    d_branch_own = (gate2 * cot_own).astype(BF16).astype(F32)

    def columns(value):
        return jnp.sum(value.astype(F32), axis=0)

    def spread(value, count):
        return lax.dynamic_update_slice_in_dim(
            jnp.zeros((count,), F32), value, c * value.shape[0], 0
        )

    g_bqv = jnp.concatenate([spread(columns(dqkv[0]), width), spread(columns(dqkv[2]), width)])
    g_b1 = spread(columns(d_hidden), ff)
    bias_terms = jnp.concatenate(
        [
            g_bqv.reshape(nf, -1),
            columns(d_attn).reshape(nf, -1),
            g_b1.reshape(nf, -1),
            columns(d_branch_own).reshape(nf, -1),
        ],
        axis=1,
    )
    n_bias = bias_terms.shape[1]
    bias_rows = -(-n_bias // ada_w)
    bias_terms = jnp.pad(bias_terms, ((0, 0), (0, bias_rows * ada_w - n_bias)))
    terms = jnp.concatenate(
        [d_mod.reshape(micro * clips, nf, ada_w).transpose(1, 0, 2), bias_terms.reshape(nf, bias_rows, ada_w)],
        axis=1,
    )
    pad_rows = -terms.shape[1] % 8
    terms = jnp.pad(terms, ((0, 0), (0, pad_rows), (0, 0)))
    terms = terms.reshape(nf, -1, 2, ada_w // 2).transpose(0, 2, 1, 3)
    total = sum_small_kernel(dims, terms).transpose(1, 0, 2).reshape(-1, ada_w)
    d_cols = total[: micro * clips]
    bias_sums = total[micro * clips : micro * clips + bias_rows].reshape(-1)[:n_bias]
    g_parts = [bias_sums[a:b] for a, b in zip(cut[:-1], cut[1:])]
    cond_grad, grad_w_ada, grad_b_ada = ada_outputs(d_cols)
    return (
        output.reshape(patches.shape),
        input_grad.reshape(patches.shape),
        cond_grad,
        grad_w_ada,
        grad_b_ada,
        grad_w_qkv,
        g_parts[0],
        o_p,
        g_parts[1],
        grad_w_fc1,
        g_parts[2],
        grad_w_fc2,
        g_parts[3],
    )


def solution(mesh):
    tokens = P(None, ("dp", "fsdp"), None)
    ids = P(None, ("dp", "fsdp"))
    both, cols = P("dp", "fsdp"), P("fsdp")
    in_specs = (tokens, tokens, P(), ids, ids) + (both, cols) * 5
    out_specs = (tokens, tokens, P(None, None, "fsdp")) + (both, cols) * 5
    return jax.shard_map(
        functools.partial(per_device, mesh.shape["dp"], mesh.shape["fsdp"]),
        mesh=mesh,
        in_specs=in_specs,
        out_specs=out_specs,
        check_vma=False,
    )
```

```python
import functools
import math
import types

import jax
import jax.numpy as jnp
from jax import lax
from jax.experimental import pallas as pl
from jax.experimental.pallas import tpu as pltpu
from jax.sharding import PartitionSpec as P

HEAD_DIM = 72
EPS = 1e-06
GELU_C = math.sqrt(2.0 / math.pi)
PRECISE = lax.Precision.HIGHEST
NEG_FILL = -1e30
SUB = 16
CORE, CHIP, PLANE, ALL = range(4)
GATHER, SPREAD = range(2)
MESH_ID = pl.DeviceIdType.MESH
F32 = jnp.float32
BF16 = jnp.bfloat16


def xor_of(index, step, size):
    result, bit = 0, 1
    while bit < size:
        mine = (index // bit) % 2
        result = result + ((mine + (step // bit) % 2) % 2) * bit
        bit *= 2
    return result


class Place:
    def __init__(self, n_chip, n_plane):
        self.n = {CORE: 2, CHIP: n_chip, PLANE: n_plane, ALL: 2 * n_chip}
        self.dp = lax.axis_index("dp")
        self.f = lax.axis_index("fsdp")
        self.c = self.dp // 2
        self.k = self.dp % 2

    def index(self, axis):
        return {CORE: self.k, CHIP: self.c, PLANE: self.f, ALL: self.dp}[axis]

    def peer(self, axis, step):
        other = xor_of(self.index(axis), step, self.n[axis])
        if axis == CORE:
            return other, (self.c * 2 + other, self.f)
        if axis == CHIP:
            return other, (other * 2 + self.k, self.f)
        if axis == PLANE:
            return other, (self.dp, other)
        return other, (other, self.f)


def greet(place, axes):
    barrier = pltpu.get_barrier_semaphore()
    count = 0
    for axis in axes:
        for step in range(1, place.n[axis]):
            pl.semaphore_signal(
                barrier, inc=1, device_id=place.peer(axis, step)[1], device_id_type=MESH_ID
            )
            count += 1
    pl.semaphore_wait(barrier, count)


class Wires:
    def __init__(self, send, recv, local):
        self.send, self.recv, self.local = send, recv, local
        self.remote_count = 0
        self.local_count = 0

    def far(self, src, dst, device):
        at = self.remote_count
        self.remote_count += 1
        copy = pltpu.make_async_remote_copy(
            src_ref=src,
            dst_ref=dst,
            send_sem=self.send.at[at],
            recv_sem=self.recv.at[at],
            device_id=device,
            device_id_type=MESH_ID,
        )
        copy.start()
        return copy

    def near(self, src, dst):
        at = self.local_count
        self.local_count += 1
        copy = pltpu.make_async_copy(src, dst, self.local.at[at])
        copy.start()
        return copy


def wait_all(copies):
    for copy in copies:
        copy.wait()


ANYWHERE = pl.BlockSpec(memory_space=pl.ANY)
ON_CHIP = pl.BlockSpec(memory_space=pltpu.VMEM)


def exchange(name, collective_id, sizes, items):
    n_chip, n_plane = sizes
    n_of = {CORE: 2, CHIP: n_chip, PLANE: n_plane, ALL: 2 * n_chip}
    axes = sorted({item[0] for item in items})
    outs = []
    n_far = 0
    for axis, kind, array in items:
        n_far += n_of[axis] - 1
        shape = array.shape if kind == SPREAD else (n_of[axis],) + array.shape
        outs.append(jax.ShapeDtypeStruct(shape, array.dtype))

    def kernel(*refs):
        ins = refs[: len(items)]
        results = refs[len(items) : 2 * len(items)]
        place = Place(n_chip, n_plane)
        wires = Wires(*refs[2 * len(items) :])
        greet(place, axes)
        copies = []
        for (axis, kind, _), src, dst in zip(items, ins, results):
            mine = place.index(axis)
            for step in range(1, n_of[axis]):
                other, device = place.peer(axis, step)
                piece = src if kind == GATHER else src.at[other]
                copies.append(wires.far(piece, dst.at[mine], device))
        for (axis, kind, _), src, dst in zip(items, ins, results):
            mine = place.index(axis)
            copies.append(wires.near(src if kind == GATHER else src.at[mine], dst.at[mine]))
        wait_all(copies)

    return pl.pallas_call(
        kernel,
        out_shape=tuple(outs),
        in_specs=[ANYWHERE] * len(items),
        out_specs=tuple([ANYWHERE] * len(items)),
        scratch_shapes=[
            pltpu.SemaphoreType.DMA((n_far,)),
            pltpu.SemaphoreType.DMA((n_far,)),
            pltpu.SemaphoreType.DMA((len(items),)),
        ],
        compiler_params=pltpu.CompilerParams(collective_id=collective_id, has_side_effects=True),
        name=name,
    )(*[item[2] for item in items])


def start_kernel(dims, x, cot, ids, bias, mod, wq, w1, wp, w2):
    nc, nf = dims.nc, dims.nf
    per_q, per_1 = dims.per_q, dims.per_1
    chip_q, chip_1 = dims.chip_q, dims.chip_1
    part_q = nc * chip_q
    rows, half = mod.shape[1], mod.shape[2]
    n_far = 5 * (nf - 1) + 3 * (nc - 1) + 4 * (nc - 1) + 4 + 1 + (nc - 1) + (nf - 1) + 1
    outs = (
        jax.ShapeDtypeStruct((nc,) + x.shape, x.dtype),
        jax.ShapeDtypeStruct((nc,) + cot.shape, cot.dtype),
        jax.ShapeDtypeStruct((nc,) + ids.shape, ids.dtype),
        jax.ShapeDtypeStruct((nf,) + bias.shape, bias.dtype),
        jax.ShapeDtypeStruct((nf, 2, rows, half), F32),
        jax.ShapeDtypeStruct((3, nc, 2, chip_q) + wq.shape[1:], BF16),
        jax.ShapeDtypeStruct((chip_1, nc, 2) + w1.shape[1:], BF16),
        jax.ShapeDtypeStruct((2, nf) + wp.shape, BF16),
        jax.ShapeDtypeStruct((2, nf) + w2.shape, BF16),
        jax.ShapeDtypeStruct((nf * per_q,) + wq.shape[1:], BF16),
        jax.ShapeDtypeStruct((nf * per_1,) + w1.shape[1:], BF16),
    )

    def kernel(
        x_in, c_in, i_in, b_in, m_in, q_in, f1_in, p_in, f2_in,
        x_all, c_all, i_all, b_all, m_all, q_chip, f1_chip, p_chip, f2_chip, q_rows, f1_rows,
        m_core, m_sum, m_chip, send, recv, local,
    ):
        place = Place(nc, nf)
        wires = Wires(send, recv, local)
        c, k, f = place.c, place.k, place.f
        greet(place, (CORE, CHIP, PLANE))
        core_other, core_peer = place.peer(CORE, 1)
        chip_peers = [place.peer(CHIP, step) for step in range(1, nc)]
        plane_peers = [place.peer(PLANE, step) for step in range(1, nf)]

        m_first = wires.far(m_in.at[core_other], m_core, core_peer)
        q_got, f1_got, p_got, f2_got, small = [], [], [], [], []
        for _, peer in plane_peers:
            q_got.append(wires.far(q_in, q_rows.at[pl.ds(f * per_q, per_q)], peer))
            small.append(wires.far(b_in, b_all.at[f], peer))
        q_got.append(wires.near(q_in, q_rows.at[pl.ds(f * per_q, per_q)]))
        small.append(wires.near(b_in, b_all.at[f]))
        for _, peer in chip_peers:
            small.append(wires.far(i_in, i_all.at[c], peer))
            small.append(wires.far(x_in, x_all.at[c], peer))
        m_first.wait()
        m_sum[...] = m_in[k] + m_core[...]
        m_chip[c] = m_sum[...]
        m_second = [wires.far(m_sum, m_chip.at[c], peer) for _, peer in chip_peers]
        for _, peer in plane_peers:
            p_got.append(wires.far(p_in, p_chip.at[k, f], peer))
        for _, peer in plane_peers:
            f1_got.append(wires.far(f1_in, f1_rows.at[pl.ds(f * per_1, per_1)], peer))
        for _, peer in plane_peers:
            f2_got.append(wires.far(f2_in, f2_chip.at[k, f], peer))
        p_got.append(wires.near(p_in, p_chip.at[k, f]))
        f1_got.append(wires.near(f1_in, f1_rows.at[pl.ds(f * per_1, per_1)]))
        f2_got.append(wires.near(f2_in, f2_chip.at[k, f]))
        small.append(wires.near(i_in, i_all.at[c]))
        small.append(wires.near(x_in, x_all.at[c]))
        for _, peer in chip_peers:
            small.append(wires.far(c_in, c_all.at[c], peer))
        small.append(wires.near(c_in, c_all.at[c]))
        wait_all(m_second)
        total = m_chip[0]
        for other in range(1, nc):
            total = total + m_chip[other]
        m_all[f, k] = total
        wait_all([wires.far(m_all.at[f, k], m_all.at[f, k], peer) for _, peer in plane_peers])
        m_last = wires.far(m_all.at[:, k], m_all.at[:, k], core_peer)

        wait_all(q_got)
        q_moved = []
        for kind in range(3):
            for other, peer in chip_peers:
                q_moved.append(
                    wires.far(
                        q_rows.at[pl.ds(kind * part_q + other * chip_q, chip_q)],
                        q_chip.at[kind, c, k],
                        peer,
                    )
                )
            q_moved.append(
                wires.near(
                    q_rows.at[pl.ds(kind * part_q + c * chip_q, chip_q)], q_chip.at[kind, c, k]
                )
            )
        wait_all(p_got)
        last = [m_last, wires.far(p_chip.at[k], p_chip.at[k], core_peer)]
        wait_all(q_moved)
        last.append(wires.far(q_chip.at[:, :, k], q_chip.at[:, :, k], core_peer))
        wait_all(f1_got)
        f1_moved = []
        for other, peer in chip_peers:
            f1_moved.append(
                wires.far(f1_rows.at[pl.ds(other * chip_1, chip_1)], f1_chip.at[:, c, k], peer)
            )
        f1_moved.append(
            wires.near(f1_rows.at[pl.ds(c * chip_1, chip_1)], f1_chip.at[:, c, k])
        )
        wait_all(f2_got)
        last.append(wires.far(f2_chip.at[k], f2_chip.at[k], core_peer))
        wait_all(f1_moved)
        last.append(wires.far(f1_chip.at[:, :, k], f1_chip.at[:, :, k], core_peer))
        wait_all(small)
        wait_all(last)

    return pl.pallas_call(
        kernel,
        out_shape=outs,
        in_specs=[ANYWHERE] * 4 + [ON_CHIP] + [ANYWHERE] * 4,
        out_specs=tuple([ANYWHERE] * 4 + [ON_CHIP] + [ANYWHERE] * 6),
        scratch_shapes=[
            pltpu.VMEM((rows, half), F32),
            pltpu.VMEM((rows, half), F32),
            pltpu.VMEM((nc, rows, half), F32),
            pltpu.SemaphoreType.DMA((n_far,)),
            pltpu.SemaphoreType.DMA((n_far,)),
            pltpu.SemaphoreType.DMA((12,)),
        ],
        compiler_params=pltpu.CompilerParams(collective_id=0, has_side_effects=True),
        name="start",
    )(x, cot, ids, bias, mod, wq, w1, wp, w2)


def sum_small_kernel(dims, terms):
    nc, nf = dims.nc, dims.nf
    _, _, rows, half = terms.shape
    n_far = (nf - 1) + 1 + (nc - 1) + 1

    def kernel(t_in, total, z_got, both, core_got, chip_got, send, recv, local):
        place = Place(nc, nf)
        wires = Wires(send, recv, local)
        c, k, f = place.c, place.k, place.f
        greet(place, (CORE, CHIP, PLANE))
        core_other, core_peer = place.peer(CORE, 1)
        copies = []
        for step in range(1, nf):
            other, peer = place.peer(PLANE, step)
            copies.append(wires.far(t_in.at[other], z_got.at[f], peer))
        z_got[f] = t_in[f]
        wait_all(copies)
        value = z_got[0]
        for other in range(1, nf):
            value = value + z_got[other]
        both[...] = value
        wires.far(both.at[core_other], core_got, core_peer).wait()
        chip_got[c] = both[k] + core_got[...]
        copies = []
        for step in range(1, nc):
            _, peer = place.peer(CHIP, step)
            copies.append(wires.far(chip_got.at[c], chip_got.at[c], peer))
        wait_all(copies)
        value = chip_got[0]
        for other in range(1, nc):
            value = value + chip_got[other]
        total[k] = value
        wires.far(total.at[k], total.at[k], core_peer).wait()

    return pl.pallas_call(
        kernel,
        out_shape=jax.ShapeDtypeStruct((2, rows, half), F32),
        in_specs=[ON_CHIP],
        out_specs=ON_CHIP,
        scratch_shapes=[
            pltpu.VMEM((nf, 2, rows, half), F32),
            pltpu.VMEM((2, rows, half), F32),
            pltpu.VMEM((rows, half), F32),
            pltpu.VMEM((nc, rows, half), F32),
            pltpu.SemaphoreType.DMA((n_far,)),
            pltpu.SemaphoreType.DMA((n_far,)),
            pltpu.SemaphoreType.DMA((1,)),
        ],
        compiler_params=pltpu.CompilerParams(collective_id=1, has_side_effects=True),
        name="sum_small",
    )(terms)


def cond_kernel(dims, part):
    nc, nf = dims.nc, dims.nf
    nd = 2 * nc
    rows, width = part.shape
    n_far = (nf - 1) + (nd - 1)

    def kernel(p_in, out, got, send, recv, local):
        place = Place(nc, nf)
        wires = Wires(send, recv, local)
        greet(place, (PLANE, ALL))
        copies = []
        for step in range(1, nf):
            copies.append(wires.far(p_in, got.at[place.f], place.peer(PLANE, step)[1]))
        got[place.f] = p_in[...]
        wait_all(copies)
        value = got[0]
        for other in range(1, nf):
            value = value + got[other]
        out[place.dp] = value
        copies = []
        for step in range(1, nd):
            copies.append(
                wires.far(out.at[place.dp], out.at[place.dp], place.peer(ALL, step)[1])
            )
        wait_all(copies)

    return pl.pallas_call(
        kernel,
        out_shape=jax.ShapeDtypeStruct((nd, rows, width), F32),
        in_specs=[ON_CHIP],
        out_specs=ON_CHIP,
        scratch_shapes=[
            pltpu.VMEM((nf, rows, width), F32),
            pltpu.SemaphoreType.DMA((n_far,)),
            pltpu.SemaphoreType.DMA((n_far,)),
            pltpu.SemaphoreType.DMA((1,)),
        ],
        compiler_params=pltpu.CompilerParams(collective_id=2, has_side_effects=True),
        name="cond_sum",
    )(part)


def dot(left, right):
    return jnp.dot(left, right, preferred_element_type=F32)


def dot_rt(left, right):
    return lax.dot_general(left, right, (((1,), (1,)), ((), ())), preferred_element_type=F32)


def dot_lt(left, right):
    return lax.dot_general(left, right, (((0,), (0,)), ((), ())), preferred_element_type=F32)


def precise(left, right, dims):
    return lax.dot_general(
        left, right, (dims, ((), ())), precision=PRECISE, preferred_element_type=F32
    )


def ln_parts(values):
    centre = values - jnp.mean(values, axis=-1, keepdims=True)
    scale = lax.rsqrt(jnp.mean(centre * centre, axis=-1, keepdims=True) + EPS)
    return centre * scale, scale


def ln_back(normal, scale, grad):
    return scale * (
        grad
        - jnp.mean(grad, axis=-1, keepdims=True)
        - normal * jnp.mean(grad * normal, axis=-1, keepdims=True)
    )


def gelu_both(h):
    square = h * h
    t = jnp.tanh(GELU_C * (h + 0.044715 * h * square))
    value = 0.5 * h * (1.0 + t)
    slope = 0.5 * (1.0 + t) + 0.5 * h * (1.0 - t * t) * GELU_C * (1.0 + 3 * 0.044715 * square)
    return value, slope


def dot3(left, right):
    wide_left = left.dtype == F32
    value = left if wide_left else right
    total = None
    for _ in range(3):
        term = value.astype(BF16)
        value = value - term.astype(F32)
        part = dot(term, right) if wide_left else dot(left, term)
        total = part if total is None else total + part
    return total


def add_low(left, right):
    return (left.astype(F32) + right.astype(F32)).astype(BF16)


def block_kernel(dims, x, cot, ids, bias, silu_part, cond_own, w_ada, wq, wp, w1, w2):
    nc, nf = dims.nc, dims.nf
    own, width = x.shape
    group = nc * own
    rows_d, q_w = wq.shape
    chip_w = q_w // 3
    ff_d, cols_f = w2.shape
    ff_c = 2 * ff_d
    ada_w = w_ada.shape[1]
    n_bias = bias.shape[1]
    heads = chip_w // HEAD_DIM
    n_rows = silu_part.shape[0]
    half = n_rows // 2
    n_sub = own // SUB
    head_scale = HEAD_DIM ** (-0.5)
    last = nf - 2

    outs = (
        jax.ShapeDtypeStruct((own, width), BF16),
        jax.ShapeDtypeStruct((own, width), BF16),
        jax.ShapeDtypeStruct((n_rows, cols_f), F32),
        jax.ShapeDtypeStruct((rows_d, ada_w), F32),
        jax.ShapeDtypeStruct((1, ada_w), F32),
        jax.ShapeDtypeStruct((rows_d, q_w), F32),
        jax.ShapeDtypeStruct((1, 2 * chip_w), F32),
        jax.ShapeDtypeStruct((rows_d, cols_f), F32),
        jax.ShapeDtypeStruct((1, cols_f), F32),
        jax.ShapeDtypeStruct((rows_d, ff_c), F32),
        jax.ShapeDtypeStruct((1, ff_c), F32),
        jax.ShapeDtypeStruct((ff_d, cols_f), F32),
        jax.ShapeDtypeStruct((1, cols_f), F32),
    )
    tokens = (nc, own, width)
    n_sem = 240
    scratch = dict(
        xg=pltpu.VMEM(tokens, BF16),
        cg=pltpu.VMEM(tokens, BF16),
        idsg=pltpu.VMEM((nc, 8, own), F32),
        biasg=pltpu.VMEM((nf, 1, n_bias), F32),
        ada=pltpu.VMEM(w_ada.shape, BF16),
        m_part=pltpu.VMEM((2, half, ada_w), F32),
        m_core=pltpu.VMEM((half, ada_w), F32),
        m_chip=pltpu.VMEM((nc, half, ada_w), F32),
        m_z=pltpu.VMEM((nf, 2, half, ada_w), F32),
        m_tab=pltpu.VMEM((n_rows, 6 * width), F32),
        tab=pltpu.VMEM((3, nc * n_sub, width), F32),
        own_tab=pltpu.VMEM((6, n_sub, width), F32),
        q_z=pltpu.VMEM((nf, rows_d, q_w), BF16),
        q_rows=pltpu.VMEM((nf * 3, rows_d, chip_w), BF16),
        w_q=pltpu.VMEM((3, nc, 2, rows_d, chip_w), BF16),
        f1_z=pltpu.VMEM((nf, rows_d, ff_c), BF16),
        w_1=pltpu.VMEM((nc, 2, rows_d, ff_c), BF16),
        p_got=pltpu.VMEM((2, nf, rows_d, cols_f), BF16),
        w_p=pltpu.VMEM((chip_w, width), BF16),
        f2_nat=pltpu.VMEM((ff_d, cols_f), BF16),
        f2_half=pltpu.VMEM((2, rows_d, ff_d), BF16),
        f2_got=pltpu.VMEM((rows_d, ff_d), BF16),
        w_2=pltpu.VMEM((nf, 2, rows_d, ff_c), BF16),
        a_in=pltpu.VMEM(tokens, BF16),
        qkv=pltpu.VMEM((3, nc, own, chip_w), BF16),
        probs=pltpu.VMEM((nc * heads, own, own), F32),
        mixed=pltpu.VMEM((nc, own, chip_w), BF16),
        sum_s=pltpu.VMEM(tokens, BF16),
        sum_r=pltpu.VMEM(tokens, BF16),
        br_s=pltpu.VMEM(tokens, BF16),
        br_r=pltpu.VMEM(tokens, BF16),
        m_all=pltpu.VMEM(tokens, BF16),
        da_all=pltpu.VMEM(tokens, BF16),
        attn=pltpu.VMEM((own, width), F32),
        after=pltpu.VMEM((own, width), F32),
        d_after=pltpu.VMEM((own, width), F32),
        hid=pltpu.VMEM((own, ff_c), F32),
        slope=pltpu.VMEM((own, ff_c), F32),
        act=pltpu.VMEM((nc, own, ff_c), BF16),
        d_hid=pltpu.VMEM((nc, own, ff_c), BF16),
        dbr=pltpu.VMEM(tokens, BF16),
        d_qkv=pltpu.VMEM((3, nc, own, chip_w), BF16),
        g_2=pltpu.VMEM((nf, 2, rows_d, ff_c), BF16),
        g_2r=pltpu.VMEM((nf, rows_d, ff_c), BF16),
        g_1r=pltpu.VMEM((nc, rows_d, ff_c), BF16),
        g_qr=pltpu.VMEM((3, nc, rows_d, chip_w), BF16),
        g_pr=pltpu.VMEM((rows_d, width), BF16),
        got_q=pltpu.VMEM((2, nf - 1, rows_d, q_w), BF16),
        got_1=pltpu.VMEM((2, nf - 1, rows_d, ff_c), BF16),
        got_p=pltpu.VMEM((2, nf - 1, rows_d, cols_f), BF16),
        got_2=pltpu.VMEM((2, nf - 1, rows_d, ff_c), BF16),
        all_2=pltpu.VMEM((2, rows_d, ff_c), F32),
        sub=pltpu.VMEM((6, n_sub, width), F32),
        d_cut=pltpu.VMEM((nf, n_rows, ada_w), F32),
        d_bias=pltpu.VMEM((8, width), F32),
        dz=pltpu.VMEM((nf, n_rows, ada_w), F32),
        dzb=pltpu.VMEM((nf, 8, width), F32),
        d_both=pltpu.VMEM((2, half, ada_w), F32),
        d_tot=pltpu.VMEM((2, half, ada_w), F32),
        d_bsum=pltpu.VMEM((8, width), F32),
        d_coreb=pltpu.VMEM((8, width), F32),
        d_chipb=pltpu.VMEM((nc, 8, width), F32),
        c_part=pltpu.VMEM((nf, n_rows, rows_d), F32),
        c_all=pltpu.VMEM((nc, 2, n_rows, rows_d), F32),
        send=pltpu.SemaphoreType.DMA((n_sem,)),
        recv=pltpu.SemaphoreType.DMA((n_sem,)),
        local=pltpu.SemaphoreType.DMA((32,)),
    )
    names = list(scratch)

    def kernel(
        x_in, c_in, ids_in, bias_in, silu_in, cond_in, ada_in, q_in, p_in, f1_in, f2_in,
        out, x_grad, o_cond, o_ada, o_bada, o_q, o_bqv, o_p, o_bp, o_1, o_b1, o_2, o_b2, *rest,
    ):
        r = types.SimpleNamespace(**dict(zip(names, rest)))
        place = Place(nc, nf)
        wires = Wires(r.send, r.recv, r.local)
        c, k, f = place.c, place.k, place.f
        core_o, core_dev = place.peer(CORE, 1)
        chip_peers = [place.peer(CHIP, step) for step in range(1, nc)]
        plane_peers = [place.peer(PLANE, step) for step in range(1, nf)]

        def loop(count, body):
            def run(i, carry):
                body(i)
                return carry

            lax.fori_loop(0, count, run, 0)

        def when(condition, body):
            pl.when(condition)(body)

        def sub_rows(g):
            return pl.ds(pl.multiple_of(g * SUB, SUB), SUB)

        def reserve(count):
            base = wires.remote_count
            wires.remote_count += count
            return base

        def pair(src, dst, device, send_at, recv_at):
            return pltpu.make_async_remote_copy(
                src_ref=src,
                dst_ref=dst,
                send_sem=r.send.at[send_at],
                recv_sem=r.recv.at[recv_at],
                device_id=device,
                device_id_type=MESH_ID,
            )

        def chip_send(src, dst, base, step):
            other, device = place.peer(CHIP, step)
            at = base + step - 1
            return pair(src(other), dst.at[c], device, at, at)

        up, down = (place.dp, f + 1), (place.dp, f - 1)

        class Gather:
            def __init__(self, slot):
                self.slot = slot
                self.up, self.down = reserve(nf - 1), reserve(nf - 1)

            def both(self, step, src=None):
                above = pair(
                    self.slot(f - step) if src is None else src,
                    self.slot(f - step), up, self.up + step, self.up + step,
                )
                below = pair(
                    self.slot(f + step) if src is None else src,
                    self.slot(f + step), down, self.down + step, self.down + step,
                )
                return (
                    ((f - step >= 0) & (f < nf - 1), above),
                    ((f + step <= nf - 1) & (f > 0), below),
                )

            def start(self, step, src=None):
                for condition, copy in self.both(step, src):
                    when(condition, copy.start)

            def arrive(self, step, then=None):
                for condition, got, base in (
                    (f - 1 - step >= 0, f - 1 - step, self.up),
                    (f + 1 + step <= nf - 1, f + 1 + step, self.down),
                ):

                    def body(got=got, base=base):
                        slot = self.slot(got)
                        pair(slot, slot, core_dev, base + step, base + step).wait_recv()
                        if then is not None:
                            then(got)

                    when(condition, body)

            def sent(self, src=None):
                for step in range(nf - 1):
                    for condition, copy in self.both(step, src if step == 0 else None):
                        when(condition, copy.wait_send)

        class Sum:
            def __init__(self, terms, got):
                self.terms, self.got = terms, got
                self.bases = (reserve(nf - 1), reserve(nf - 1))

            def both(self, step):
                for way in range(2):
                    target = f + (nf - 1) - step if way == 0 else f - (nf - 1) + step
                    condition = (f <= step) & (f < nf - 1) if way == 0 else (target >= 0) & (f > 0)
                    more = condition & (f > 0 if way == 0 else f < nf - 1)
                    at = self.bases[way] + step
                    copy = pair(
                        self.terms(target), self.got.at[way, step], up if way == 0 else down, at, at
                    )
                    yield way, target, condition, more, copy

            def wait(self, way, step):
                at = self.bases[way] + step
                ref = self.got.at[way, step]
                pair(ref, ref, core_dev, at, at).wait_recv()

            def start(self, step):
                for way, target, condition, more, copy in self.both(step):
                    if step > 0:

                        def body(way=way, target=target):
                            self.wait(way, step - 1)
                            ref = self.terms(target)
                            ref[...] = add_low(ref[...], self.got[way, step - 1])

                        when(more, body)
                    when(condition, copy.start)

            def finish(self, result):
                result[...] = self.terms(f)[...].astype(F32)
                for way, condition in ((0, f > 0), (1, f < nf - 1)):

                    def body(way=way):
                        self.wait(way, last)
                        result[...] = result[...] + self.got[way, last].astype(F32)

                    when(condition, body)
                for step in range(nf - 1):
                    for _, _, condition, _, copy in self.both(step):
                        when(condition, copy.wait_send)

        greet(place, (CORE, CHIP, PLANE))

        q_line = Gather(lambda g: r.q_z.at[g])
        p_line = Gather(lambda g: r.p_got.at[k, g])
        f1_line = Gather(lambda g: r.f1_z.at[g])
        f2_line = Gather(lambda g: r.w_2.at[g, k])
        q_line.start(0, q_in)
        ada_near = wires.near(ada_in, r.ada)
        q_near = wires.near(q_in, r.q_z.at[f])
        f2_near = wires.near(f2_in, r.f2_nat)
        first = []
        for _, peer in chip_peers:
            first.append(wires.far(ids_in, r.idsg.at[c], peer))
        for _, peer in plane_peers:
            first.append(wires.far(bias_in, r.biasg.at[f], peer))
        first.append(wires.near(x_in, r.xg.at[c]))
        first.append(wires.near(c_in, r.cg.at[c]))
        p_near = wires.near(p_in, r.p_got.at[k, f])
        f1_near = wires.near(f1_in, r.f1_z.at[f])
        r.idsg[c] = ids_in[...]
        r.biasg[f] = bias_in[...]
        ada_near.wait()
        ada_bias = jnp.where(place.dp == 0, bias_in[:, n_bias - ada_w :], 0.0)
        value = dot(silu_in[...], r.ada[...]) + ada_bias
        r.m_part[...] = value.reshape(2, half, ada_w)
        m_first = wires.far(r.m_part.at[core_o], r.m_core, core_dev)

        w_q, q_rows = r.w_q, r.q_rows
        q_base = reserve(3 * nc)
        q_local = wires.local_count
        wires.local_count += 3

        def q_copies(plane, i):
            piece = 3 * plane + i
            kind, chip = piece // nc, piece % nc
            src, dst = q_rows.at[piece], w_q.at[kind, c, k]
            far = pair(src, dst, (chip * 2 + k, f), q_base + kind * nc + chip, q_base + kind * nc + c)
            return chip, far, pltpu.make_async_copy(src, dst, r.local.at[q_local + kind])

        def q_forward(plane):
            for i in range(3):
                q_rows[3 * plane + i] = r.q_z[plane, :, chip_w * i : chip_w * (i + 1)]
                chip, far, near = q_copies(plane, i)
                when(chip != c, far.start)
                when(chip == c, near.start)

        f1_base = reserve(nc)
        f1_local = wires.local_count
        wires.local_count += 1

        def f1_copies(plane):
            src, dst = r.f1_z.at[plane], r.w_1.at[c, k]
            far = pair(src, dst, (plane * 2 + k, f), f1_base + plane, f1_base + c)
            return far, pltpu.make_async_copy(src, dst, r.local.at[f1_local])

        def f1_forward(plane):
            far, near = f1_copies(plane)
            when(plane != c, far.start)
            when(plane == c, near.start)

        q_near.wait()
        q_forward(f)
        m_first.wait()
        m_chip = r.m_chip
        m_chip[c] = r.m_part[k] + r.m_core[...]
        m_second = [wires.far(m_chip.at[c], m_chip.at[c], peer) for _, peer in chip_peers]
        for _, peer in chip_peers:
            first.append(wires.far(x_in, r.xg.at[c], peer))
        q_line.arrive(0, q_forward)
        q_line.start(1)
        wait_all(m_second)
        total = m_chip[0]
        for other in range(1, nc):
            total = total + m_chip[other]
        r.m_z[f, k] = total
        m_third = [wires.far(r.m_z.at[f, k], r.m_z.at[f, k], peer) for _, peer in plane_peers]
        p_line.start(0, p_in)
        f2_near.wait()
        turned = r.f2_nat[...].T
        r.f2_half[...] = turned.reshape(2, rows_d, ff_d)
        f2_swap = wires.far(r.f2_half.at[core_o], r.f2_got, core_dev)
        q_line.arrive(1, q_forward)
        q_line.start(2)
        p_line.arrive(0)
        p_line.start(1)
        f1_line.start(0, f1_in)
        f2_swap.wait()

        def join_even():
            r.w_2[f, k] = jnp.concatenate([r.f2_half[0], r.f2_got[...]], axis=1)

        def join_odd():
            r.w_2[f, k] = jnp.concatenate([r.f2_got[...], r.f2_half[1]], axis=1)

        when(k == 0, join_even)
        when(k == 1, join_odd)
        q_line.arrive(2, q_forward)
        p_line.arrive(1)
        p_line.start(2)
        wait_all(m_third)
        m_last = wires.far(r.m_z.at[:, k], r.m_z.at[:, k], core_dev)
        f2_line.start(0)

        wait_all(first)
        m_last.wait()
        m_rows = [r.m_z[plane].reshape(n_rows, ada_w) for plane in range(nf)]
        r.m_tab[...] = jnp.concatenate(m_rows, axis=1)
        lead = lax.broadcasted_iota(jnp.int32, (n_sub, own), 1)
        lead = lead == SUB * lax.broadcasted_iota(jnp.int32, (n_sub, own), 0)
        lead = jnp.where(lead, 1.0, 0.0).astype(BF16)
        places = lax.broadcasted_iota(jnp.int32, (own, n_rows), 1).astype(F32)

        def hot_rows(blk):
            clip = r.idsg[blk].T[:, 1:2]
            return dot(lead, jnp.where(clip == places, 1.0, 0.0).astype(BF16)).astype(BF16)

        hot_all = jnp.concatenate([hot_rows(blk) for blk in range(nc)], axis=0)
        own_hot = hot_rows(c)
        for kind in range(6):
            value = r.m_tab[:, width * kind : width * (kind + 1)]
            if kind in (0, 1, 5):
                r.tab[kind % 3] = dot3(hot_all, value)
            r.own_tab[kind] = dot3(own_hot, value)

        def tab_row(kind, blk, g):
            return r.tab[kind % 3, pl.ds(blk * n_sub + g, 1), :]

        def own_row(kind, g):
            return r.own_tab[kind, pl.ds(g, 1), :]

        def make_a(blk):
            def body(g):
                rows = sub_rows(g)
                normal, _ = ln_parts(r.xg[blk, rows, :].astype(F32))
                value = normal * (1.0 + tab_row(1, blk, g)) + tab_row(0, blk, g)
                r.a_in[blk, rows, :] = value.astype(BF16)

            loop(n_sub, body)

        loop(nc, make_a)

        q_core = []
        for kind in range(3):
            for other, _ in chip_peers:
                ref = w_q.at[kind, other, k]
                at = q_base + kind * nc + other
                pair(ref, ref, core_dev, at, at).wait()
            ref = w_q.at[kind, c, k]
            pltpu.make_async_copy(ref, ref, r.local.at[q_local + kind]).wait()
            q_core.append(wires.far(w_q.at[kind, :, k], w_q.at[kind, :, k], core_dev))
        p_line.arrive(2)
        p_near.wait()
        p_core = wires.far(r.p_got.at[k], r.p_got.at[k], core_dev)
        f1_near.wait()
        f1_forward(f)
        f1_line.arrive(0, f1_forward)
        f1_line.start(1)
        c_far = [wires.far(c_in, r.cg.at[c], peer) for _, peer in chip_peers]
        p_core.wait()
        for side in range(2):
            row = [r.p_got[side, plane] for plane in range(nf)]
            r.w_p[side * rows_d : (side + 1) * rows_d, :] = jnp.concatenate(row, axis=1)
        wait_all(q_core)

        lane = lax.broadcasted_iota(jnp.int32, (1, chip_w), 1)
        head_of = [
            jnp.where((lane >= HEAD_DIM * h) & (lane < HEAD_DIM * (h + 1)), 1.0, 0.0).astype(BF16)
            for h in range(heads)
        ]

        def weight_q(kind):
            return w_q[kind].reshape(width, chip_w)

        def qv_bias(plane):
            row = r.biasg[plane]
            return jnp.where(c % 2 == 0, row[:, :chip_w], row[:, chip_w : 2 * chip_w])

        bias_q, bias_v = qv_bias(c // 2), qv_bias(nf // 2 + c // 2)
        at_p = 2 * chip_w
        at_1 = at_p + cols_f
        at_2 = at_1 + ff_c
        bias_p = jnp.concatenate([r.biasg[g][:, at_p : at_p + cols_f] for g in range(nf)], axis=1)
        bias_o = jnp.concatenate([r.biasg[g][:, at_2 : at_2 + cols_f] for g in range(nf)], axis=1)
        bias_1 = r.biasg[c][:, at_1 : at_1 + ff_c]
        sum_base = reserve(nc - 1)
        sum_s, sum_r = r.sum_s, r.sum_r

        def hand_on(step, blk, part, s_ref, r_ref, base):
            def away():
                s_ref[blk] = part
                chip_send(lambda other: s_ref.at[other], r_ref, base, step).start()

            def stay():
                r_ref[c] = part

            when(step != 0, away)
            when(step == 0, stay)

        def attend(i):
            step = (i + 1) % nc
            blk = xor_of(c, step, nc)
            a_now = r.a_in[blk]
            r.qkv[0, blk] = (dot(a_now, weight_q(0)) + bias_q).astype(BF16)
            r.qkv[1, blk] = dot(a_now, weight_q(1)).astype(BF16)
            r.qkv[2, blk] = (dot(a_now, weight_q(2)) + bias_v).astype(BF16)
            q_now, k_now, v_now = r.qkv[0, blk], r.qkv[1, blk], r.qkv[2, blk]
            frames = r.idsg[blk]
            same = frames.T[:, 0:1] == frames[0:1, :]
            mixed = jnp.zeros((own, chip_w), F32)
            for h in range(heads):
                scores = dot_rt(q_now * head_of[h], k_now) * head_scale
                scores = jnp.where(same, scores, NEG_FILL)
                raised = jnp.exp(scores - jnp.max(scores, axis=-1, keepdims=True))
                share = raised / jnp.sum(raised, axis=-1, keepdims=True)
                r.probs[blk * heads + h] = share
                mixed = mixed + dot(share.astype(BF16), v_now * head_of[h])
            mixed = mixed.astype(BF16)
            r.mixed[blk] = mixed
            hand_on(step, blk, dot(mixed, r.w_p[...]).astype(BF16), sum_s, sum_r, sum_base)

        loop(nc, attend)
        f1_line.arrive(1, f1_forward)
        f1_line.start(2)
        f2_line.arrive(0)
        f2_line.start(1)

        for step in range(1, nc):
            chip_send(lambda other: sum_s.at[other], sum_r, sum_base, step).wait()

        def after_attention(g):
            rows = sub_rows(g)
            value = sum_r[0, rows, :].astype(F32)
            for other in range(1, nc):
                value = value + sum_r[other, rows, :].astype(F32)
            value = value + bias_p
            r.attn[rows, :] = value
            after = r.xg[c, rows, :].astype(F32) + own_row(2, g) * value
            r.after[rows, :] = after
            normal, _ = ln_parts(after)
            r.m_all[c, rows, :] = (normal * (1.0 + own_row(4, g)) + own_row(3, g)).astype(BF16)

        loop(n_sub, after_attention)
        m_all = r.m_all
        m_base = reserve(nc - 1)
        for step in range(1, nc):
            chip_send(lambda other: m_all.at[c], m_all, m_base, step).start()
        f1_line.arrive(2, f1_forward)
        f2_line.arrive(1)
        f2_line.start(2)
        wait_all(c_far)

        def make_dbr(blk):
            def body(g):
                rows = sub_rows(g)
                value = r.cg[blk, rows, :].astype(F32) * tab_row(5, blk, g)
                r.dbr[blk, rows, :] = value.astype(BF16)

            loop(n_sub, body)

        loop(nc, make_dbr)
        for other, _ in chip_peers:
            ref = r.w_1.at[other, k]
            pair(ref, ref, core_dev, f1_base + other, f1_base + other).wait()
        ref = r.w_1.at[c, k]
        pltpu.make_async_copy(ref, ref, r.local.at[f1_local]).wait()
        f1_line.sent(f1_in)
        f1_core = wires.far(r.w_1.at[:, k], r.w_1.at[:, k], core_dev)
        f2_line.arrive(2)
        f2_core = wires.far(r.w_2.at[:, k], r.w_2.at[:, k], core_dev)
        f1_core.wait()
        f2_core.wait()

        def weight_1():
            return r.w_1[...].reshape(width, ff_c)

        def weight_2():
            return r.w_2[...].reshape(width, ff_c)

        dm_base = reserve(nc - 1)
        br_base = reserve(nc - 1)
        br_s, br_r = r.br_s, r.br_r

        def feed(step):
            blk = xor_of(c, step, nc)
            when(
                step != 0,
                lambda: chip_send(lambda other: m_all.at[c], m_all, m_base, step).wait_recv(),
            )
            r.hid[...] = dot(m_all[blk], weight_1()) + bias_1

            def gelu_rows(g):
                rows = sub_rows(g)
                value, slope = gelu_both(r.hid[rows, :])
                r.act[blk, rows, :] = value.astype(BF16)
                r.slope[rows, :] = slope

            loop(n_sub, gelu_rows)
            r.hid[...] = dot(r.dbr[blk], weight_2())

            def back_rows(g):
                rows = sub_rows(g)
                r.d_hid[blk, rows, :] = (r.hid[rows, :] * r.slope[rows, :]).astype(BF16)

            loop(n_sub, back_rows)
            part = dot_rt(r.d_hid[blk], weight_1()).astype(BF16)
            hand_on(step, blk, part, sum_s, sum_r, dm_base)

        loop(nc, feed)
        for step in range(1, nc):
            chip_send(lambda other: m_all.at[c], m_all, m_base, step).wait_send()

        def column_cuts(count):
            return [(at, min(at + 256, count)) for at in range(0, count, 256)]

        def all_rows(ref):
            return ref[...].reshape(group, ref.shape[-1])

        dbr_all = all_rows(r.dbr)
        for lo, hi in column_cuts(ff_c):
            value = dot_lt(dbr_all, r.act[:, :, lo:hi].reshape(group, hi - lo))
            r.g_2[:, :, :, lo:hi] = value.astype(BF16).reshape(nf, 2, rows_d, hi - lo)
        g2_core = wires.far(r.g_2.at[:, core_o], r.g_2r, core_dev)

        def branch_out(i):
            step = (i + 1) % nc
            blk = xor_of(c, step, nc)
            part = dot_rt(r.act[blk], weight_2()).astype(BF16)
            hand_on(step, blk, part, br_s, br_r, br_base)

        loop(nc, branch_out)
        g2_core.wait()
        for plane in range(nf):
            r.g_2[plane, k] = add_low(r.g_2[plane, k], r.g_2r[plane])
        sum_2 = Sum(lambda t: r.g_2.at[t, k], r.got_2)
        sum_2.start(0)

        for step in range(1, nc):
            chip_send(lambda other: sum_s.at[other], sum_r, dm_base, step).wait()
        da_all = r.da_all

        def back_norm2(g):
            rows = sub_rows(g)
            d_m = sum_r[0, rows, :].astype(F32)
            for other in range(1, nc):
                d_m = d_m + sum_r[other, rows, :].astype(F32)
            normal, scale = ln_parts(r.after[rows, :])
            cot_now = r.cg[c, rows, :].astype(F32)
            d_after = cot_now + ln_back(normal, scale, d_m * (1.0 + own_row(4, g)))
            r.d_after[rows, :] = d_after
            da_all[c, rows, :] = (own_row(2, g) * d_after).astype(BF16)
            at = pl.ds(g, 1)
            r.sub[3, at, :] = jnp.sum(d_m, axis=0, keepdims=True)
            r.sub[4, at, :] = jnp.sum(d_m * normal, axis=0, keepdims=True)
            r.sub[2, at, :] = jnp.sum(d_after * r.attn[rows, :], axis=0, keepdims=True)

        loop(n_sub, back_norm2)
        da_base = reserve(nc - 1)
        for step in range(1, nc):
            chip_send(lambda other: da_all.at[c], da_all, da_base, step).start()
        sum_2.start(1)

        g_1 = r.w_1
        m_rows_all = all_rows(m_all)
        for lo, hi in column_cuts(ff_c):
            value = dot_lt(m_rows_all, r.d_hid[:, :, lo:hi].reshape(group, hi - lo))
            g_1[:, :, :, lo:hi] = value.astype(BF16).reshape(nc, 2, rows_d, hi - lo)
        g1_core = wires.far(g_1.at[:, core_o], r.g_1r, core_dev)

        for step in range(1, nc):
            chip_send(lambda other: br_s.at[other], br_r, br_base, step).wait()

        def finish_out(g):
            rows = sub_rows(g)
            branch = br_r[0, rows, :].astype(F32)
            for other in range(1, nc):
                branch = branch + br_r[other, rows, :].astype(F32)
            branch = branch + bias_o
            out[rows, :] = (r.after[rows, :] + own_row(5, g) * branch).astype(BF16)
            cot_now = r.cg[c, rows, :].astype(F32)
            r.sub[5, pl.ds(g, 1), :] = jnp.sum(cot_now * branch, axis=0, keepdims=True)

        loop(n_sub, finish_out)
        g1_core.wait()
        for chip in range(nc):
            g_1[chip, k] = add_low(g_1[chip, k], r.g_1r[chip])
        y_1 = r.f1_z
        y_1[c] = g_1[c, k]
        y1_far = [wires.far(g_1.at[other, k], y_1.at[c], peer) for other, peer in chip_peers]
        sum_2.start(2)

        back_base = reserve(nc - 1)

        def attend_back(step):
            blk = xor_of(c, step, nc)
            when(
                step != 0,
                lambda: chip_send(lambda other: da_all.at[c], da_all, da_base, step).wait_recv(),
            )
            d_mix = dot_rt(da_all[blk], r.w_p[...]).astype(BF16)
            q_now, k_now, v_now = r.qkv[0, blk], r.qkv[1, blk], r.qkv[2, blk]
            d_q = jnp.zeros((own, chip_w), F32)
            d_k = jnp.zeros((own, chip_w), F32)
            d_v = jnp.zeros((own, chip_w), F32)
            for h in range(heads):
                d_mix_h = d_mix * head_of[h]
                share = r.probs[blk * heads + h]
                d_share = dot_rt(d_mix_h, v_now)
                d_score = share * (d_share - jnp.sum(share * d_share, axis=-1, keepdims=True))
                d_score = d_score.astype(BF16)
                d_q = d_q + dot(d_score, k_now * head_of[h])
                d_k = d_k + dot_lt(d_score, q_now * head_of[h])
                d_v = d_v + dot_lt(share.astype(BF16), d_mix_h)
            d_q = (d_q * head_scale).astype(BF16)
            d_k = (d_k * head_scale).astype(BF16)
            d_v = d_v.astype(BF16)
            r.d_qkv[0, blk] = d_q
            r.d_qkv[1, blk] = d_k
            r.d_qkv[2, blk] = d_v
            part = dot_rt(d_q, weight_q(0)) + dot_rt(d_k, weight_q(1)) + dot_rt(d_v, weight_q(2))
            hand_on(step, blk, part.astype(BF16), sum_s, sum_r, back_base)

        loop(nc, attend_back)
        for step in range(1, nc):
            chip_send(lambda other: da_all.at[c], da_all, da_base, step).wait_send()
        wait_all(y1_far)
        sum_1 = Sum(lambda t: y_1.at[t], r.got_1)
        sum_1.start(0)

        g_q, g_p = w_q, r.w_p
        a_rows = all_rows(r.a_in)
        q_core_back = []
        for kind in range(3):
            for lo, hi in column_cuts(chip_w):
                value = dot_lt(a_rows, r.d_qkv[kind, :, :, lo:hi].reshape(group, hi - lo))
                g_q[kind, :, :, :, lo:hi] = value.astype(BF16).reshape(nc, 2, rows_d, hi - lo)
            q_core_back.append(wires.far(g_q.at[kind, :, core_o], r.g_qr.at[kind], core_dev))
        g_p[...] = dot_lt(all_rows(r.mixed), all_rows(da_all)).astype(BF16)

        def own_side(ref, side):
            return ref.at[pl.ds(pl.multiple_of(side * rows_d, SUB), rows_d)]

        p_core_back = wires.far(own_side(g_p, core_o), r.g_pr, core_dev)
        yq_far = []
        for kind in range(3):
            q_core_back[kind].wait()
            for chip in range(nc):
                g_q[kind, chip, k] = add_low(g_q[kind, chip, k], r.g_qr[kind, chip])
            q_rows[kind * nc + c] = g_q[kind, c, k]
            for other, peer in chip_peers:
                yq_far.append(wires.far(g_q.at[kind, other, k], q_rows.at[kind * nc + c], peer))
        p_core_back.wait()
        p_line.sent(p_in)
        y_p = r.p_got
        total = add_low(own_side(g_p, k)[...], r.g_pr[...])
        for plane in range(nf):
            y_p[k, plane] = total[:, plane * cols_f : (plane + 1) * cols_f]
        sum_p = Sum(lambda t: y_p.at[k, t], r.got_p)
        sum_p.start(0)
        sum_1.start(1)

        for step in range(1, nc):
            chip_send(lambda other: sum_s.at[other], sum_r, back_base, step).wait()

        def back_norm1(g):
            rows = sub_rows(g)
            d_a = sum_r[0, rows, :].astype(F32)
            for other in range(1, nc):
                d_a = d_a + sum_r[other, rows, :].astype(F32)
            normal, scale = ln_parts(r.xg[c, rows, :].astype(F32))
            value = r.d_after[rows, :] + ln_back(normal, scale, d_a * (1.0 + own_row(1, g)))
            x_grad[rows, :] = value.astype(BF16)
            at = pl.ds(g, 1)
            r.sub[0, at, :] = jnp.sum(d_a, axis=0, keepdims=True)
            r.sub[1, at, :] = jnp.sum(d_a * normal, axis=0, keepdims=True)

        loop(n_sub, back_norm1)
        hot_turned = own_hot.astype(F32).T.astype(BF16)
        for kind in range(6):
            r.m_tab[:, width * kind : width * (kind + 1)] = dot3(hot_turned, r.sub[kind])
        for plane in range(nf):
            r.d_cut[plane] = r.m_tab[:, ada_w * plane : ada_w * (plane + 1)]
        ones_own = jnp.ones((8, own), BF16)
        ones_all = jnp.ones((8, group), BF16)
        r.d_bias[...] = jnp.zeros((8, width), F32)
        r.d_bias[0:1, :] = dot(ones_own, da_all[c])[0:1]
        r.d_bias[1:2, :] = dot(ones_own, r.dbr[c])[0:1]
        r.d_bias[2:3, 0:chip_w] = dot(ones_all, all_rows(r.d_qkv.at[0]))[0:1]
        r.d_bias[3:4, 0:chip_w] = dot(ones_all, all_rows(r.d_qkv.at[2]))[0:1]

        ones_ff = dot(ones_all, all_rows(r.d_hid))[0:1]
        r.d_bias[4:5, :] = ones_ff[:, :width]
        for part in range(1, ff_c // width):
            r.d_bias[4 + part : 5 + part, :] = ones_ff[:, part * width : (part + 1) * width]
        small = []
        for other, peer in plane_peers:
            small.append(wires.far(r.d_cut.at[other], r.dz.at[f], peer))
            small.append(wires.far(r.d_bias, r.dzb.at[f], peer))
        r.dz[f] = r.d_cut[f]
        r.dzb[f] = r.d_bias[...]
        sum_1.start(2)
        wait_all(yq_far)
        q_line.sent(q_in)
        y_q = r.q_z
        for plane in range(nf):
            row = [q_rows[3 * plane + i] for i in range(3)]
            y_q[plane] = jnp.concatenate(row, axis=1)
        sum_q = Sum(lambda t: y_q.at[t], r.got_q)
        sum_q.start(0)
        sum_p.start(1)
        wait_all(small)
        value, value_b = r.dz[0], r.dzb[0]
        for plane in range(1, nf):
            value = value + r.dz[plane]
            value_b = value_b + r.dzb[plane]
        r.d_both[...] = value.reshape(2, half, ada_w)
        r.d_bsum[...] = value_b
        small = [
            wires.far(r.d_both.at[core_o], r.m_core, core_dev),
            wires.far(r.d_bsum, r.d_coreb, core_dev),
        ]
        sum_q.start(1)
        sum_p.start(2)
        wait_all(small)
        m_chip[c] = r.d_both[k] + r.m_core[...]
        r.d_chipb[c] = r.d_bsum[...] + r.d_coreb[...]
        small = []
        for _, peer in chip_peers:
            small.append(wires.far(m_chip.at[c], m_chip.at[c], peer))
            small.append(wires.far(r.d_chipb.at[c], r.d_chipb.at[c], peer))

        sum_2.finish(r.all_2.at[k])
        o2_swap = wires.far(r.all_2.at[k], r.all_2.at[k], core_dev)
        wait_all(small)
        value = m_chip[0]
        for chip in range(1, nc):
            value = value + m_chip[chip]
        r.d_tot[k] = value
        d_swap = wires.far(r.d_tot.at[k], r.d_tot.at[k], core_dev)
        sum_q.start(2)
        d_swap.wait()
        d_cols = r.d_tot[...].reshape(n_rows, ada_w)
        silu_turned = silu_in[...].astype(F32).T.astype(BF16)
        o_bada[...] = jnp.sum(d_cols, axis=0, keepdims=True)
        value, total = d_cols, None
        for _ in range(3):
            term = value.astype(BF16)
            value = value - term.astype(F32)
            part = dot_rt(term, r.ada[...])
            total = part if total is None else total + part
        r.c_part[f] = total
        c_far = [wires.far(r.c_part.at[f], r.c_part.at[f], peer) for _, peer in plane_peers]
        for lo, hi in column_cuts(ada_w):
            o_ada[:, lo:hi] = dot3(silu_turned, d_cols[:, lo:hi])
        sum_1.finish(o_1)
        o2_swap.wait()

        def own_columns(lo):
            def body():
                both = r.all_2[:, :, lo : lo + ff_d].reshape(cols_f, ff_d)
                o_2[...] = both.T

            return body

        when(k == 0, own_columns(0))
        when(k == 1, own_columns(ff_d))
        wait_all(c_far)
        value = r.c_part[0]
        for plane in range(1, nf):
            value = value + r.c_part[plane]
        r.c_all[c, k] = value
        wait_all([wires.far(r.c_all.at[c, k], r.c_all.at[c, k], peer) for _, peer in chip_peers])
        c_swap = wires.far(r.c_all.at[:, k], r.c_all.at[:, k], core_dev)
        sum_p.finish(o_p)
        own_sums = r.d_chipb[0]
        for chip in range(1, nc):
            own_sums = own_sums + r.d_chipb[chip]
        for plane in range(nf):

            def bias_columns(plane=plane):
                at = plane * cols_f
                o_bp[...] = own_sums[0:1, at : at + cols_f]
                o_b2[...] = own_sums[1:2, at : at + cols_f]
                kind, chip = 2 * plane // nc, 2 * plane % nc
                o_bqv[...] = jnp.concatenate(
                    [r.d_chipb[chip + i, 2 + kind : 3 + kind, 0:chip_w] for i in range(2)], axis=1
                )
                parts = [r.d_chipb[plane, 4 + i : 5 + i, :] for i in range(ff_c // width)]
                o_b1[...] = parts[0] if len(parts) == 1 else jnp.concatenate(parts, axis=1)

            when(f == plane, bias_columns)
        c_swap.wait()
        d_silu = jnp.concatenate([r.c_all[f, 0], r.c_all[f, 1]], axis=1)
        cond_now = cond_in[...]
        gate = 1.0 / (1.0 + jnp.exp(-cond_now))
        o_cond[...] = d_silu * (gate * (1.0 + cond_now * (1.0 - gate)))
        sum_q.finish(o_q)
        f2_line.sent()
        assert wires.remote_count <= n_sem and wires.local_count <= 32

    return pl.pallas_call(
        kernel,
        out_shape=outs,
        in_specs=[ANYWHERE] * 2 + [ON_CHIP] * 4 + [ANYWHERE] * 5,
        out_specs=tuple([ON_CHIP] * len(outs)),
        scratch_shapes=list(scratch.values()),
        compiler_params=pltpu.CompilerParams(
            collective_id=0, has_side_effects=True, vmem_limit_bytes=63 * 2**20
        ),
        name="block",
    )(x, cot, ids, bias, silu_part, cond_own, w_ada, wq, wp, w1, w2)


def fits_block(n_dp, nf, width, ff, own, micro):
    nc = n_dp // 2
    return (
        nc == nf
        and nf == 4
        and width % (128 * nf) == 128
        and ff == 4 * width
        and (width // n_dp) % 16 == 0
        and (width // nc) % HEAD_DIM == 0
        and own % (2 * SUB) == 0
    )


def per_device(
    n_dp, nf, patches, cotangent, conditioning, frame_of_slot, clip_of_slot,
    w_ada, b_ada, w_qkv, b_qv, w_proj, b_proj, w_fc1, b_fc1, w_fc2, b_fc2,
):
    nc = n_dp // 2
    sizes = (nc, nf)
    micro, block, width = patches.shape
    own = micro * block
    clips = conditioning.shape[1]
    rows_d = width // n_dp
    cols_f = width // nf
    ff = w_fc1.shape[1] * nf
    ff_d = ff // n_dp
    chip_w = width // nc
    piece_q = math.gcd(3 * width // nf, chip_w)
    piece_1 = math.gcd(ff // nf, ff_d)
    dims = types.SimpleNamespace(
        nc=nc,
        nf=nf,
        per_q=3 * width // nf // piece_q,
        per_1=ff // nf // piece_1,
        chip_q=chip_w // piece_q,
        chip_1=ff // nc // piece_1,
    )
    dp = lax.axis_index("dp")
    f = lax.axis_index("fsdp")
    c, k = dp // 2, dp % 2

    q_send = w_qkv.reshape(rows_d, dims.per_q, piece_q).transpose(1, 0, 2)
    f1_send = w_fc1.reshape(rows_d, dims.per_1, piece_1).transpose(1, 0, 2)
    f2_send = w_fc2.T
    cond = conditioning.reshape(micro * clips, width)
    silu_cond = jax.nn.silu(cond)
    silu_low = silu_cond.astype(BF16)
    ada_w = w_ada.shape[1]
    silu_part = lax.dynamic_slice_in_dim(silu_low, dp * rows_d, rows_d, 1)
    mod_part = dot(silu_part, w_ada) + jnp.where(dp == 0, b_ada.astype(F32), 0.0)[None]
    mod_send = mod_part.reshape(-1, 2, ada_w // 2).transpose(1, 0, 2)
    cut = [0, 2 * cols_f, 3 * cols_f, 3 * cols_f + ff // nf, 4 * cols_f + ff // nf]
    cond_own = lax.dynamic_slice_in_dim(cond, f * cols_f, cols_f, 1)

    def ada_outputs(d_cols):
        grad_w_ada = precise(silu_part.astype(F32), d_cols, ((0,), (0,)))
        d_silu_part = precise(d_cols, w_ada.astype(F32), ((1,), (1,)))
        d_silu = cond_kernel(dims, d_silu_part).transpose(1, 0, 2).reshape(micro * clips, width)
        d_silu_own = lax.dynamic_slice_in_dim(d_silu, f * cols_f, cols_f, 1)
        _, silu_back = jax.vjp(jax.nn.silu, cond_own)
        cond_grad = silu_back(d_silu_own)[0].reshape(micro, clips, cols_f)
        return cond_grad, grad_w_ada, jnp.sum(d_cols, axis=0)

    if fits_block(n_dp, nf, width, ff, own, micro):
        bias_send = jnp.concatenate([b_qv, b_proj, b_fc1, b_fc2, b_ada]).astype(F32)[None]
        order = jnp.arange(micro, dtype=jnp.int32)[:, None]
        pair_rows = jnp.stack(
            [(frame_of_slot + order * 65536).reshape(own), (clip_of_slot + order * clips).reshape(own)]
        )
        id_rows = jnp.concatenate([pair_rows.astype(F32), jnp.zeros((6, own), F32)])
        (
            output, input_grad, cond_grad, grad_ada, grad_b_ada, grad_qkv, grad_b_qv,
            grad_proj, grad_b_proj, grad_fc1, grad_b_fc1, grad_fc2, grad_b_fc2,
        ) = block_kernel(
            dims, patches.reshape(own, width), cotangent.reshape(own, width), id_rows, bias_send,
            silu_part, cond_own, w_ada, w_qkv, w_proj, w_fc1, w_fc2,
        )
        return (
            output.reshape(patches.shape),
            input_grad.reshape(patches.shape),
            cond_grad.reshape(micro, clips, cols_f),
            grad_ada,
            grad_b_ada[0],
            grad_qkv,
            grad_b_qv[0],
            grad_proj,
            grad_b_proj[0],
            grad_fc1,
            grad_b_fc1[0],
            grad_fc2,
            grad_b_fc2[0],
        )

    ids = jnp.stack([frame_of_slot.reshape(own), clip_of_slot.reshape(own)])
    ids = jnp.concatenate([ids, jnp.zeros((6, own), jnp.int32)])
    bias_send = jnp.concatenate([b_qv, b_proj, b_fc1, b_fc2]).astype(F32)[None]

    (x_all, c_all, ids_all, bias_all, mod_all, q_chip, f1_chip, p_chip, f2_chip, _, _) = start_kernel(
        dims, patches.reshape(own, width), cotangent.reshape(own, width), ids, bias_send, mod_send,
        q_send, f1_send, w_proj, f2_send,
    )
    group = nc * own
    modulation = mod_all.transpose(2, 0, 1, 3).reshape(micro * clips, 6 * width)
    q_parts = [
        q_chip[i].reshape(nc, 2, dims.chip_q, rows_d, piece_q).transpose(0, 1, 3, 2, 4).reshape(width, chip_w)
        for i in range(3)
    ]
    w1 = f1_chip.transpose(1, 2, 3, 0, 4).reshape(width, ff // nc)
    wp = p_chip.transpose(0, 2, 1, 3).reshape(chip_w, width)
    w2t = f2_chip.reshape(2, width, ff_d).transpose(1, 0, 2).reshape(width, 2 * ff_d)
    b_parts = [bias_all[:, 0, a:b].reshape(-1) for a, b in zip(cut[:-1], cut[1:])]
    bq = lax.dynamic_slice_in_dim(b_parts[0], c * chip_w, chip_w, 0)
    bv = lax.dynamic_slice_in_dim(b_parts[0], width + c * chip_w, chip_w, 0)
    b1 = lax.dynamic_slice_in_dim(b_parts[2], c * (ff // nc), ff // nc, 0)

    def hot_of(clip_ids):
        count = clip_ids.shape[0]
        row = (jnp.arange(count, dtype=jnp.int32) // block) % micro * clips + clip_ids
        return (row[:, None] == jnp.arange(micro * clips, dtype=jnp.int32)[None]).astype(F32)

    hot_group = hot_of(ids_all[:, 1].reshape(group))
    hot_own = hot_of(clip_of_slot.reshape(own))
    mod_group = precise(hot_group, modulation, ((1,), (0,)))
    mod_own = precise(hot_own, modulation, ((1,), (0,)))
    shift1, scale1 = mod_group[:, :width], mod_group[:, width : 2 * width]
    gate1 = mod_own[:, 2 * width : 3 * width]
    shift2, scale2 = mod_own[:, 3 * width : 4 * width], mod_own[:, 4 * width : 5 * width]
    gate2_group, gate2 = mod_group[:, 5 * width :], mod_own[:, 5 * width :]

    x_group = x_all.reshape(group, width).astype(F32)
    norm1, rstd1 = ln_parts(x_group)
    a_in = (norm1 * (1.0 + scale1) + shift1).astype(BF16)
    zero = jnp.zeros_like(bq)
    q, kk, v = [
        (dot(a_in, w) + b[None]).astype(BF16) for w, b in zip(q_parts, (bq, zero, bv))
    ]
    heads = chip_w // HEAD_DIM
    blocks = group // block
    q4, k4, v4 = [t.reshape(blocks, block, heads, HEAD_DIM) for t in (q, kk, v)]
    frames = ids_all[:, 0].reshape(blocks, block)
    same = (frames[:, :, None] == frames[:, None, :])[:, None]
    scores = jnp.einsum("bqhd,bkhd->bhqk", q4, k4, preferred_element_type=F32) * HEAD_DIM ** (-0.5)
    scores = jnp.where(same, scores, NEG_FILL)
    top = jnp.max(scores, axis=-1, keepdims=True)
    raised = jnp.exp(scores - top)
    probs = raised / jnp.sum(raised, axis=-1, keepdims=True)
    probs_low = probs.astype(BF16)
    mixed = jnp.einsum("bhqk,bkhd->bqhd", probs_low, v4, preferred_element_type=F32)
    mixed = mixed.reshape(group, chip_w).astype(BF16)
    attn_part = dot(mixed, wp)
    (attn_got,) = exchange(
        "attn_sum", 3, sizes, [(CHIP, SPREAD, attn_part.astype(BF16).reshape(nc, own, width))]
    )
    attn = jnp.sum(attn_got.astype(F32), axis=0) + b_parts[1][None]
    x_own = patches.reshape(own, width).astype(F32)
    after = x_own + gate1 * attn
    norm2, rstd2 = ln_parts(after)
    m_own = (norm2 * (1.0 + scale2) + shift2).astype(BF16)
    (m_all,) = exchange("m_gather", 4, sizes, [(CHIP, GATHER, m_own)])
    m_in = m_all.reshape(group, width)

    hidden = dot(m_in, w1) + b1[None]
    act, slope = gelu_both(hidden)
    act = act.astype(BF16)
    branch_part = dot_rt(act, w2t)
    cot_group = c_all.reshape(group, width).astype(F32)
    d_branch = (gate2_group * cot_group).astype(BF16)
    grad_2t = dot_lt(d_branch, act)
    d_hidden = (dot(d_branch, w2t) * slope).astype(BF16)
    grad_1 = dot_lt(m_in, d_hidden)
    d_m_part = dot_rt(d_hidden, w1)
    branch_got, d_m_got = exchange(
        "ff_sum",
        5,
        sizes,
        [
            (CHIP, SPREAD, d_m_part.astype(BF16).reshape(nc, own, width)),
            (CHIP, SPREAD, branch_part.astype(BF16).reshape(nc, own, width)),
        ],
    )[::-1]
    branch = jnp.sum(branch_got.astype(F32), axis=0) + b_parts[3][None]
    output = (after + gate2 * branch).astype(BF16)
    d_m = jnp.sum(d_m_got.astype(F32), axis=0)
    cot_own = cotangent.reshape(own, width).astype(F32)
    d_after = cot_own + ln_back(norm2, rstd2, d_m * (1.0 + scale2))
    d_attn = (gate1 * d_after).astype(BF16)
    (d_attn_all,) = exchange("d_attn_gather", 6, sizes, [(CHIP, GATHER, d_attn)])
    d_attn_group = d_attn_all.reshape(group, width)
    grad_p = dot_lt(mixed, d_attn_group)
    d_mix = dot_rt(d_attn_group, wp).astype(BF16).reshape(blocks, block, heads, HEAD_DIM)
    d_probs = jnp.einsum("bqhd,bkhd->bhqk", d_mix, v4, preferred_element_type=F32)
    d_scores = probs * (d_probs - jnp.sum(probs * d_probs, axis=-1, keepdims=True))
    d_scores = d_scores.astype(BF16)
    dq = jnp.einsum("bhqk,bkhd->bqhd", d_scores, k4, preferred_element_type=F32) * HEAD_DIM ** (-0.5)
    dk = jnp.einsum("bhqk,bqhd->bkhd", d_scores, q4, preferred_element_type=F32) * HEAD_DIM ** (-0.5)
    dv = jnp.einsum("bhqk,bqhd->bkhd", probs_low, d_mix, preferred_element_type=F32)
    dqkv = [t.reshape(group, chip_w).astype(BF16) for t in (dq, dk, dv)]
    d_a_part = sum(dot_rt(t, w) for t, w in zip(dqkv, q_parts))
    grad_q = jnp.stack([dot_lt(a_in, t) for t in dqkv])
    (d_a_got,) = exchange(
        "d_a_sum", 7, sizes, [(CHIP, SPREAD, d_a_part.astype(BF16).reshape(nc, own, width))]
    )
    d_a = jnp.sum(d_a_got.astype(F32), axis=0)
    norm1_own, rstd1_own = ln_parts(x_own)
    scale1_own = mod_own[:, width : 2 * width]
    input_grad = (d_after + ln_back(norm1_own, rstd1_own, d_a * (1.0 + scale1_own))).astype(BF16)

    g_q = grad_q.reshape(3, nc, 2, rows_d, dims.chip_q, piece_q).transpose(2, 1, 0, 4, 3, 5)
    g_1 = grad_1.reshape(nc, 2, rows_d, dims.chip_1, piece_1).transpose(1, 0, 3, 2, 4)
    g_p = grad_p.reshape(2, rows_d, nf, cols_f).transpose(0, 2, 1, 3)
    g_2 = grad_2t.reshape(nf, cols_f, 2, ff_d).transpose(2, 0, 1, 3)
    got = exchange("grad_core", 8, sizes, [(CORE, SPREAD, g.astype(BF16)) for g in (g_q, g_1, g_p, g_2)])
    s_q, s_1, s_p, s_2 = [jnp.sum(g.astype(F32), axis=0).astype(BF16) for g in got]
    r_q, r_1 = exchange("grad_chip", 9, sizes, [(CHIP, SPREAD, s_q), (CHIP, SPREAD, s_1)])
    z_q = r_q.transpose(1, 0, 2, 3, 4).reshape(nf, dims.per_q, rows_d, piece_q)
    z_1 = r_1.reshape(nf, dims.per_1, rows_d, piece_1)
    got = exchange("grad_plane", 10, sizes, [(PLANE, SPREAD, g) for g in (z_q, z_1, s_p, s_2)])
    o_q, o_1, o_p, o_2 = [jnp.sum(g.astype(F32), axis=0) for g in got]
    grad_w_qkv = o_q.transpose(1, 0, 2).reshape(rows_d, 3 * width // nf)
    grad_w_fc1 = o_1.transpose(1, 0, 2).reshape(rows_d, ff // nf)
    grad_w_fc2 = o_2.T

    d_token = jnp.concatenate(
        [d_a, d_a * norm1_own, d_after * attn, d_m, d_m * norm2, cot_own * branch], axis=1
    )
    d_mod = precise(hot_own, d_token, ((0,), (0,)))
    d_branch_own = (gate2 * cot_own).astype(BF16).astype(F32)

    def columns(value):
        return jnp.sum(value.astype(F32), axis=0)

    def spread(value, count):
        return lax.dynamic_update_slice_in_dim(
            jnp.zeros((count,), F32), value, c * value.shape[0], 0
        )

    g_bqv = jnp.concatenate([spread(columns(dqkv[0]), width), spread(columns(dqkv[2]), width)])
    g_b1 = spread(columns(d_hidden), ff)
    bias_terms = jnp.concatenate(
        [
            g_bqv.reshape(nf, -1),
            columns(d_attn).reshape(nf, -1),
            g_b1.reshape(nf, -1),
            columns(d_branch_own).reshape(nf, -1),
        ],
        axis=1,
    )
    n_bias = bias_terms.shape[1]
    bias_rows = -(-n_bias // ada_w)
    bias_terms = jnp.pad(bias_terms, ((0, 0), (0, bias_rows * ada_w - n_bias)))
    terms = jnp.concatenate(
        [d_mod.reshape(micro * clips, nf, ada_w).transpose(1, 0, 2), bias_terms.reshape(nf, bias_rows, ada_w)],
        axis=1,
    )
    pad_rows = -terms.shape[1] % 8
    terms = jnp.pad(terms, ((0, 0), (0, pad_rows), (0, 0)))
    terms = terms.reshape(nf, -1, 2, ada_w // 2).transpose(0, 2, 1, 3)
    total = sum_small_kernel(dims, terms).transpose(1, 0, 2).reshape(-1, ada_w)
    d_cols = total[: micro * clips]
    bias_sums = total[micro * clips : micro * clips + bias_rows].reshape(-1)[:n_bias]
    g_parts = [bias_sums[a:b] for a, b in zip(cut[:-1], cut[1:])]
    cond_grad, grad_w_ada, grad_b_ada = ada_outputs(d_cols)
    return (
        output.reshape(patches.shape),
        input_grad.reshape(patches.shape),
        cond_grad,
        grad_w_ada,
        grad_b_ada,
        grad_w_qkv,
        g_parts[0],
        o_p,
        g_parts[1],
        grad_w_fc1,
        g_parts[2],
        grad_w_fc2,
        g_parts[3],
    )


def solution(mesh):
    tokens = P(None, ("dp", "fsdp"), None)
    ids = P(None, ("dp", "fsdp"))
    both, cols = P("dp", "fsdp"), P("fsdp")
    in_specs = (tokens, tokens, P(), ids, ids) + (both, cols) * 5
    out_specs = (tokens, tokens, P(None, None, "fsdp")) + (both, cols) * 5
    return jax.shard_map(
        functools.partial(per_device, mesh.shape["dp"], mesh.shape["fsdp"]),
        mesh=mesh,
        in_specs=in_specs,
        out_specs=out_specs,
        check_vma=False,
    )
```

```python
import functools
import math
import types

import jax
import jax.numpy as jnp
from jax import lax
from jax.experimental import pallas as pl
from jax.experimental.pallas import tpu as pltpu
from jax.sharding import PartitionSpec as P

HEAD_DIM = 72
EPS = 1e-06
GELU_C = math.sqrt(2.0 / math.pi)
PRECISE = lax.Precision.HIGHEST
NEG_FILL = -1e30
SUB = 16
CORE, CHIP, PLANE, ALL = range(4)
GATHER, SPREAD = range(2)
MESH_ID = pl.DeviceIdType.MESH
F32 = jnp.float32
BF16 = jnp.bfloat16


def xor_of(index, step, size):
    result, bit = 0, 1
    while bit < size:
        mine = (index // bit) % 2
        result = result + ((mine + (step // bit) % 2) % 2) * bit
        bit *= 2
    return result


class Place:
    def __init__(self, n_chip, n_plane):
        self.n = {CORE: 2, CHIP: n_chip, PLANE: n_plane, ALL: 2 * n_chip}
        self.dp = lax.axis_index("dp")
        self.f = lax.axis_index("fsdp")
        self.c = self.dp // 2
        self.k = self.dp % 2

    def index(self, axis):
        return {CORE: self.k, CHIP: self.c, PLANE: self.f, ALL: self.dp}[axis]

    def peer(self, axis, step):
        other = xor_of(self.index(axis), step, self.n[axis])
        if axis == CORE:
            return other, (self.c * 2 + other, self.f)
        if axis == CHIP:
            return other, (other * 2 + self.k, self.f)
        if axis == PLANE:
            return other, (self.dp, other)
        return other, (other, self.f)


def greet(place, axes):
    barrier = pltpu.get_barrier_semaphore()
    count = 0
    for axis in axes:
        for step in range(1, place.n[axis]):
            pl.semaphore_signal(
                barrier, inc=1, device_id=place.peer(axis, step)[1], device_id_type=MESH_ID
            )
            count += 1
    pl.semaphore_wait(barrier, count)


class Wires:
    def __init__(self, send, recv, local):
        self.send, self.recv, self.local = send, recv, local
        self.remote_count = 0
        self.local_count = 0

    def far(self, src, dst, device):
        at = self.remote_count
        self.remote_count += 1
        copy = pltpu.make_async_remote_copy(
            src_ref=src,
            dst_ref=dst,
            send_sem=self.send.at[at],
            recv_sem=self.recv.at[at],
            device_id=device,
            device_id_type=MESH_ID,
        )
        copy.start()
        return copy

    def near(self, src, dst):
        at = self.local_count
        self.local_count += 1
        copy = pltpu.make_async_copy(src, dst, self.local.at[at])
        copy.start()
        return copy


def wait_all(copies):
    for copy in copies:
        copy.wait()


ANYWHERE = pl.BlockSpec(memory_space=pl.ANY)
ON_CHIP = pl.BlockSpec(memory_space=pltpu.VMEM)


def exchange(name, collective_id, sizes, items):
    n_chip, n_plane = sizes
    n_of = {CORE: 2, CHIP: n_chip, PLANE: n_plane, ALL: 2 * n_chip}
    axes = sorted({item[0] for item in items})
    outs = []
    n_far = 0
    for axis, kind, array in items:
        n_far += n_of[axis] - 1
        shape = array.shape if kind == SPREAD else (n_of[axis],) + array.shape
        outs.append(jax.ShapeDtypeStruct(shape, array.dtype))

    def kernel(*refs):
        ins = refs[: len(items)]
        results = refs[len(items) : 2 * len(items)]
        place = Place(n_chip, n_plane)
        wires = Wires(*refs[2 * len(items) :])
        greet(place, axes)
        copies = []
        for (axis, kind, _), src, dst in zip(items, ins, results):
            mine = place.index(axis)
            for step in range(1, n_of[axis]):
                other, device = place.peer(axis, step)
                piece = src if kind == GATHER else src.at[other]
                copies.append(wires.far(piece, dst.at[mine], device))
        for (axis, kind, _), src, dst in zip(items, ins, results):
            mine = place.index(axis)
            copies.append(wires.near(src if kind == GATHER else src.at[mine], dst.at[mine]))
        wait_all(copies)

    return pl.pallas_call(
        kernel,
        out_shape=tuple(outs),
        in_specs=[ANYWHERE] * len(items),
        out_specs=tuple([ANYWHERE] * len(items)),
        scratch_shapes=[
            pltpu.SemaphoreType.DMA((n_far,)),
            pltpu.SemaphoreType.DMA((n_far,)),
            pltpu.SemaphoreType.DMA((len(items),)),
        ],
        compiler_params=pltpu.CompilerParams(collective_id=collective_id, has_side_effects=True),
        name=name,
    )(*[item[2] for item in items])


def start_kernel(dims, x, cot, ids, bias, mod, wq, w1, wp, w2):
    nc, nf = dims.nc, dims.nf
    per_q, per_1 = dims.per_q, dims.per_1
    chip_q, chip_1 = dims.chip_q, dims.chip_1
    part_q = nc * chip_q
    rows, half = mod.shape[1], mod.shape[2]
    n_far = 5 * (nf - 1) + 3 * (nc - 1) + 4 * (nc - 1) + 4 + 1 + (nc - 1) + (nf - 1) + 1
    outs = (
        jax.ShapeDtypeStruct((nc,) + x.shape, x.dtype),
        jax.ShapeDtypeStruct((nc,) + cot.shape, cot.dtype),
        jax.ShapeDtypeStruct((nc,) + ids.shape, ids.dtype),
        jax.ShapeDtypeStruct((nf,) + bias.shape, bias.dtype),
        jax.ShapeDtypeStruct((nf, 2, rows, half), F32),
        jax.ShapeDtypeStruct((3, nc, 2, chip_q) + wq.shape[1:], BF16),
        jax.ShapeDtypeStruct((chip_1, nc, 2) + w1.shape[1:], BF16),
        jax.ShapeDtypeStruct((2, nf) + wp.shape, BF16),
        jax.ShapeDtypeStruct((2, nf) + w2.shape, BF16),
        jax.ShapeDtypeStruct((nf * per_q,) + wq.shape[1:], BF16),
        jax.ShapeDtypeStruct((nf * per_1,) + w1.shape[1:], BF16),
    )

    def kernel(
        x_in, c_in, i_in, b_in, m_in, q_in, f1_in, p_in, f2_in,
        x_all, c_all, i_all, b_all, m_all, q_chip, f1_chip, p_chip, f2_chip, q_rows, f1_rows,
        m_core, m_sum, m_chip, send, recv, local,
    ):
        place = Place(nc, nf)
        wires = Wires(send, recv, local)
        c, k, f = place.c, place.k, place.f
        greet(place, (CORE, CHIP, PLANE))
        core_other, core_peer = place.peer(CORE, 1)
        chip_peers = [place.peer(CHIP, step) for step in range(1, nc)]
        plane_peers = [place.peer(PLANE, step) for step in range(1, nf)]

        m_first = wires.far(m_in.at[core_other], m_core, core_peer)
        q_got, f1_got, p_got, f2_got, small = [], [], [], [], []
        for _, peer in plane_peers:
            q_got.append(wires.far(q_in, q_rows.at[pl.ds(f * per_q, per_q)], peer))
            small.append(wires.far(b_in, b_all.at[f], peer))
        q_got.append(wires.near(q_in, q_rows.at[pl.ds(f * per_q, per_q)]))
        small.append(wires.near(b_in, b_all.at[f]))
        for _, peer in chip_peers:
            small.append(wires.far(i_in, i_all.at[c], peer))
            small.append(wires.far(x_in, x_all.at[c], peer))
        m_first.wait()
        m_sum[...] = m_in[k] + m_core[...]
        m_chip[c] = m_sum[...]
        m_second = [wires.far(m_sum, m_chip.at[c], peer) for _, peer in chip_peers]
        for _, peer in plane_peers:
            p_got.append(wires.far(p_in, p_chip.at[k, f], peer))
        for _, peer in plane_peers:
            f1_got.append(wires.far(f1_in, f1_rows.at[pl.ds(f * per_1, per_1)], peer))
        for _, peer in plane_peers:
            f2_got.append(wires.far(f2_in, f2_chip.at[k, f], peer))
        p_got.append(wires.near(p_in, p_chip.at[k, f]))
        f1_got.append(wires.near(f1_in, f1_rows.at[pl.ds(f * per_1, per_1)]))
        f2_got.append(wires.near(f2_in, f2_chip.at[k, f]))
        small.append(wires.near(i_in, i_all.at[c]))
        small.append(wires.near(x_in, x_all.at[c]))
        for _, peer in chip_peers:
            small.append(wires.far(c_in, c_all.at[c], peer))
        small.append(wires.near(c_in, c_all.at[c]))
        wait_all(m_second)
        total = m_chip[0]
        for other in range(1, nc):
            total = total + m_chip[other]
        m_all[f, k] = total
        wait_all([wires.far(m_all.at[f, k], m_all.at[f, k], peer) for _, peer in plane_peers])
        m_last = wires.far(m_all.at[:, k], m_all.at[:, k], core_peer)

        wait_all(q_got)
        q_moved = []
        for kind in range(3):
            for other, peer in chip_peers:
                q_moved.append(
                    wires.far(
                        q_rows.at[pl.ds(kind * part_q + other * chip_q, chip_q)],
                        q_chip.at[kind, c, k],
                        peer,
                    )
                )
            q_moved.append(
                wires.near(
                    q_rows.at[pl.ds(kind * part_q + c * chip_q, chip_q)], q_chip.at[kind, c, k]
                )
            )
        wait_all(p_got)
        last = [m_last, wires.far(p_chip.at[k], p_chip.at[k], core_peer)]
        wait_all(q_moved)
        last.append(wires.far(q_chip.at[:, :, k], q_chip.at[:, :, k], core_peer))
        wait_all(f1_got)
        f1_moved = []
        for other, peer in chip_peers:
            f1_moved.append(
                wires.far(f1_rows.at[pl.ds(other * chip_1, chip_1)], f1_chip.at[:, c, k], peer)
            )
        f1_moved.append(
            wires.near(f1_rows.at[pl.ds(c * chip_1, chip_1)], f1_chip.at[:, c, k])
        )
        wait_all(f2_got)
        last.append(wires.far(f2_chip.at[k], f2_chip.at[k], core_peer))
        wait_all(f1_moved)
        last.append(wires.far(f1_chip.at[:, :, k], f1_chip.at[:, :, k], core_peer))
        wait_all(small)
        wait_all(last)

    return pl.pallas_call(
        kernel,
        out_shape=outs,
        in_specs=[ANYWHERE] * 4 + [ON_CHIP] + [ANYWHERE] * 4,
        out_specs=tuple([ANYWHERE] * 4 + [ON_CHIP] + [ANYWHERE] * 6),
        scratch_shapes=[
            pltpu.VMEM((rows, half), F32),
            pltpu.VMEM((rows, half), F32),
            pltpu.VMEM((nc, rows, half), F32),
            pltpu.SemaphoreType.DMA((n_far,)),
            pltpu.SemaphoreType.DMA((n_far,)),
            pltpu.SemaphoreType.DMA((12,)),
        ],
        compiler_params=pltpu.CompilerParams(collective_id=0, has_side_effects=True),
        name="start",
    )(x, cot, ids, bias, mod, wq, w1, wp, w2)


def sum_small_kernel(dims, terms):
    nc, nf = dims.nc, dims.nf
    _, _, rows, half = terms.shape
    n_far = (nf - 1) + 1 + (nc - 1) + 1

    def kernel(t_in, total, z_got, both, core_got, chip_got, send, recv, local):
        place = Place(nc, nf)
        wires = Wires(send, recv, local)
        c, k, f = place.c, place.k, place.f
        greet(place, (CORE, CHIP, PLANE))
        core_other, core_peer = place.peer(CORE, 1)
        copies = []
        for step in range(1, nf):
            other, peer = place.peer(PLANE, step)
            copies.append(wires.far(t_in.at[other], z_got.at[f], peer))
        z_got[f] = t_in[f]
        wait_all(copies)
        value = z_got[0]
        for other in range(1, nf):
            value = value + z_got[other]
        both[...] = value
        wires.far(both.at[core_other], core_got, core_peer).wait()
        chip_got[c] = both[k] + core_got[...]
        copies = []
        for step in range(1, nc):
            _, peer = place.peer(CHIP, step)
            copies.append(wires.far(chip_got.at[c], chip_got.at[c], peer))
        wait_all(copies)
        value = chip_got[0]
        for other in range(1, nc):
            value = value + chip_got[other]
        total[k] = value
        wires.far(total.at[k], total.at[k], core_peer).wait()

    return pl.pallas_call(
        kernel,
        out_shape=jax.ShapeDtypeStruct((2, rows, half), F32),
        in_specs=[ON_CHIP],
        out_specs=ON_CHIP,
        scratch_shapes=[
            pltpu.VMEM((nf, 2, rows, half), F32),
            pltpu.VMEM((2, rows, half), F32),
            pltpu.VMEM((rows, half), F32),
            pltpu.VMEM((nc, rows, half), F32),
            pltpu.SemaphoreType.DMA((n_far,)),
            pltpu.SemaphoreType.DMA((n_far,)),
            pltpu.SemaphoreType.DMA((1,)),
        ],
        compiler_params=pltpu.CompilerParams(collective_id=1, has_side_effects=True),
        name="sum_small",
    )(terms)


def cond_kernel(dims, part):
    nc, nf = dims.nc, dims.nf
    nd = 2 * nc
    rows, width = part.shape
    n_far = (nf - 1) + (nd - 1)

    def kernel(p_in, out, got, send, recv, local):
        place = Place(nc, nf)
        wires = Wires(send, recv, local)
        greet(place, (PLANE, ALL))
        copies = []
        for step in range(1, nf):
            copies.append(wires.far(p_in, got.at[place.f], place.peer(PLANE, step)[1]))
        got[place.f] = p_in[...]
        wait_all(copies)
        value = got[0]
        for other in range(1, nf):
            value = value + got[other]
        out[place.dp] = value
        copies = []
        for step in range(1, nd):
            copies.append(
                wires.far(out.at[place.dp], out.at[place.dp], place.peer(ALL, step)[1])
            )
        wait_all(copies)

    return pl.pallas_call(
        kernel,
        out_shape=jax.ShapeDtypeStruct((nd, rows, width), F32),
        in_specs=[ON_CHIP],
        out_specs=ON_CHIP,
        scratch_shapes=[
            pltpu.VMEM((nf, rows, width), F32),
            pltpu.SemaphoreType.DMA((n_far,)),
            pltpu.SemaphoreType.DMA((n_far,)),
            pltpu.SemaphoreType.DMA((1,)),
        ],
        compiler_params=pltpu.CompilerParams(collective_id=2, has_side_effects=True),
        name="cond_sum",
    )(part)


def dot(left, right):
    return jnp.dot(left, right, preferred_element_type=F32)


def dot_rt(left, right):
    return lax.dot_general(left, right, (((1,), (1,)), ((), ())), preferred_element_type=F32)


def dot_lt(left, right):
    return lax.dot_general(left, right, (((0,), (0,)), ((), ())), preferred_element_type=F32)


def precise(left, right, dims):
    return lax.dot_general(
        left, right, (dims, ((), ())), precision=PRECISE, preferred_element_type=F32
    )


def ln_parts(values):
    centre = values - jnp.mean(values, axis=-1, keepdims=True)
    scale = lax.rsqrt(jnp.mean(centre * centre, axis=-1, keepdims=True) + EPS)
    return centre * scale, scale


def ln_back(normal, scale, grad):
    return scale * (
        grad
        - jnp.mean(grad, axis=-1, keepdims=True)
        - normal * jnp.mean(grad * normal, axis=-1, keepdims=True)
    )


def gelu_both(h):
    square = h * h
    t = jnp.tanh(GELU_C * (h + 0.044715 * h * square))
    value = 0.5 * h * (1.0 + t)
    slope = 0.5 * (1.0 + t) + 0.5 * h * (1.0 - t * t) * GELU_C * (1.0 + 3 * 0.044715 * square)
    return value, slope


def dot3(left, right):
    wide_left = left.dtype == F32
    value = left if wide_left else right
    total = None
    for _ in range(3):
        term = value.astype(BF16)
        value = value - term.astype(F32)
        part = dot(term, right) if wide_left else dot(left, term)
        total = part if total is None else total + part
    return total


def add_low(left, right):
    return (left.astype(F32) + right.astype(F32)).astype(BF16)


def block_kernel(dims, x, cot, ids, bias, silu_part, cond_own, w_ada, wq, wp, w1, w2):
    nc, nf = dims.nc, dims.nf
    own, width = x.shape
    group = nc * own
    rows_d, q_w = wq.shape
    chip_w = q_w // 3
    ff_d, cols_f = w2.shape
    ff_c = 2 * ff_d
    ada_w = w_ada.shape[1]
    n_bias = bias.shape[1]
    heads = chip_w // HEAD_DIM
    n_rows = silu_part.shape[0]
    half = n_rows // 2
    n_sub = own // SUB
    head_scale = HEAD_DIM ** (-0.5)
    last = nf - 2

    outs = (
        jax.ShapeDtypeStruct((own, width), BF16),
        jax.ShapeDtypeStruct((own, width), BF16),
        jax.ShapeDtypeStruct((n_rows, cols_f), F32),
        jax.ShapeDtypeStruct((rows_d, ada_w), F32),
        jax.ShapeDtypeStruct((1, ada_w), F32),
        jax.ShapeDtypeStruct((rows_d, q_w), F32),
        jax.ShapeDtypeStruct((1, 2 * chip_w), F32),
        jax.ShapeDtypeStruct((rows_d, cols_f), F32),
        jax.ShapeDtypeStruct((1, cols_f), F32),
        jax.ShapeDtypeStruct((rows_d, ff_c), F32),
        jax.ShapeDtypeStruct((1, ff_c), F32),
        jax.ShapeDtypeStruct((ff_d, cols_f), F32),
        jax.ShapeDtypeStruct((1, cols_f), F32),
    )
    tokens = (nc, own, width)
    n_sem = 240
    scratch = dict(
        xg=pltpu.VMEM(tokens, BF16),
        cg=pltpu.VMEM(tokens, BF16),
        idsg=pltpu.VMEM((nc, 8, own), F32),
        biasg=pltpu.VMEM((nf, 1, n_bias), F32),
        ada=pltpu.VMEM(w_ada.shape, BF16),
        m_part=pltpu.VMEM((2, half, ada_w), F32),
        m_core=pltpu.VMEM((half, ada_w), F32),
        m_chip=pltpu.VMEM((nc, half, ada_w), F32),
        m_z=pltpu.VMEM((nf, 2, half, ada_w), F32),
        m_tab=pltpu.VMEM((n_rows, 6 * width), F32),
        tab=pltpu.VMEM((3, nc * n_sub, width), F32),
        own_tab=pltpu.VMEM((6, n_sub, width), F32),
        q_z=pltpu.VMEM((nf, rows_d, q_w), BF16),
        q_rows=pltpu.VMEM((nf * 3, rows_d, chip_w), BF16),
        q_got=pltpu.VMEM((3, nc, rows_d, chip_w), BF16),
        w_q=pltpu.VMEM((nc, 2, rows_d, q_w), BF16),
        y_got=pltpu.VMEM((nc, rows_d, q_w), BF16),
        f1_z=pltpu.VMEM((nf, rows_d, ff_c), BF16),
        w_1=pltpu.VMEM((nc, 2, rows_d, ff_c), BF16),
        p_got=pltpu.VMEM((2, nf, rows_d, cols_f), BF16),
        w_p=pltpu.VMEM((chip_w, width), BF16),
        f2_nat=pltpu.VMEM((ff_d, cols_f), BF16),
        f2_half=pltpu.VMEM((2, rows_d, ff_d), BF16),
        f2_got=pltpu.VMEM((rows_d, ff_d), BF16),
        w_2=pltpu.VMEM((nf, 2, rows_d, ff_c), BF16),
        a_in=pltpu.VMEM(tokens, BF16),
        qkv=pltpu.VMEM((3, nc, own, chip_w), BF16),
        probs=pltpu.VMEM((nc * heads, own, own), F32),
        mixed=pltpu.VMEM((nc, own, chip_w), BF16),
        sum_s=pltpu.VMEM(tokens, BF16),
        sum_r=pltpu.VMEM((2, own, width), BF16),
        sum_st=pltpu.VMEM((2, own // 2, width), BF16),
        br_s=pltpu.VMEM(tokens, BF16),
        br_r=pltpu.VMEM((2, own, width), BF16),
        br_st=pltpu.VMEM((2, own // 2, width), BF16),
        m_all=pltpu.VMEM(tokens, BF16),
        da_all=pltpu.VMEM(tokens, BF16),
        attn=pltpu.VMEM((own, width), F32),
        after=pltpu.VMEM((own, width), F32),
        d_after=pltpu.VMEM((own, width), F32),
        hid=pltpu.VMEM((own, ff_c), F32),
        slope=pltpu.VMEM((own, ff_c), F32),
        act=pltpu.VMEM((nc, own, ff_c), BF16),
        d_hid=pltpu.VMEM((nc, own, ff_c), BF16),
        dbr=pltpu.VMEM(tokens, BF16),
        d_qkv=pltpu.VMEM((nc, own, q_w), BF16),
        g_2=pltpu.VMEM((nf, 2, rows_d, ff_c), BF16),
        g_2r=pltpu.VMEM((nf, rows_d, ff_c), BF16),
        g_1r=pltpu.VMEM((nc, rows_d, ff_c), BF16),
        g_qr=pltpu.VMEM((nc, rows_d, q_w), BF16),
        g_pr=pltpu.VMEM((rows_d, width), BF16),
        got_q=pltpu.VMEM((2, nf - 1, rows_d, q_w), BF16),
        got_1=pltpu.VMEM((2, nf - 1, rows_d, ff_c), BF16),
        got_p=pltpu.VMEM((2, nf - 1, rows_d, cols_f), BF16),
        got_2=pltpu.VMEM((2, nf - 1, rows_d, ff_c), BF16),
        all_2=pltpu.VMEM((2, rows_d, ff_c), F32),
        sub=pltpu.VMEM((6, n_sub, width), F32),
        d_part=pltpu.VMEM((2, half, 6 * width), F32),
        d_core=pltpu.VMEM((half, 6 * width), F32),
        d_cut=pltpu.VMEM((nf, half, ada_w), F32),
        d_bias=pltpu.VMEM((8, width), F32),
        dz=pltpu.VMEM((nf, half, ada_w), F32),
        dzb=pltpu.VMEM((nf, 8, width), F32),
        d_tot=pltpu.VMEM((2, half, ada_w), F32),
        d_bsum=pltpu.VMEM((8, width), F32),
        d_coreb=pltpu.VMEM((8, width), F32),
        d_chipb=pltpu.VMEM((nc, 8, width), F32),
        c_part=pltpu.VMEM((nf, n_rows, rows_d), F32),
        c_all=pltpu.VMEM((nc, 2, n_rows, rows_d), F32),
        send=pltpu.SemaphoreType.DMA((n_sem,)),
        recv=pltpu.SemaphoreType.DMA((n_sem,)),
        local=pltpu.SemaphoreType.DMA((32,)),
    )
    names = list(scratch)

    def kernel(
        x_in, c_in, ids_in, bias_in, silu_in, cond_in, ada_in, q_in, p_in, f1_in, f2_in,
        out, x_grad, o_cond, o_ada, o_bada, o_q, o_bqv, o_p, o_bp, o_1, o_b1, o_2, o_b2, *rest,
    ):
        r = types.SimpleNamespace(**dict(zip(names, rest)))
        place = Place(nc, nf)
        wires = Wires(r.send, r.recv, r.local)
        c, k, f = place.c, place.k, place.f
        core_o, core_dev = place.peer(CORE, 1)
        chip_peers = [place.peer(CHIP, step) for step in range(1, nc)]
        plane_peers = [place.peer(PLANE, step) for step in range(1, nf)]

        def loop(count, body, unroll=1):
            def run(i, carry):
                body(i)
                return carry

            lax.fori_loop(0, count, run, 0, unroll=unroll)

        def loop_rows(body):
            loop(n_sub, body, 2)

        def when(condition, body):
            pl.when(condition)(body)

        def sub_rows(g):
            return pl.ds(pl.multiple_of(g * SUB, SUB), SUB)

        def reserve(count):
            base = wires.remote_count
            wires.remote_count += count
            return base

        def pair(src, dst, device, send_at, recv_at):
            return pltpu.make_async_remote_copy(
                src_ref=src,
                dst_ref=dst,
                send_sem=r.send.at[send_at],
                recv_sem=r.recv.at[recv_at],
                device_id=device,
                device_id_type=MESH_ID,
            )

        chip_x, dev_x = place.peer(CHIP, 1)
        chip_y, dev_y = place.peer(CHIP, 2)
        chip_d, _ = place.peer(CHIP, 3)
        first_half, second_half = pl.ds(0, own // 2), pl.ds(own // 2, own // 2)

        class Share:
            def __init__(self, ref, src=None):
                def copy(chip, rows, device, at, own_src=None):
                    from_ref = ref.at[chip, rows] if own_src is None else own_src.at[rows]
                    return pair(from_ref, ref.at[chip, rows], device, at, at)

                at = reserve(6)
                self.x_a = copy(c, first_half, dev_x, at, src)
                self.x_b = copy(c, second_half, dev_x, at + 1, src)
                self.y_b = copy(c, second_half, dev_y, at + 2, src)
                self.y_a = copy(c, first_half, dev_y, at + 3, src)
                self.on_y = copy(chip_x, first_half, dev_y, at + 4)
                self.on_x = copy(chip_y, second_half, dev_x, at + 5)

            def start(self):
                for item in (self.x_a, self.y_b, self.x_b, self.y_a):
                    item.start()

            def relay(self):
                self.x_a.wait_recv()
                self.on_y.start()
                self.y_b.wait_recv()
                self.on_x.start()

            def arrive(self, step):
                if step == 1:
                    self.x_b.wait_recv()
                elif step == 2:
                    self.y_a.wait_recv()
                else:
                    self.on_y.wait_recv()
                    self.on_x.wait_recv()

            def sent(self):
                for item in (self.x_a, self.x_b, self.y_b, self.y_a, self.on_y, self.on_x):
                    item.wait_send()

        class Merge:
            def __init__(self, terms, got, stage):
                self.terms, self.got, self.stage = terms, got, stage
                at = reserve(6)
                self.d_x = pair(terms.at[chip_d, first_half], stage.at[0], dev_x, at, at)
                self.d_y = pair(terms.at[chip_d, second_half], stage.at[1], dev_y, at + 1, at + 1)

                def copy(chip, rows, to, device, index):
                    return pair(
                        terms.at[chip, rows], got.at[to, rows], device, at + index, at + index
                    )

                self.x_a = copy(chip_x, first_half, 0, dev_x, 2)
                self.x_b = copy(chip_x, second_half, 0, dev_x, 3)
                self.y_b = copy(chip_y, second_half, 1, dev_y, 4)
                self.y_a = copy(chip_y, first_half, 1, dev_y, 5)

            def put(self, step, blk, part):
                self.terms[blk] = part

                def far():
                    self.d_x.start()
                    self.d_y.start()

                when(step == 3, far)
                when(step == 2, self.y_b.start)
                when(step == 1, self.x_a.start)

            def combine(self):
                self.d_y.wait()
                ref = self.terms.at[chip_x, second_half]
                ref[...] = add_low(ref[...], self.stage[1])
                self.x_b.start()
                self.d_x.wait()
                ref = self.terms.at[chip_y, first_half]
                ref[...] = add_low(ref[...], self.stage[0])
                self.y_a.start()

            def finish(self):
                for item in (self.x_a, self.x_b, self.y_b, self.y_a):
                    item.wait()

            def rows(self, at):
                value = self.terms[c, at, :].astype(F32) + self.got[0, at, :].astype(F32)
                return value + self.got[1, at, :].astype(F32)

        up, down = (place.dp, f + 1), (place.dp, f - 1)

        class Gather:
            def __init__(self, slot):
                self.slot = slot
                self.up, self.down = reserve(nf - 1), reserve(nf - 1)

            def both(self, step, src=None):
                above = pair(
                    self.slot(f - step) if src is None else src,
                    self.slot(f - step), up, self.up + step, self.up + step,
                )
                below = pair(
                    self.slot(f + step) if src is None else src,
                    self.slot(f + step), down, self.down + step, self.down + step,
                )
                return (
                    ((f - step >= 0) & (f < nf - 1), above),
                    ((f + step <= nf - 1) & (f > 0), below),
                )

            def start(self, step, src=None):
                for condition, copy in self.both(step, src):
                    when(condition, copy.start)

            def arrive(self, step, then=None):
                for condition, got, base in (
                    (f - 1 - step >= 0, f - 1 - step, self.up),
                    (f + 1 + step <= nf - 1, f + 1 + step, self.down),
                ):

                    def body(got=got, base=base):
                        slot = self.slot(got)
                        pair(slot, slot, core_dev, base + step, base + step).wait_recv()
                        if then is not None:
                            then(got)

                    when(condition, body)

            def sent(self, src=None):
                for step in range(nf - 1):
                    for condition, copy in self.both(step, src if step == 0 else None):
                        when(condition, copy.wait_send)

        class Sum:
            def __init__(self, terms, got):
                self.terms, self.got = terms, got
                self.bases = (reserve(nf - 1), reserve(nf - 1))

            def both(self, step):
                for way in range(2):
                    target = f + (nf - 1) - step if way == 0 else f - (nf - 1) + step
                    condition = (f <= step) & (f < nf - 1) if way == 0 else (target >= 0) & (f > 0)
                    more = condition & (f > 0 if way == 0 else f < nf - 1)
                    at = self.bases[way] + step
                    copy = pair(
                        self.terms(target), self.got.at[way, step], up if way == 0 else down, at, at
                    )
                    yield way, target, condition, more, copy

            def wait(self, way, step):
                at = self.bases[way] + step
                ref = self.got.at[way, step]
                pair(ref, ref, core_dev, at, at).wait_recv()

            def start(self, step):
                for way, target, condition, more, copy in self.both(step):
                    if step > 0:

                        def body(way=way, target=target):
                            self.wait(way, step - 1)
                            ref = self.terms(target)
                            ref[...] = add_low(ref[...], self.got[way, step - 1])

                        when(more, body)
                    when(condition, copy.start)

            def finish(self, result):
                result[...] = self.terms(f)[...].astype(F32)
                for way, condition in ((0, f > 0), (1, f < nf - 1)):

                    def body(way=way):
                        self.wait(way, last)
                        result[...] = result[...] + self.got[way, last].astype(F32)

                    when(condition, body)
                for step in range(nf - 1):
                    for _, _, condition, _, copy in self.both(step):
                        when(condition, copy.wait_send)

        barrier = pltpu.get_barrier_semaphore()
        peers = [core_dev] + [peer for _, peer in chip_peers + plane_peers]
        for peer in peers:
            pl.semaphore_signal(barrier, inc=1, device_id=peer, device_id_type=MESH_ID)

        q_line = Gather(lambda g: r.q_z.at[g])
        p_line = Gather(lambda g: r.p_got.at[k, g])
        f1_line = Gather(lambda g: r.f1_z.at[g])
        f2_line = Gather(lambda g: r.w_2.at[g, k])
        ada_near = wires.near(ada_in, r.ada)
        q_near = wires.near(q_in, r.q_z.at[f])
        f2_near = wires.near(f2_in, r.f2_nat)
        first = []
        first.append(wires.near(x_in, r.xg.at[c]))
        first.append(wires.near(c_in, r.cg.at[c]))
        p_near = wires.near(p_in, r.p_got.at[k, f])
        f1_near = wires.near(f1_in, r.f1_z.at[f])
        r.idsg[c] = ids_in[...]
        r.biasg[f] = bias_in[...]
        ada_near.wait()
        ada_bias = jnp.where(place.dp == 0, bias_in[:, n_bias - ada_w :], 0.0)
        value = dot(silu_in[...], r.ada[...]) + ada_bias
        r.m_part[...] = value.reshape(2, half, ada_w)
        f2_near.wait()
        turned = r.f2_nat[...].T
        r.f2_half[...] = turned.reshape(2, rows_d, ff_d)
        q_near.wait()
        pl.semaphore_wait(barrier, len(peers))
        m_first = wires.far(r.m_part.at[core_o], r.m_core, core_dev)
        q_line.start(0, q_in)
        for _, peer in chip_peers:
            first.append(wires.far(ids_in, r.idsg.at[c], peer))
        f2_swap = wires.far(r.f2_half.at[core_o], r.f2_got, core_dev)
        for _, peer in plane_peers:
            first.append(wires.far(bias_in, r.biasg.at[f], peer))

        w_q, q_rows = r.w_q, r.q_rows
        q_base = reserve(3 * nc)
        q_local = wires.local_count
        wires.local_count += 3

        def q_copies(plane, i):
            piece = 3 * plane + i
            kind, chip = piece // nc, piece % nc
            src, dst = q_rows.at[piece], r.q_got.at[kind, c]
            far = pair(src, dst, (chip * 2 + k, f), q_base + kind * nc + chip, q_base + kind * nc + c)
            return chip, far, pltpu.make_async_copy(src, dst, r.local.at[q_local + kind])

        def q_forward(plane):
            for i in range(3):
                q_rows[3 * plane + i] = r.q_z[plane, :, chip_w * i : chip_w * (i + 1)]
                chip, far, near = q_copies(plane, i)
                when(chip != c, far.start)
                when(chip == c, near.start)

        f1_base = reserve(nc)
        f1_local = wires.local_count
        wires.local_count += 1

        def f1_copies(plane):
            src, dst = r.f1_z.at[plane], r.w_1.at[c, k]
            far = pair(src, dst, (plane * 2 + k, f), f1_base + plane, f1_base + c)
            return far, pltpu.make_async_copy(src, dst, r.local.at[f1_local])

        def f1_forward(plane):
            far, near = f1_copies(plane)
            when(plane != c, far.start)
            when(plane == c, near.start)

        m_first.wait()
        m_chip = r.m_chip
        m_chip[c] = r.m_part[k] + r.m_core[...]
        m_second = [wires.far(m_chip.at[c], m_chip.at[c], peer) for _, peer in chip_peers]
        q_forward(f)
        x_share = Share(r.xg, x_in)
        x_share.start()
        q_line.arrive(0, q_forward)
        q_line.start(1)
        wait_all(m_second)
        total = m_chip[0]
        for other in range(1, nc):
            total = total + m_chip[other]
        r.m_z[f, k] = total
        m_third = [wires.far(r.m_z.at[f, k], r.m_z.at[f, k], peer) for _, peer in plane_peers]
        x_share.relay()
        p_line.start(0, p_in)
        q_line.arrive(1, q_forward)
        q_line.start(2)
        p_line.arrive(0)
        p_line.start(1)
        f1_line.start(0, f1_in)
        f2_swap.wait()

        def join_even():
            r.w_2[f, k] = jnp.concatenate([r.f2_half[0], r.f2_got[...]], axis=1)

        def join_odd():
            r.w_2[f, k] = jnp.concatenate([r.f2_got[...], r.f2_half[1]], axis=1)

        when(k == 0, join_even)
        when(k == 1, join_odd)
        f2_base = reserve(nf)

        def f2_across(plane):
            ref = r.w_2.at[plane, k]
            return pair(ref, ref, core_dev, f2_base + plane, f2_base + plane)

        def f2_forward(plane):
            f2_across(plane).start()

        q_line.arrive(2, q_forward)
        p_line.arrive(1)
        p_line.start(2)
        wait_all(m_third)
        m_last = wires.far(r.m_z.at[:, k], r.m_z.at[:, k], core_dev)
        f2_line.start(0)
        f2_forward(f)

        wait_all(first)
        for step in range(1, nc):
            x_share.arrive(step)
        m_last.wait()
        m_rows = [r.m_z[plane].reshape(n_rows, ada_w) for plane in range(nf)]
        r.m_tab[...] = jnp.concatenate(m_rows, axis=1)
        lead = lax.broadcasted_iota(jnp.int32, (n_sub, own), 1)
        lead = lead == SUB * lax.broadcasted_iota(jnp.int32, (n_sub, own), 0)
        lead = jnp.where(lead, 1.0, 0.0).astype(BF16)
        places = lax.broadcasted_iota(jnp.int32, (own, n_rows), 1).astype(F32)

        def hot_rows(blk):
            clip = r.idsg[blk].T[:, 1:2]
            return dot(lead, jnp.where(clip == places, 1.0, 0.0).astype(BF16)).astype(BF16)

        hot_all = jnp.concatenate([hot_rows(blk) for blk in range(nc)], axis=0)
        own_hot = hot_rows(c)
        for kind in range(6):
            value = r.m_tab[:, width * kind : width * (kind + 1)]
            if kind in (0, 1, 5):
                r.tab[kind % 3] = dot3(hot_all, value)
            r.own_tab[kind] = dot3(own_hot, value)

        def tab_row(kind, blk, g):
            return r.tab[kind % 3, pl.ds(blk * n_sub + g, 1), :]

        def own_row(kind, g):
            return r.own_tab[kind, pl.ds(g, 1), :]

        def make_a(blk):
            def body(g):
                rows = sub_rows(g)
                normal, _ = ln_parts(r.xg[blk, rows, :].astype(F32))
                value = normal * (1.0 + tab_row(1, blk, g)) + tab_row(0, blk, g)
                r.a_in[blk, rows, :] = value.astype(BF16)

            loop_rows(body)

        loop(nc, make_a)

        for kind in range(3):
            for other, _ in chip_peers:
                ref = r.q_got.at[kind, other]
                at = q_base + kind * nc + other
                pair(ref, ref, core_dev, at, at).wait()
            ref = r.q_got.at[kind, c]
            pltpu.make_async_copy(ref, ref, r.local.at[q_local + kind]).wait()
        q_core = []
        for chip in range(nc):
            row = [r.q_got[kind, chip] for kind in range(3)]
            w_q[chip, k] = jnp.concatenate(row, axis=1)
            q_core.append(wires.far(w_q.at[chip, k], w_q.at[chip, k], core_dev))
        p_line.arrive(2)
        p_near.wait()
        p_core = wires.far(r.p_got.at[k], r.p_got.at[k], core_dev)
        f1_near.wait()
        f1_forward(f)
        f1_line.arrive(0, f1_forward)
        f1_line.start(1)
        c_share = Share(r.cg, c_in)
        c_share.start()
        x_share.sent()
        p_core.wait()
        for side in range(2):
            row = [r.p_got[side, plane] for plane in range(nf)]
            r.w_p[side * rows_d : (side + 1) * rows_d, :] = jnp.concatenate(row, axis=1)
        wait_all(q_core)

        lane = lax.broadcasted_iota(jnp.int32, (1, chip_w), 1)
        head_of = [
            jnp.where((lane >= HEAD_DIM * h) & (lane < HEAD_DIM * (h + 1)), 1.0, 0.0).astype(BF16)
            for h in range(heads)
        ]

        def weight_q():
            return w_q[...].reshape(width, q_w)

        def qv_bias(plane):
            row = r.biasg[plane]
            return jnp.where(c % 2 == 0, row[:, :chip_w], row[:, chip_w : 2 * chip_w])

        bias_q, bias_v = qv_bias(c // 2), qv_bias(nf // 2 + c // 2)
        at_p = 2 * chip_w
        at_1 = at_p + cols_f
        at_2 = at_1 + ff_c
        bias_p = jnp.concatenate([r.biasg[g][:, at_p : at_p + cols_f] for g in range(nf)], axis=1)
        bias_o = jnp.concatenate([r.biasg[g][:, at_2 : at_2 + cols_f] for g in range(nf)], axis=1)
        bias_1 = r.biasg[c][:, at_1 : at_1 + ff_c]
        zero = jnp.zeros_like(bias_q)
        bias_qkv = jnp.concatenate([bias_q, zero, bias_v], axis=1)
        attn_merge = Merge(r.sum_s, r.sum_r, r.sum_st)

        def attend(i):
            step = nc - 1 - i
            blk = xor_of(c, step, nc)
            value = (dot(r.a_in[blk], weight_q()) + bias_qkv).astype(BF16)
            for kind in range(3):
                r.qkv[kind, blk] = value[:, chip_w * kind : chip_w * (kind + 1)]
            q_now, k_now, v_now = r.qkv[0, blk], r.qkv[1, blk], r.qkv[2, blk]
            frames = r.idsg[blk]
            same = frames.T[:, 0:1] == frames[0:1, :]
            mixed = jnp.zeros((own, chip_w), F32)
            for h in range(heads):
                scores = dot_rt(q_now * head_of[h], k_now) * head_scale
                scores = jnp.where(same, scores, NEG_FILL)
                raised = jnp.exp(scores - jnp.max(scores, axis=-1, keepdims=True))
                share = raised / jnp.sum(raised, axis=-1, keepdims=True)
                r.probs[blk * heads + h] = share
                mixed = mixed + dot(share.astype(BF16), v_now * head_of[h])
            mixed = mixed.astype(BF16)
            r.mixed[blk] = mixed
            attn_merge.put(step, blk, dot(mixed, r.w_p[...]).astype(BF16))

        loop(nc, attend)
        attn_merge.combine()
        c_share.relay()
        f1_line.arrive(1, f1_forward)
        f1_line.start(2)
        f2_line.arrive(0, f2_forward)
        f2_line.start(1)

        attn_merge.finish()

        def after_attention(g):
            rows = sub_rows(g)
            value = attn_merge.rows(rows) + bias_p
            r.attn[rows, :] = value
            after = r.xg[c, rows, :].astype(F32) + own_row(2, g) * value
            r.after[rows, :] = after
            normal, _ = ln_parts(after)
            r.m_all[c, rows, :] = (normal * (1.0 + own_row(4, g)) + own_row(3, g)).astype(BF16)

        loop_rows(after_attention)
        m_all = r.m_all
        m_share = Share(m_all)
        m_share.start()
        f1_line.arrive(2, f1_forward)
        f2_line.arrive(1, f2_forward)
        f2_line.start(2)
        for step in range(1, nc):
            c_share.arrive(step)

        def make_dbr(blk):
            def body(g):
                rows = sub_rows(g)
                value = r.cg[blk, rows, :].astype(F32) * tab_row(5, blk, g)
                r.dbr[blk, rows, :] = value.astype(BF16)

            loop_rows(body)

        loop(nc, make_dbr)
        m_share.relay()
        f1_core = []
        ref = r.w_1.at[c, k]
        pltpu.make_async_copy(ref, ref, r.local.at[f1_local]).wait()
        f1_core.append(wires.far(ref, ref, core_dev))
        for other, _ in chip_peers:
            ref = r.w_1.at[other, k]
            pair(ref, ref, core_dev, f1_base + other, f1_base + other).wait()
            f1_core.append(wires.far(ref, ref, core_dev))
        f1_line.sent(f1_in)
        c_share.sent()
        f2_line.arrive(2, f2_forward)
        wait_all(f1_core)
        for plane in range(nf):
            f2_across(plane).wait()

        def weight_1():
            return r.w_1[...].reshape(width, ff_c)

        def weight_2():
            return r.w_2[...].reshape(width, ff_c)

        dm_merge = Merge(r.sum_s, r.sum_r, r.sum_st)
        br_merge = Merge(r.br_s, r.br_r, r.br_st)

        def feed(step):
            blk = xor_of(c, step, nc)
            for at in range(1, nc):
                when(step == at, functools.partial(m_share.arrive, at))
            r.hid[...] = dot(m_all[blk], weight_1()) + bias_1

            def gelu_rows(g):
                rows = sub_rows(g)
                value, slope = gelu_both(r.hid[rows, :])
                r.act[blk, rows, :] = value.astype(BF16)
                r.slope[rows, :] = slope

            loop_rows(gelu_rows)
            r.hid[...] = dot(r.dbr[blk], weight_2())

            def back_rows(g):
                rows = sub_rows(g)
                r.d_hid[blk, rows, :] = (r.hid[rows, :] * r.slope[rows, :]).astype(BF16)

            loop_rows(back_rows)
            dm_merge.put(step, blk, dot_rt(r.d_hid[blk], weight_1()).astype(BF16))

        loop(nc, feed)
        m_share.sent()

        def column_cuts(count):
            return [(at, min(at + 256, count)) for at in range(0, count, 256)]

        def all_rows(ref):
            return ref[...].reshape(group, ref.shape[-1])

        dbr_all = all_rows(r.dbr)
        for lo, hi in column_cuts(ff_c):
            value = dot_lt(dbr_all, r.act[:, :, lo:hi].reshape(group, hi - lo))
            r.g_2[:, :, :, lo:hi] = value.astype(BF16).reshape(nf, 2, rows_d, hi - lo)
        g2_core = wires.far(r.g_2.at[:, core_o], r.g_2r, core_dev)

        def branch_out(i):
            step = nc - 1 - i
            blk = xor_of(c, step, nc)
            br_merge.put(step, blk, dot_rt(r.act[blk], weight_2()).astype(BF16))

        dm_merge.combine()
        loop(nc, branch_out)
        g2_core.wait()
        for plane in range(nf):
            r.g_2[plane, k] = add_low(r.g_2[plane, k], r.g_2r[plane])
        sum_2 = Sum(lambda t: r.g_2.at[t, k], r.got_2)
        sum_2.start(0)

        dm_merge.finish()
        da_all = r.da_all

        def back_norm2(g):
            rows = sub_rows(g)
            d_m = dm_merge.rows(rows)
            normal, scale = ln_parts(r.after[rows, :])
            cot_now = r.cg[c, rows, :].astype(F32)
            d_after = cot_now + ln_back(normal, scale, d_m * (1.0 + own_row(4, g)))
            r.d_after[rows, :] = d_after
            da_all[c, rows, :] = (own_row(2, g) * d_after).astype(BF16)
            at = pl.ds(g, 1)
            r.sub[3, at, :] = jnp.sum(d_m, axis=0, keepdims=True)
            r.sub[4, at, :] = jnp.sum(d_m * normal, axis=0, keepdims=True)
            r.sub[2, at, :] = jnp.sum(d_after * r.attn[rows, :], axis=0, keepdims=True)

        loop_rows(back_norm2)
        da_share = Share(da_all)
        da_share.start()
        br_merge.combine()
        sum_2.start(1)

        g_1 = r.w_1
        m_rows_all = all_rows(m_all)
        for lo, hi in column_cuts(ff_c):
            value = dot_lt(m_rows_all, r.d_hid[:, :, lo:hi].reshape(group, hi - lo))
            g_1[:, :, :, lo:hi] = value.astype(BF16).reshape(nc, 2, rows_d, hi - lo)
        g1_core = wires.far(g_1.at[:, core_o], r.g_1r, core_dev)
        da_share.relay()

        br_merge.finish()

        def finish_out(g):
            rows = sub_rows(g)
            branch = br_merge.rows(rows) + bias_o
            out[rows, :] = (r.after[rows, :] + own_row(5, g) * branch).astype(BF16)
            cot_now = r.cg[c, rows, :].astype(F32)
            r.sub[5, pl.ds(g, 1), :] = jnp.sum(cot_now * branch, axis=0, keepdims=True)

        loop_rows(finish_out)
        g1_core.wait()
        for chip in range(nc):
            g_1[chip, k] = add_low(g_1[chip, k], r.g_1r[chip])
        y_1 = r.f1_z
        y_1[c] = g_1[c, k]
        y1_far = [wires.far(g_1.at[other, k], y_1.at[c], peer) for other, peer in chip_peers]
        sum_2.start(2)

        back_merge = Merge(r.sum_s, r.sum_r, r.sum_st)

        def attend_back(step):
            blk = xor_of(c, step, nc)
            for at in range(1, nc):
                when(step == at, functools.partial(da_share.arrive, at))
            d_mix = dot_rt(da_all[blk], r.w_p[...]).astype(BF16)
            q_now, k_now, v_now = r.qkv[0, blk], r.qkv[1, blk], r.qkv[2, blk]
            d_q = jnp.zeros((own, chip_w), F32)
            d_k = jnp.zeros((own, chip_w), F32)
            d_v = jnp.zeros((own, chip_w), F32)
            for h in range(heads):
                d_mix_h = d_mix * head_of[h]
                share = r.probs[blk * heads + h]
                d_share = dot_rt(d_mix_h, v_now)
                d_score = share * (d_share - jnp.sum(share * d_share, axis=-1, keepdims=True))
                d_score = d_score.astype(BF16)
                d_q = d_q + dot(d_score, k_now * head_of[h])
                d_k = d_k + dot_lt(d_score, q_now * head_of[h])
                d_v = d_v + dot_lt(share.astype(BF16), d_mix_h)
            all_three = jnp.concatenate([d_q * head_scale, d_k * head_scale, d_v], axis=1).astype(BF16)
            r.d_qkv[blk] = all_three
            back_merge.put(step, blk, dot_rt(all_three, weight_q()).astype(BF16))

        loop(nc, attend_back)
        da_share.sent()
        back_merge.combine()

        g_q, g_p = w_q, r.w_p
        a_rows = all_rows(r.a_in)
        for lo, hi in column_cuts(q_w):
            value = dot_lt(a_rows, r.d_qkv[:, :, lo:hi].reshape(group, hi - lo))
            g_q[:, :, :, lo:hi] = value.astype(BF16).reshape(nc, 2, rows_d, hi - lo)
        q_core_back = wires.far(g_q.at[:, core_o], r.g_qr, core_dev)
        g_p[...] = dot_lt(all_rows(r.mixed), all_rows(da_all)).astype(BF16)

        def own_side(ref, side):
            return ref.at[pl.ds(pl.multiple_of(side * rows_d, SUB), rows_d)]

        p_core_back = wires.far(own_side(g_p, core_o), r.g_pr, core_dev)
        q_core_back.wait()
        for chip in range(nc):
            g_q[chip, k] = add_low(g_q[chip, k], r.g_qr[chip])
        r.y_got[c] = g_q[c, k]
        yq_far = [wires.far(g_q.at[other, k], r.y_got.at[c], peer) for other, peer in chip_peers]
        wait_all(y1_far)
        sum_1 = Sum(lambda t: y_1.at[t], r.got_1)
        sum_1.start(0)
        p_core_back.wait()
        p_line.sent(p_in)
        y_p = r.p_got
        total = add_low(own_side(g_p, k)[...], r.g_pr[...])
        for plane in range(nf):
            y_p[k, plane] = total[:, plane * cols_f : (plane + 1) * cols_f]
        sum_p = Sum(lambda t: y_p.at[k, t], r.got_p)
        sum_p.start(0)
        sum_1.start(1)

        back_merge.finish()

        def back_norm1(g):
            rows = sub_rows(g)
            d_a = back_merge.rows(rows)
            normal, scale = ln_parts(r.xg[c, rows, :].astype(F32))
            value = r.d_after[rows, :] + ln_back(normal, scale, d_a * (1.0 + own_row(1, g)))
            x_grad[rows, :] = value.astype(BF16)
            at = pl.ds(g, 1)
            r.sub[0, at, :] = jnp.sum(d_a, axis=0, keepdims=True)
            r.sub[1, at, :] = jnp.sum(d_a * normal, axis=0, keepdims=True)

        loop_rows(back_norm1)
        hot_turned = own_hot.astype(F32).T.astype(BF16)
        for kind in range(6):
            value = dot3(hot_turned, r.sub[kind])
            r.d_part[:, :, width * kind : width * (kind + 1)] = value.reshape(2, half, width)
        d_core = wires.far(r.d_part.at[core_o], r.d_core, core_dev)
        ones_own = jnp.ones((8, own), BF16)
        ones_all = jnp.ones((8, group), BF16)
        r.d_bias[...] = jnp.zeros((8, width), F32)
        r.d_bias[0:1, :] = dot(ones_own, da_all[c])[0:1]
        r.d_bias[1:2, :] = dot(ones_own, r.dbr[c])[0:1]
        qkv_sums = dot(ones_all, all_rows(r.d_qkv))[0:1]
        r.d_bias[2:3, 0:chip_w] = qkv_sums[:, :chip_w]
        r.d_bias[3:4, 0:chip_w] = qkv_sums[:, 2 * chip_w :]

        ones_ff = dot(ones_all, all_rows(r.d_hid))[0:1]
        r.d_bias[4:5, :] = ones_ff[:, :width]
        for part in range(1, ff_c // width):
            r.d_bias[4 + part : 5 + part, :] = ones_ff[:, part * width : (part + 1) * width]
        d_core.wait()
        r.d_core[...] = r.d_core[...] + r.d_part[k]
        for plane in range(nf):
            r.d_cut[plane] = r.d_core[:, ada_w * plane : ada_w * (plane + 1)]
        small = []
        for other, peer in plane_peers:
            small.append(wires.far(r.d_cut.at[other], r.dz.at[f], peer))
            small.append(wires.far(r.d_bias, r.dzb.at[f], peer))
        r.dz[f] = r.d_cut[f]
        r.dzb[f] = r.d_bias[...]
        sum_1.start(2)
        wait_all(yq_far)
        q_line.sent(q_in)
        y_q = r.q_z
        for plane in range(nf):
            row = []
            for i in range(3):
                kind, chip = (3 * plane + i) // nc, (3 * plane + i) % nc
                row.append(r.y_got[chip, :, chip_w * kind : chip_w * (kind + 1)])
            y_q[plane] = jnp.concatenate(row, axis=1)
        sum_q = Sum(lambda t: y_q.at[t], r.got_q)
        sum_q.start(0)
        sum_p.start(1)
        wait_all(small)
        value, value_b = r.dz[0], r.dzb[0]
        for plane in range(1, nf):
            value = value + r.dz[plane]
            value_b = value_b + r.dzb[plane]
        m_chip[c] = value
        r.d_bsum[...] = value_b
        b_swap = wires.far(r.d_bsum, r.d_coreb, core_dev)
        small = [wires.far(m_chip.at[c], m_chip.at[c], peer) for _, peer in chip_peers]
        sum_q.start(1)
        sum_p.start(2)
        b_swap.wait()
        r.d_chipb[c] = r.d_bsum[...] + r.d_coreb[...]
        for _, peer in chip_peers:
            small.append(wires.far(r.d_chipb.at[c], r.d_chipb.at[c], peer))

        sum_2.finish(r.all_2.at[k])
        o2_swap = wires.far(r.all_2.at[k], r.all_2.at[k], core_dev)
        wait_all(small)
        value = m_chip[0]
        for chip in range(1, nc):
            value = value + m_chip[chip]
        r.d_tot[k] = value
        d_swap = wires.far(r.d_tot.at[k], r.d_tot.at[k], core_dev)
        sum_q.start(2)
        d_swap.wait()
        d_cols = r.d_tot[...].reshape(n_rows, ada_w)
        silu_turned = silu_in[...].astype(F32).T.astype(BF16)
        o_bada[...] = jnp.sum(d_cols, axis=0, keepdims=True)
        value, total = d_cols, None
        for _ in range(3):
            term = value.astype(BF16)
            value = value - term.astype(F32)
            part = dot_rt(term, r.ada[...])
            total = part if total is None else total + part
        r.c_part[f] = total
        c_far = [wires.far(r.c_part.at[f], r.c_part.at[f], peer) for _, peer in plane_peers]
        for lo, hi in column_cuts(ada_w):
            o_ada[:, lo:hi] = dot3(silu_turned, d_cols[:, lo:hi])
        sum_1.finish(o_1)
        o2_swap.wait()

        def own_columns(lo):
            def body():
                both = r.all_2[:, :, lo : lo + ff_d].reshape(cols_f, ff_d)
                o_2[...] = both.T

            return body

        when(k == 0, own_columns(0))
        when(k == 1, own_columns(ff_d))
        wait_all(c_far)
        value = r.c_part[0]
        for plane in range(1, nf):
            value = value + r.c_part[plane]
        r.c_all[c, k] = value
        wait_all([wires.far(r.c_all.at[c, k], r.c_all.at[c, k], peer) for _, peer in chip_peers])
        c_swap = wires.far(r.c_all.at[:, k], r.c_all.at[:, k], core_dev)
        sum_p.finish(o_p)
        own_sums = r.d_chipb[0]
        for chip in range(1, nc):
            own_sums = own_sums + r.d_chipb[chip]
        for plane in range(nf):

            def bias_columns(plane=plane):
                at = plane * cols_f
                o_bp[...] = own_sums[0:1, at : at + cols_f]
                o_b2[...] = own_sums[1:2, at : at + cols_f]
                kind, chip = 2 * plane // nc, 2 * plane % nc
                o_bqv[...] = jnp.concatenate(
                    [r.d_chipb[chip + i, 2 + kind : 3 + kind, 0:chip_w] for i in range(2)], axis=1
                )
                parts = [r.d_chipb[plane, 4 + i : 5 + i, :] for i in range(ff_c // width)]
                o_b1[...] = parts[0] if len(parts) == 1 else jnp.concatenate(parts, axis=1)

            when(f == plane, bias_columns)
        c_swap.wait()
        d_silu = jnp.concatenate([r.c_all[f, 0], r.c_all[f, 1]], axis=1)
        cond_now = cond_in[...]
        gate = 1.0 / (1.0 + jnp.exp(-cond_now))
        o_cond[...] = d_silu * (gate * (1.0 + cond_now * (1.0 - gate)))
        sum_q.finish(o_q)
        f2_line.sent()
        assert wires.remote_count <= n_sem and wires.local_count <= 32

    return pl.pallas_call(
        kernel,
        out_shape=outs,
        in_specs=[ANYWHERE] * 2 + [ON_CHIP] * 4 + [ANYWHERE] * 5,
        out_specs=tuple([ON_CHIP] * len(outs)),
        scratch_shapes=list(scratch.values()),
        compiler_params=pltpu.CompilerParams(
            collective_id=0, has_side_effects=True, vmem_limit_bytes=63 * 2**20
        ),
        name="block",
    )(x, cot, ids, bias, silu_part, cond_own, w_ada, wq, wp, w1, w2)


def fits_block(n_dp, nf, width, ff, own, micro):
    nc = n_dp // 2
    return (
        nc == nf
        and nf == 4
        and width % (128 * nf) == 128
        and ff == 4 * width
        and (width // n_dp) % 16 == 0
        and (width // nc) % HEAD_DIM == 0
        and own % (2 * SUB) == 0
    )


def per_device(
    n_dp, nf, patches, cotangent, conditioning, frame_of_slot, clip_of_slot,
    w_ada, b_ada, w_qkv, b_qv, w_proj, b_proj, w_fc1, b_fc1, w_fc2, b_fc2,
):
    nc = n_dp // 2
    sizes = (nc, nf)
    micro, block, width = patches.shape
    own = micro * block
    clips = conditioning.shape[1]
    rows_d = width // n_dp
    cols_f = width // nf
    ff = w_fc1.shape[1] * nf
    ff_d = ff // n_dp
    chip_w = width // nc
    piece_q = math.gcd(3 * width // nf, chip_w)
    piece_1 = math.gcd(ff // nf, ff_d)
    dims = types.SimpleNamespace(
        nc=nc,
        nf=nf,
        per_q=3 * width // nf // piece_q,
        per_1=ff // nf // piece_1,
        chip_q=chip_w // piece_q,
        chip_1=ff // nc // piece_1,
    )
    dp = lax.axis_index("dp")
    f = lax.axis_index("fsdp")
    c, k = dp // 2, dp % 2

    q_send = w_qkv.reshape(rows_d, dims.per_q, piece_q).transpose(1, 0, 2)
    f1_send = w_fc1.reshape(rows_d, dims.per_1, piece_1).transpose(1, 0, 2)
    f2_send = w_fc2.T
    cond = conditioning.reshape(micro * clips, width)
    silu_cond = jax.nn.silu(cond)
    silu_low = silu_cond.astype(BF16)
    ada_w = w_ada.shape[1]
    silu_part = lax.dynamic_slice_in_dim(silu_low, dp * rows_d, rows_d, 1)
    mod_part = dot(silu_part, w_ada) + jnp.where(dp == 0, b_ada.astype(F32), 0.0)[None]
    mod_send = mod_part.reshape(-1, 2, ada_w // 2).transpose(1, 0, 2)
    cut = [0, 2 * cols_f, 3 * cols_f, 3 * cols_f + ff // nf, 4 * cols_f + ff // nf]
    cond_own = lax.dynamic_slice_in_dim(cond, f * cols_f, cols_f, 1)

    def ada_outputs(d_cols):
        grad_w_ada = precise(silu_part.astype(F32), d_cols, ((0,), (0,)))
        d_silu_part = precise(d_cols, w_ada.astype(F32), ((1,), (1,)))
        d_silu = cond_kernel(dims, d_silu_part).transpose(1, 0, 2).reshape(micro * clips, width)
        d_silu_own = lax.dynamic_slice_in_dim(d_silu, f * cols_f, cols_f, 1)
        _, silu_back = jax.vjp(jax.nn.silu, cond_own)
        cond_grad = silu_back(d_silu_own)[0].reshape(micro, clips, cols_f)
        return cond_grad, grad_w_ada, jnp.sum(d_cols, axis=0)

    if fits_block(n_dp, nf, width, ff, own, micro):
        bias_send = jnp.concatenate([b_qv, b_proj, b_fc1, b_fc2, b_ada]).astype(F32)[None]
        order = jnp.arange(micro, dtype=jnp.int32)[:, None]
        pair_rows = jnp.stack(
            [(frame_of_slot + order * 65536).reshape(own), (clip_of_slot + order * clips).reshape(own)]
        )
        id_rows = jnp.concatenate([pair_rows.astype(F32), jnp.zeros((6, own), F32)])
        (
            output, input_grad, cond_grad, grad_ada, grad_b_ada, grad_qkv, grad_b_qv,
            grad_proj, grad_b_proj, grad_fc1, grad_b_fc1, grad_fc2, grad_b_fc2,
        ) = block_kernel(
            dims, patches.reshape(own, width), cotangent.reshape(own, width), id_rows, bias_send,
            silu_part, cond_own, w_ada, w_qkv, w_proj, w_fc1, w_fc2,
        )
        return (
            output.reshape(patches.shape),
            input_grad.reshape(patches.shape),
            cond_grad.reshape(micro, clips, cols_f),
            grad_ada,
            grad_b_ada[0],
            grad_qkv,
            grad_b_qv[0],
            grad_proj,
            grad_b_proj[0],
            grad_fc1,
            grad_b_fc1[0],
            grad_fc2,
            grad_b_fc2[0],
        )

    ids = jnp.stack([frame_of_slot.reshape(own), clip_of_slot.reshape(own)])
    ids = jnp.concatenate([ids, jnp.zeros((6, own), jnp.int32)])
    bias_send = jnp.concatenate([b_qv, b_proj, b_fc1, b_fc2]).astype(F32)[None]

    (x_all, c_all, ids_all, bias_all, mod_all, q_chip, f1_chip, p_chip, f2_chip, _, _) = start_kernel(
        dims, patches.reshape(own, width), cotangent.reshape(own, width), ids, bias_send, mod_send,
        q_send, f1_send, w_proj, f2_send,
    )
    group = nc * own
    modulation = mod_all.transpose(2, 0, 1, 3).reshape(micro * clips, 6 * width)
    q_parts = [
        q_chip[i].reshape(nc, 2, dims.chip_q, rows_d, piece_q).transpose(0, 1, 3, 2, 4).reshape(width, chip_w)
        for i in range(3)
    ]
    w1 = f1_chip.transpose(1, 2, 3, 0, 4).reshape(width, ff // nc)
    wp = p_chip.transpose(0, 2, 1, 3).reshape(chip_w, width)
    w2t = f2_chip.reshape(2, width, ff_d).transpose(1, 0, 2).reshape(width, 2 * ff_d)
    b_parts = [bias_all[:, 0, a:b].reshape(-1) for a, b in zip(cut[:-1], cut[1:])]
    bq = lax.dynamic_slice_in_dim(b_parts[0], c * chip_w, chip_w, 0)
    bv = lax.dynamic_slice_in_dim(b_parts[0], width + c * chip_w, chip_w, 0)
    b1 = lax.dynamic_slice_in_dim(b_parts[2], c * (ff // nc), ff // nc, 0)

    def hot_of(clip_ids):
        count = clip_ids.shape[0]
        row = (jnp.arange(count, dtype=jnp.int32) // block) % micro * clips + clip_ids
        return (row[:, None] == jnp.arange(micro * clips, dtype=jnp.int32)[None]).astype(F32)

    hot_group = hot_of(ids_all[:, 1].reshape(group))
    hot_own = hot_of(clip_of_slot.reshape(own))
    mod_group = precise(hot_group, modulation, ((1,), (0,)))
    mod_own = precise(hot_own, modulation, ((1,), (0,)))
    shift1, scale1 = mod_group[:, :width], mod_group[:, width : 2 * width]
    gate1 = mod_own[:, 2 * width : 3 * width]
    shift2, scale2 = mod_own[:, 3 * width : 4 * width], mod_own[:, 4 * width : 5 * width]
    gate2_group, gate2 = mod_group[:, 5 * width :], mod_own[:, 5 * width :]

    x_group = x_all.reshape(group, width).astype(F32)
    norm1, rstd1 = ln_parts(x_group)
    a_in = (norm1 * (1.0 + scale1) + shift1).astype(BF16)
    zero = jnp.zeros_like(bq)
    q, kk, v = [
        (dot(a_in, w) + b[None]).astype(BF16) for w, b in zip(q_parts, (bq, zero, bv))
    ]
    heads = chip_w // HEAD_DIM
    blocks = group // block
    q4, k4, v4 = [t.reshape(blocks, block, heads, HEAD_DIM) for t in (q, kk, v)]
    frames = ids_all[:, 0].reshape(blocks, block)
    same = (frames[:, :, None] == frames[:, None, :])[:, None]
    scores = jnp.einsum("bqhd,bkhd->bhqk", q4, k4, preferred_element_type=F32) * HEAD_DIM ** (-0.5)
    scores = jnp.where(same, scores, NEG_FILL)
    top = jnp.max(scores, axis=-1, keepdims=True)
    raised = jnp.exp(scores - top)
    probs = raised / jnp.sum(raised, axis=-1, keepdims=True)
    probs_low = probs.astype(BF16)
    mixed = jnp.einsum("bhqk,bkhd->bqhd", probs_low, v4, preferred_element_type=F32)
    mixed = mixed.reshape(group, chip_w).astype(BF16)
    attn_part = dot(mixed, wp)
    (attn_got,) = exchange(
        "attn_sum", 3, sizes, [(CHIP, SPREAD, attn_part.astype(BF16).reshape(nc, own, width))]
    )
    attn = jnp.sum(attn_got.astype(F32), axis=0) + b_parts[1][None]
    x_own = patches.reshape(own, width).astype(F32)
    after = x_own + gate1 * attn
    norm2, rstd2 = ln_parts(after)
    m_own = (norm2 * (1.0 + scale2) + shift2).astype(BF16)
    (m_all,) = exchange("m_gather", 4, sizes, [(CHIP, GATHER, m_own)])
    m_in = m_all.reshape(group, width)

    hidden = dot(m_in, w1) + b1[None]
    act, slope = gelu_both(hidden)
    act = act.astype(BF16)
    branch_part = dot_rt(act, w2t)
    cot_group = c_all.reshape(group, width).astype(F32)
    d_branch = (gate2_group * cot_group).astype(BF16)
    grad_2t = dot_lt(d_branch, act)
    d_hidden = (dot(d_branch, w2t) * slope).astype(BF16)
    grad_1 = dot_lt(m_in, d_hidden)
    d_m_part = dot_rt(d_hidden, w1)
    branch_got, d_m_got = exchange(
        "ff_sum",
        5,
        sizes,
        [
            (CHIP, SPREAD, d_m_part.astype(BF16).reshape(nc, own, width)),
            (CHIP, SPREAD, branch_part.astype(BF16).reshape(nc, own, width)),
        ],
    )[::-1]
    branch = jnp.sum(branch_got.astype(F32), axis=0) + b_parts[3][None]
    output = (after + gate2 * branch).astype(BF16)
    d_m = jnp.sum(d_m_got.astype(F32), axis=0)
    cot_own = cotangent.reshape(own, width).astype(F32)
    d_after = cot_own + ln_back(norm2, rstd2, d_m * (1.0 + scale2))
    d_attn = (gate1 * d_after).astype(BF16)
    (d_attn_all,) = exchange("d_attn_gather", 6, sizes, [(CHIP, GATHER, d_attn)])
    d_attn_group = d_attn_all.reshape(group, width)
    grad_p = dot_lt(mixed, d_attn_group)
    d_mix = dot_rt(d_attn_group, wp).astype(BF16).reshape(blocks, block, heads, HEAD_DIM)
    d_probs = jnp.einsum("bqhd,bkhd->bhqk", d_mix, v4, preferred_element_type=F32)
    d_scores = probs * (d_probs - jnp.sum(probs * d_probs, axis=-1, keepdims=True))
    d_scores = d_scores.astype(BF16)
    dq = jnp.einsum("bhqk,bkhd->bqhd", d_scores, k4, preferred_element_type=F32) * HEAD_DIM ** (-0.5)
    dk = jnp.einsum("bhqk,bqhd->bkhd", d_scores, q4, preferred_element_type=F32) * HEAD_DIM ** (-0.5)
    dv = jnp.einsum("bhqk,bqhd->bkhd", probs_low, d_mix, preferred_element_type=F32)
    dqkv = [t.reshape(group, chip_w).astype(BF16) for t in (dq, dk, dv)]
    d_a_part = sum(dot_rt(t, w) for t, w in zip(dqkv, q_parts))
    grad_q = jnp.stack([dot_lt(a_in, t) for t in dqkv])
    (d_a_got,) = exchange(
        "d_a_sum", 7, sizes, [(CHIP, SPREAD, d_a_part.astype(BF16).reshape(nc, own, width))]
    )
    d_a = jnp.sum(d_a_got.astype(F32), axis=0)
    norm1_own, rstd1_own = ln_parts(x_own)
    scale1_own = mod_own[:, width : 2 * width]
    input_grad = (d_after + ln_back(norm1_own, rstd1_own, d_a * (1.0 + scale1_own))).astype(BF16)

    g_q = grad_q.reshape(3, nc, 2, rows_d, dims.chip_q, piece_q).transpose(2, 1, 0, 4, 3, 5)
    g_1 = grad_1.reshape(nc, 2, rows_d, dims.chip_1, piece_1).transpose(1, 0, 3, 2, 4)
    g_p = grad_p.reshape(2, rows_d, nf, cols_f).transpose(0, 2, 1, 3)
    g_2 = grad_2t.reshape(nf, cols_f, 2, ff_d).transpose(2, 0, 1, 3)
    got = exchange("grad_core", 8, sizes, [(CORE, SPREAD, g.astype(BF16)) for g in (g_q, g_1, g_p, g_2)])
    s_q, s_1, s_p, s_2 = [jnp.sum(g.astype(F32), axis=0).astype(BF16) for g in got]
    r_q, r_1 = exchange("grad_chip", 9, sizes, [(CHIP, SPREAD, s_q), (CHIP, SPREAD, s_1)])
    z_q = r_q.transpose(1, 0, 2, 3, 4).reshape(nf, dims.per_q, rows_d, piece_q)
    z_1 = r_1.reshape(nf, dims.per_1, rows_d, piece_1)
    got = exchange("grad_plane", 10, sizes, [(PLANE, SPREAD, g) for g in (z_q, z_1, s_p, s_2)])
    o_q, o_1, o_p, o_2 = [jnp.sum(g.astype(F32), axis=0) for g in got]
    grad_w_qkv = o_q.transpose(1, 0, 2).reshape(rows_d, 3 * width // nf)
    grad_w_fc1 = o_1.transpose(1, 0, 2).reshape(rows_d, ff // nf)
    grad_w_fc2 = o_2.T

    d_token = jnp.concatenate(
        [d_a, d_a * norm1_own, d_after * attn, d_m, d_m * norm2, cot_own * branch], axis=1
    )
    d_mod = precise(hot_own, d_token, ((0,), (0,)))
    d_branch_own = (gate2 * cot_own).astype(BF16).astype(F32)

    def columns(value):
        return jnp.sum(value.astype(F32), axis=0)

    def spread(value, count):
        return lax.dynamic_update_slice_in_dim(
            jnp.zeros((count,), F32), value, c * value.shape[0], 0
        )

    g_bqv = jnp.concatenate([spread(columns(dqkv[0]), width), spread(columns(dqkv[2]), width)])
    g_b1 = spread(columns(d_hidden), ff)
    bias_terms = jnp.concatenate(
        [
            g_bqv.reshape(nf, -1),
            columns(d_attn).reshape(nf, -1),
            g_b1.reshape(nf, -1),
            columns(d_branch_own).reshape(nf, -1),
        ],
        axis=1,
    )
    n_bias = bias_terms.shape[1]
    bias_rows = -(-n_bias // ada_w)
    bias_terms = jnp.pad(bias_terms, ((0, 0), (0, bias_rows * ada_w - n_bias)))
    terms = jnp.concatenate(
        [d_mod.reshape(micro * clips, nf, ada_w).transpose(1, 0, 2), bias_terms.reshape(nf, bias_rows, ada_w)],
        axis=1,
    )
    pad_rows = -terms.shape[1] % 8
    terms = jnp.pad(terms, ((0, 0), (0, pad_rows), (0, 0)))
    terms = terms.reshape(nf, -1, 2, ada_w // 2).transpose(0, 2, 1, 3)
    total = sum_small_kernel(dims, terms).transpose(1, 0, 2).reshape(-1, ada_w)
    d_cols = total[: micro * clips]
    bias_sums = total[micro * clips : micro * clips + bias_rows].reshape(-1)[:n_bias]
    g_parts = [bias_sums[a:b] for a, b in zip(cut[:-1], cut[1:])]
    cond_grad, grad_w_ada, grad_b_ada = ada_outputs(d_cols)
    return (
        output.reshape(patches.shape),
        input_grad.reshape(patches.shape),
        cond_grad,
        grad_w_ada,
        grad_b_ada,
        grad_w_qkv,
        g_parts[0],
        o_p,
        g_parts[1],
        grad_w_fc1,
        g_parts[2],
        grad_w_fc2,
        g_parts[3],
    )


def solution(mesh):
    tokens = P(None, ("dp", "fsdp"), None)
    ids = P(None, ("dp", "fsdp"))
    both, cols = P("dp", "fsdp"), P("fsdp")
    in_specs = (tokens, tokens, P(), ids, ids) + (both, cols) * 5
    out_specs = (tokens, tokens, P(None, None, "fsdp")) + (both, cols) * 5
    return jax.shard_map(
        functools.partial(per_device, mesh.shape["dp"], mesh.shape["fsdp"]),
        mesh=mesh,
        in_specs=in_specs,
        out_specs=out_specs,
        check_vma=False,
    )
```

```python
import functools
import math
import types

import jax
import jax.numpy as jnp
from jax import lax
from jax.experimental import pallas as pl
from jax.experimental.pallas import tpu as pltpu
from jax.sharding import PartitionSpec as P

HEAD_DIM = 72
EPS = 1e-06
GELU_C = math.sqrt(2.0 / math.pi)
PRECISE = lax.Precision.HIGHEST
NEG_FILL = -1e30
SUB = 16
CORE, CHIP, PLANE, ALL = range(4)
GATHER, SPREAD = range(2)
MESH_ID = pl.DeviceIdType.MESH
F32 = jnp.float32
BF16 = jnp.bfloat16


def xor_of(index, step, size):
    result, bit = 0, 1
    while bit < size:
        mine = (index // bit) % 2
        result = result + ((mine + (step // bit) % 2) % 2) * bit
        bit *= 2
    return result


class Place:
    def __init__(self, n_chip, n_plane):
        self.n = {CORE: 2, CHIP: n_chip, PLANE: n_plane, ALL: 2 * n_chip}
        self.dp = lax.axis_index("dp")
        self.f = lax.axis_index("fsdp")
        self.c = self.dp // 2
        self.k = self.dp % 2

    def index(self, axis):
        return {CORE: self.k, CHIP: self.c, PLANE: self.f, ALL: self.dp}[axis]

    def peer(self, axis, step):
        other = xor_of(self.index(axis), step, self.n[axis])
        if axis == CORE:
            return other, (self.c * 2 + other, self.f)
        if axis == CHIP:
            return other, (other * 2 + self.k, self.f)
        if axis == PLANE:
            return other, (self.dp, other)
        return other, (other, self.f)


def greet(place, axes):
    barrier = pltpu.get_barrier_semaphore()
    count = 0
    for axis in axes:
        for step in range(1, place.n[axis]):
            pl.semaphore_signal(
                barrier, inc=1, device_id=place.peer(axis, step)[1], device_id_type=MESH_ID
            )
            count += 1
    pl.semaphore_wait(barrier, count)


class Wires:
    def __init__(self, send, recv, local):
        self.send, self.recv, self.local = send, recv, local
        self.remote_count = 0
        self.local_count = 0

    def far(self, src, dst, device):
        at = self.remote_count
        self.remote_count += 1
        copy = pltpu.make_async_remote_copy(
            src_ref=src,
            dst_ref=dst,
            send_sem=self.send.at[at],
            recv_sem=self.recv.at[at],
            device_id=device,
            device_id_type=MESH_ID,
        )
        copy.start()
        return copy

    def near(self, src, dst):
        at = self.local_count
        self.local_count += 1
        copy = pltpu.make_async_copy(src, dst, self.local.at[at])
        copy.start()
        return copy


def wait_all(copies):
    for copy in copies:
        copy.wait()


ANYWHERE = pl.BlockSpec(memory_space=pl.ANY)
ON_CHIP = pl.BlockSpec(memory_space=pltpu.VMEM)


def exchange(name, collective_id, sizes, items):
    n_chip, n_plane = sizes
    n_of = {CORE: 2, CHIP: n_chip, PLANE: n_plane, ALL: 2 * n_chip}
    axes = sorted({item[0] for item in items})
    outs = []
    n_far = 0
    for axis, kind, array in items:
        n_far += n_of[axis] - 1
        shape = array.shape if kind == SPREAD else (n_of[axis],) + array.shape
        outs.append(jax.ShapeDtypeStruct(shape, array.dtype))

    def kernel(*refs):
        ins = refs[: len(items)]
        results = refs[len(items) : 2 * len(items)]
        place = Place(n_chip, n_plane)
        wires = Wires(*refs[2 * len(items) :])
        greet(place, axes)
        copies = []
        for (axis, kind, _), src, dst in zip(items, ins, results):
            mine = place.index(axis)
            for step in range(1, n_of[axis]):
                other, device = place.peer(axis, step)
                piece = src if kind == GATHER else src.at[other]
                copies.append(wires.far(piece, dst.at[mine], device))
        for (axis, kind, _), src, dst in zip(items, ins, results):
            mine = place.index(axis)
            copies.append(wires.near(src if kind == GATHER else src.at[mine], dst.at[mine]))
        wait_all(copies)

    return pl.pallas_call(
        kernel,
        out_shape=tuple(outs),
        in_specs=[ANYWHERE] * len(items),
        out_specs=tuple([ANYWHERE] * len(items)),
        scratch_shapes=[
            pltpu.SemaphoreType.DMA((n_far,)),
            pltpu.SemaphoreType.DMA((n_far,)),
            pltpu.SemaphoreType.DMA((len(items),)),
        ],
        compiler_params=pltpu.CompilerParams(collective_id=collective_id, has_side_effects=True),
        name=name,
    )(*[item[2] for item in items])


def start_kernel(dims, x, cot, ids, bias, mod, wq, w1, wp, w2):
    nc, nf = dims.nc, dims.nf
    per_q, per_1 = dims.per_q, dims.per_1
    chip_q, chip_1 = dims.chip_q, dims.chip_1
    part_q = nc * chip_q
    rows, half = mod.shape[1], mod.shape[2]
    n_far = 5 * (nf - 1) + 3 * (nc - 1) + 4 * (nc - 1) + 4 + 1 + (nc - 1) + (nf - 1) + 1
    outs = (
        jax.ShapeDtypeStruct((nc,) + x.shape, x.dtype),
        jax.ShapeDtypeStruct((nc,) + cot.shape, cot.dtype),
        jax.ShapeDtypeStruct((nc,) + ids.shape, ids.dtype),
        jax.ShapeDtypeStruct((nf,) + bias.shape, bias.dtype),
        jax.ShapeDtypeStruct((nf, 2, rows, half), F32),
        jax.ShapeDtypeStruct((3, nc, 2, chip_q) + wq.shape[1:], BF16),
        jax.ShapeDtypeStruct((chip_1, nc, 2) + w1.shape[1:], BF16),
        jax.ShapeDtypeStruct((2, nf) + wp.shape, BF16),
        jax.ShapeDtypeStruct((2, nf) + w2.shape, BF16),
        jax.ShapeDtypeStruct((nf * per_q,) + wq.shape[1:], BF16),
        jax.ShapeDtypeStruct((nf * per_1,) + w1.shape[1:], BF16),
    )

    def kernel(
        x_in, c_in, i_in, b_in, m_in, q_in, f1_in, p_in, f2_in,
        x_all, c_all, i_all, b_all, m_all, q_chip, f1_chip, p_chip, f2_chip, q_rows, f1_rows,
        m_core, m_sum, m_chip, send, recv, local,
    ):
        place = Place(nc, nf)
        wires = Wires(send, recv, local)
        c, k, f = place.c, place.k, place.f
        greet(place, (CORE, CHIP, PLANE))
        core_other, core_peer = place.peer(CORE, 1)
        chip_peers = [place.peer(CHIP, step) for step in range(1, nc)]
        plane_peers = [place.peer(PLANE, step) for step in range(1, nf)]

        m_first = wires.far(m_in.at[core_other], m_core, core_peer)
        q_got, f1_got, p_got, f2_got, small = [], [], [], [], []
        for _, peer in plane_peers:
            q_got.append(wires.far(q_in, q_rows.at[pl.ds(f * per_q, per_q)], peer))
            small.append(wires.far(b_in, b_all.at[f], peer))
        q_got.append(wires.near(q_in, q_rows.at[pl.ds(f * per_q, per_q)]))
        small.append(wires.near(b_in, b_all.at[f]))
        for _, peer in chip_peers:
            small.append(wires.far(i_in, i_all.at[c], peer))
            small.append(wires.far(x_in, x_all.at[c], peer))
        m_first.wait()
        m_sum[...] = m_in[k] + m_core[...]
        m_chip[c] = m_sum[...]
        m_second = [wires.far(m_sum, m_chip.at[c], peer) for _, peer in chip_peers]
        for _, peer in plane_peers:
            p_got.append(wires.far(p_in, p_chip.at[k, f], peer))
        for _, peer in plane_peers:
            f1_got.append(wires.far(f1_in, f1_rows.at[pl.ds(f * per_1, per_1)], peer))
        for _, peer in plane_peers:
            f2_got.append(wires.far(f2_in, f2_chip.at[k, f], peer))
        p_got.append(wires.near(p_in, p_chip.at[k, f]))
        f1_got.append(wires.near(f1_in, f1_rows.at[pl.ds(f * per_1, per_1)]))
        f2_got.append(wires.near(f2_in, f2_chip.at[k, f]))
        small.append(wires.near(i_in, i_all.at[c]))
        small.append(wires.near(x_in, x_all.at[c]))
        for _, peer in chip_peers:
            small.append(wires.far(c_in, c_all.at[c], peer))
        small.append(wires.near(c_in, c_all.at[c]))
        wait_all(m_second)
        total = m_chip[0]
        for other in range(1, nc):
            total = total + m_chip[other]
        m_all[f, k] = total
        wait_all([wires.far(m_all.at[f, k], m_all.at[f, k], peer) for _, peer in plane_peers])
        m_last = wires.far(m_all.at[:, k], m_all.at[:, k], core_peer)

        wait_all(q_got)
        q_moved = []
        for kind in range(3):
            for other, peer in chip_peers:
                q_moved.append(
                    wires.far(
                        q_rows.at[pl.ds(kind * part_q + other * chip_q, chip_q)],
                        q_chip.at[kind, c, k],
                        peer,
                    )
                )
            q_moved.append(
                wires.near(
                    q_rows.at[pl.ds(kind * part_q + c * chip_q, chip_q)], q_chip.at[kind, c, k]
                )
            )
        wait_all(p_got)
        last = [m_last, wires.far(p_chip.at[k], p_chip.at[k], core_peer)]
        wait_all(q_moved)
        last.append(wires.far(q_chip.at[:, :, k], q_chip.at[:, :, k], core_peer))
        wait_all(f1_got)
        f1_moved = []
        for other, peer in chip_peers:
            f1_moved.append(
                wires.far(f1_rows.at[pl.ds(other * chip_1, chip_1)], f1_chip.at[:, c, k], peer)
            )
        f1_moved.append(
            wires.near(f1_rows.at[pl.ds(c * chip_1, chip_1)], f1_chip.at[:, c, k])
        )
        wait_all(f2_got)
        last.append(wires.far(f2_chip.at[k], f2_chip.at[k], core_peer))
        wait_all(f1_moved)
        last.append(wires.far(f1_chip.at[:, :, k], f1_chip.at[:, :, k], core_peer))
        wait_all(small)
        wait_all(last)

    return pl.pallas_call(
        kernel,
        out_shape=outs,
        in_specs=[ANYWHERE] * 4 + [ON_CHIP] + [ANYWHERE] * 4,
        out_specs=tuple([ANYWHERE] * 4 + [ON_CHIP] + [ANYWHERE] * 6),
        scratch_shapes=[
            pltpu.VMEM((rows, half), F32),
            pltpu.VMEM((rows, half), F32),
            pltpu.VMEM((nc, rows, half), F32),
            pltpu.SemaphoreType.DMA((n_far,)),
            pltpu.SemaphoreType.DMA((n_far,)),
            pltpu.SemaphoreType.DMA((12,)),
        ],
        compiler_params=pltpu.CompilerParams(collective_id=0, has_side_effects=True),
        name="start",
    )(x, cot, ids, bias, mod, wq, w1, wp, w2)


def sum_small_kernel(dims, terms):
    nc, nf = dims.nc, dims.nf
    _, _, rows, half = terms.shape
    n_far = (nf - 1) + 1 + (nc - 1) + 1

    def kernel(t_in, total, z_got, both, core_got, chip_got, send, recv, local):
        place = Place(nc, nf)
        wires = Wires(send, recv, local)
        c, k, f = place.c, place.k, place.f
        greet(place, (CORE, CHIP, PLANE))
        core_other, core_peer = place.peer(CORE, 1)
        copies = []
        for step in range(1, nf):
            other, peer = place.peer(PLANE, step)
            copies.append(wires.far(t_in.at[other], z_got.at[f], peer))
        z_got[f] = t_in[f]
        wait_all(copies)
        value = z_got[0]
        for other in range(1, nf):
            value = value + z_got[other]
        both[...] = value
        wires.far(both.at[core_other], core_got, core_peer).wait()
        chip_got[c] = both[k] + core_got[...]
        copies = []
        for step in range(1, nc):
            _, peer = place.peer(CHIP, step)
            copies.append(wires.far(chip_got.at[c], chip_got.at[c], peer))
        wait_all(copies)
        value = chip_got[0]
        for other in range(1, nc):
            value = value + chip_got[other]
        total[k] = value
        wires.far(total.at[k], total.at[k], core_peer).wait()

    return pl.pallas_call(
        kernel,
        out_shape=jax.ShapeDtypeStruct((2, rows, half), F32),
        in_specs=[ON_CHIP],
        out_specs=ON_CHIP,
        scratch_shapes=[
            pltpu.VMEM((nf, 2, rows, half), F32),
            pltpu.VMEM((2, rows, half), F32),
            pltpu.VMEM((rows, half), F32),
            pltpu.VMEM((nc, rows, half), F32),
            pltpu.SemaphoreType.DMA((n_far,)),
            pltpu.SemaphoreType.DMA((n_far,)),
            pltpu.SemaphoreType.DMA((1,)),
        ],
        compiler_params=pltpu.CompilerParams(collective_id=1, has_side_effects=True),
        name="sum_small",
    )(terms)


def cond_kernel(dims, part):
    nc, nf = dims.nc, dims.nf
    nd = 2 * nc
    rows, width = part.shape
    n_far = (nf - 1) + (nd - 1)

    def kernel(p_in, out, got, send, recv, local):
        place = Place(nc, nf)
        wires = Wires(send, recv, local)
        greet(place, (PLANE, ALL))
        copies = []
        for step in range(1, nf):
            copies.append(wires.far(p_in, got.at[place.f], place.peer(PLANE, step)[1]))
        got[place.f] = p_in[...]
        wait_all(copies)
        value = got[0]
        for other in range(1, nf):
            value = value + got[other]
        out[place.dp] = value
        copies = []
        for step in range(1, nd):
            copies.append(
                wires.far(out.at[place.dp], out.at[place.dp], place.peer(ALL, step)[1])
            )
        wait_all(copies)

    return pl.pallas_call(
        kernel,
        out_shape=jax.ShapeDtypeStruct((nd, rows, width), F32),
        in_specs=[ON_CHIP],
        out_specs=ON_CHIP,
        scratch_shapes=[
            pltpu.VMEM((nf, rows, width), F32),
            pltpu.SemaphoreType.DMA((n_far,)),
            pltpu.SemaphoreType.DMA((n_far,)),
            pltpu.SemaphoreType.DMA((1,)),
        ],
        compiler_params=pltpu.CompilerParams(collective_id=2, has_side_effects=True),
        name="cond_sum",
    )(part)


def dot(left, right):
    return jnp.dot(left, right, preferred_element_type=F32)


def dot_rt(left, right):
    return lax.dot_general(left, right, (((1,), (1,)), ((), ())), preferred_element_type=F32)


def dot_lt(left, right):
    return lax.dot_general(left, right, (((0,), (0,)), ((), ())), preferred_element_type=F32)


def precise(left, right, dims):
    return lax.dot_general(
        left, right, (dims, ((), ())), precision=PRECISE, preferred_element_type=F32
    )


def ln_parts(values):
    centre = values - jnp.mean(values, axis=-1, keepdims=True)
    scale = lax.rsqrt(jnp.mean(centre * centre, axis=-1, keepdims=True) + EPS)
    return centre * scale, scale


def ln_back(normal, scale, grad):
    return scale * (
        grad
        - jnp.mean(grad, axis=-1, keepdims=True)
        - normal * jnp.mean(grad * normal, axis=-1, keepdims=True)
    )


def gelu_both(h):
    square = h * h
    t = jnp.tanh(GELU_C * (h + 0.044715 * h * square))
    value = 0.5 * h * (1.0 + t)
    slope = 0.5 * (1.0 + t) + 0.5 * h * (1.0 - t * t) * GELU_C * (1.0 + 3 * 0.044715 * square)
    return value, slope


def dot3(left, right):
    wide_left = left.dtype == F32
    value = left if wide_left else right
    total = None
    for _ in range(3):
        term = value.astype(BF16)
        value = value - term.astype(F32)
        part = dot(term, right) if wide_left else dot(left, term)
        total = part if total is None else total + part
    return total


def add_low(left, right):
    return (left.astype(F32) + right.astype(F32)).astype(BF16)


def block_kernel(dims, x, cot, ids, bias, silu_part, cond_own, w_ada, wq, wp, w1, w2):
    nc, nf = dims.nc, dims.nf
    own, width = x.shape
    group = nc * own
    rows_d, q_w = wq.shape
    chip_w = q_w // 3
    cols_f, ff_d = w2.shape
    ff_c = 2 * ff_d
    ada_w = w_ada.shape[1]
    n_bias = bias.shape[1]
    heads = chip_w // HEAD_DIM
    n_rows = silu_part.shape[0]
    half = n_rows // 2
    n_sub = own // SUB
    head_scale = HEAD_DIM ** (-0.5)
    last = nf - 2

    outs = (
        jax.ShapeDtypeStruct((own, width), BF16),
        jax.ShapeDtypeStruct((own, width), BF16),
        jax.ShapeDtypeStruct((n_rows, cols_f), F32),
        jax.ShapeDtypeStruct((rows_d, ada_w), F32),
        jax.ShapeDtypeStruct((ada_w,), F32),
        jax.ShapeDtypeStruct((rows_d, q_w), F32),
        jax.ShapeDtypeStruct((2 * chip_w,), F32),
        jax.ShapeDtypeStruct((rows_d, cols_f), F32),
        jax.ShapeDtypeStruct((cols_f,), F32),
        jax.ShapeDtypeStruct((rows_d, ff_c), F32),
        jax.ShapeDtypeStruct((ff_c,), F32),
        jax.ShapeDtypeStruct((cols_f, ff_d), F32),
        jax.ShapeDtypeStruct((cols_f,), F32),
    )
    tokens = (nc, own, width)
    n_sem = 240
    scratch = dict(
        xg=pltpu.VMEM(tokens, BF16),
        cg=pltpu.VMEM(tokens, BF16),
        idsg=pltpu.VMEM((nc, 8, own), F32),
        biasg=pltpu.VMEM((nf, 1, n_bias), F32),
        ada=pltpu.VMEM(w_ada.shape, BF16),
        m_part=pltpu.VMEM((2, half, ada_w), F32),
        m_core=pltpu.VMEM((half, ada_w), F32),
        m_chip=pltpu.VMEM((nc, half, ada_w), F32),
        m_z=pltpu.VMEM((nf, 2, half, ada_w), F32),
        m_tab=pltpu.VMEM((n_rows, 6 * width), F32),
        tab=pltpu.VMEM((3, nc * n_sub, width), F32),
        own_tab=pltpu.VMEM((6, n_sub, width), F32),
        q_z=pltpu.VMEM((nf, rows_d, q_w + cols_f), BF16),
        q_rows=pltpu.VMEM((nf * 3, rows_d, chip_w), BF16),
        q_got=pltpu.VMEM((3, nc, rows_d, chip_w), BF16),
        w_q=pltpu.VMEM((nc, 2, rows_d, q_w), BF16),
        y_got=pltpu.VMEM((nc, rows_d, q_w), BF16),
        f1_z=pltpu.VMEM((nf, rows_d, ff_c), BF16),
        w_1=pltpu.VMEM((nc, 2, rows_d, ff_c), BF16),
        p_got=pltpu.VMEM((2, nf, rows_d, cols_f), BF16),
        w_p=pltpu.VMEM((chip_w, width), BF16),
        f2_half=pltpu.VMEM((cols_f, ff_d), BF16),
        f2_got=pltpu.VMEM((rows_d, ff_d), BF16),
        w_2=pltpu.VMEM((nf, 2, rows_d, ff_c), BF16),
        a_in=pltpu.VMEM(tokens, BF16),
        qkv=pltpu.VMEM((3, nc, own, chip_w), BF16),
        probs=pltpu.VMEM((nc * heads, own, own), F32),
        mixed=pltpu.VMEM((nc, own, chip_w), BF16),
        sum_s=pltpu.VMEM(tokens, BF16),
        sum_r=pltpu.VMEM((2, own, width), BF16),
        sum_st=pltpu.VMEM((2, own // 2, width), BF16),
        br_s=pltpu.VMEM(tokens, BF16),
        br_r=pltpu.VMEM((2, own, width), BF16),
        br_st=pltpu.VMEM((2, own // 2, width), BF16),
        m_all=pltpu.VMEM(tokens, BF16),
        da_all=pltpu.VMEM(tokens, BF16),
        attn=pltpu.VMEM((own, width), F32),
        after=pltpu.VMEM((own, width), F32),
        d_after=pltpu.VMEM((own, width), F32),
        hid=pltpu.VMEM((own, ff_c), F32),
        act=pltpu.VMEM((nc, own, ff_c), BF16),
        d_hid=pltpu.VMEM((nc, own, ff_c), BF16),
        dbr=pltpu.VMEM(tokens, BF16),
        d_qkv=pltpu.VMEM((nc, own, q_w), BF16),
        g_2=pltpu.VMEM((nf, 2, rows_d, ff_c), BF16),
        g_2r=pltpu.VMEM((nf, rows_d, ff_c), BF16),
        g_1r=pltpu.VMEM((nc, rows_d, ff_c), BF16),
        g_qr=pltpu.VMEM((nc, rows_d, q_w), BF16),
        g_pr=pltpu.VMEM((rows_d, width), BF16),
        got_q=pltpu.VMEM((2, nf - 1, rows_d, q_w + cols_f), BF16),
        got_1=pltpu.VMEM((2, nf - 1, rows_d, ff_c), BF16),
        got_2=pltpu.VMEM((2, nf - 1, rows_d, ff_c), BF16),
        all_2=pltpu.VMEM((2, rows_d, ff_c), F32),
        sub=pltpu.VMEM((6, n_sub, width), F32),
        q_nat=pltpu.VMEM((rows_d, q_w), BF16),
        p_nat=pltpu.VMEM((rows_d, cols_f), BF16),
        all_q=pltpu.VMEM((rows_d, q_w + cols_f), F32),
        sub_gate=pltpu.VMEM((nc * n_sub, width), F32),
        d_part=pltpu.VMEM((2, half, 6 * width), F32),
        d_core=pltpu.VMEM((half, 6 * width), F32),
        d_cut=pltpu.VMEM((nf, half, ada_w), F32),
        d_bias=pltpu.VMEM((8, width), F32),
        dz=pltpu.VMEM((nf, half, ada_w), F32),
        dzb=pltpu.VMEM((nf, 8, width), F32),
        d_tot=pltpu.VMEM((2, half, ada_w), F32),
        d_bsum=pltpu.VMEM((8, width), F32),
        d_coreb=pltpu.VMEM((8, width), F32),
        d_chipb=pltpu.VMEM((nc, 8, width), F32),
        c_part=pltpu.VMEM((nf, n_rows, rows_d), F32),
        c_all=pltpu.VMEM((nc, 2, n_rows, rows_d), F32),
        send=pltpu.SemaphoreType.DMA((n_sem,)),
        recv=pltpu.SemaphoreType.DMA((n_sem,)),
        local=pltpu.SemaphoreType.DMA((32,)),
    )
    names = list(scratch)

    def kernel(
        x_in, c_in, ids_in, bias_in, silu_in, cond_in, ada_in, q_in, p_in, f1_in, f2_in,
        out, x_grad, o_cond, o_ada, o_bada, o_q, o_bqv, o_p, o_bp, o_1, o_b1, o_2, o_b2, *rest,
    ):
        r = types.SimpleNamespace(**dict(zip(names, rest)))
        place = Place(nc, nf)
        wires = Wires(r.send, r.recv, r.local)
        c, k, f = place.c, place.k, place.f
        core_o, core_dev = place.peer(CORE, 1)
        chip_peers = [place.peer(CHIP, step) for step in range(1, nc)]
        plane_peers = [place.peer(PLANE, step) for step in range(1, nf)]

        def loop(count, body, unroll=1):
            def run(i, carry):
                body(i)
                return carry

            lax.fori_loop(0, count, run, 0, unroll=unroll)

        def loop_rows(body):
            loop(n_sub, body, 2)

        def when(condition, body):
            pl.when(condition)(body)

        def sub_rows(g):
            return pl.ds(pl.multiple_of(g * SUB, SUB), SUB)

        def reserve(count):
            base = wires.remote_count
            wires.remote_count += count
            return base

        def pair(src, dst, device, send_at, recv_at):
            return pltpu.make_async_remote_copy(
                src_ref=src,
                dst_ref=dst,
                send_sem=r.send.at[send_at],
                recv_sem=r.recv.at[recv_at],
                device_id=device,
                device_id_type=MESH_ID,
            )

        chip_x, dev_x = place.peer(CHIP, 1)
        chip_y, dev_y = place.peer(CHIP, 2)
        chip_d, _ = place.peer(CHIP, 3)
        first_half, second_half = pl.ds(0, own // 2), pl.ds(own // 2, own // 2)

        class Share:
            def __init__(self, ref, src=None):
                def copy(chip, rows, device, at, own_src=None):
                    from_ref = ref.at[chip, rows] if own_src is None else own_src.at[rows]
                    return pair(from_ref, ref.at[chip, rows], device, at, at)

                at = reserve(6)
                self.x_a = copy(c, first_half, dev_x, at, src)
                self.x_b = copy(c, second_half, dev_x, at + 1, src)
                self.y_b = copy(c, second_half, dev_y, at + 2, src)
                self.y_a = copy(c, first_half, dev_y, at + 3, src)
                self.on_y = copy(chip_x, first_half, dev_y, at + 4)
                self.on_x = copy(chip_y, second_half, dev_x, at + 5)

            def start(self):
                for item in (self.x_a, self.y_b, self.x_b, self.y_a):
                    item.start()

            def relay(self):
                self.x_a.wait_recv()
                self.on_y.start()
                self.y_b.wait_recv()
                self.on_x.start()

            def arrive(self, step):
                if step == 1:
                    self.x_b.wait_recv()
                elif step == 2:
                    self.y_a.wait_recv()
                else:
                    self.on_y.wait_recv()
                    self.on_x.wait_recv()

            def sent(self):
                for item in (self.x_a, self.x_b, self.y_b, self.y_a, self.on_y, self.on_x):
                    item.wait_send()

        class Merge:
            def __init__(self, terms, got, stage):
                self.terms, self.got, self.stage = terms, got, stage
                at = reserve(6)
                self.d_x = pair(terms.at[chip_d, first_half], stage.at[0], dev_x, at, at)
                self.d_y = pair(terms.at[chip_d, second_half], stage.at[1], dev_y, at + 1, at + 1)

                def copy(chip, rows, to, device, index):
                    return pair(
                        terms.at[chip, rows], got.at[to, rows], device, at + index, at + index
                    )

                self.x_a = copy(chip_x, first_half, 0, dev_x, 2)
                self.x_b = copy(chip_x, second_half, 0, dev_x, 3)
                self.y_b = copy(chip_y, second_half, 1, dev_y, 4)
                self.y_a = copy(chip_y, first_half, 1, dev_y, 5)

            def put(self, step, blk, part):
                self.terms[blk] = part

                def far():
                    self.d_x.start()
                    self.d_y.start()

                when(step == 3, far)
                when(step == 2, self.y_b.start)
                when(step == 1, self.x_a.start)

            def launch(self):
                for item in (self.d_x, self.d_y, self.y_b, self.x_a):
                    item.start()

            def combine(self):
                self.d_y.wait()
                ref = self.terms.at[chip_x, second_half]
                ref[...] = add_low(ref[...], self.stage[1])
                self.x_b.start()
                self.d_x.wait()
                ref = self.terms.at[chip_y, first_half]
                ref[...] = add_low(ref[...], self.stage[0])
                self.y_a.start()

            def finish(self):
                for item in (self.x_a, self.x_b, self.y_b, self.y_a):
                    item.wait()

            def rows(self, at):
                value = self.terms[c, at, :].astype(F32) + self.got[0, at, :].astype(F32)
                return value + self.got[1, at, :].astype(F32)

        up, down = (place.dp, f + 1), (place.dp, f - 1)

        class Gather:
            def __init__(self, slot):
                self.slot = slot
                self.up, self.down = reserve(nf - 1), reserve(nf - 1)

            def both(self, step, src=None):
                above = pair(
                    self.slot(f - step) if src is None else src,
                    self.slot(f - step), up, self.up + step, self.up + step,
                )
                below = pair(
                    self.slot(f + step) if src is None else src,
                    self.slot(f + step), down, self.down + step, self.down + step,
                )
                return (
                    ((f - step >= 0) & (f < nf - 1), above),
                    ((f + step <= nf - 1) & (f > 0), below),
                )

            def start(self, step, src=None):
                for condition, copy in self.both(step, src):
                    when(condition, copy.start)

            def arrive(self, step, then=None, wait=True):
                for condition, got, base in (
                    (f - 1 - step >= 0, f - 1 - step, self.up),
                    (f + 1 + step <= nf - 1, f + 1 + step, self.down),
                ):

                    def body(got=got, base=base):
                        slot = self.slot(got)
                        if wait:
                            pair(slot, slot, core_dev, base + step, base + step).wait_recv()
                        if then is not None:
                            then(got)

                    when(condition, body)

            def sent(self, src=None):
                for step in range(nf - 1):
                    for condition, copy in self.both(step, src if step == 0 else None):
                        when(condition, copy.wait_send)

        class Sum:
            def __init__(self, terms, got):
                self.terms, self.got = terms, got
                self.bases = (reserve(nf - 1), reserve(nf - 1))

            def both(self, step):
                for way in range(2):
                    target = f + (nf - 1) - step if way == 0 else f - (nf - 1) + step
                    condition = (f <= step) & (f < nf - 1) if way == 0 else (target >= 0) & (f > 0)
                    more = condition & (f > 0 if way == 0 else f < nf - 1)
                    at = self.bases[way] + step
                    copy = pair(
                        self.terms(target), self.got.at[way, step], up if way == 0 else down, at, at
                    )
                    yield way, target, condition, more, copy

            def wait(self, way, step):
                at = self.bases[way] + step
                ref = self.got.at[way, step]
                pair(ref, ref, core_dev, at, at).wait_recv()

            def start(self, step):
                for way, target, condition, more, copy in self.both(step):
                    if step > 0:

                        def body(way=way, target=target):
                            self.wait(way, step - 1)
                            ref = self.terms(target)
                            ref[...] = add_low(ref[...], self.got[way, step - 1])

                        when(more, body)
                    when(condition, copy.start)

            def finish(self, result):
                result[...] = self.terms(f)[...].astype(F32)
                for way, condition in ((0, f > 0), (1, f < nf - 1)):

                    def body(way=way):
                        self.wait(way, last)
                        result[...] = result[...] + self.got[way, last].astype(F32)

                    when(condition, body)
                for step in range(nf - 1):
                    for _, _, condition, _, copy in self.both(step):
                        when(condition, copy.wait_send)

        def own_side(ref, side):
            return ref.at[pl.ds(pl.multiple_of(side * rows_d, SUB), rows_d)]

        barrier = pltpu.get_barrier_semaphore()
        peers = [core_dev] + [peer for _, peer in chip_peers + plane_peers]
        for peer in peers:
            pl.semaphore_signal(barrier, inc=1, device_id=peer, device_id_type=MESH_ID)

        q_line = Gather(lambda g: r.q_z.at[g])
        f1_line = Gather(lambda g: r.f1_z.at[g])
        f2_line = Gather(lambda g: r.w_2.at[g, k])
        ada_near = wires.near(ada_in, r.ada)
        q_near = wires.near(q_in, r.q_nat)
        p_near = wires.near(p_in, r.p_nat)
        f2_near = wires.near(f2_in, r.f2_half)
        first = []
        first.append(wires.near(x_in, r.xg.at[c]))
        first.append(wires.near(c_in, r.cg.at[c]))
        f1_near = wires.near(f1_in, r.f1_z.at[f])
        r.idsg[c] = ids_in[...]
        r.biasg[f] = bias_in[...]
        ada_near.wait()
        ada_bias = jnp.where(place.dp == 0, bias_in[:, n_bias - ada_w :], 0.0)
        value = dot(silu_in[...], r.ada[...]) + ada_bias
        r.m_part[...] = value.reshape(2, half, ada_w)
        q_near.wait()
        p_near.wait()
        r.q_z[f] = jnp.concatenate([r.q_nat[...], r.p_nat[...]], axis=1)
        f2_near.wait()
        pl.semaphore_wait(barrier, len(peers))
        m_first = wires.far(r.m_part.at[core_o], r.m_core, core_dev)
        q_line.start(0)
        for _, peer in chip_peers:
            first.append(wires.far(ids_in, r.idsg.at[c], peer))
        f2_swap = wires.far(own_side(r.f2_half, core_o), r.f2_got, core_dev)

        w_q, q_rows = r.w_q, r.q_rows
        q_base = reserve(3 * nc)
        q_local = wires.local_count
        wires.local_count += 3

        def q_copies(plane, i):
            piece = 3 * plane + i
            kind, chip = piece // nc, piece % nc
            src, dst = q_rows.at[piece], r.q_got.at[kind, c]
            far = pair(src, dst, (chip * 2 + k, f), q_base + kind * nc + chip, q_base + kind * nc + c)
            return chip, far, pltpu.make_async_copy(src, dst, r.local.at[q_local + kind])

        def q_forward(plane):
            r.p_got[k, plane] = r.q_z[plane, :, q_w:]
            for i in range(3):
                q_rows[3 * plane + i] = r.q_z[plane, :, chip_w * i : chip_w * (i + 1)]
                chip, far, near = q_copies(plane, i)
                when(chip != c, far.start)
                when(chip == c, near.start)

        f1_base = reserve(nc)
        f1_local = wires.local_count
        wires.local_count += 1

        def f1_copies(plane):
            src, dst = r.f1_z.at[plane], r.w_1.at[c, k]
            far = pair(src, dst, (plane * 2 + k, f), f1_base + plane, f1_base + c)
            return far, pltpu.make_async_copy(src, dst, r.local.at[f1_local])

        def f1_forward(plane):
            far, near = f1_copies(plane)
            when(plane != c, far.start)
            when(plane == c, near.start)

        m_first.wait()
        m_chip = r.m_chip
        m_chip[c] = r.m_part[k] + r.m_core[...]
        m_second = [wires.far(m_chip.at[c], m_chip.at[c], peer) for _, peer in chip_peers]
        q_forward(f)
        x_share = Share(r.xg, x_in)
        x_share.start()
        wait_all(m_second)
        total = m_chip[0]
        for other in range(1, nc):
            total = total + m_chip[other]
        r.m_z[f, k] = total
        m_third = [wires.far(r.m_z.at[f, k], r.m_z.at[f, k], peer) for _, peer in plane_peers]
        for _, peer in plane_peers:
            first.append(wires.far(bias_in, r.biasg.at[f], peer))
        q_line.arrive(0, q_forward)
        q_line.start(1)
        x_share.relay()
        f2_swap.wait()

        def join_even():
            r.w_2[f, k] = jnp.concatenate([r.f2_half[:rows_d], r.f2_got[...]], axis=1)

        def join_odd():
            r.w_2[f, k] = jnp.concatenate([r.f2_got[...], r.f2_half[rows_d:]], axis=1)

        when(k == 0, join_even)
        when(k == 1, join_odd)
        f2_base = reserve(nf)

        def f2_across(plane):
            ref = r.w_2.at[plane, k]
            return pair(ref, ref, core_dev, f2_base + plane, f2_base + plane)

        def f2_forward(plane):
            f2_across(plane).start()

        f2_forward(f)
        wait_all(m_third)
        m_last = wires.far(r.m_z.at[:, k], r.m_z.at[:, k], core_dev)

        wait_all(first)
        m_last.wait()
        m_rows = [r.m_z[plane].reshape(n_rows, ada_w) for plane in range(nf)]
        r.m_tab[...] = jnp.concatenate(m_rows, axis=1)
        lead = lax.broadcasted_iota(jnp.int32, (n_sub, own), 1)
        lead = lead == SUB * lax.broadcasted_iota(jnp.int32, (n_sub, own), 0)
        lead = jnp.where(lead, 1.0, 0.0).astype(BF16)
        places = lax.broadcasted_iota(jnp.int32, (own, n_rows), 1).astype(F32)

        def hot_rows(blk):
            clip = r.idsg[blk].T[:, 1:2]
            return dot(lead, jnp.where(clip == places, 1.0, 0.0).astype(BF16)).astype(BF16)

        hot_all = jnp.concatenate([hot_rows(blk) for blk in range(nc)], axis=0)
        own_hot = hot_rows(c)
        for kind in range(6):
            value = r.m_tab[:, width * kind : width * (kind + 1)]
            if kind in (0, 1, 5):
                r.tab[kind % 3] = dot3(hot_all, value)
            r.own_tab[kind] = dot3(own_hot, value)

        def tab_row(kind, blk, g):
            return r.tab[kind % 3, pl.ds(blk * n_sub + g, 1), :]

        def own_row(kind, g):
            return r.own_tab[kind, pl.ds(g, 1), :]

        def make_a(blk):
            def body(g):
                rows = sub_rows(g)
                normal, _ = ln_parts(r.xg[blk, rows, :].astype(F32))
                value = normal * (1.0 + tab_row(1, blk, g)) + tab_row(0, blk, g)
                r.a_in[blk, rows, :] = value.astype(BF16)

            loop_rows(body)

        make_a(c)
        for step in (1, 2):
            x_share.arrive(step)
            make_a(xor_of(c, step, nc))
        q_line.arrive(1, q_forward)
        q_line.start(2)
        f1_line.start(0, f1_in)
        x_share.arrive(3)
        make_a(chip_d)
        q_line.arrive(2, q_forward)

        for kind in range(3):
            for other, _ in chip_peers:
                ref = r.q_got.at[kind, other]
                at = q_base + kind * nc + other
                pair(ref, ref, core_dev, at, at).wait()
            ref = r.q_got.at[kind, c]
            pltpu.make_async_copy(ref, ref, r.local.at[q_local + kind]).wait()
        q_core = []
        for chip in range(nc):
            row = [r.q_got[kind, chip] for kind in range(3)]
            w_q[chip, k] = jnp.concatenate(row, axis=1)
            q_core.append(wires.far(w_q.at[chip, k], w_q.at[chip, k], core_dev))
        p_core = wires.far(r.p_got.at[k], r.p_got.at[k], core_dev)
        f1_near.wait()
        f1_forward(f)
        f1_line.arrive(0, f1_forward)
        f1_line.start(1)
        x_share.sent()
        p_core.wait()
        for side in range(2):
            row = [r.p_got[side, plane] for plane in range(nf)]
            r.w_p[side * rows_d : (side + 1) * rows_d, :] = jnp.concatenate(row, axis=1)
        wait_all(q_core)

        lane = lax.broadcasted_iota(jnp.int32, (1, chip_w), 1)
        head_of = [
            jnp.where((lane >= HEAD_DIM * h) & (lane < HEAD_DIM * (h + 1)), 1.0, 0.0).astype(BF16)
            for h in range(heads)
        ]

        def weight_q():
            return w_q[...].reshape(width, q_w)

        def qv_bias(plane):
            row = r.biasg[plane]
            return jnp.where(c % 2 == 0, row[:, :chip_w], row[:, chip_w : 2 * chip_w])

        bias_q, bias_v = qv_bias(c // 2), qv_bias(nf // 2 + c // 2)
        at_p = 2 * chip_w
        at_1 = at_p + cols_f
        at_2 = at_1 + ff_c
        bias_p = jnp.concatenate([r.biasg[g][:, at_p : at_p + cols_f] for g in range(nf)], axis=1)
        bias_o = jnp.concatenate([r.biasg[g][:, at_2 : at_2 + cols_f] for g in range(nf)], axis=1)
        bias_1 = r.biasg[c][:, at_1 : at_1 + ff_c]
        zero = jnp.zeros_like(bias_q)
        bias_qkv = jnp.concatenate([bias_q, zero, bias_v], axis=1)
        attn_merge = Merge(r.sum_s, r.sum_r, r.sum_st)

        def attend(i):
            step = nc - 1 - i
            blk = xor_of(c, step, nc)
            value = (dot(r.a_in[blk], weight_q()) + bias_qkv).astype(BF16)
            for kind in range(3):
                r.qkv[kind, blk] = value[:, chip_w * kind : chip_w * (kind + 1)]
            q_now, k_now, v_now = r.qkv[0, blk], r.qkv[1, blk], r.qkv[2, blk]
            frames = r.idsg[blk]
            same = frames.T[:, 0:1] == frames[0:1, :]
            mixed = jnp.zeros((own, chip_w), F32)
            for h in range(heads):
                scores = dot_rt(q_now * head_of[h], k_now) * head_scale
                scores = jnp.where(same, scores, NEG_FILL)
                raised = jnp.exp(scores - jnp.max(scores, axis=-1, keepdims=True))
                share = raised / jnp.sum(raised, axis=-1, keepdims=True)
                r.probs[blk * heads + h] = share
                mixed = mixed + dot(share.astype(BF16), v_now * head_of[h])
            mixed = mixed.astype(BF16)
            r.mixed[blk] = mixed
            attn_merge.put(step, blk, dot(mixed, r.w_p[...]).astype(BF16))

            def next_lines():
                f1_line.arrive(1)
                f1_line.start(2)
                f2_line.start(0)

            when(i == 0, next_lines)

        loop(nc, attend)
        attn_merge.combine()
        f1_line.arrive(1, f1_forward, False)
        f1_line.arrive(2, f1_forward)

        attn_merge.finish()

        def after_attention(g):
            rows = sub_rows(g)
            value = attn_merge.rows(rows) + bias_p
            r.attn[rows, :] = value
            after = r.xg[c, rows, :].astype(F32) + own_row(2, g) * value
            r.after[rows, :] = after
            normal, _ = ln_parts(after)
            r.m_all[c, rows, :] = (normal * (1.0 + own_row(4, g)) + own_row(3, g)).astype(BF16)

        loop_rows(after_attention)
        m_all = r.m_all
        m_share = Share(m_all)
        m_share.start()
        c_share = Share(r.cg, c_in)
        c_share.start()
        f2_line.arrive(0, f2_forward)
        f2_line.start(1)
        m_share.relay()
        f1_core = []
        ref = r.w_1.at[c, k]
        pltpu.make_async_copy(ref, ref, r.local.at[f1_local]).wait()
        f1_core.append(wires.far(ref, ref, core_dev))
        for other, _ in chip_peers:
            ref = r.w_1.at[other, k]
            pair(ref, ref, core_dev, f1_base + other, f1_base + other).wait()
            f1_core.append(wires.far(ref, ref, core_dev))
        f1_line.sent(f1_in)
        f2_line.arrive(1, f2_forward)
        f2_line.start(2)
        wait_all(f1_core)

        def weight_1():
            return r.w_1[...].reshape(width, ff_c)

        def weight_2():
            return r.w_2[...].reshape(width, ff_c)

        dm_merge = Merge(r.sum_s, r.sum_r, r.sum_st)
        br_merge = Merge(r.br_s, r.br_r, r.br_st)

        def mixed_order(i):
            return (1 + 2 * i) * (1 - i // 2) + (6 - 2 * i) * (i // 2)

        def feed(step):
            blk = xor_of(c, step, nc)
            for at in range(1, nc):
                when(step == at, functools.partial(m_share.arrive, at))
            r.hid[...] = dot(m_all[blk], weight_1()) + bias_1

            def gelu_rows(g):
                rows = sub_rows(g)
                value, slope = gelu_both(r.hid[rows, :])
                r.act[blk, rows, :] = value.astype(BF16)
                r.d_hid[blk, rows, :] = slope.astype(BF16)

            loop_rows(gelu_rows)
            when(step == 1, c_share.relay)

        def feed_back(i):
            step = mixed_order(i)
            blk = xor_of(c, step, nc)
            for at in range(1, nc):
                when(step == at, functools.partial(c_share.arrive, at))

            def dbr_rows(g):
                rows = sub_rows(g)
                value = r.cg[blk, rows, :].astype(F32) * tab_row(5, blk, g)
                r.dbr[blk, rows, :] = value.astype(BF16)

            loop_rows(dbr_rows)
            r.hid[...] = dot(r.dbr[blk], weight_2())

            def back_rows(g):
                rows = sub_rows(g)
                value = r.hid[rows, :] * r.d_hid[blk, rows, :].astype(F32)
                r.d_hid[blk, rows, :] = value.astype(BF16)

            loop_rows(back_rows)
            dm_merge.put(step, blk, dot_rt(r.d_hid[blk], weight_1()).astype(BF16))

        loop(nc, feed)
        f2_line.arrive(2, f2_forward)
        for plane in range(nf):
            f2_across(plane).wait()
        loop(nc, feed_back)
        dm_merge.combine()
        c_share.sent()

        def column_cuts(count):
            return [(at, min(at + 256, count)) for at in range(0, count, 256)]

        def all_rows(ref):
            return ref[...].reshape(group, ref.shape[-1])

        dbr_all = all_rows(r.dbr)
        for lo, hi in column_cuts(ff_c):
            value = dot_lt(dbr_all, r.act[:, :, lo:hi].reshape(group, hi - lo))
            r.g_2[:, :, :, lo:hi] = value.astype(BF16).reshape(nf, 2, rows_d, hi - lo)
        g2_core = wires.far(r.g_2.at[:, core_o], r.g_2r, core_dev)

        dm_merge.finish()
        da_all = r.da_all

        def back_norm2(g):
            rows = sub_rows(g)
            d_m = dm_merge.rows(rows)
            normal, scale = ln_parts(r.after[rows, :])
            cot_now = r.cg[c, rows, :].astype(F32)
            d_after = cot_now + ln_back(normal, scale, d_m * (1.0 + own_row(4, g)))
            r.d_after[rows, :] = d_after
            da_all[c, rows, :] = (own_row(2, g) * d_after).astype(BF16)
            at = pl.ds(g, 1)
            r.sub[3, at, :] = jnp.sum(d_m, axis=0, keepdims=True)
            r.sub[4, at, :] = jnp.sum(d_m * normal, axis=0, keepdims=True)
            r.sub[2, at, :] = jnp.sum(d_after * r.attn[rows, :], axis=0, keepdims=True)

        loop_rows(back_norm2)
        da_share = Share(da_all)
        da_share.start()
        m_share.sent()
        g2_core.wait()
        for plane in range(nf):
            r.g_2[plane, k] = add_low(r.g_2[plane, k], r.g_2r[plane])
        sum_2 = Sum(lambda t: r.g_2.at[t, k], r.got_2)
        sum_2.start(0)

        g_1 = r.w_1
        m_rows_all = all_rows(m_all)
        for lo, hi in column_cuts(ff_c):
            value = dot_lt(m_rows_all, r.d_hid[:, :, lo:hi].reshape(group, hi - lo))
            g_1[:, :, :, lo:hi] = value.astype(BF16).reshape(nc, 2, rows_d, hi - lo)
        g1_core = wires.far(g_1.at[:, core_o], r.g_1r, core_dev)
        da_share.relay()

        g1_core.wait()
        for chip in range(nc):
            g_1[chip, k] = add_low(g_1[chip, k], r.g_1r[chip])
        y_1 = r.f1_z
        y_1[c] = g_1[c, k]
        y1_far = [wires.far(g_1.at[other, k], y_1.at[c], peer) for other, peer in chip_peers]

        def gray_order(i):
            return i + i // 2 - 2 * (i // 3)

        back_merge = Merge(r.sum_s, r.sum_r, r.sum_st)

        def attend_back(i):
            step = gray_order(i)
            blk = xor_of(c, step, nc)
            for at in range(1, nc):
                when(step == at, functools.partial(da_share.arrive, at))
            d_mix = dot_rt(da_all[blk], r.w_p[...]).astype(BF16)
            q_now, k_now, v_now = r.qkv[0, blk], r.qkv[1, blk], r.qkv[2, blk]
            d_q = jnp.zeros((own, chip_w), F32)
            d_k = jnp.zeros((own, chip_w), F32)
            d_v = jnp.zeros((own, chip_w), F32)
            for h in range(heads):
                d_mix_h = d_mix * head_of[h]
                share = r.probs[blk * heads + h]
                d_share = dot_rt(d_mix_h, v_now)
                d_score = share * (d_share - jnp.sum(share * d_share, axis=-1, keepdims=True))
                d_score = d_score.astype(BF16)
                d_q = d_q + dot(d_score, k_now * head_of[h])
                d_k = d_k + dot_lt(d_score, q_now * head_of[h])
                d_v = d_v + dot_lt(share.astype(BF16), d_mix_h)
            all_three = jnp.concatenate([d_q * head_scale, d_k * head_scale, d_v], axis=1).astype(BF16)
            r.d_qkv[blk] = all_three
            back_merge.put(step, blk, dot_rt(all_three, weight_q()).astype(BF16))
            when(i == 1, lambda: sum_2.start(1))
            when(i == 3, lambda: sum_2.start(2))

        loop(nc, attend_back)
        da_share.sent()

        g_q, g_p = w_q, r.w_p
        a_rows = all_rows(r.a_in)
        for lo, hi in column_cuts(q_w):
            value = dot_lt(a_rows, r.d_qkv[:, :, lo:hi].reshape(group, hi - lo))
            g_q[:, :, :, lo:hi] = value.astype(BF16).reshape(nc, 2, rows_d, hi - lo)
        q_core_back = wires.far(g_q.at[:, core_o], r.g_qr, core_dev)
        back_merge.combine()
        g_p[...] = dot_lt(all_rows(r.mixed), all_rows(da_all)).astype(BF16)

        p_core_back = wires.far(own_side(g_p, core_o), r.g_pr, core_dev)
        q_core_back.wait()
        for chip in range(nc):
            g_q[chip, k] = add_low(g_q[chip, k], r.g_qr[chip])
        r.y_got[c] = g_q[c, k]
        yq_far = [wires.far(g_q.at[other, k], r.y_got.at[c], peer) for other, peer in chip_peers]
        wait_all(y1_far)
        sum_1 = Sum(lambda t: y_1.at[t], r.got_1)
        sum_1.start(0)
        p_core_back.wait()
        y_p = add_low(own_side(g_p, k)[...], r.g_pr[...])
        own_side(g_p, k)[...] = y_p

        ones_own = jnp.ones((8, own), BF16)
        ones_all = jnp.ones((8, group), BF16)
        r.d_bias[...] = jnp.zeros((8, width), F32)
        r.d_bias[0:1, :] = dot(ones_own, da_all[c])[0:1]
        r.d_bias[1:2, :] = dot(ones_own, r.dbr[c])[0:1]
        qkv_sums = dot(ones_all, all_rows(r.d_qkv))[0:1]
        r.d_bias[2:3, 0:chip_w] = qkv_sums[:, :chip_w]
        r.d_bias[3:4, 0:chip_w] = qkv_sums[:, 2 * chip_w :]
        ones_ff = dot(ones_all, all_rows(r.d_hid))[0:1]
        r.d_bias[4:5, :] = ones_ff[:, :width]
        for part in range(1, ff_c // width):
            r.d_bias[4 + part : 5 + part, :] = ones_ff[:, part * width : (part + 1) * width]
        bias_far = [wires.far(r.d_bias, r.dzb.at[f], peer) for _, peer in plane_peers]
        r.dzb[f] = r.d_bias[...]

        def branch_out(i):
            step = nc - 1 - i
            blk = xor_of(c, step, nc)
            r.hid[...] = dot_rt(r.act[blk], weight_2())
            r.br_s[blk] = r.hid[...].astype(BF16)
            bias_once = bias_o * jnp.where(step == 0, 1.0, 0.0)

            def gate_rows(g):
                rows = sub_rows(g)
                value = (r.hid[rows, :] + bias_once) * r.cg[blk, rows, :].astype(F32)
                r.sub_gate[pl.ds(blk * n_sub + g, 1), :] = jnp.sum(value, axis=0, keepdims=True)

            loop_rows(gate_rows)

        loop(nc, branch_out)
        sum_1.start(1)

        back_merge.finish()

        def back_norm1(g):
            rows = sub_rows(g)
            d_a = back_merge.rows(rows)
            normal, scale = ln_parts(r.xg[c, rows, :].astype(F32))
            value = r.d_after[rows, :] + ln_back(normal, scale, d_a * (1.0 + own_row(1, g)))
            x_grad[rows, :] = value.astype(BF16)
            at = pl.ds(g, 1)
            r.sub[0, at, :] = jnp.sum(d_a, axis=0, keepdims=True)
            r.sub[1, at, :] = jnp.sum(d_a * normal, axis=0, keepdims=True)

        loop_rows(back_norm1)
        hot_turned = own_hot.astype(F32).T.astype(BF16)
        for kind in range(6):
            if kind == 5:
                value = dot3(hot_all.astype(F32).T.astype(BF16), r.sub_gate[...])
            else:
                value = dot3(hot_turned, r.sub[kind])
            r.d_part[:, :, width * kind : width * (kind + 1)] = value.reshape(2, half, width)
        d_core = wires.far(r.d_part.at[core_o], r.d_core, core_dev)
        d_core.wait()
        r.d_core[...] = r.d_core[...] + r.d_part[k]
        for plane in range(nf):
            r.d_cut[plane] = r.d_core[:, ada_w * plane : ada_w * (plane + 1)]
        small = []
        for other, peer in plane_peers:
            small.append(wires.far(r.d_cut.at[other], r.dz.at[f], peer))
        r.dz[f] = r.d_cut[f]
        wait_all(yq_far)
        q_line.sent()
        y_q = r.q_z
        for plane in range(nf):
            row = []
            for i in range(3):
                kind, chip = (3 * plane + i) // nc, (3 * plane + i) % nc
                row.append(r.y_got[chip, :, chip_w * kind : chip_w * (kind + 1)])
            row.append(own_side(g_p, k)[:, plane * cols_f : (plane + 1) * cols_f])
            y_q[plane] = jnp.concatenate(row, axis=1)
        sum_q = Sum(lambda t: y_q.at[t], r.got_q)
        sum_q.start(0)
        wait_all(bias_far)
        wait_all(small)
        value, value_b = r.dz[0], r.dzb[0]
        for plane in range(1, nf):
            value = value + r.dz[plane]
            value_b = value_b + r.dzb[plane]
        m_chip[c] = value
        r.d_bsum[...] = value_b
        b_swap = wires.far(r.d_bsum, r.d_coreb, core_dev)
        small = [wires.far(m_chip.at[c], m_chip.at[c], peer) for _, peer in chip_peers]
        sum_q.start(1)
        b_swap.wait()
        r.d_chipb[c] = r.d_bsum[...] + r.d_coreb[...]
        for _, peer in chip_peers:
            small.append(wires.far(r.d_chipb.at[c], r.d_chipb.at[c], peer))
        br_merge.launch()
        sum_1.start(2)

        wait_all(small)
        value = m_chip[0]
        for chip in range(1, nc):
            value = value + m_chip[chip]
        r.d_tot[k] = value
        d_swap = wires.far(r.d_tot.at[k], r.d_tot.at[k], core_dev)
        d_swap.wait()
        d_cols = r.d_tot[...].reshape(n_rows, ada_w)
        silu_turned = silu_in[...].astype(F32).T.astype(BF16)
        o_bada[...] = jnp.sum(d_cols, axis=0)
        value, total = d_cols, None
        for _ in range(3):
            term = value.astype(BF16)
            value = value - term.astype(F32)
            part = dot_rt(term, r.ada[...])
            total = part if total is None else total + part
        r.c_part[f] = total
        c_far = [wires.far(r.c_part.at[f], r.c_part.at[f], peer) for _, peer in plane_peers]
        sum_q.start(2)
        for lo, hi in column_cuts(ada_w):
            o_ada[:, lo:hi] = dot3(silu_turned, d_cols[:, lo:hi])
        sum_2.finish(r.all_2.at[k])
        o2_swap = wires.far(r.all_2.at[k], r.all_2.at[k], core_dev)
        br_merge.combine()
        wait_all(c_far)
        value = r.c_part[0]
        for plane in range(1, nf):
            value = value + r.c_part[plane]
        r.c_all[c, k] = value
        c_chip = [wires.far(r.c_all.at[c, k], r.c_all.at[c, k], peer) for _, peer in chip_peers]


        br_merge.finish()

        def finish_out(g):
            rows = sub_rows(g)
            branch = br_merge.rows(rows) + bias_o
            out[rows, :] = (r.after[rows, :] + own_row(5, g) * branch).astype(BF16)

        loop_rows(finish_out)
        wait_all(c_chip)
        c_swap = wires.far(r.c_all.at[:, k], r.c_all.at[:, k], core_dev)
        o2_swap.wait()

        def own_columns(lo):
            def body():
                o_2[...] = r.all_2[:, :, lo : lo + ff_d].reshape(cols_f, ff_d)

            return body

        when(k == 0, own_columns(0))
        when(k == 1, own_columns(ff_d))
        own_sums = r.d_chipb[0]
        for chip in range(1, nc):
            own_sums = own_sums + r.d_chipb[chip]
        for plane in range(nf):

            def bias_columns(plane=plane):
                at = plane * cols_f
                o_bp[...] = own_sums[0, at : at + cols_f]
                o_b2[...] = own_sums[1, at : at + cols_f]
                kind, chip = 2 * plane // nc, 2 * plane % nc
                pieces = [r.d_chipb[chip + i, 2 + kind : 3 + kind, 0:chip_w] for i in range(2)]
                o_bqv[...] = jnp.concatenate(pieces, axis=1)[0]
                o_b1[...] = r.d_chipb[plane, 4, :]

            when(f == plane, bias_columns)
        c_swap.wait()
        d_silu = jnp.concatenate([r.c_all[f, 0], r.c_all[f, 1]], axis=1)
        cond_now = cond_in[...]
        gate = 1.0 / (1.0 + jnp.exp(-cond_now))
        o_cond[...] = d_silu * (gate * (1.0 + cond_now * (1.0 - gate)))
        f2_line.sent()
        sum_1.finish(o_1)
        sum_q.finish(r.all_q)
        o_q[...] = r.all_q[:, :q_w]
        o_p[...] = r.all_q[:, q_w:]
        assert wires.remote_count <= n_sem and wires.local_count <= 32

    return pl.pallas_call(
        kernel,
        out_shape=outs,
        in_specs=[ANYWHERE] * 2 + [ON_CHIP] * 4 + [ANYWHERE] * 5,
        out_specs=tuple([ON_CHIP] * len(outs)),
        scratch_shapes=list(scratch.values()),
        compiler_params=pltpu.CompilerParams(
            collective_id=0, has_side_effects=True, vmem_limit_bytes=63 * 2**20
        ),
        name="block",
    )(x, cot, ids, bias, silu_part, cond_own, w_ada, wq, wp, w1, w2)


def fits_block(n_dp, nf, width, ff, own, micro):
    nc = n_dp // 2
    return (
        nc == nf
        and nf == 4
        and width % (128 * nf) == 128
        and ff == 4 * width
        and (width // n_dp) % 16 == 0
        and (width // nc) % HEAD_DIM == 0
        and own % (2 * SUB) == 0
    )


def per_device(
    n_dp, nf, patches, cotangent, conditioning, frame_of_slot, clip_of_slot,
    w_ada, b_ada, w_qkv, b_qv, w_proj, b_proj, w_fc1, b_fc1, w_fc2, b_fc2,
):
    nc = n_dp // 2
    sizes = (nc, nf)
    micro, block, width = patches.shape
    own = micro * block
    clips = conditioning.shape[1]
    rows_d = width // n_dp
    cols_f = width // nf
    ff = w_fc1.shape[1] * nf
    ff_d = ff // n_dp
    chip_w = width // nc
    piece_q = math.gcd(3 * width // nf, chip_w)
    piece_1 = math.gcd(ff // nf, ff_d)
    dims = types.SimpleNamespace(
        nc=nc,
        nf=nf,
        per_q=3 * width // nf // piece_q,
        per_1=ff // nf // piece_1,
        chip_q=chip_w // piece_q,
        chip_1=ff // nc // piece_1,
    )
    dp = lax.axis_index("dp")
    f = lax.axis_index("fsdp")
    c, k = dp // 2, dp % 2

    q_send = w_qkv.reshape(rows_d, dims.per_q, piece_q).transpose(1, 0, 2)
    f1_send = w_fc1.reshape(rows_d, dims.per_1, piece_1).transpose(1, 0, 2)
    f2_send = w_fc2.T
    cond = conditioning.reshape(micro * clips, width)
    silu_cond = jax.nn.silu(cond)
    silu_low = silu_cond.astype(BF16)
    ada_w = w_ada.shape[1]
    silu_part = lax.dynamic_slice_in_dim(silu_low, dp * rows_d, rows_d, 1)
    mod_part = dot(silu_part, w_ada) + jnp.where(dp == 0, b_ada.astype(F32), 0.0)[None]
    mod_send = mod_part.reshape(-1, 2, ada_w // 2).transpose(1, 0, 2)
    cut = [0, 2 * cols_f, 3 * cols_f, 3 * cols_f + ff // nf, 4 * cols_f + ff // nf]
    cond_own = lax.dynamic_slice_in_dim(cond, f * cols_f, cols_f, 1)

    def ada_outputs(d_cols):
        grad_w_ada = precise(silu_part.astype(F32), d_cols, ((0,), (0,)))
        d_silu_part = precise(d_cols, w_ada.astype(F32), ((1,), (1,)))
        d_silu = cond_kernel(dims, d_silu_part).transpose(1, 0, 2).reshape(micro * clips, width)
        d_silu_own = lax.dynamic_slice_in_dim(d_silu, f * cols_f, cols_f, 1)
        _, silu_back = jax.vjp(jax.nn.silu, cond_own)
        cond_grad = silu_back(d_silu_own)[0].reshape(micro, clips, cols_f)
        return cond_grad, grad_w_ada, jnp.sum(d_cols, axis=0)

    if fits_block(n_dp, nf, width, ff, own, micro):
        bias_send = jnp.concatenate([b_qv, b_proj, b_fc1, b_fc2, b_ada]).astype(F32)[None]
        order = jnp.arange(micro, dtype=jnp.int32)[:, None]
        pair_rows = jnp.stack(
            [(frame_of_slot + order * 65536).reshape(own), (clip_of_slot + order * clips).reshape(own)]
        )
        id_rows = jnp.concatenate([pair_rows.astype(F32), jnp.zeros((6, own), F32)])
        (
            output, input_grad, cond_grad, grad_ada, grad_b_ada, grad_qkv, grad_b_qv,
            grad_proj, grad_b_proj, grad_fc1, grad_b_fc1, grad_fc2, grad_b_fc2,
        ) = block_kernel(
            dims, patches.reshape(own, width), cotangent.reshape(own, width), id_rows, bias_send,
            silu_part, cond_own, w_ada, w_qkv, w_proj, w_fc1, w_fc2.T,
        )
        return (
            output.reshape(patches.shape),
            input_grad.reshape(patches.shape),
            cond_grad.reshape(micro, clips, cols_f),
            grad_ada,
            grad_b_ada,
            grad_qkv,
            grad_b_qv,
            grad_proj,
            grad_b_proj,
            grad_fc1,
            grad_b_fc1,
            grad_fc2.T,
            grad_b_fc2,
        )

    ids = jnp.stack([frame_of_slot.reshape(own), clip_of_slot.reshape(own)])
    ids = jnp.concatenate([ids, jnp.zeros((6, own), jnp.int32)])
    bias_send = jnp.concatenate([b_qv, b_proj, b_fc1, b_fc2]).astype(F32)[None]

    (x_all, c_all, ids_all, bias_all, mod_all, q_chip, f1_chip, p_chip, f2_chip, _, _) = start_kernel(
        dims, patches.reshape(own, width), cotangent.reshape(own, width), ids, bias_send, mod_send,
        q_send, f1_send, w_proj, f2_send,
    )
    group = nc * own
    modulation = mod_all.transpose(2, 0, 1, 3).reshape(micro * clips, 6 * width)
    q_parts = [
        q_chip[i].reshape(nc, 2, dims.chip_q, rows_d, piece_q).transpose(0, 1, 3, 2, 4).reshape(width, chip_w)
        for i in range(3)
    ]
    w1 = f1_chip.transpose(1, 2, 3, 0, 4).reshape(width, ff // nc)
    wp = p_chip.transpose(0, 2, 1, 3).reshape(chip_w, width)
    w2t = f2_chip.reshape(2, width, ff_d).transpose(1, 0, 2).reshape(width, 2 * ff_d)
    b_parts = [bias_all[:, 0, a:b].reshape(-1) for a, b in zip(cut[:-1], cut[1:])]
    bq = lax.dynamic_slice_in_dim(b_parts[0], c * chip_w, chip_w, 0)
    bv = lax.dynamic_slice_in_dim(b_parts[0], width + c * chip_w, chip_w, 0)
    b1 = lax.dynamic_slice_in_dim(b_parts[2], c * (ff // nc), ff // nc, 0)

    def hot_of(clip_ids):
        count = clip_ids.shape[0]
        row = (jnp.arange(count, dtype=jnp.int32) // block) % micro * clips + clip_ids
        return (row[:, None] == jnp.arange(micro * clips, dtype=jnp.int32)[None]).astype(F32)

    hot_group = hot_of(ids_all[:, 1].reshape(group))
    hot_own = hot_of(clip_of_slot.reshape(own))
    mod_group = precise(hot_group, modulation, ((1,), (0,)))
    mod_own = precise(hot_own, modulation, ((1,), (0,)))
    shift1, scale1 = mod_group[:, :width], mod_group[:, width : 2 * width]
    gate1 = mod_own[:, 2 * width : 3 * width]
    shift2, scale2 = mod_own[:, 3 * width : 4 * width], mod_own[:, 4 * width : 5 * width]
    gate2_group, gate2 = mod_group[:, 5 * width :], mod_own[:, 5 * width :]

    x_group = x_all.reshape(group, width).astype(F32)
    norm1, rstd1 = ln_parts(x_group)
    a_in = (norm1 * (1.0 + scale1) + shift1).astype(BF16)
    zero = jnp.zeros_like(bq)
    q, kk, v = [
        (dot(a_in, w) + b[None]).astype(BF16) for w, b in zip(q_parts, (bq, zero, bv))
    ]
    heads = chip_w // HEAD_DIM
    blocks = group // block
    q4, k4, v4 = [t.reshape(blocks, block, heads, HEAD_DIM) for t in (q, kk, v)]
    frames = ids_all[:, 0].reshape(blocks, block)
    same = (frames[:, :, None] == frames[:, None, :])[:, None]
    scores = jnp.einsum("bqhd,bkhd->bhqk", q4, k4, preferred_element_type=F32) * HEAD_DIM ** (-0.5)
    scores = jnp.where(same, scores, NEG_FILL)
    top = jnp.max(scores, axis=-1, keepdims=True)
    raised = jnp.exp(scores - top)
    probs = raised / jnp.sum(raised, axis=-1, keepdims=True)
    probs_low = probs.astype(BF16)
    mixed = jnp.einsum("bhqk,bkhd->bqhd", probs_low, v4, preferred_element_type=F32)
    mixed = mixed.reshape(group, chip_w).astype(BF16)
    attn_part = dot(mixed, wp)
    (attn_got,) = exchange(
        "attn_sum", 3, sizes, [(CHIP, SPREAD, attn_part.astype(BF16).reshape(nc, own, width))]
    )
    attn = jnp.sum(attn_got.astype(F32), axis=0) + b_parts[1][None]
    x_own = patches.reshape(own, width).astype(F32)
    after = x_own + gate1 * attn
    norm2, rstd2 = ln_parts(after)
    m_own = (norm2 * (1.0 + scale2) + shift2).astype(BF16)
    (m_all,) = exchange("m_gather", 4, sizes, [(CHIP, GATHER, m_own)])
    m_in = m_all.reshape(group, width)

    hidden = dot(m_in, w1) + b1[None]
    act, slope = gelu_both(hidden)
    act = act.astype(BF16)
    branch_part = dot_rt(act, w2t)
    cot_group = c_all.reshape(group, width).astype(F32)
    d_branch = (gate2_group * cot_group).astype(BF16)
    grad_2t = dot_lt(d_branch, act)
    d_hidden = (dot(d_branch, w2t) * slope).astype(BF16)
    grad_1 = dot_lt(m_in, d_hidden)
    d_m_part = dot_rt(d_hidden, w1)
    branch_got, d_m_got = exchange(
        "ff_sum",
        5,
        sizes,
        [
            (CHIP, SPREAD, d_m_part.astype(BF16).reshape(nc, own, width)),
            (CHIP, SPREAD, branch_part.astype(BF16).reshape(nc, own, width)),
        ],
    )[::-1]
    branch = jnp.sum(branch_got.astype(F32), axis=0) + b_parts[3][None]
    output = (after + gate2 * branch).astype(BF16)
    d_m = jnp.sum(d_m_got.astype(F32), axis=0)
    cot_own = cotangent.reshape(own, width).astype(F32)
    d_after = cot_own + ln_back(norm2, rstd2, d_m * (1.0 + scale2))
    d_attn = (gate1 * d_after).astype(BF16)
    (d_attn_all,) = exchange("d_attn_gather", 6, sizes, [(CHIP, GATHER, d_attn)])
    d_attn_group = d_attn_all.reshape(group, width)
    grad_p = dot_lt(mixed, d_attn_group)
    d_mix = dot_rt(d_attn_group, wp).astype(BF16).reshape(blocks, block, heads, HEAD_DIM)
    d_probs = jnp.einsum("bqhd,bkhd->bhqk", d_mix, v4, preferred_element_type=F32)
    d_scores = probs * (d_probs - jnp.sum(probs * d_probs, axis=-1, keepdims=True))
    d_scores = d_scores.astype(BF16)
    dq = jnp.einsum("bhqk,bkhd->bqhd", d_scores, k4, preferred_element_type=F32) * HEAD_DIM ** (-0.5)
    dk = jnp.einsum("bhqk,bqhd->bkhd", d_scores, q4, preferred_element_type=F32) * HEAD_DIM ** (-0.5)
    dv = jnp.einsum("bhqk,bqhd->bkhd", probs_low, d_mix, preferred_element_type=F32)
    dqkv = [t.reshape(group, chip_w).astype(BF16) for t in (dq, dk, dv)]
    d_a_part = sum(dot_rt(t, w) for t, w in zip(dqkv, q_parts))
    grad_q = jnp.stack([dot_lt(a_in, t) for t in dqkv])
    (d_a_got,) = exchange(
        "d_a_sum", 7, sizes, [(CHIP, SPREAD, d_a_part.astype(BF16).reshape(nc, own, width))]
    )
    d_a = jnp.sum(d_a_got.astype(F32), axis=0)
    norm1_own, rstd1_own = ln_parts(x_own)
    scale1_own = mod_own[:, width : 2 * width]
    input_grad = (d_after + ln_back(norm1_own, rstd1_own, d_a * (1.0 + scale1_own))).astype(BF16)

    g_q = grad_q.reshape(3, nc, 2, rows_d, dims.chip_q, piece_q).transpose(2, 1, 0, 4, 3, 5)
    g_1 = grad_1.reshape(nc, 2, rows_d, dims.chip_1, piece_1).transpose(1, 0, 3, 2, 4)
    g_p = grad_p.reshape(2, rows_d, nf, cols_f).transpose(0, 2, 1, 3)
    g_2 = grad_2t.reshape(nf, cols_f, 2, ff_d).transpose(2, 0, 1, 3)
    got = exchange("grad_core", 8, sizes, [(CORE, SPREAD, g.astype(BF16)) for g in (g_q, g_1, g_p, g_2)])
    s_q, s_1, s_p, s_2 = [jnp.sum(g.astype(F32), axis=0).astype(BF16) for g in got]
    r_q, r_1 = exchange("grad_chip", 9, sizes, [(CHIP, SPREAD, s_q), (CHIP, SPREAD, s_1)])
    z_q = r_q.transpose(1, 0, 2, 3, 4).reshape(nf, dims.per_q, rows_d, piece_q)
    z_1 = r_1.reshape(nf, dims.per_1, rows_d, piece_1)
    got = exchange("grad_plane", 10, sizes, [(PLANE, SPREAD, g) for g in (z_q, z_1, s_p, s_2)])
    o_q, o_1, o_p, o_2 = [jnp.sum(g.astype(F32), axis=0) for g in got]
    grad_w_qkv = o_q.transpose(1, 0, 2).reshape(rows_d, 3 * width // nf)
    grad_w_fc1 = o_1.transpose(1, 0, 2).reshape(rows_d, ff // nf)
    grad_w_fc2 = o_2.T

    d_token = jnp.concatenate(
        [d_a, d_a * norm1_own, d_after * attn, d_m, d_m * norm2, cot_own * branch], axis=1
    )
    d_mod = precise(hot_own, d_token, ((0,), (0,)))
    d_branch_own = (gate2 * cot_own).astype(BF16).astype(F32)

    def columns(value):
        return jnp.sum(value.astype(F32), axis=0)

    def spread(value, count):
        return lax.dynamic_update_slice_in_dim(
            jnp.zeros((count,), F32), value, c * value.shape[0], 0
        )

    g_bqv = jnp.concatenate([spread(columns(dqkv[0]), width), spread(columns(dqkv[2]), width)])
    g_b1 = spread(columns(d_hidden), ff)
    bias_terms = jnp.concatenate(
        [
            g_bqv.reshape(nf, -1),
            columns(d_attn).reshape(nf, -1),
            g_b1.reshape(nf, -1),
            columns(d_branch_own).reshape(nf, -1),
        ],
        axis=1,
    )
    n_bias = bias_terms.shape[1]
    bias_rows = -(-n_bias // ada_w)
    bias_terms = jnp.pad(bias_terms, ((0, 0), (0, bias_rows * ada_w - n_bias)))
    terms = jnp.concatenate(
        [d_mod.reshape(micro * clips, nf, ada_w).transpose(1, 0, 2), bias_terms.reshape(nf, bias_rows, ada_w)],
        axis=1,
    )
    pad_rows = -terms.shape[1] % 8
    terms = jnp.pad(terms, ((0, 0), (0, pad_rows), (0, 0)))
    terms = terms.reshape(nf, -1, 2, ada_w // 2).transpose(0, 2, 1, 3)
    total = sum_small_kernel(dims, terms).transpose(1, 0, 2).reshape(-1, ada_w)
    d_cols = total[: micro * clips]
    bias_sums = total[micro * clips : micro * clips + bias_rows].reshape(-1)[:n_bias]
    g_parts = [bias_sums[a:b] for a, b in zip(cut[:-1], cut[1:])]
    cond_grad, grad_w_ada, grad_b_ada = ada_outputs(d_cols)
    return (
        output.reshape(patches.shape),
        input_grad.reshape(patches.shape),
        cond_grad,
        grad_w_ada,
        grad_b_ada,
        grad_w_qkv,
        g_parts[0],
        o_p,
        g_parts[1],
        grad_w_fc1,
        g_parts[2],
        grad_w_fc2,
        g_parts[3],
    )


def solution(mesh):
    tokens = P(None, ("dp", "fsdp"), None)
    ids = P(None, ("dp", "fsdp"))
    both, cols = P("dp", "fsdp"), P("fsdp")
    in_specs = (tokens, tokens, P(), ids, ids) + (both, cols) * 5
    out_specs = (tokens, tokens, P(None, None, "fsdp")) + (both, cols) * 5
    return jax.shard_map(
        functools.partial(per_device, mesh.shape["dp"], mesh.shape["fsdp"]),
        mesh=mesh,
        in_specs=in_specs,
        out_specs=out_specs,
        check_vma=False,
    )
```

```python
import functools
import math
import types

import jax
import jax.numpy as jnp
from jax import lax
from jax.experimental import pallas as pl
from jax.experimental.pallas import tpu as pltpu
from jax.sharding import PartitionSpec as P

HEAD_DIM = 72
EPS = 1e-06
GELU_C = math.sqrt(2.0 / math.pi)
PRECISE = lax.Precision.HIGHEST
NEG_FILL = -1e30
SUB = 16
CORE, CHIP, PLANE, ALL = range(4)
GATHER, SPREAD = range(2)
MESH_ID = pl.DeviceIdType.MESH
F32 = jnp.float32
BF16 = jnp.bfloat16


def xor_of(index, step, size):
    result, bit = 0, 1
    while bit < size:
        mine = (index // bit) % 2
        result = result + ((mine + (step // bit) % 2) % 2) * bit
        bit *= 2
    return result


class Place:
    def __init__(self, n_chip, n_plane):
        self.n = {CORE: 2, CHIP: n_chip, PLANE: n_plane, ALL: 2 * n_chip}
        self.dp = lax.axis_index("dp")
        self.f = lax.axis_index("fsdp")
        self.c = self.dp // 2
        self.k = self.dp % 2

    def index(self, axis):
        return {CORE: self.k, CHIP: self.c, PLANE: self.f, ALL: self.dp}[axis]

    def peer(self, axis, step):
        other = xor_of(self.index(axis), step, self.n[axis])
        if axis == CORE:
            return other, (self.c * 2 + other, self.f)
        if axis == CHIP:
            return other, (other * 2 + self.k, self.f)
        if axis == PLANE:
            return other, (self.dp, other)
        return other, (other, self.f)


def greet(place, axes):
    barrier = pltpu.get_barrier_semaphore()
    count = 0
    for axis in axes:
        for step in range(1, place.n[axis]):
            pl.semaphore_signal(
                barrier, inc=1, device_id=place.peer(axis, step)[1], device_id_type=MESH_ID
            )
            count += 1
    pl.semaphore_wait(barrier, count)


class Wires:
    def __init__(self, send, recv, local):
        self.send, self.recv, self.local = send, recv, local
        self.remote_count = 0
        self.local_count = 0

    def far(self, src, dst, device):
        at = self.remote_count
        self.remote_count += 1
        copy = pltpu.make_async_remote_copy(
            src_ref=src,
            dst_ref=dst,
            send_sem=self.send.at[at],
            recv_sem=self.recv.at[at],
            device_id=device,
            device_id_type=MESH_ID,
        )
        copy.start()
        return copy

    def near(self, src, dst):
        at = self.local_count
        self.local_count += 1
        copy = pltpu.make_async_copy(src, dst, self.local.at[at])
        copy.start()
        return copy


def wait_all(copies):
    for copy in copies:
        copy.wait()


ANYWHERE = pl.BlockSpec(memory_space=pl.ANY)
ON_CHIP = pl.BlockSpec(memory_space=pltpu.VMEM)


def exchange(name, collective_id, sizes, items):
    n_chip, n_plane = sizes
    n_of = {CORE: 2, CHIP: n_chip, PLANE: n_plane, ALL: 2 * n_chip}
    axes = sorted({item[0] for item in items})
    outs = []
    n_far = 0
    for axis, kind, array in items:
        n_far += n_of[axis] - 1
        shape = array.shape if kind == SPREAD else (n_of[axis],) + array.shape
        outs.append(jax.ShapeDtypeStruct(shape, array.dtype))

    def kernel(*refs):
        ins = refs[: len(items)]
        results = refs[len(items) : 2 * len(items)]
        place = Place(n_chip, n_plane)
        wires = Wires(*refs[2 * len(items) :])
        greet(place, axes)
        copies = []
        for (axis, kind, _), src, dst in zip(items, ins, results):
            mine = place.index(axis)
            for step in range(1, n_of[axis]):
                other, device = place.peer(axis, step)
                piece = src if kind == GATHER else src.at[other]
                copies.append(wires.far(piece, dst.at[mine], device))
        for (axis, kind, _), src, dst in zip(items, ins, results):
            mine = place.index(axis)
            copies.append(wires.near(src if kind == GATHER else src.at[mine], dst.at[mine]))
        wait_all(copies)

    return pl.pallas_call(
        kernel,
        out_shape=tuple(outs),
        in_specs=[ANYWHERE] * len(items),
        out_specs=tuple([ANYWHERE] * len(items)),
        scratch_shapes=[
            pltpu.SemaphoreType.DMA((n_far,)),
            pltpu.SemaphoreType.DMA((n_far,)),
            pltpu.SemaphoreType.DMA((len(items),)),
        ],
        compiler_params=pltpu.CompilerParams(collective_id=collective_id, has_side_effects=True),
        name=name,
    )(*[item[2] for item in items])


def start_kernel(dims, x, cot, ids, bias, mod, wq, w1, wp, w2):
    nc, nf = dims.nc, dims.nf
    per_q, per_1 = dims.per_q, dims.per_1
    chip_q, chip_1 = dims.chip_q, dims.chip_1
    part_q = nc * chip_q
    rows, half = mod.shape[1], mod.shape[2]
    n_far = 5 * (nf - 1) + 3 * (nc - 1) + 4 * (nc - 1) + 4 + 1 + (nc - 1) + (nf - 1) + 1
    outs = (
        jax.ShapeDtypeStruct((nc,) + x.shape, x.dtype),
        jax.ShapeDtypeStruct((nc,) + cot.shape, cot.dtype),
        jax.ShapeDtypeStruct((nc,) + ids.shape, ids.dtype),
        jax.ShapeDtypeStruct((nf,) + bias.shape, bias.dtype),
        jax.ShapeDtypeStruct((nf, 2, rows, half), F32),
        jax.ShapeDtypeStruct((3, nc, 2, chip_q) + wq.shape[1:], BF16),
        jax.ShapeDtypeStruct((chip_1, nc, 2) + w1.shape[1:], BF16),
        jax.ShapeDtypeStruct((2, nf) + wp.shape, BF16),
        jax.ShapeDtypeStruct((2, nf) + w2.shape, BF16),
        jax.ShapeDtypeStruct((nf * per_q,) + wq.shape[1:], BF16),
        jax.ShapeDtypeStruct((nf * per_1,) + w1.shape[1:], BF16),
    )

    def kernel(
        x_in, c_in, i_in, b_in, m_in, q_in, f1_in, p_in, f2_in,
        x_all, c_all, i_all, b_all, m_all, q_chip, f1_chip, p_chip, f2_chip, q_rows, f1_rows,
        m_core, m_sum, m_chip, send, recv, local,
    ):
        place = Place(nc, nf)
        wires = Wires(send, recv, local)
        c, k, f = place.c, place.k, place.f
        greet(place, (CORE, CHIP, PLANE))
        core_other, core_peer = place.peer(CORE, 1)
        chip_peers = [place.peer(CHIP, step) for step in range(1, nc)]
        plane_peers = [place.peer(PLANE, step) for step in range(1, nf)]

        m_first = wires.far(m_in.at[core_other], m_core, core_peer)
        q_got, f1_got, p_got, f2_got, small = [], [], [], [], []
        for _, peer in plane_peers:
            q_got.append(wires.far(q_in, q_rows.at[pl.ds(f * per_q, per_q)], peer))
            small.append(wires.far(b_in, b_all.at[f], peer))
        q_got.append(wires.near(q_in, q_rows.at[pl.ds(f * per_q, per_q)]))
        small.append(wires.near(b_in, b_all.at[f]))
        for _, peer in chip_peers:
            small.append(wires.far(i_in, i_all.at[c], peer))
            small.append(wires.far(x_in, x_all.at[c], peer))
        m_first.wait()
        m_sum[...] = m_in[k] + m_core[...]
        m_chip[c] = m_sum[...]
        m_second = [wires.far(m_sum, m_chip.at[c], peer) for _, peer in chip_peers]
        for _, peer in plane_peers:
            p_got.append(wires.far(p_in, p_chip.at[k, f], peer))
        for _, peer in plane_peers:
            f1_got.append(wires.far(f1_in, f1_rows.at[pl.ds(f * per_1, per_1)], peer))
        for _, peer in plane_peers:
            f2_got.append(wires.far(f2_in, f2_chip.at[k, f], peer))
        p_got.append(wires.near(p_in, p_chip.at[k, f]))
        f1_got.append(wires.near(f1_in, f1_rows.at[pl.ds(f * per_1, per_1)]))
        f2_got.append(wires.near(f2_in, f2_chip.at[k, f]))
        small.append(wires.near(i_in, i_all.at[c]))
        small.append(wires.near(x_in, x_all.at[c]))
        for _, peer in chip_peers:
            small.append(wires.far(c_in, c_all.at[c], peer))
        small.append(wires.near(c_in, c_all.at[c]))
        wait_all(m_second)
        total = m_chip[0]
        for other in range(1, nc):
            total = total + m_chip[other]
        m_all[f, k] = total
        wait_all([wires.far(m_all.at[f, k], m_all.at[f, k], peer) for _, peer in plane_peers])
        m_last = wires.far(m_all.at[:, k], m_all.at[:, k], core_peer)

        wait_all(q_got)
        q_moved = []
        for kind in range(3):
            for other, peer in chip_peers:
                q_moved.append(
                    wires.far(
                        q_rows.at[pl.ds(kind * part_q + other * chip_q, chip_q)],
                        q_chip.at[kind, c, k],
                        peer,
                    )
                )
            q_moved.append(
                wires.near(
                    q_rows.at[pl.ds(kind * part_q + c * chip_q, chip_q)], q_chip.at[kind, c, k]
                )
            )
        wait_all(p_got)
        last = [m_last, wires.far(p_chip.at[k], p_chip.at[k], core_peer)]
        wait_all(q_moved)
        last.append(wires.far(q_chip.at[:, :, k], q_chip.at[:, :, k], core_peer))
        wait_all(f1_got)
        f1_moved = []
        for other, peer in chip_peers:
            f1_moved.append(
                wires.far(f1_rows.at[pl.ds(other * chip_1, chip_1)], f1_chip.at[:, c, k], peer)
            )
        f1_moved.append(
            wires.near(f1_rows.at[pl.ds(c * chip_1, chip_1)], f1_chip.at[:, c, k])
        )
        wait_all(f2_got)
        last.append(wires.far(f2_chip.at[k], f2_chip.at[k], core_peer))
        wait_all(f1_moved)
        last.append(wires.far(f1_chip.at[:, :, k], f1_chip.at[:, :, k], core_peer))
        wait_all(small)
        wait_all(last)

    return pl.pallas_call(
        kernel,
        out_shape=outs,
        in_specs=[ANYWHERE] * 4 + [ON_CHIP] + [ANYWHERE] * 4,
        out_specs=tuple([ANYWHERE] * 4 + [ON_CHIP] + [ANYWHERE] * 6),
        scratch_shapes=[
            pltpu.VMEM((rows, half), F32),
            pltpu.VMEM((rows, half), F32),
            pltpu.VMEM((nc, rows, half), F32),
            pltpu.SemaphoreType.DMA((n_far,)),
            pltpu.SemaphoreType.DMA((n_far,)),
            pltpu.SemaphoreType.DMA((12,)),
        ],
        compiler_params=pltpu.CompilerParams(collective_id=0, has_side_effects=True),
        name="start",
    )(x, cot, ids, bias, mod, wq, w1, wp, w2)


def sum_small_kernel(dims, terms):
    nc, nf = dims.nc, dims.nf
    _, _, rows, half = terms.shape
    n_far = (nf - 1) + 1 + (nc - 1) + 1

    def kernel(t_in, total, z_got, both, core_got, chip_got, send, recv, local):
        place = Place(nc, nf)
        wires = Wires(send, recv, local)
        c, k, f = place.c, place.k, place.f
        greet(place, (CORE, CHIP, PLANE))
        core_other, core_peer = place.peer(CORE, 1)
        copies = []
        for step in range(1, nf):
            other, peer = place.peer(PLANE, step)
            copies.append(wires.far(t_in.at[other], z_got.at[f], peer))
        z_got[f] = t_in[f]
        wait_all(copies)
        value = z_got[0]
        for other in range(1, nf):
            value = value + z_got[other]
        both[...] = value
        wires.far(both.at[core_other], core_got, core_peer).wait()
        chip_got[c] = both[k] + core_got[...]
        copies = []
        for step in range(1, nc):
            _, peer = place.peer(CHIP, step)
            copies.append(wires.far(chip_got.at[c], chip_got.at[c], peer))
        wait_all(copies)
        value = chip_got[0]
        for other in range(1, nc):
            value = value + chip_got[other]
        total[k] = value
        wires.far(total.at[k], total.at[k], core_peer).wait()

    return pl.pallas_call(
        kernel,
        out_shape=jax.ShapeDtypeStruct((2, rows, half), F32),
        in_specs=[ON_CHIP],
        out_specs=ON_CHIP,
        scratch_shapes=[
            pltpu.VMEM((nf, 2, rows, half), F32),
            pltpu.VMEM((2, rows, half), F32),
            pltpu.VMEM((rows, half), F32),
            pltpu.VMEM((nc, rows, half), F32),
            pltpu.SemaphoreType.DMA((n_far,)),
            pltpu.SemaphoreType.DMA((n_far,)),
            pltpu.SemaphoreType.DMA((1,)),
        ],
        compiler_params=pltpu.CompilerParams(collective_id=1, has_side_effects=True),
        name="sum_small",
    )(terms)


def cond_kernel(dims, part):
    nc, nf = dims.nc, dims.nf
    nd = 2 * nc
    rows, width = part.shape
    n_far = (nf - 1) + (nd - 1)

    def kernel(p_in, out, got, send, recv, local):
        place = Place(nc, nf)
        wires = Wires(send, recv, local)
        greet(place, (PLANE, ALL))
        copies = []
        for step in range(1, nf):
            copies.append(wires.far(p_in, got.at[place.f], place.peer(PLANE, step)[1]))
        got[place.f] = p_in[...]
        wait_all(copies)
        value = got[0]
        for other in range(1, nf):
            value = value + got[other]
        out[place.dp] = value
        copies = []
        for step in range(1, nd):
            copies.append(
                wires.far(out.at[place.dp], out.at[place.dp], place.peer(ALL, step)[1])
            )
        wait_all(copies)

    return pl.pallas_call(
        kernel,
        out_shape=jax.ShapeDtypeStruct((nd, rows, width), F32),
        in_specs=[ON_CHIP],
        out_specs=ON_CHIP,
        scratch_shapes=[
            pltpu.VMEM((nf, rows, width), F32),
            pltpu.SemaphoreType.DMA((n_far,)),
            pltpu.SemaphoreType.DMA((n_far,)),
            pltpu.SemaphoreType.DMA((1,)),
        ],
        compiler_params=pltpu.CompilerParams(collective_id=2, has_side_effects=True),
        name="cond_sum",
    )(part)


def dot(left, right):
    return jnp.dot(left, right, preferred_element_type=F32)


def dot_rt(left, right):
    return lax.dot_general(left, right, (((1,), (1,)), ((), ())), preferred_element_type=F32)


def dot_lt(left, right):
    return lax.dot_general(left, right, (((0,), (0,)), ((), ())), preferred_element_type=F32)


def precise(left, right, dims):
    return lax.dot_general(
        left, right, (dims, ((), ())), precision=PRECISE, preferred_element_type=F32
    )


def ln_parts(values):
    centre = values - jnp.mean(values, axis=-1, keepdims=True)
    scale = lax.rsqrt(jnp.mean(centre * centre, axis=-1, keepdims=True) + EPS)
    return centre * scale, scale


def ln_back(normal, scale, grad):
    return scale * (
        grad
        - jnp.mean(grad, axis=-1, keepdims=True)
        - normal * jnp.mean(grad * normal, axis=-1, keepdims=True)
    )


def gelu_both(h):
    square = h * h
    t = jnp.tanh(GELU_C * (h + 0.044715 * h * square))
    value = 0.5 * h * (1.0 + t)
    slope = 0.5 * (1.0 + t) + 0.5 * h * (1.0 - t * t) * GELU_C * (1.0 + 3 * 0.044715 * square)
    return value, slope


def dot3(left, right):
    wide_left = left.dtype == F32
    value = left if wide_left else right
    total = None
    for _ in range(3):
        term = value.astype(BF16)
        value = value - term.astype(F32)
        part = dot(term, right) if wide_left else dot(left, term)
        total = part if total is None else total + part
    return total


def add_low(left, right):
    return (left.astype(F32) + right.astype(F32)).astype(BF16)


def block_kernel(dims, x, cot, frames, clips, biases, cond, w_ada, wq, wp, w1, w2):
    nc, nf = dims.nc, dims.nf
    own, width = x.shape
    group = nc * own
    rows_d, q_w = wq.shape
    chip_w = q_w // 3
    cols_f, ff_d = w2.shape
    ff_c = 2 * ff_d
    ada_w = w_ada.shape[1]
    n_bias = sum(item.shape[0] for item in biases)
    heads = chip_w // HEAD_DIM
    micro, n_clips, _ = cond.shape
    n_rows = micro * n_clips
    half = n_rows // 2
    n_sub = own // SUB
    head_scale = HEAD_DIM ** (-0.5)
    last = nf - 2
    third = rows_d // 3

    outs = (
        jax.ShapeDtypeStruct((own, width), BF16),
        jax.ShapeDtypeStruct((own, width), BF16),
        jax.ShapeDtypeStruct((n_rows, cols_f), F32),
        jax.ShapeDtypeStruct((rows_d, ada_w), F32),
        jax.ShapeDtypeStruct((ada_w,), F32),
        jax.ShapeDtypeStruct((rows_d, q_w), F32),
        jax.ShapeDtypeStruct((2 * chip_w,), F32),
        jax.ShapeDtypeStruct((rows_d, cols_f), F32),
        jax.ShapeDtypeStruct((cols_f,), F32),
        jax.ShapeDtypeStruct((rows_d, ff_c), F32),
        jax.ShapeDtypeStruct((ff_c,), F32),
        jax.ShapeDtypeStruct((cols_f, ff_d), F32),
        jax.ShapeDtypeStruct((cols_f,), F32),
    )
    tokens = (nc, own, width)
    n_sem = 240
    scratch = dict(
        xg=pltpu.VMEM(tokens, BF16),
        cg=pltpu.VMEM(tokens, BF16),
        idsg=pltpu.VMEM((nc, 2, own), F32),
        biasg=pltpu.VMEM((nf, 1, n_bias), F32),
        ada=pltpu.VMEM(w_ada.shape, BF16),
        silu=pltpu.VMEM((n_rows, rows_d), BF16),
        cond_own=pltpu.VMEM((n_rows, cols_f), F32),
        m_part=pltpu.VMEM((2, half, ada_w), F32),
        m_core=pltpu.VMEM((half, ada_w), F32),
        m_chip=pltpu.VMEM((nc, half, ada_w), F32),
        m_z=pltpu.VMEM((nf, 2, half, ada_w), F32),
        m_tab=pltpu.VMEM((n_rows, 6 * width), F32),
        tab=pltpu.VMEM((3, nc * n_sub, width), F32),
        own_tab=pltpu.VMEM((6, n_sub, width), F32),
        q_z=pltpu.VMEM((nf, rows_d, q_w + cols_f), BF16),
        q_rows=pltpu.VMEM((nf * 3, third, q_w), BF16),
        q_got=pltpu.VMEM((3, nc, third, q_w), BF16),
        w_q=pltpu.VMEM((nc, 2, rows_d, q_w), BF16),
        y_got=pltpu.VMEM((nc, rows_d, q_w), BF16),
        f1_z=pltpu.VMEM((nf, rows_d, ff_c), BF16),
        w_1=pltpu.VMEM((nc, 2, rows_d, ff_c), BF16),
        p_got=pltpu.VMEM((2, nf, rows_d, cols_f), BF16),
        w_p=pltpu.VMEM((chip_w, width), BF16),
        f2_half=pltpu.VMEM((cols_f, ff_d), BF16),
        f2_got=pltpu.VMEM((rows_d, ff_d), BF16),
        w_2=pltpu.VMEM((nf, 2, rows_d, ff_c), BF16),
        a_in=pltpu.VMEM(tokens, BF16),
        qkv=pltpu.VMEM((3, nc, own, chip_w), BF16),
        probs=pltpu.VMEM((nc * heads, own, own), F32),
        mixed=pltpu.VMEM((nc, own, chip_w), BF16),
        sum_s=pltpu.VMEM(tokens, BF16),
        sum_r=pltpu.VMEM((2, own, width), BF16),
        sum_st=pltpu.VMEM((2, own // 2, width), BF16),
        br_s=pltpu.VMEM(tokens, BF16),
        br_r=pltpu.VMEM((2, own, width), BF16),
        br_st=pltpu.VMEM((2, own // 2, width), BF16),
        m_all=pltpu.VMEM(tokens, BF16),
        da_all=pltpu.VMEM(tokens, BF16),
        attn=pltpu.VMEM((own, width), F32),
        after=pltpu.VMEM((own, width), F32),
        d_after=pltpu.VMEM((own, width), F32),
        hid=pltpu.VMEM((own, ff_c), F32),
        act=pltpu.VMEM((nc, own, ff_c), BF16),
        d_hid=pltpu.VMEM((nc, own, ff_c), BF16),
        dbr=pltpu.VMEM(tokens, BF16),
        d_qkv=pltpu.VMEM((nc, own, q_w), BF16),
        g_2=pltpu.VMEM((nf, 2, rows_d, ff_c), BF16),
        g_2r=pltpu.VMEM((nf, rows_d, ff_c), BF16),
        g_1r=pltpu.VMEM((nc, rows_d, ff_c), BF16),
        g_qr=pltpu.VMEM((nc, rows_d, q_w), BF16),
        g_pr=pltpu.VMEM((rows_d, width), BF16),
        got_q=pltpu.VMEM((2, nf - 1, rows_d, q_w + cols_f), BF16),
        got_1=pltpu.VMEM((2, nf - 1, rows_d, ff_c), BF16),
        got_2=pltpu.VMEM((2, nf - 1, rows_d, ff_c), BF16),
        all_2=pltpu.VMEM((2, rows_d, ff_c), F32),
        sub=pltpu.VMEM((6, n_sub, width), F32),
        q_nat=pltpu.VMEM((rows_d, q_w), BF16),
        p_nat=pltpu.VMEM((rows_d, cols_f), BF16),
        all_q=pltpu.VMEM((rows_d, q_w + cols_f), F32),
        sub_lin=pltpu.VMEM((2, nc * n_sub, width), F32),
        sub_gate=pltpu.VMEM((nc * n_sub, width), F32),
        d_part=pltpu.VMEM((2, half, 6 * width), F32),
        d_core=pltpu.VMEM((half, 6 * width), F32),
        d_cut=pltpu.VMEM((nf, half, ada_w), F32),
        d_bias=pltpu.VMEM((8, width), F32),
        dz=pltpu.VMEM((nf, half, ada_w), F32),
        dzb=pltpu.VMEM((nf, 8, width), F32),
        d_tot=pltpu.VMEM((2, half, ada_w), F32),
        d_bsum=pltpu.VMEM((8, width), F32),
        d_coreb=pltpu.VMEM((8, width), F32),
        d_chipb=pltpu.VMEM((nc, 8, width), F32),
        c_part=pltpu.VMEM((nf, n_rows, rows_d), F32),
        c_all=pltpu.VMEM((nc, 2, n_rows, rows_d), F32),
        send=pltpu.SemaphoreType.DMA((n_sem,)),
        recv=pltpu.SemaphoreType.DMA((n_sem,)),
        local=pltpu.SemaphoreType.DMA((32,)),
    )
    names = list(scratch)

    def kernel(
        x_in, c_in, frames_in, clips_in, bq_in, bp_in, b1_in, b2_in, ba_in, cond_in, ada_in,
        q_in, p_in, f1_in, f2_in,
        out, x_grad, o_cond, o_ada, o_bada, o_q, o_bqv, o_p, o_bp, o_1, o_b1, o_2, o_b2, *rest,
    ):
        r = types.SimpleNamespace(**dict(zip(names, rest)))
        place = Place(nc, nf)
        wires = Wires(r.send, r.recv, r.local)
        c, k, f = place.c, place.k, place.f
        core_o, core_dev = place.peer(CORE, 1)
        chip_peers = [place.peer(CHIP, step) for step in range(1, nc)]
        plane_peers = [place.peer(PLANE, step) for step in range(1, nf)]

        def loop(count, body, unroll=1):
            def run(i, carry):
                body(i)
                return carry

            lax.fori_loop(0, count, run, 0, unroll=unroll)

        def loop_rows(body):
            loop(n_sub, body, 2)

        def when(condition, body):
            pl.when(condition)(body)

        def sub_rows(g):
            return pl.ds(pl.multiple_of(g * SUB, SUB), SUB)

        def reserve(count):
            base = wires.remote_count
            wires.remote_count += count
            return base

        def pair(src, dst, device, send_at, recv_at):
            return pltpu.make_async_remote_copy(
                src_ref=src,
                dst_ref=dst,
                send_sem=r.send.at[send_at],
                recv_sem=r.recv.at[recv_at],
                device_id=device,
                device_id_type=MESH_ID,
            )

        chip_x, dev_x = place.peer(CHIP, 1)
        chip_y, dev_y = place.peer(CHIP, 2)
        chip_d, _ = place.peer(CHIP, 3)
        first_half, second_half = pl.ds(0, own // 2), pl.ds(own // 2, own // 2)

        class Share:
            def __init__(self, ref, src=None):
                def copy(chip, rows, device, at, own_src=None):
                    from_ref = ref.at[chip, rows] if own_src is None else own_src.at[rows]
                    return pair(from_ref, ref.at[chip, rows], device, at, at)

                at = reserve(6)
                self.x_a = copy(c, first_half, dev_x, at, src)
                self.x_b = copy(c, second_half, dev_x, at + 1, src)
                self.y_b = copy(c, second_half, dev_y, at + 2, src)
                self.y_a = copy(c, first_half, dev_y, at + 3, src)
                self.on_y = copy(chip_x, first_half, dev_y, at + 4)
                self.on_x = copy(chip_y, second_half, dev_x, at + 5)

            def start(self):
                for item in (self.x_a, self.y_b, self.x_b, self.y_a):
                    item.start()

            def relay(self):
                self.x_a.wait_recv()
                self.on_y.start()
                self.y_b.wait_recv()
                self.on_x.start()

            def arrive(self, step):
                if step == 1:
                    self.x_b.wait_recv()
                elif step == 2:
                    self.y_a.wait_recv()
                else:
                    self.on_y.wait_recv()
                    self.on_x.wait_recv()

            def sent(self):
                for item in (self.x_a, self.x_b, self.y_b, self.y_a, self.on_y, self.on_x):
                    item.wait_send()

        class Merge:
            def __init__(self, terms, got, stage):
                self.terms, self.got, self.stage = terms, got, stage
                at = reserve(6)
                self.d_x = pair(terms.at[chip_d, first_half], stage.at[0], dev_x, at, at)
                self.d_y = pair(terms.at[chip_d, second_half], stage.at[1], dev_y, at + 1, at + 1)

                def copy(chip, rows, to, device, index):
                    return pair(
                        terms.at[chip, rows], got.at[to, rows], device, at + index, at + index
                    )

                self.x_a = copy(chip_x, first_half, 0, dev_x, 2)
                self.x_b = copy(chip_x, second_half, 0, dev_x, 3)
                self.y_b = copy(chip_y, second_half, 1, dev_y, 4)
                self.y_a = copy(chip_y, first_half, 1, dev_y, 5)

            def put(self, step, blk, part):
                self.terms[blk] = part

                def far():
                    self.d_x.start()
                    self.d_y.start()

                when(step == 3, far)
                when(step == 2, self.y_b.start)
                when(step == 1, self.x_a.start)

            def launch(self):
                for item in (self.d_x, self.d_y, self.y_b, self.x_a):
                    item.start()

            def combine(self):
                self.d_y.wait()
                ref = self.terms.at[chip_x, second_half]
                ref[...] = add_low(ref[...], self.stage[1])
                self.x_b.start()
                self.d_x.wait()
                ref = self.terms.at[chip_y, first_half]
                ref[...] = add_low(ref[...], self.stage[0])
                self.y_a.start()

            def finish(self):
                for item in (self.x_a, self.x_b, self.y_b, self.y_a):
                    item.wait()

            def rows(self, at):
                value = self.terms[c, at, :].astype(F32) + self.got[0, at, :].astype(F32)
                return value + self.got[1, at, :].astype(F32)

        up, down = (place.dp, f + 1), (place.dp, f - 1)

        class Gather:
            def __init__(self, slot):
                self.slot = slot
                self.up, self.down = reserve(nf - 1), reserve(nf - 1)

            def both(self, step, src=None):
                above = pair(
                    self.slot(f - step) if src is None else src,
                    self.slot(f - step), up, self.up + step, self.up + step,
                )
                below = pair(
                    self.slot(f + step) if src is None else src,
                    self.slot(f + step), down, self.down + step, self.down + step,
                )
                return (
                    ((f - step >= 0) & (f < nf - 1), above),
                    ((f + step <= nf - 1) & (f > 0), below),
                )

            def start(self, step, src=None):
                for condition, copy in self.both(step, src):
                    when(condition, copy.start)

            def arrive(self, step, then=None, wait=True):
                for condition, got, base in (
                    (f - 1 - step >= 0, f - 1 - step, self.up),
                    (f + 1 + step <= nf - 1, f + 1 + step, self.down),
                ):

                    def body(got=got, base=base):
                        slot = self.slot(got)
                        if wait:
                            pair(slot, slot, core_dev, base + step, base + step).wait_recv()
                        if then is not None:
                            then(got)

                    when(condition, body)

            def sent(self, src=None):
                for step in range(nf - 1):
                    for condition, copy in self.both(step, src if step == 0 else None):
                        when(condition, copy.wait_send)

        class Sum:
            def __init__(self, terms, got):
                self.terms, self.got = terms, got
                self.bases = (reserve(nf - 1), reserve(nf - 1))

            def both(self, step):
                for way in range(2):
                    target = f + (nf - 1) - step if way == 0 else f - (nf - 1) + step
                    condition = (f <= step) & (f < nf - 1) if way == 0 else (target >= 0) & (f > 0)
                    more = condition & (f > 0 if way == 0 else f < nf - 1)
                    at = self.bases[way] + step
                    copy = pair(
                        self.terms(target), self.got.at[way, step], up if way == 0 else down, at, at
                    )
                    yield way, target, condition, more, copy

            def wait(self, way, step):
                at = self.bases[way] + step
                ref = self.got.at[way, step]
                pair(ref, ref, core_dev, at, at).wait_recv()

            def start(self, step):
                for way, target, condition, more, copy in self.both(step):
                    if step > 0:

                        def body(way=way, target=target):
                            self.wait(way, step - 1)
                            ref = self.terms(target)
                            ref[...] = add_low(ref[...], self.got[way, step - 1])

                        when(more, body)
                    when(condition, copy.start)

            def finish(self, result):
                result[...] = self.terms(f)[...].astype(F32)
                for way, condition in ((0, f > 0), (1, f < nf - 1)):

                    def body(way=way):
                        self.wait(way, last)
                        result[...] = result[...] + self.got[way, last].astype(F32)

                    when(condition, body)
                for step in range(nf - 1):
                    for _, _, condition, _, copy in self.both(step):
                        when(condition, copy.wait_send)

        def own_side(ref, side):
            return ref.at[pl.ds(pl.multiple_of(side * rows_d, SUB), rows_d)]

        barrier = pltpu.get_barrier_semaphore()
        peers = [core_dev] + [peer for _, peer in chip_peers + plane_peers]
        for peer in peers:
            pl.semaphore_signal(barrier, inc=1, device_id=peer, device_id_type=MESH_ID)

        q_line = Gather(lambda g: r.q_z.at[g])
        f1_line = Gather(lambda g: r.f1_z.at[g])
        f2_line = Gather(lambda g: r.w_2.at[g, k])
        ada_near = wires.near(ada_in, r.ada)
        q_near = wires.near(q_in, r.q_nat)
        p_near = wires.near(p_in, r.p_nat)
        f2_near = wires.near(f2_in, r.f2_half)
        first = []
        first.append(wires.near(x_in, r.xg.at[c]))
        first.append(wires.near(c_in, r.cg.at[c]))
        f1_near = wires.near(f1_in, r.f1_z.at[f])
        order = lax.broadcasted_iota(jnp.int32, frames_in.shape, 0)
        for at, value in ((0, frames_in[...] + 65536 * order), (1, clips_in[...] + n_clips * order)):
            row = [value[i : i + 1].astype(F32) for i in range(micro)]
            r.idsg[c, at : at + 1, :] = jnp.concatenate(row, axis=1)
        row = [ref[...].astype(F32).reshape(1, ref.shape[0]) for ref in (bq_in, bp_in, b1_in, b2_in, ba_in)]
        r.biasg[f] = jnp.concatenate(row, axis=1)
        cond_rows = cond_in[...].reshape(n_rows, width)

        def own_silu(at):
            part = cond_rows[:, rows_d * at : rows_d * (at + 1)]
            r.silu[...] = (part / (1.0 + jnp.exp(-part))).astype(BF16)

        def own_cond(at):
            r.cond_own[...] = cond_rows[:, cols_f * at : cols_f * (at + 1)]

        for at in range(2 * nc):
            when(place.dp == at, functools.partial(own_silu, at))
        for at in range(nf):
            when(f == at, functools.partial(own_cond, at))
        ada_near.wait()
        ada_bias = jnp.where(place.dp == 0, row[4], 0.0)
        value = dot(r.silu[...], r.ada[...]) + ada_bias
        r.m_part[...] = value.reshape(2, half, ada_w)
        q_near.wait()
        p_near.wait()
        r.q_z[f] = jnp.concatenate([r.q_nat[...], r.p_nat[...]], axis=1)
        f2_near.wait()
        pl.semaphore_wait(barrier, len(peers))
        m_first = wires.far(r.m_part.at[core_o], r.m_core, core_dev)
        q_line.start(0)
        for _, peer in chip_peers:
            first.append(wires.far(r.idsg.at[c], r.idsg.at[c], peer))
        f2_swap = wires.far(own_side(r.f2_half, core_o), r.f2_got, core_dev)

        w_q, q_rows = r.w_q, r.q_rows
        q_base = reserve(3 * nc)
        q_local = wires.local_count
        wires.local_count += 3

        def q_copies(plane, i):
            piece = 3 * plane + i
            kind, chip = piece // nc, piece % nc
            src, dst = q_rows.at[piece], r.q_got.at[kind, c]
            far = pair(src, dst, (chip * 2 + k, f), q_base + kind * nc + chip, q_base + kind * nc + c)
            return chip, far, pltpu.make_async_copy(src, dst, r.local.at[q_local + kind])

        def q_forward(plane):
            r.p_got[k, plane] = r.q_z[plane, :, q_w:]
            for i in range(3):
                piece = r.q_z[plane, :, chip_w * i : chip_w * (i + 1)]
                parts = [piece[third * j : third * (j + 1)] for j in range(3)]
                q_rows[3 * plane + i] = jnp.concatenate(parts, axis=1)
                chip, far, near = q_copies(plane, i)
                when(chip != c, far.start)
                when(chip == c, near.start)

        f1_base = reserve(nc)
        f1_local = wires.local_count
        wires.local_count += 1

        def f1_copies(plane):
            src, dst = r.f1_z.at[plane], r.w_1.at[c, k]
            far = pair(src, dst, (plane * 2 + k, f), f1_base + plane, f1_base + c)
            return far, pltpu.make_async_copy(src, dst, r.local.at[f1_local])

        def f1_forward(plane):
            far, near = f1_copies(plane)
            when(plane != c, far.start)
            when(plane == c, near.start)

        m_first.wait()
        m_chip = r.m_chip
        m_chip[c] = r.m_part[k] + r.m_core[...]
        m_second = [wires.far(m_chip.at[c], m_chip.at[c], peer) for _, peer in chip_peers]
        q_forward(f)
        x_share = Share(r.xg, x_in)
        x_share.start()
        wait_all(m_second)
        total = m_chip[0]
        for other in range(1, nc):
            total = total + m_chip[other]
        r.m_z[f, k] = total
        m_third = [wires.far(r.m_z.at[f, k], r.m_z.at[f, k], peer) for _, peer in plane_peers]
        for _, peer in plane_peers:
            first.append(wires.far(r.biasg.at[f], r.biasg.at[f], peer))
        q_line.arrive(0, q_forward)
        q_line.start(1)
        x_share.relay()
        f2_swap.wait()

        def join_even():
            r.w_2[f, k] = jnp.concatenate([r.f2_half[:rows_d], r.f2_got[...]], axis=1)

        def join_odd():
            r.w_2[f, k] = jnp.concatenate([r.f2_got[...], r.f2_half[rows_d:]], axis=1)

        when(k == 0, join_even)
        when(k == 1, join_odd)
        f2_base = reserve(nf)

        def f2_across(plane):
            ref = r.w_2.at[plane, k]
            return pair(ref, ref, core_dev, f2_base + plane, f2_base + plane)

        def f2_forward(plane):
            f2_across(plane).start()

        f2_forward(f)
        wait_all(m_third)
        m_last = wires.far(r.m_z.at[:, k], r.m_z.at[:, k], core_dev)

        wait_all(first)
        m_last.wait()
        m_rows = [r.m_z[plane].reshape(n_rows, ada_w) for plane in range(nf)]
        r.m_tab[...] = jnp.concatenate(m_rows, axis=1)
        lead = lax.broadcasted_iota(jnp.int32, (n_sub, own), 1)
        lead = lead == SUB * lax.broadcasted_iota(jnp.int32, (n_sub, own), 0)
        lead = jnp.where(lead, 1.0, 0.0).astype(BF16)
        places = lax.broadcasted_iota(jnp.int32, (own, n_rows), 1).astype(F32)

        def hot_rows(blk):
            clip = r.idsg[blk].T[:, 1:2]
            return dot(lead, jnp.where(clip == places, 1.0, 0.0).astype(BF16)).astype(BF16)

        hot_all = jnp.concatenate([hot_rows(blk) for blk in range(nc)], axis=0)
        own_hot = hot_rows(c)
        for kind in range(6):
            value = r.m_tab[:, width * kind : width * (kind + 1)]
            if kind in (0, 1, 5):
                r.tab[kind % 3] = dot3(hot_all, value)
            r.own_tab[kind] = dot3(own_hot, value)

        def tab_row(kind, blk, g):
            return r.tab[kind % 3, pl.ds(blk * n_sub + g, 1), :]

        def own_row(kind, g):
            return r.own_tab[kind, pl.ds(g, 1), :]

        def make_a(blk):
            def body(g):
                rows = sub_rows(g)
                normal, _ = ln_parts(r.xg[blk, rows, :].astype(F32))
                value = normal * (1.0 + tab_row(1, blk, g)) + tab_row(0, blk, g)
                r.a_in[blk, rows, :] = value.astype(BF16)

            loop_rows(body)

        make_a(c)
        for step in (1, 2):
            x_share.arrive(step)
            make_a(xor_of(c, step, nc))
        q_line.arrive(1, q_forward)
        q_line.start(2)
        f1_line.start(0, f1_in)
        x_share.arrive(3)
        make_a(chip_d)
        q_line.arrive(2, q_forward)

        for kind in range(3):
            for other, _ in chip_peers:
                ref = r.q_got.at[kind, other]
                at = q_base + kind * nc + other
                pair(ref, ref, core_dev, at, at).wait()
            ref = r.q_got.at[kind, c]
            pltpu.make_async_copy(ref, ref, r.local.at[q_local + kind]).wait()
        q_core = []
        for chip in range(nc):
            for j in range(3):
                at = chip_w * j
                row = [r.q_got[kind, chip, :, at : at + chip_w] for kind in range(3)]
                w_q[chip, k, third * j : third * (j + 1), :] = jnp.concatenate(row, axis=1)
            q_core.append(wires.far(w_q.at[chip, k], w_q.at[chip, k], core_dev))
        p_core = wires.far(r.p_got.at[k], r.p_got.at[k], core_dev)
        f1_near.wait()
        f1_forward(f)
        f1_line.arrive(0, f1_forward)
        f1_line.start(1)
        x_share.sent()
        p_core.wait()
        for side in range(2):
            row = [r.p_got[side, plane] for plane in range(nf)]
            r.w_p[side * rows_d : (side + 1) * rows_d, :] = jnp.concatenate(row, axis=1)
        wait_all(q_core)

        lane = lax.broadcasted_iota(jnp.int32, (1, chip_w), 1)
        head_of = [
            jnp.where((lane >= HEAD_DIM * h) & (lane < HEAD_DIM * (h + 1)), 1.0, 0.0).astype(BF16)
            for h in range(heads)
        ]

        def weight_q():
            return w_q[...].reshape(width, q_w)

        def qv_bias(plane):
            row = r.biasg[plane]
            return jnp.where(c % 2 == 0, row[:, :chip_w], row[:, chip_w : 2 * chip_w])

        bias_q, bias_v = qv_bias(c // 2), qv_bias(nf // 2 + c // 2)
        at_p = 2 * chip_w
        at_1 = at_p + cols_f
        at_2 = at_1 + ff_c
        bias_p = jnp.concatenate([r.biasg[g][:, at_p : at_p + cols_f] for g in range(nf)], axis=1)
        bias_o = jnp.concatenate([r.biasg[g][:, at_2 : at_2 + cols_f] for g in range(nf)], axis=1)
        bias_1 = r.biasg[c][:, at_1 : at_1 + ff_c]
        zero = jnp.zeros_like(bias_q)
        bias_qkv = jnp.concatenate([bias_q, zero, bias_v], axis=1)
        attn_merge = Merge(r.sum_s, r.sum_r, r.sum_st)

        def attend(i):
            step = nc - 1 - i
            blk = xor_of(c, step, nc)
            value = (dot(r.a_in[blk], weight_q()) + bias_qkv).astype(BF16)
            for kind in range(3):
                r.qkv[kind, blk] = value[:, chip_w * kind : chip_w * (kind + 1)]
            q_now, k_now, v_now = r.qkv[0, blk], r.qkv[1, blk], r.qkv[2, blk]
            frames = r.idsg[blk]
            same = frames.T[:, 0:1] == frames[0:1, :]
            mixed = jnp.zeros((own, chip_w), F32)
            for h in range(heads):
                scores = dot_rt(q_now * head_of[h], k_now) * head_scale
                scores = jnp.where(same, scores, NEG_FILL)
                raised = jnp.exp(scores - jnp.max(scores, axis=-1, keepdims=True))
                share = raised / jnp.sum(raised, axis=-1, keepdims=True)
                r.probs[blk * heads + h] = share
                mixed = mixed + dot(share.astype(BF16), v_now * head_of[h])
            mixed = mixed.astype(BF16)
            r.mixed[blk] = mixed
            attn_merge.put(step, blk, dot(mixed, r.w_p[...]).astype(BF16))

            def next_lines():
                f1_line.arrive(1)
                f1_line.start(2)
                f2_line.start(0)

            when(i == 1, next_lines)

        loop(nc, attend)
        attn_merge.combine()
        f1_line.arrive(1, f1_forward, False)
        f1_line.arrive(2, f1_forward)

        attn_merge.finish()

        def after_attention(g):
            rows = sub_rows(g)
            value = attn_merge.rows(rows) + bias_p
            r.attn[rows, :] = value
            after = r.xg[c, rows, :].astype(F32) + own_row(2, g) * value
            r.after[rows, :] = after
            normal, _ = ln_parts(after)
            r.m_all[c, rows, :] = (normal * (1.0 + own_row(4, g)) + own_row(3, g)).astype(BF16)

        loop_rows(after_attention)
        m_all = r.m_all
        m_share = Share(m_all)
        m_share.start()
        c_share = Share(r.cg, c_in)
        c_share.start()
        f2_line.arrive(0, f2_forward)
        f2_line.start(1)
        f1_core = []
        ref = r.w_1.at[c, k]
        pltpu.make_async_copy(ref, ref, r.local.at[f1_local]).wait()
        f1_core.append(wires.far(ref, ref, core_dev))
        for other, _ in chip_peers:
            ref = r.w_1.at[other, k]
            pair(ref, ref, core_dev, f1_base + other, f1_base + other).wait()
            f1_core.append(wires.far(ref, ref, core_dev))
        m_share.relay()
        f1_line.sent(f1_in)
        f2_line.arrive(1, f2_forward)
        f2_line.start(2)
        wait_all(f1_core)

        def weight_1():
            return r.w_1[...].reshape(width, ff_c)

        def weight_2():
            return r.w_2[...].reshape(width, ff_c)

        dm_merge = Merge(r.sum_s, r.sum_r, r.sum_st)
        br_merge = Merge(r.br_s, r.br_r, r.br_st)

        def mixed_order(i):
            return (1 + 2 * i) * (1 - i // 2) + (6 - 2 * i) * (i // 2)

        def feed(step):
            blk = xor_of(c, step, nc)
            for at in range(1, nc):
                when(step == at, functools.partial(m_share.arrive, at))
            r.hid[...] = dot(m_all[blk], weight_1()) + bias_1

            def gelu_rows(g):
                rows = sub_rows(g)
                value, slope = gelu_both(r.hid[rows, :])
                r.act[blk, rows, :] = value.astype(BF16)
                r.d_hid[blk, rows, :] = slope.astype(BF16)

            loop_rows(gelu_rows)
            when(step == 1, c_share.relay)

        def feed_back(i):
            step = mixed_order(i)
            blk = xor_of(c, step, nc)
            for at in range(1, nc):
                when(step == at, functools.partial(c_share.arrive, at))

            def dbr_rows(g):
                rows = sub_rows(g)
                value = r.cg[blk, rows, :].astype(F32) * tab_row(5, blk, g)
                r.dbr[blk, rows, :] = value.astype(BF16)

            loop_rows(dbr_rows)
            r.hid[...] = dot(r.dbr[blk], weight_2())

            def back_rows(g):
                rows = sub_rows(g)
                value = r.hid[rows, :] * r.d_hid[blk, rows, :].astype(F32)
                r.d_hid[blk, rows, :] = value.astype(BF16)

            loop_rows(back_rows)
            dm_merge.put(step, blk, dot_rt(r.d_hid[blk], weight_1()).astype(BF16))

        loop(nc, feed)
        f2_line.arrive(2, f2_forward)
        for plane in range(nf):
            f2_across(plane).wait()
        loop(nc, feed_back)
        dm_merge.combine()
        c_share.sent()

        def column_cuts(count):
            return [(at, min(at + 256, count)) for at in range(0, count, 256)]

        def all_rows(ref):
            return ref[...].reshape(group, ref.shape[-1])

        dbr_all = all_rows(r.dbr)
        for lo, hi in column_cuts(ff_c):
            value = dot_lt(dbr_all, r.act[:, :, lo:hi].reshape(group, hi - lo))
            r.g_2[:, :, :, lo:hi] = value.astype(BF16).reshape(nf, 2, rows_d, hi - lo)
        g2_core = wires.far(r.g_2.at[:, core_o], r.g_2r, core_dev)

        dm_merge.finish()
        da_all = r.da_all

        def back_norm2(g):
            rows = sub_rows(g)
            d_m = dm_merge.rows(rows)
            normal, scale = ln_parts(r.after[rows, :])
            cot_now = r.cg[c, rows, :].astype(F32)
            d_after = cot_now + ln_back(normal, scale, d_m * (1.0 + own_row(4, g)))
            r.d_after[rows, :] = d_after
            da_all[c, rows, :] = (own_row(2, g) * d_after).astype(BF16)
            at = pl.ds(g, 1)
            r.sub[3, at, :] = jnp.sum(d_m, axis=0, keepdims=True)
            r.sub[4, at, :] = jnp.sum(d_m * normal, axis=0, keepdims=True)
            r.sub[2, at, :] = jnp.sum(d_after * r.attn[rows, :], axis=0, keepdims=True)

        loop_rows(back_norm2)
        da_share = Share(da_all)
        da_share.start()
        m_share.sent()
        g2_core.wait()
        for plane in range(nf):
            r.g_2[plane, k] = add_low(r.g_2[plane, k], r.g_2r[plane])
        sum_2 = Sum(lambda t: r.g_2.at[t, k], r.got_2)
        sum_2.start(0)

        g_1 = r.w_1
        m_rows_all = all_rows(m_all)
        for lo, hi in column_cuts(ff_c):
            value = dot_lt(m_rows_all, r.d_hid[:, :, lo:hi].reshape(group, hi - lo))
            g_1[:, :, :, lo:hi] = value.astype(BF16).reshape(nc, 2, rows_d, hi - lo)
        g1_core = wires.far(g_1.at[:, core_o], r.g_1r, core_dev)
        da_share.relay()

        g1_core.wait()
        for chip in range(nc):
            g_1[chip, k] = add_low(g_1[chip, k], r.g_1r[chip])
        y_1 = r.f1_z
        y_1[c] = g_1[c, k]
        y1_far = [wires.far(g_1.at[other, k], y_1.at[c], peer) for other, peer in chip_peers]

        def branch_out(i):
            step = nc - 1 - i
            blk = xor_of(c, step, nc)
            r.hid[...] = dot_rt(r.act[blk], weight_2())
            r.br_s[blk] = r.hid[...].astype(BF16)
            bias_once = bias_o * jnp.where(step == 0, 1.0, 0.0)

            def gate_rows(g):
                rows = sub_rows(g)
                value = (r.hid[rows, :] + bias_once) * r.cg[blk, rows, :].astype(F32)
                r.sub_gate[pl.ds(blk * n_sub + g, 1), :] = jnp.sum(value, axis=0, keepdims=True)

            loop_rows(gate_rows)

        loop(nc, branch_out)
        sum_2.start(1)

        def gray_order(i):
            return i + i // 2 - 2 * (i // 3)

        back_merge = Merge(r.sum_s, r.sum_r, r.sum_st)

        def attend_back(i):
            step = gray_order(i)
            blk = xor_of(c, step, nc)
            for at in range(1, nc):
                when(step == at, functools.partial(da_share.arrive, at))
            d_mix = dot_rt(da_all[blk], r.w_p[...]).astype(BF16)
            q_now, k_now, v_now = r.qkv[0, blk], r.qkv[1, blk], r.qkv[2, blk]
            d_q = jnp.zeros((own, chip_w), F32)
            d_k = jnp.zeros((own, chip_w), F32)
            d_v = jnp.zeros((own, chip_w), F32)
            for h in range(heads):
                d_mix_h = d_mix * head_of[h]
                share = r.probs[blk * heads + h]
                d_share = dot_rt(d_mix_h, v_now)
                d_score = share * (d_share - jnp.sum(share * d_share, axis=-1, keepdims=True))
                d_score = d_score.astype(BF16)
                d_q = d_q + dot(d_score, k_now * head_of[h])
                d_k = d_k + dot_lt(d_score, q_now * head_of[h])
                d_v = d_v + dot_lt(share.astype(BF16), d_mix_h)
            all_three = jnp.concatenate([d_q * head_scale, d_k * head_scale, d_v], axis=1).astype(BF16)
            r.d_qkv[blk] = all_three
            back_merge.put(step, blk, dot_rt(all_three, weight_q()).astype(BF16))
            when(i == 3, lambda: sum_2.start(2))

        loop(nc, attend_back)
        da_share.sent()

        g_q, g_p = w_q, r.w_p
        a_rows = all_rows(r.a_in)
        for lo, hi in column_cuts(q_w):
            value = dot_lt(a_rows, r.d_qkv[:, :, lo:hi].reshape(group, hi - lo))
            g_q[:, :, :, lo:hi] = value.astype(BF16).reshape(nc, 2, rows_d, hi - lo)
        q_core_back = wires.far(g_q.at[:, core_o], r.g_qr, core_dev)
        wait_all(y1_far)
        sum_1 = Sum(lambda t: y_1.at[t], r.got_1)
        sum_1.start(0)
        g_p[...] = dot_lt(all_rows(r.mixed), all_rows(da_all)).astype(BF16)
        p_core_back = wires.far(own_side(g_p, core_o), r.g_pr, core_dev)
        q_core_back.wait()
        for chip in range(nc):
            g_q[chip, k] = add_low(g_q[chip, k], r.g_qr[chip])
        r.y_got[c] = g_q[c, k]
        yq_far = [wires.far(g_q.at[other, k], r.y_got.at[c], peer) for other, peer in chip_peers]

        def own_terms(step):
            blk = xor_of(c, step, nc)

            def body(g):
                rows = sub_rows(g)
                part = r.sum_s[blk, rows, :].astype(F32)
                normal, _ = ln_parts(r.xg[blk, rows, :].astype(F32))
                at = pl.ds(blk * n_sub + g, 1)
                r.sub_lin[0, at, :] = jnp.sum(part, axis=0, keepdims=True)
                r.sub_lin[1, at, :] = jnp.sum(part * normal, axis=0, keepdims=True)

            loop_rows(body)

        loop(nc, own_terms)
        back_merge.combine()
        all_turned = hot_all.astype(F32).T.astype(BF16)
        hot_turned = own_hot.astype(F32).T.astype(BF16)
        for kind in range(6):
            if kind < 2:
                value = dot3(all_turned, r.sub_lin[kind])
            elif kind < 5:
                value = dot3(hot_turned, r.sub[kind])
            else:
                value = dot3(all_turned, r.sub_gate[...])
            r.d_part[:, :, width * kind : width * (kind + 1)] = value.reshape(2, half, width)
        d_core = wires.far(r.d_part.at[core_o], r.d_core, core_dev)
        d_core.wait()
        r.d_core[...] = r.d_core[...] + r.d_part[k]
        for plane in range(nf):
            r.d_cut[plane] = r.d_core[:, ada_w * plane : ada_w * (plane + 1)]
        small = []
        for other, peer in plane_peers:
            small.append(wires.far(r.d_cut.at[other], r.dz.at[f], peer))
        r.dz[f] = r.d_cut[f]
        sum_1.start(1)
        p_core_back.wait()
        own_side(g_p, k)[...] = add_low(own_side(g_p, k)[...], r.g_pr[...])
        ones_own = jnp.ones((8, own), BF16)
        ones_all = jnp.ones((8, group), BF16)
        r.d_bias[...] = jnp.zeros((8, width), F32)
        r.d_bias[0:1, :] = dot(ones_own, da_all[c])[0:1]
        r.d_bias[1:2, :] = dot(ones_own, r.dbr[c])[0:1]
        qkv_sums = dot(ones_all, all_rows(r.d_qkv))[0:1]
        r.d_bias[2:3, 0:chip_w] = qkv_sums[:, :chip_w]
        r.d_bias[3:4, 0:chip_w] = qkv_sums[:, 2 * chip_w :]
        ones_ff = dot(ones_all, all_rows(r.d_hid))[0:1]
        r.d_bias[4:5, :] = ones_ff[:, :width]
        for part in range(1, ff_c // width):
            r.d_bias[4 + part : 5 + part, :] = ones_ff[:, part * width : (part + 1) * width]
        bias_far = [wires.far(r.d_bias, r.dzb.at[f], peer) for _, peer in plane_peers]
        r.dzb[f] = r.d_bias[...]
        wait_all(small)
        value = r.dz[0]
        for plane in range(1, nf):
            value = value + r.dz[plane]
        m_chip[c] = value
        small = [wires.far(m_chip.at[c], m_chip.at[c], peer) for _, peer in chip_peers]
        wait_all(yq_far)
        q_line.sent()
        y_q = r.q_z
        for plane in range(nf):
            row = []
            for i in range(3):
                kind, chip = (3 * plane + i) // nc, (3 * plane + i) % nc
                row.append(r.y_got[chip, :, chip_w * kind : chip_w * (kind + 1)])
            row.append(own_side(g_p, k)[:, plane * cols_f : (plane + 1) * cols_f])
            y_q[plane] = jnp.concatenate(row, axis=1)
        sum_q = Sum(lambda t: y_q.at[t], r.got_q)
        sum_q.start(0)
        sum_1.start(2)
        wait_all(bias_far)
        value = r.dzb[0]
        for plane in range(1, nf):
            value = value + r.dzb[plane]
        r.d_bsum[...] = value
        b_swap = wires.far(r.d_bsum, r.d_coreb, core_dev)

        back_merge.finish()

        def back_norm1(g):
            rows = sub_rows(g)
            d_a = back_merge.rows(rows)
            normal, scale = ln_parts(r.xg[c, rows, :].astype(F32))
            value = r.d_after[rows, :] + ln_back(normal, scale, d_a * (1.0 + own_row(1, g)))
            x_grad[rows, :] = value.astype(BF16)

        loop_rows(back_norm1)
        wait_all(small)
        value = m_chip[0]
        for chip in range(1, nc):
            value = value + m_chip[chip]
        r.d_tot[k] = value
        d_swap = wires.far(r.d_tot.at[k], r.d_tot.at[k], core_dev)
        b_swap.wait()
        r.d_chipb[c] = r.d_bsum[...] + r.d_coreb[...]
        bias_far = [wires.far(r.d_chipb.at[c], r.d_chipb.at[c], peer) for _, peer in chip_peers]
        br_merge.launch()
        sum_q.start(1)
        d_swap.wait()
        d_cols = r.d_tot[...].reshape(n_rows, ada_w)
        silu_turned = r.silu[...].astype(F32).T.astype(BF16)
        o_bada[...] = jnp.sum(d_cols, axis=0)
        value, total = d_cols, None
        for _ in range(3):
            term = value.astype(BF16)
            value = value - term.astype(F32)
            part = dot_rt(term, r.ada[...])
            total = part if total is None else total + part
        r.c_part[f] = total
        c_far = [wires.far(r.c_part.at[f], r.c_part.at[f], peer) for _, peer in plane_peers]
        sum_q.start(2)
        for lo, hi in column_cuts(ada_w):
            o_ada[:, lo:hi] = dot3(silu_turned, d_cols[:, lo:hi])
        sum_2.finish(r.all_2.at[k])
        o2_swap = wires.far(r.all_2.at[k], r.all_2.at[k], core_dev)
        br_merge.combine()
        wait_all(c_far)
        value = r.c_part[0]
        for plane in range(1, nf):
            value = value + r.c_part[plane]
        r.c_all[c, k] = value
        c_chip = [wires.far(r.c_all.at[c, k], r.c_all.at[c, k], peer) for _, peer in chip_peers]


        br_merge.finish()

        def finish_out(g):
            rows = sub_rows(g)
            branch = br_merge.rows(rows) + bias_o
            out[rows, :] = (r.after[rows, :] + own_row(5, g) * branch).astype(BF16)

        loop_rows(finish_out)
        wait_all(c_chip)
        c_swap = wires.far(r.c_all.at[:, k], r.c_all.at[:, k], core_dev)
        o2_swap.wait()

        def own_columns(lo):
            def body():
                o_2[...] = r.all_2[:, :, lo : lo + ff_d].reshape(cols_f, ff_d)

            return body

        when(k == 0, own_columns(0))
        when(k == 1, own_columns(ff_d))
        wait_all(bias_far)
        own_sums = r.d_chipb[0]
        for chip in range(1, nc):
            own_sums = own_sums + r.d_chipb[chip]
        for plane in range(nf):

            def bias_columns(plane=plane):
                at = plane * cols_f
                o_bp[...] = own_sums[0, at : at + cols_f]
                o_b2[...] = own_sums[1, at : at + cols_f]
                kind, chip = 2 * plane // nc, 2 * plane % nc
                pieces = [r.d_chipb[chip + i, 2 + kind : 3 + kind, 0:chip_w] for i in range(2)]
                o_bqv[...] = jnp.concatenate(pieces, axis=1)[0]
                o_b1[...] = r.d_chipb[plane, 4, :]

            when(f == plane, bias_columns)
        c_swap.wait()
        d_silu = jnp.concatenate([r.c_all[f, 0], r.c_all[f, 1]], axis=1)
        cond_now = r.cond_own[...]
        gate = 1.0 / (1.0 + jnp.exp(-cond_now))
        o_cond[...] = d_silu * (gate * (1.0 + cond_now * (1.0 - gate)))
        f2_line.sent()
        sum_1.finish(o_1)
        sum_q.finish(r.all_q)
        o_q[...] = r.all_q[:, :q_w]
        o_p[...] = r.all_q[:, q_w:]
        assert wires.remote_count <= n_sem and wires.local_count <= 32

    return pl.pallas_call(
        kernel,
        out_shape=outs,
        in_specs=[ANYWHERE] * 2 + [ON_CHIP] * 8 + [ANYWHERE] * 5,
        out_specs=tuple([ON_CHIP] * len(outs)),
        scratch_shapes=list(scratch.values()),
        compiler_params=pltpu.CompilerParams(
            collective_id=0, has_side_effects=True, vmem_limit_bytes=63 * 2**20
        ),
        name="block",
    )(x, cot, frames, clips, *biases, cond, w_ada, wq, wp, w1, w2)


def land_kernel(arrays):
    count = len(arrays)

    def kernel(*refs):
        ins, results, sems = refs[:count], refs[count : 2 * count], refs[-1]
        copies = [pltpu.make_async_copy(a, b, sems.at[i]) for i, (a, b) in enumerate(zip(ins, results))]
        for copy in copies:
            copy.start()
        wait_all(copies)

    return pl.pallas_call(
        kernel,
        out_shape=tuple(jax.ShapeDtypeStruct(a.shape, a.dtype) for a in arrays),
        in_specs=[ON_CHIP] * count,
        out_specs=tuple([ANYWHERE] * count),
        scratch_shapes=[pltpu.SemaphoreType.DMA((count,))],
        name="land",
    )(*arrays)


def fits_block(n_dp, nf, width, ff, own, micro):
    nc = n_dp // 2
    return (
        nc == nf
        and nf == 4
        and width % (128 * nf) == 128
        and ff == 4 * width
        and (width // n_dp) % 16 == 0
        and (width // nc) % HEAD_DIM == 0
        and own % (2 * SUB) == 0
    )


def per_device(
    n_dp, nf, patches, cotangent, conditioning, frame_of_slot, clip_of_slot,
    w_ada, b_ada, w_qkv, b_qv, w_proj, b_proj, w_fc1, b_fc1, w_fc2, b_fc2,
):
    nc = n_dp // 2
    sizes = (nc, nf)
    micro, block, width = patches.shape
    own = micro * block
    clips = conditioning.shape[1]
    rows_d = width // n_dp
    cols_f = width // nf
    ff = w_fc1.shape[1] * nf
    ff_d = ff // n_dp
    chip_w = width // nc
    piece_q = math.gcd(3 * width // nf, chip_w)
    piece_1 = math.gcd(ff // nf, ff_d)
    dims = types.SimpleNamespace(
        nc=nc,
        nf=nf,
        per_q=3 * width // nf // piece_q,
        per_1=ff // nf // piece_1,
        chip_q=chip_w // piece_q,
        chip_1=ff // nc // piece_1,
    )
    dp = lax.axis_index("dp")
    f = lax.axis_index("fsdp")
    c, k = dp // 2, dp % 2

    q_send = w_qkv.reshape(rows_d, dims.per_q, piece_q).transpose(1, 0, 2)
    f1_send = w_fc1.reshape(rows_d, dims.per_1, piece_1).transpose(1, 0, 2)
    f2_send = w_fc2.T
    cond = conditioning.reshape(micro * clips, width)
    silu_cond = jax.nn.silu(cond)
    silu_low = silu_cond.astype(BF16)
    ada_w = w_ada.shape[1]
    silu_part = lax.dynamic_slice_in_dim(silu_low, dp * rows_d, rows_d, 1)
    mod_part = dot(silu_part, w_ada) + jnp.where(dp == 0, b_ada.astype(F32), 0.0)[None]
    mod_send = mod_part.reshape(-1, 2, ada_w // 2).transpose(1, 0, 2)
    cut = [0, 2 * cols_f, 3 * cols_f, 3 * cols_f + ff // nf, 4 * cols_f + ff // nf]
    cond_own = lax.dynamic_slice_in_dim(cond, f * cols_f, cols_f, 1)

    def ada_outputs(d_cols):
        grad_w_ada = precise(silu_part.astype(F32), d_cols, ((0,), (0,)))
        d_silu_part = precise(d_cols, w_ada.astype(F32), ((1,), (1,)))
        d_silu = cond_kernel(dims, d_silu_part).transpose(1, 0, 2).reshape(micro * clips, width)
        d_silu_own = lax.dynamic_slice_in_dim(d_silu, f * cols_f, cols_f, 1)
        _, silu_back = jax.vjp(jax.nn.silu, cond_own)
        cond_grad = silu_back(d_silu_own)[0].reshape(micro, clips, cols_f)
        return cond_grad, grad_w_ada, jnp.sum(d_cols, axis=0)

    if fits_block(n_dp, nf, width, ff, own, micro):
        results = block_kernel(
            dims, patches.reshape(own, width), cotangent.reshape(own, width), frame_of_slot,
            clip_of_slot, (b_qv, b_proj, b_fc1, b_fc2, b_ada), conditioning, w_ada, w_qkv, w_proj,
            w_fc1, w_fc2.T,
        )
        (
            output, input_grad, cond_grad, grad_ada, grad_b_ada, grad_qkv, grad_b_qv,
            grad_proj, grad_b_proj, grad_fc1, grad_b_fc1, grad_fc2, grad_b_fc2,
        ) = land_kernel(results)
        return (
            output.reshape(patches.shape),
            input_grad.reshape(patches.shape),
            cond_grad.reshape(micro, clips, cols_f),
            grad_ada,
            grad_b_ada,
            grad_qkv,
            grad_b_qv,
            grad_proj,
            grad_b_proj,
            grad_fc1,
            grad_b_fc1,
            grad_fc2.T,
            grad_b_fc2,
        )

    ids = jnp.stack([frame_of_slot.reshape(own), clip_of_slot.reshape(own)])
    ids = jnp.concatenate([ids, jnp.zeros((6, own), jnp.int32)])
    bias_send = jnp.concatenate([b_qv, b_proj, b_fc1, b_fc2]).astype(F32)[None]

    (x_all, c_all, ids_all, bias_all, mod_all, q_chip, f1_chip, p_chip, f2_chip, _, _) = start_kernel(
        dims, patches.reshape(own, width), cotangent.reshape(own, width), ids, bias_send, mod_send,
        q_send, f1_send, w_proj, f2_send,
    )
    group = nc * own
    modulation = mod_all.transpose(2, 0, 1, 3).reshape(micro * clips, 6 * width)
    q_parts = [
        q_chip[i].reshape(nc, 2, dims.chip_q, rows_d, piece_q).transpose(0, 1, 3, 2, 4).reshape(width, chip_w)
        for i in range(3)
    ]
    w1 = f1_chip.transpose(1, 2, 3, 0, 4).reshape(width, ff // nc)
    wp = p_chip.transpose(0, 2, 1, 3).reshape(chip_w, width)
    w2t = f2_chip.reshape(2, width, ff_d).transpose(1, 0, 2).reshape(width, 2 * ff_d)
    b_parts = [bias_all[:, 0, a:b].reshape(-1) for a, b in zip(cut[:-1], cut[1:])]
    bq = lax.dynamic_slice_in_dim(b_parts[0], c * chip_w, chip_w, 0)
    bv = lax.dynamic_slice_in_dim(b_parts[0], width + c * chip_w, chip_w, 0)
    b1 = lax.dynamic_slice_in_dim(b_parts[2], c * (ff // nc), ff // nc, 0)

    def hot_of(clip_ids):
        count = clip_ids.shape[0]
        row = (jnp.arange(count, dtype=jnp.int32) // block) % micro * clips + clip_ids
        return (row[:, None] == jnp.arange(micro * clips, dtype=jnp.int32)[None]).astype(F32)

    hot_group = hot_of(ids_all[:, 1].reshape(group))
    hot_own = hot_of(clip_of_slot.reshape(own))
    mod_group = precise(hot_group, modulation, ((1,), (0,)))
    mod_own = precise(hot_own, modulation, ((1,), (0,)))
    shift1, scale1 = mod_group[:, :width], mod_group[:, width : 2 * width]
    gate1 = mod_own[:, 2 * width : 3 * width]
    shift2, scale2 = mod_own[:, 3 * width : 4 * width], mod_own[:, 4 * width : 5 * width]
    gate2_group, gate2 = mod_group[:, 5 * width :], mod_own[:, 5 * width :]

    x_group = x_all.reshape(group, width).astype(F32)
    norm1, rstd1 = ln_parts(x_group)
    a_in = (norm1 * (1.0 + scale1) + shift1).astype(BF16)
    zero = jnp.zeros_like(bq)
    q, kk, v = [
        (dot(a_in, w) + b[None]).astype(BF16) for w, b in zip(q_parts, (bq, zero, bv))
    ]
    heads = chip_w // HEAD_DIM
    blocks = group // block
    q4, k4, v4 = [t.reshape(blocks, block, heads, HEAD_DIM) for t in (q, kk, v)]
    frames = ids_all[:, 0].reshape(blocks, block)
    same = (frames[:, :, None] == frames[:, None, :])[:, None]
    scores = jnp.einsum("bqhd,bkhd->bhqk", q4, k4, preferred_element_type=F32) * HEAD_DIM ** (-0.5)
    scores = jnp.where(same, scores, NEG_FILL)
    top = jnp.max(scores, axis=-1, keepdims=True)
    raised = jnp.exp(scores - top)
    probs = raised / jnp.sum(raised, axis=-1, keepdims=True)
    probs_low = probs.astype(BF16)
    mixed = jnp.einsum("bhqk,bkhd->bqhd", probs_low, v4, preferred_element_type=F32)
    mixed = mixed.reshape(group, chip_w).astype(BF16)
    attn_part = dot(mixed, wp)
    (attn_got,) = exchange(
        "attn_sum", 3, sizes, [(CHIP, SPREAD, attn_part.astype(BF16).reshape(nc, own, width))]
    )
    attn = jnp.sum(attn_got.astype(F32), axis=0) + b_parts[1][None]
    x_own = patches.reshape(own, width).astype(F32)
    after = x_own + gate1 * attn
    norm2, rstd2 = ln_parts(after)
    m_own = (norm2 * (1.0 + scale2) + shift2).astype(BF16)
    (m_all,) = exchange("m_gather", 4, sizes, [(CHIP, GATHER, m_own)])
    m_in = m_all.reshape(group, width)

    hidden = dot(m_in, w1) + b1[None]
    act, slope = gelu_both(hidden)
    act = act.astype(BF16)
    branch_part = dot_rt(act, w2t)
    cot_group = c_all.reshape(group, width).astype(F32)
    d_branch = (gate2_group * cot_group).astype(BF16)
    grad_2t = dot_lt(d_branch, act)
    d_hidden = (dot(d_branch, w2t) * slope).astype(BF16)
    grad_1 = dot_lt(m_in, d_hidden)
    d_m_part = dot_rt(d_hidden, w1)
    branch_got, d_m_got = exchange(
        "ff_sum",
        5,
        sizes,
        [
            (CHIP, SPREAD, d_m_part.astype(BF16).reshape(nc, own, width)),
            (CHIP, SPREAD, branch_part.astype(BF16).reshape(nc, own, width)),
        ],
    )[::-1]
    branch = jnp.sum(branch_got.astype(F32), axis=0) + b_parts[3][None]
    output = (after + gate2 * branch).astype(BF16)
    d_m = jnp.sum(d_m_got.astype(F32), axis=0)
    cot_own = cotangent.reshape(own, width).astype(F32)
    d_after = cot_own + ln_back(norm2, rstd2, d_m * (1.0 + scale2))
    d_attn = (gate1 * d_after).astype(BF16)
    (d_attn_all,) = exchange("d_attn_gather", 6, sizes, [(CHIP, GATHER, d_attn)])
    d_attn_group = d_attn_all.reshape(group, width)
    grad_p = dot_lt(mixed, d_attn_group)
    d_mix = dot_rt(d_attn_group, wp).astype(BF16).reshape(blocks, block, heads, HEAD_DIM)
    d_probs = jnp.einsum("bqhd,bkhd->bhqk", d_mix, v4, preferred_element_type=F32)
    d_scores = probs * (d_probs - jnp.sum(probs * d_probs, axis=-1, keepdims=True))
    d_scores = d_scores.astype(BF16)
    dq = jnp.einsum("bhqk,bkhd->bqhd", d_scores, k4, preferred_element_type=F32) * HEAD_DIM ** (-0.5)
    dk = jnp.einsum("bhqk,bqhd->bkhd", d_scores, q4, preferred_element_type=F32) * HEAD_DIM ** (-0.5)
    dv = jnp.einsum("bhqk,bqhd->bkhd", probs_low, d_mix, preferred_element_type=F32)
    dqkv = [t.reshape(group, chip_w).astype(BF16) for t in (dq, dk, dv)]
    d_a_part = sum(dot_rt(t, w) for t, w in zip(dqkv, q_parts))
    grad_q = jnp.stack([dot_lt(a_in, t) for t in dqkv])
    (d_a_got,) = exchange(
        "d_a_sum", 7, sizes, [(CHIP, SPREAD, d_a_part.astype(BF16).reshape(nc, own, width))]
    )
    d_a = jnp.sum(d_a_got.astype(F32), axis=0)
    norm1_own, rstd1_own = ln_parts(x_own)
    scale1_own = mod_own[:, width : 2 * width]
    input_grad = (d_after + ln_back(norm1_own, rstd1_own, d_a * (1.0 + scale1_own))).astype(BF16)

    g_q = grad_q.reshape(3, nc, 2, rows_d, dims.chip_q, piece_q).transpose(2, 1, 0, 4, 3, 5)
    g_1 = grad_1.reshape(nc, 2, rows_d, dims.chip_1, piece_1).transpose(1, 0, 3, 2, 4)
    g_p = grad_p.reshape(2, rows_d, nf, cols_f).transpose(0, 2, 1, 3)
    g_2 = grad_2t.reshape(nf, cols_f, 2, ff_d).transpose(2, 0, 1, 3)
    got = exchange("grad_core", 8, sizes, [(CORE, SPREAD, g.astype(BF16)) for g in (g_q, g_1, g_p, g_2)])
    s_q, s_1, s_p, s_2 = [jnp.sum(g.astype(F32), axis=0).astype(BF16) for g in got]
    r_q, r_1 = exchange("grad_chip", 9, sizes, [(CHIP, SPREAD, s_q), (CHIP, SPREAD, s_1)])
    z_q = r_q.transpose(1, 0, 2, 3, 4).reshape(nf, dims.per_q, rows_d, piece_q)
    z_1 = r_1.reshape(nf, dims.per_1, rows_d, piece_1)
    got = exchange("grad_plane", 10, sizes, [(PLANE, SPREAD, g) for g in (z_q, z_1, s_p, s_2)])
    o_q, o_1, o_p, o_2 = [jnp.sum(g.astype(F32), axis=0) for g in got]
    grad_w_qkv = o_q.transpose(1, 0, 2).reshape(rows_d, 3 * width // nf)
    grad_w_fc1 = o_1.transpose(1, 0, 2).reshape(rows_d, ff // nf)
    grad_w_fc2 = o_2.T

    d_token = jnp.concatenate(
        [d_a, d_a * norm1_own, d_after * attn, d_m, d_m * norm2, cot_own * branch], axis=1
    )
    d_mod = precise(hot_own, d_token, ((0,), (0,)))
    d_branch_own = (gate2 * cot_own).astype(BF16).astype(F32)

    def columns(value):
        return jnp.sum(value.astype(F32), axis=0)

    def spread(value, count):
        return lax.dynamic_update_slice_in_dim(
            jnp.zeros((count,), F32), value, c * value.shape[0], 0
        )

    g_bqv = jnp.concatenate([spread(columns(dqkv[0]), width), spread(columns(dqkv[2]), width)])
    g_b1 = spread(columns(d_hidden), ff)
    bias_terms = jnp.concatenate(
        [
            g_bqv.reshape(nf, -1),
            columns(d_attn).reshape(nf, -1),
            g_b1.reshape(nf, -1),
            columns(d_branch_own).reshape(nf, -1),
        ],
        axis=1,
    )
    n_bias = bias_terms.shape[1]
    bias_rows = -(-n_bias // ada_w)
    bias_terms = jnp.pad(bias_terms, ((0, 0), (0, bias_rows * ada_w - n_bias)))
    terms = jnp.concatenate(
        [d_mod.reshape(micro * clips, nf, ada_w).transpose(1, 0, 2), bias_terms.reshape(nf, bias_rows, ada_w)],
        axis=1,
    )
    pad_rows = -terms.shape[1] % 8
    terms = jnp.pad(terms, ((0, 0), (0, pad_rows), (0, 0)))
    terms = terms.reshape(nf, -1, 2, ada_w // 2).transpose(0, 2, 1, 3)
    total = sum_small_kernel(dims, terms).transpose(1, 0, 2).reshape(-1, ada_w)
    d_cols = total[: micro * clips]
    bias_sums = total[micro * clips : micro * clips + bias_rows].reshape(-1)[:n_bias]
    g_parts = [bias_sums[a:b] for a, b in zip(cut[:-1], cut[1:])]
    cond_grad, grad_w_ada, grad_b_ada = ada_outputs(d_cols)
    return (
        output.reshape(patches.shape),
        input_grad.reshape(patches.shape),
        cond_grad,
        grad_w_ada,
        grad_b_ada,
        grad_w_qkv,
        g_parts[0],
        o_p,
        g_parts[1],
        grad_w_fc1,
        g_parts[2],
        grad_w_fc2,
        g_parts[3],
    )


def solution(mesh):
    tokens = P(None, ("dp", "fsdp"), None)
    ids = P(None, ("dp", "fsdp"))
    both, cols = P("dp", "fsdp"), P("fsdp")
    in_specs = (tokens, tokens, P(), ids, ids) + (both, cols) * 5
    out_specs = (tokens, tokens, P(None, None, "fsdp")) + (both, cols) * 5
    return jax.shard_map(
        functools.partial(per_device, mesh.shape["dp"], mesh.shape["fsdp"]),
        mesh=mesh,
        in_specs=in_specs,
        out_specs=out_specs,
        check_vma=False,
    )
```

```python
import functools
import math
import types

import jax
import jax.numpy as jnp
from jax import lax
from jax.experimental import pallas as pl
from jax.experimental.pallas import tpu as pltpu
from jax.sharding import PartitionSpec as P

HEAD_DIM = 72
EPS = 1e-06
GELU_C = math.sqrt(2.0 / math.pi)
PRECISE = lax.Precision.HIGHEST
NEG_FILL = -1e30
SUB = 16
CORE, CHIP, PLANE, ALL = range(4)
GATHER, SPREAD = range(2)
MESH_ID = pl.DeviceIdType.MESH
F32 = jnp.float32
BF16 = jnp.bfloat16


def xor_of(index, step, size):
    result, bit = 0, 1
    while bit < size:
        mine = (index // bit) % 2
        result = result + ((mine + (step // bit) % 2) % 2) * bit
        bit *= 2
    return result


class Place:
    def __init__(self, n_chip, n_plane):
        self.n = {CORE: 2, CHIP: n_chip, PLANE: n_plane, ALL: 2 * n_chip}
        self.dp = lax.axis_index("dp")
        self.f = lax.axis_index("fsdp")
        self.c = self.dp // 2
        self.k = self.dp % 2

    def index(self, axis):
        return {CORE: self.k, CHIP: self.c, PLANE: self.f, ALL: self.dp}[axis]

    def peer(self, axis, step):
        other = xor_of(self.index(axis), step, self.n[axis])
        if axis == CORE:
            return other, (self.c * 2 + other, self.f)
        if axis == CHIP:
            return other, (other * 2 + self.k, self.f)
        if axis == PLANE:
            return other, (self.dp, other)
        return other, (other, self.f)


def greet(place, axes):
    barrier = pltpu.get_barrier_semaphore()
    count = 0
    for axis in axes:
        for step in range(1, place.n[axis]):
            pl.semaphore_signal(
                barrier, inc=1, device_id=place.peer(axis, step)[1], device_id_type=MESH_ID
            )
            count += 1
    pl.semaphore_wait(barrier, count)


class Wires:
    def __init__(self, send, recv, local):
        self.send, self.recv, self.local = send, recv, local
        self.remote_count = 0
        self.local_count = 0

    def far(self, src, dst, device):
        at = self.remote_count
        self.remote_count += 1
        copy = pltpu.make_async_remote_copy(
            src_ref=src,
            dst_ref=dst,
            send_sem=self.send.at[at],
            recv_sem=self.recv.at[at],
            device_id=device,
            device_id_type=MESH_ID,
        )
        copy.start()
        return copy

    def near(self, src, dst):
        at = self.local_count
        self.local_count += 1
        copy = pltpu.make_async_copy(src, dst, self.local.at[at])
        copy.start()
        return copy


def wait_all(copies):
    for copy in copies:
        copy.wait()


ANYWHERE = pl.BlockSpec(memory_space=pl.ANY)
ON_CHIP = pl.BlockSpec(memory_space=pltpu.VMEM)


def exchange(name, collective_id, sizes, items):
    n_chip, n_plane = sizes
    n_of = {CORE: 2, CHIP: n_chip, PLANE: n_plane, ALL: 2 * n_chip}
    axes = sorted({item[0] for item in items})
    outs = []
    n_far = 0
    for axis, kind, array in items:
        n_far += n_of[axis] - 1
        shape = array.shape if kind == SPREAD else (n_of[axis],) + array.shape
        outs.append(jax.ShapeDtypeStruct(shape, array.dtype))

    def kernel(*refs):
        ins = refs[: len(items)]
        results = refs[len(items) : 2 * len(items)]
        place = Place(n_chip, n_plane)
        wires = Wires(*refs[2 * len(items) :])
        greet(place, axes)
        copies = []
        for (axis, kind, _), src, dst in zip(items, ins, results):
            mine = place.index(axis)
            for step in range(1, n_of[axis]):
                other, device = place.peer(axis, step)
                piece = src if kind == GATHER else src.at[other]
                copies.append(wires.far(piece, dst.at[mine], device))
        for (axis, kind, _), src, dst in zip(items, ins, results):
            mine = place.index(axis)
            copies.append(wires.near(src if kind == GATHER else src.at[mine], dst.at[mine]))
        wait_all(copies)

    return pl.pallas_call(
        kernel,
        out_shape=tuple(outs),
        in_specs=[ANYWHERE] * len(items),
        out_specs=tuple([ANYWHERE] * len(items)),
        scratch_shapes=[
            pltpu.SemaphoreType.DMA((n_far,)),
            pltpu.SemaphoreType.DMA((n_far,)),
            pltpu.SemaphoreType.DMA((len(items),)),
        ],
        compiler_params=pltpu.CompilerParams(collective_id=collective_id, has_side_effects=True),
        name=name,
    )(*[item[2] for item in items])


def start_kernel(dims, x, cot, ids, bias, mod, wq, w1, wp, w2):
    nc, nf = dims.nc, dims.nf
    per_q, per_1 = dims.per_q, dims.per_1
    chip_q, chip_1 = dims.chip_q, dims.chip_1
    part_q = nc * chip_q
    rows, half = mod.shape[1], mod.shape[2]
    n_far = 5 * (nf - 1) + 3 * (nc - 1) + 4 * (nc - 1) + 4 + 1 + (nc - 1) + (nf - 1) + 1
    outs = (
        jax.ShapeDtypeStruct((nc,) + x.shape, x.dtype),
        jax.ShapeDtypeStruct((nc,) + cot.shape, cot.dtype),
        jax.ShapeDtypeStruct((nc,) + ids.shape, ids.dtype),
        jax.ShapeDtypeStruct((nf,) + bias.shape, bias.dtype),
        jax.ShapeDtypeStruct((nf, 2, rows, half), F32),
        jax.ShapeDtypeStruct((3, nc, 2, chip_q) + wq.shape[1:], BF16),
        jax.ShapeDtypeStruct((chip_1, nc, 2) + w1.shape[1:], BF16),
        jax.ShapeDtypeStruct((2, nf) + wp.shape, BF16),
        jax.ShapeDtypeStruct((2, nf) + w2.shape, BF16),
        jax.ShapeDtypeStruct((nf * per_q,) + wq.shape[1:], BF16),
        jax.ShapeDtypeStruct((nf * per_1,) + w1.shape[1:], BF16),
    )

    def kernel(
        x_in, c_in, i_in, b_in, m_in, q_in, f1_in, p_in, f2_in,
        x_all, c_all, i_all, b_all, m_all, q_chip, f1_chip, p_chip, f2_chip, q_rows, f1_rows,
        m_core, m_sum, m_chip, send, recv, local,
    ):
        place = Place(nc, nf)
        wires = Wires(send, recv, local)
        c, k, f = place.c, place.k, place.f
        greet(place, (CORE, CHIP, PLANE))
        core_other, core_peer = place.peer(CORE, 1)
        chip_peers = [place.peer(CHIP, step) for step in range(1, nc)]
        plane_peers = [place.peer(PLANE, step) for step in range(1, nf)]

        m_first = wires.far(m_in.at[core_other], m_core, core_peer)
        q_got, f1_got, p_got, f2_got, small = [], [], [], [], []
        for _, peer in plane_peers:
            q_got.append(wires.far(q_in, q_rows.at[pl.ds(f * per_q, per_q)], peer))
            small.append(wires.far(b_in, b_all.at[f], peer))
        q_got.append(wires.near(q_in, q_rows.at[pl.ds(f * per_q, per_q)]))
        small.append(wires.near(b_in, b_all.at[f]))
        for _, peer in chip_peers:
            small.append(wires.far(i_in, i_all.at[c], peer))
            small.append(wires.far(x_in, x_all.at[c], peer))
        m_first.wait()
        m_sum[...] = m_in[k] + m_core[...]
        m_chip[c] = m_sum[...]
        m_second = [wires.far(m_sum, m_chip.at[c], peer) for _, peer in chip_peers]
        for _, peer in plane_peers:
            p_got.append(wires.far(p_in, p_chip.at[k, f], peer))
        for _, peer in plane_peers:
            f1_got.append(wires.far(f1_in, f1_rows.at[pl.ds(f * per_1, per_1)], peer))
        for _, peer in plane_peers:
            f2_got.append(wires.far(f2_in, f2_chip.at[k, f], peer))
        p_got.append(wires.near(p_in, p_chip.at[k, f]))
        f1_got.append(wires.near(f1_in, f1_rows.at[pl.ds(f * per_1, per_1)]))
        f2_got.append(wires.near(f2_in, f2_chip.at[k, f]))
        small.append(wires.near(i_in, i_all.at[c]))
        small.append(wires.near(x_in, x_all.at[c]))
        for _, peer in chip_peers:
            small.append(wires.far(c_in, c_all.at[c], peer))
        small.append(wires.near(c_in, c_all.at[c]))
        wait_all(m_second)
        total = m_chip[0]
        for other in range(1, nc):
            total = total + m_chip[other]
        m_all[f, k] = total
        wait_all([wires.far(m_all.at[f, k], m_all.at[f, k], peer) for _, peer in plane_peers])
        m_last = wires.far(m_all.at[:, k], m_all.at[:, k], core_peer)

        wait_all(q_got)
        q_moved = []
        for kind in range(3):
            for other, peer in chip_peers:
                q_moved.append(
                    wires.far(
                        q_rows.at[pl.ds(kind * part_q + other * chip_q, chip_q)],
                        q_chip.at[kind, c, k],
                        peer,
                    )
                )
            q_moved.append(
                wires.near(
                    q_rows.at[pl.ds(kind * part_q + c * chip_q, chip_q)], q_chip.at[kind, c, k]
                )
            )
        wait_all(p_got)
        last = [m_last, wires.far(p_chip.at[k], p_chip.at[k], core_peer)]
        wait_all(q_moved)
        last.append(wires.far(q_chip.at[:, :, k], q_chip.at[:, :, k], core_peer))
        wait_all(f1_got)
        f1_moved = []
        for other, peer in chip_peers:
            f1_moved.append(
                wires.far(f1_rows.at[pl.ds(other * chip_1, chip_1)], f1_chip.at[:, c, k], peer)
            )
        f1_moved.append(
            wires.near(f1_rows.at[pl.ds(c * chip_1, chip_1)], f1_chip.at[:, c, k])
        )
        wait_all(f2_got)
        last.append(wires.far(f2_chip.at[k], f2_chip.at[k], core_peer))
        wait_all(f1_moved)
        last.append(wires.far(f1_chip.at[:, :, k], f1_chip.at[:, :, k], core_peer))
        wait_all(small)
        wait_all(last)

    return pl.pallas_call(
        kernel,
        out_shape=outs,
        in_specs=[ANYWHERE] * 4 + [ON_CHIP] + [ANYWHERE] * 4,
        out_specs=tuple([ANYWHERE] * 4 + [ON_CHIP] + [ANYWHERE] * 6),
        scratch_shapes=[
            pltpu.VMEM((rows, half), F32),
            pltpu.VMEM((rows, half), F32),
            pltpu.VMEM((nc, rows, half), F32),
            pltpu.SemaphoreType.DMA((n_far,)),
            pltpu.SemaphoreType.DMA((n_far,)),
            pltpu.SemaphoreType.DMA((12,)),
        ],
        compiler_params=pltpu.CompilerParams(collective_id=0, has_side_effects=True),
        name="start",
    )(x, cot, ids, bias, mod, wq, w1, wp, w2)


def sum_small_kernel(dims, terms):
    nc, nf = dims.nc, dims.nf
    _, _, rows, half = terms.shape
    n_far = (nf - 1) + 1 + (nc - 1) + 1

    def kernel(t_in, total, z_got, both, core_got, chip_got, send, recv, local):
        place = Place(nc, nf)
        wires = Wires(send, recv, local)
        c, k, f = place.c, place.k, place.f
        greet(place, (CORE, CHIP, PLANE))
        core_other, core_peer = place.peer(CORE, 1)
        copies = []
        for step in range(1, nf):
            other, peer = place.peer(PLANE, step)
            copies.append(wires.far(t_in.at[other], z_got.at[f], peer))
        z_got[f] = t_in[f]
        wait_all(copies)
        value = z_got[0]
        for other in range(1, nf):
            value = value + z_got[other]
        both[...] = value
        wires.far(both.at[core_other], core_got, core_peer).wait()
        chip_got[c] = both[k] + core_got[...]
        copies = []
        for step in range(1, nc):
            _, peer = place.peer(CHIP, step)
            copies.append(wires.far(chip_got.at[c], chip_got.at[c], peer))
        wait_all(copies)
        value = chip_got[0]
        for other in range(1, nc):
            value = value + chip_got[other]
        total[k] = value
        wires.far(total.at[k], total.at[k], core_peer).wait()

    return pl.pallas_call(
        kernel,
        out_shape=jax.ShapeDtypeStruct((2, rows, half), F32),
        in_specs=[ON_CHIP],
        out_specs=ON_CHIP,
        scratch_shapes=[
            pltpu.VMEM((nf, 2, rows, half), F32),
            pltpu.VMEM((2, rows, half), F32),
            pltpu.VMEM((rows, half), F32),
            pltpu.VMEM((nc, rows, half), F32),
            pltpu.SemaphoreType.DMA((n_far,)),
            pltpu.SemaphoreType.DMA((n_far,)),
            pltpu.SemaphoreType.DMA((1,)),
        ],
        compiler_params=pltpu.CompilerParams(collective_id=1, has_side_effects=True),
        name="sum_small",
    )(terms)


def cond_kernel(dims, part):
    nc, nf = dims.nc, dims.nf
    nd = 2 * nc
    rows, width = part.shape
    n_far = (nf - 1) + (nd - 1)

    def kernel(p_in, out, got, send, recv, local):
        place = Place(nc, nf)
        wires = Wires(send, recv, local)
        greet(place, (PLANE, ALL))
        copies = []
        for step in range(1, nf):
            copies.append(wires.far(p_in, got.at[place.f], place.peer(PLANE, step)[1]))
        got[place.f] = p_in[...]
        wait_all(copies)
        value = got[0]
        for other in range(1, nf):
            value = value + got[other]
        out[place.dp] = value
        copies = []
        for step in range(1, nd):
            copies.append(
                wires.far(out.at[place.dp], out.at[place.dp], place.peer(ALL, step)[1])
            )
        wait_all(copies)

    return pl.pallas_call(
        kernel,
        out_shape=jax.ShapeDtypeStruct((nd, rows, width), F32),
        in_specs=[ON_CHIP],
        out_specs=ON_CHIP,
        scratch_shapes=[
            pltpu.VMEM((nf, rows, width), F32),
            pltpu.SemaphoreType.DMA((n_far,)),
            pltpu.SemaphoreType.DMA((n_far,)),
            pltpu.SemaphoreType.DMA((1,)),
        ],
        compiler_params=pltpu.CompilerParams(collective_id=2, has_side_effects=True),
        name="cond_sum",
    )(part)


def dot(left, right):
    return jnp.dot(left, right, preferred_element_type=F32)


def dot_rt(left, right):
    return lax.dot_general(left, right, (((1,), (1,)), ((), ())), preferred_element_type=F32)


def dot_lt(left, right):
    return lax.dot_general(left, right, (((0,), (0,)), ((), ())), preferred_element_type=F32)


def precise(left, right, dims):
    return lax.dot_general(
        left, right, (dims, ((), ())), precision=PRECISE, preferred_element_type=F32
    )


def ln_parts(values):
    centre = values - jnp.mean(values, axis=-1, keepdims=True)
    scale = lax.rsqrt(jnp.mean(centre * centre, axis=-1, keepdims=True) + EPS)
    return centre * scale, scale


def ln_back(normal, scale, grad):
    return scale * (
        grad
        - jnp.mean(grad, axis=-1, keepdims=True)
        - normal * jnp.mean(grad * normal, axis=-1, keepdims=True)
    )


def gelu_both(h):
    square = h * h
    t = jnp.tanh(GELU_C * (h + 0.044715 * h * square))
    value = 0.5 * h * (1.0 + t)
    slope = 0.5 * (1.0 + t) + 0.5 * h * (1.0 - t * t) * GELU_C * (1.0 + 3 * 0.044715 * square)
    return value, slope


def dot3(left, right):
    wide_left = left.dtype == F32
    value = left if wide_left else right
    total = None
    for _ in range(3):
        term = value.astype(BF16)
        value = value - term.astype(F32)
        part = dot(term, right) if wide_left else dot(left, term)
        total = part if total is None else total + part
    return total


def add_low(left, right):
    return (left.astype(F32) + right.astype(F32)).astype(BF16)


def block_kernel(dims, x, cot, frames, clips, biases, cond, w_ada, wq, wp, w1, w2):
    nc, nf = dims.nc, dims.nf
    own, width = x.shape
    group = nc * own
    rows_d, q_w = wq.shape
    chip_w = q_w // 3
    cols_f, ff_d = w2.shape
    ff_c = 2 * ff_d
    ada_w = w_ada.shape[1]
    n_bias = sum(item.shape[0] for item in biases)
    heads = chip_w // HEAD_DIM
    micro, n_clips, _ = cond.shape
    n_rows = micro * n_clips
    half = n_rows // 2
    n_sub = own // SUB
    head_scale = HEAD_DIM ** (-0.5)
    last = nf - 2
    third = rows_d // 3

    outs = (
        jax.ShapeDtypeStruct((own, width), BF16),
        jax.ShapeDtypeStruct((own, width), BF16),
        jax.ShapeDtypeStruct((n_rows, cols_f), F32),
        jax.ShapeDtypeStruct((rows_d, ada_w), F32),
        jax.ShapeDtypeStruct((ada_w,), F32),
        jax.ShapeDtypeStruct((rows_d, q_w), F32),
        jax.ShapeDtypeStruct((2 * chip_w,), F32),
        jax.ShapeDtypeStruct((rows_d, cols_f), F32),
        jax.ShapeDtypeStruct((cols_f,), F32),
        jax.ShapeDtypeStruct((rows_d, ff_c), F32),
        jax.ShapeDtypeStruct((ff_c,), F32),
        jax.ShapeDtypeStruct((cols_f, ff_d), F32),
        jax.ShapeDtypeStruct((cols_f,), F32),
    )
    tokens = (nc, own, width)
    n_sem = 240
    scratch = dict(
        xg=pltpu.VMEM(tokens, BF16),
        cg=pltpu.VMEM(tokens, BF16),
        idsg=pltpu.VMEM((nc, 2, own), F32),
        biasg=pltpu.VMEM((nf, 1, n_bias), F32),
        ada=pltpu.VMEM(w_ada.shape, BF16),
        silu=pltpu.VMEM((n_rows, rows_d), BF16),
        cond_own=pltpu.VMEM((n_rows, cols_f), F32),
        m_part=pltpu.VMEM((2, half, ada_w), F32),
        m_core=pltpu.VMEM((half, ada_w), F32),
        m_chip=pltpu.VMEM((nc, half, ada_w), F32),
        m_z=pltpu.VMEM((nf, 2, half, ada_w), F32),
        m_tab=pltpu.VMEM((n_rows, 6 * width), F32),
        tab=pltpu.VMEM((3, nc * n_sub, width), F32),
        own_tab=pltpu.VMEM((6, n_sub, width), F32),
        q_z=pltpu.VMEM((nf, rows_d, q_w + cols_f), BF16),
        q_rows=pltpu.VMEM((nf * 3, third, q_w), BF16),
        q_got=pltpu.VMEM((3, nc, third, q_w), BF16),
        w_q=pltpu.VMEM((nc, 2, rows_d, q_w), BF16),
        y_got=pltpu.VMEM((nc, rows_d, q_w), BF16),
        f1_z=pltpu.VMEM((nf, rows_d, ff_c), BF16),
        w_1=pltpu.VMEM((nc, 2, rows_d, ff_c), BF16),
        p_got=pltpu.VMEM((2, nf, rows_d, cols_f), BF16),
        w_p=pltpu.VMEM((chip_w, width), BF16),
        f2_half=pltpu.VMEM((cols_f, ff_d), BF16),
        f2_got=pltpu.VMEM((rows_d, ff_d), BF16),
        w_2=pltpu.VMEM((nf, 2, rows_d, ff_c), BF16),
        a_in=pltpu.VMEM(tokens, BF16),
        qkv=pltpu.VMEM((3, nc, own, chip_w), BF16),
        probs=pltpu.VMEM((nc * heads, own, own), F32),
        mixed=pltpu.VMEM((nc, own, chip_w), BF16),
        sum_s=pltpu.VMEM(tokens, BF16),
        sum_r=pltpu.VMEM((2, own, width), BF16),
        sum_st=pltpu.VMEM((2, own // 2, width), BF16),
        br_s=pltpu.VMEM(tokens, BF16),
        br_r=pltpu.VMEM((2, own, width), BF16),
        br_st=pltpu.VMEM((2, own // 2, width), BF16),
        m_all=pltpu.VMEM(tokens, BF16),
        da_all=pltpu.VMEM(tokens, BF16),
        attn=pltpu.VMEM((own, width), F32),
        after=pltpu.VMEM((own, width), F32),
        d_after=pltpu.VMEM((own, width), F32),
        hid=pltpu.VMEM((own, ff_c), F32),
        act=pltpu.VMEM((nc, own, ff_c), BF16),
        d_hid=pltpu.VMEM((nc, own, ff_c), BF16),
        dbr=pltpu.VMEM(tokens, BF16),
        d_qkv=pltpu.VMEM((nc, own, q_w), BF16),
        g_2=pltpu.VMEM((nf, 2, rows_d, ff_c), BF16),
        g_2r=pltpu.VMEM((nf, rows_d, ff_c), BF16),
        g_1r=pltpu.VMEM((nc, rows_d, ff_c), BF16),
        g_qr=pltpu.VMEM((nc, rows_d, q_w), BF16),
        g_pr=pltpu.VMEM((rows_d, width), BF16),
        got_q=pltpu.VMEM((2, nf - 1, rows_d, q_w + cols_f), BF16),
        got_1=pltpu.VMEM((2, nf - 1, rows_d, ff_c), BF16),
        got_2=pltpu.VMEM((2, nf - 1, rows_d, ff_c), BF16),
        all_2=pltpu.VMEM((2, rows_d, ff_c), F32),
        sub=pltpu.VMEM((6, n_sub, width), F32),
        q_nat=pltpu.VMEM((rows_d, q_w), BF16),
        p_nat=pltpu.VMEM((rows_d, cols_f), BF16),
        all_q=pltpu.VMEM((rows_d, q_w + cols_f), F32),
        sub_lin=pltpu.VMEM((2, nc * n_sub, width), F32),
        sub_gate=pltpu.VMEM((nc * n_sub, width), F32),
        d_part=pltpu.VMEM((2, half, 6 * width), F32),
        d_core=pltpu.VMEM((half, 6 * width), F32),
        d_cut=pltpu.VMEM((nf, half, ada_w), BF16),
        d_bias=pltpu.VMEM((8, width), F32),
        dz=pltpu.VMEM((nf, half, ada_w), BF16),
        dzb=pltpu.VMEM((nf, 8, width), BF16),
        d_tot=pltpu.VMEM((2, half, ada_w), F32),
        d_low=pltpu.VMEM((8, width), BF16),
        d_bsum=pltpu.VMEM((8, width), F32),
        d_coreb=pltpu.VMEM((8, width), F32),
        d_chipb=pltpu.VMEM((nc, 8, width), F32),
        c_part=pltpu.VMEM((nf, n_rows, rows_d), F32),
        c_all=pltpu.VMEM((nc, 2, n_rows, rows_d), F32),
        send=pltpu.SemaphoreType.DMA((n_sem,)),
        recv=pltpu.SemaphoreType.DMA((n_sem,)),
        local=pltpu.SemaphoreType.DMA((40,)),
    )
    names = list(scratch)

    def kernel(
        x_in, c_in, frames_in, clips_in, bq_in, bp_in, b1_in, b2_in, ba_in, cond_in, ada_in,
        q_in, p_in, f1_in, f2_in,
        *rest,
    ):
        homes, rest = rest[: len(outs)], rest[len(outs) :]
        held, rest = rest[: len(outs)], rest[len(outs) :]
        (out, x_grad, o_cond, o_ada, o_bada, o_q, o_bqv, o_p, o_bp, o_1, o_b1, o_2, o_b2) = held
        home_of = {id(ref): home for ref, home in zip(held, homes)}
        landed = []
        r = types.SimpleNamespace(**dict(zip(names, rest)))
        place = Place(nc, nf)
        wires = Wires(r.send, r.recv, r.local)
        c, k, f = place.c, place.k, place.f
        core_o, core_dev = place.peer(CORE, 1)
        chip_peers = [place.peer(CHIP, step) for step in range(1, nc)]
        plane_peers = [place.peer(PLANE, step) for step in range(1, nf)]

        def loop(count, body, unroll=1):
            def run(i, carry):
                body(i)
                return carry

            lax.fori_loop(0, count, run, 0, unroll=unroll)

        def loop_rows(body):
            loop(n_sub, body, 2)

        def when(condition, body):
            pl.when(condition)(body)

        def sub_rows(g):
            return pl.ds(pl.multiple_of(g * SUB, SUB), SUB)

        def reserve(count):
            base = wires.remote_count
            wires.remote_count += count
            return base

        def pair(src, dst, device, send_at, recv_at):
            return pltpu.make_async_remote_copy(
                src_ref=src,
                dst_ref=dst,
                send_sem=r.send.at[send_at],
                recv_sem=r.recv.at[recv_at],
                device_id=device,
                device_id_type=MESH_ID,
            )

        chip_x, dev_x = place.peer(CHIP, 1)
        chip_y, dev_y = place.peer(CHIP, 2)
        chip_d, _ = place.peer(CHIP, 3)
        first_half, second_half = pl.ds(0, own // 2), pl.ds(own // 2, own // 2)

        class Share:
            def __init__(self, ref, src=None):
                def copy(chip, rows, device, at, own_src=None):
                    from_ref = ref.at[chip, rows] if own_src is None else own_src.at[rows]
                    return pair(from_ref, ref.at[chip, rows], device, at, at)

                at = reserve(6)
                self.x_a = copy(c, first_half, dev_x, at, src)
                self.x_b = copy(c, second_half, dev_x, at + 1, src)
                self.y_b = copy(c, second_half, dev_y, at + 2, src)
                self.y_a = copy(c, first_half, dev_y, at + 3, src)
                self.on_y = copy(chip_x, first_half, dev_y, at + 4)
                self.on_x = copy(chip_y, second_half, dev_x, at + 5)

            def start(self):
                for item in (self.x_a, self.y_b, self.x_b, self.y_a):
                    item.start()

            def relay(self):
                self.x_a.wait_recv()
                self.on_y.start()
                self.y_b.wait_recv()
                self.on_x.start()

            def arrive(self, step):
                if step == 1:
                    self.x_b.wait_recv()
                elif step == 2:
                    self.y_a.wait_recv()
                else:
                    self.on_y.wait_recv()
                    self.on_x.wait_recv()

            def sent(self):
                for item in (self.x_a, self.x_b, self.y_b, self.y_a, self.on_y, self.on_x):
                    item.wait_send()

        class Merge:
            def __init__(self, terms, got, stage):
                self.terms, self.got, self.stage = terms, got, stage
                at = reserve(6)
                self.d_x = pair(terms.at[chip_d, first_half], stage.at[0], dev_x, at, at)
                self.d_y = pair(terms.at[chip_d, second_half], stage.at[1], dev_y, at + 1, at + 1)

                def copy(chip, rows, to, device, index):
                    return pair(
                        terms.at[chip, rows], got.at[to, rows], device, at + index, at + index
                    )

                self.x_a = copy(chip_x, first_half, 0, dev_x, 2)
                self.x_b = copy(chip_x, second_half, 0, dev_x, 3)
                self.y_b = copy(chip_y, second_half, 1, dev_y, 4)
                self.y_a = copy(chip_y, first_half, 1, dev_y, 5)

            def put(self, step, blk, part):
                self.terms[blk] = part

                def far():
                    self.d_x.start()
                    self.d_y.start()

                when(step == 3, far)
                when(step == 2, self.y_b.start)
                when(step == 1, self.x_a.start)

            def launch(self):
                for item in (self.d_x, self.d_y, self.y_b, self.x_a):
                    item.start()

            def combine(self):
                self.d_y.wait()
                ref = self.terms.at[chip_x, second_half]
                ref[...] = add_low(ref[...], self.stage[1])
                self.x_b.start()
                self.d_x.wait()
                ref = self.terms.at[chip_y, first_half]
                ref[...] = add_low(ref[...], self.stage[0])
                self.y_a.start()

            def finish(self):
                for item in (self.x_a, self.x_b, self.y_b, self.y_a):
                    item.wait()

            def rows(self, at):
                value = self.terms[c, at, :].astype(F32) + self.got[0, at, :].astype(F32)
                return value + self.got[1, at, :].astype(F32)

        def land(*refs):
            for ref in refs:
                landed.append(wires.near(ref, home_of[id(ref)]))

        up, down = (place.dp, f + 1), (place.dp, f - 1)

        class Gather:
            def __init__(self, slot):
                self.slot = slot
                self.up, self.down = reserve(nf - 1), reserve(nf - 1)

            def both(self, step, src=None):
                above = pair(
                    self.slot(f - step) if src is None else src,
                    self.slot(f - step), up, self.up + step, self.up + step,
                )
                below = pair(
                    self.slot(f + step) if src is None else src,
                    self.slot(f + step), down, self.down + step, self.down + step,
                )
                return (
                    ((f - step >= 0) & (f < nf - 1), above),
                    ((f + step <= nf - 1) & (f > 0), below),
                )

            def start(self, step, src=None):
                for condition, copy in self.both(step, src):
                    when(condition, copy.start)

            def arrive(self, step, then=None, wait=True):
                for condition, got, base in (
                    (f - 1 - step >= 0, f - 1 - step, self.up),
                    (f + 1 + step <= nf - 1, f + 1 + step, self.down),
                ):

                    def body(got=got, base=base):
                        slot = self.slot(got)
                        if wait:
                            pair(slot, slot, core_dev, base + step, base + step).wait_recv()
                        if then is not None:
                            then(got)

                    when(condition, body)

            def sent(self, src=None):
                for step in range(nf - 1):
                    for condition, copy in self.both(step, src if step == 0 else None):
                        when(condition, copy.wait_send)

        class Sum:
            def __init__(self, terms, got):
                self.terms, self.got = terms, got
                self.bases = (reserve(nf - 1), reserve(nf - 1))

            def both(self, step):
                for way in range(2):
                    target = f + (nf - 1) - step if way == 0 else f - (nf - 1) + step
                    condition = (f <= step) & (f < nf - 1) if way == 0 else (target >= 0) & (f > 0)
                    more = condition & (f > 0 if way == 0 else f < nf - 1)
                    at = self.bases[way] + step
                    copy = pair(
                        self.terms(target), self.got.at[way, step], up if way == 0 else down, at, at
                    )
                    yield way, target, condition, more, copy

            def wait(self, way, step):
                at = self.bases[way] + step
                ref = self.got.at[way, step]
                pair(ref, ref, core_dev, at, at).wait_recv()

            def start(self, step):
                for way, target, condition, more, copy in self.both(step):
                    if step > 0:

                        def body(way=way, target=target):
                            self.wait(way, step - 1)
                            ref = self.terms(target)
                            ref[...] = add_low(ref[...], self.got[way, step - 1])

                        when(more, body)
                    when(condition, copy.start)

            def finish(self, result):
                result[...] = self.terms(f)[...].astype(F32)
                for way, condition in ((0, f > 0), (1, f < nf - 1)):

                    def body(way=way):
                        self.wait(way, last)
                        result[...] = result[...] + self.got[way, last].astype(F32)

                    when(condition, body)
                for step in range(nf - 1):
                    for _, _, condition, _, copy in self.both(step):
                        when(condition, copy.wait_send)

        def own_side(ref, side):
            return ref.at[pl.ds(pl.multiple_of(side * rows_d, SUB), rows_d)]

        barrier = pltpu.get_barrier_semaphore()
        peers = [core_dev] + [peer for _, peer in chip_peers + plane_peers]
        for peer in peers:
            pl.semaphore_signal(barrier, inc=1, device_id=peer, device_id_type=MESH_ID)

        q_line = Gather(lambda g: r.q_z.at[g])
        f1_line = Gather(lambda g: r.f1_z.at[g])
        f2_line = Gather(lambda g: r.w_2.at[g, k])
        ada_near = wires.near(ada_in, r.ada)
        q_near = wires.near(q_in, r.q_nat)
        p_near = wires.near(p_in, r.p_nat)
        f2_near = wires.near(f2_in, r.f2_half)
        first = []
        first.append(wires.near(x_in, r.xg.at[c]))
        first.append(wires.near(c_in, r.cg.at[c]))
        f1_near = wires.near(f1_in, r.f1_z.at[f])
        order = lax.broadcasted_iota(jnp.int32, frames_in.shape, 0)
        for at, value in ((0, frames_in[...] + 65536 * order), (1, clips_in[...] + n_clips * order)):
            row = [value[i : i + 1].astype(F32) for i in range(micro)]
            r.idsg[c, at : at + 1, :] = jnp.concatenate(row, axis=1)
        row = [ref[...].astype(F32).reshape(1, ref.shape[0]) for ref in (bq_in, bp_in, b1_in, b2_in, ba_in)]
        r.biasg[f] = jnp.concatenate(row, axis=1)
        cond_rows = cond_in[...].reshape(n_rows, width)

        def own_silu(at):
            part = cond_rows[:, rows_d * at : rows_d * (at + 1)]
            r.silu[...] = (part / (1.0 + jnp.exp(-part))).astype(BF16)

        def own_cond(at):
            r.cond_own[...] = cond_rows[:, cols_f * at : cols_f * (at + 1)]

        for at in range(2 * nc):
            when(place.dp == at, functools.partial(own_silu, at))
        for at in range(nf):
            when(f == at, functools.partial(own_cond, at))
        ada_near.wait()
        ada_bias = jnp.where(place.dp == 0, row[4], 0.0)
        value = dot(r.silu[...], r.ada[...]) + ada_bias
        r.m_part[...] = value.reshape(2, half, ada_w)
        q_near.wait()
        p_near.wait()
        r.q_z[f] = jnp.concatenate([r.q_nat[...], r.p_nat[...]], axis=1)
        f2_near.wait()
        pl.semaphore_wait(barrier, len(peers))
        m_first = wires.far(r.m_part.at[core_o], r.m_core, core_dev)
        q_line.start(0)
        for _, peer in chip_peers:
            first.append(wires.far(r.idsg.at[c], r.idsg.at[c], peer))
        f2_swap = wires.far(own_side(r.f2_half, core_o), r.f2_got, core_dev)

        w_q, q_rows = r.w_q, r.q_rows
        q_base = reserve(3 * nc)
        q_local = wires.local_count
        wires.local_count += 3

        def q_copies(plane, i):
            piece = 3 * plane + i
            kind, chip = piece // nc, piece % nc
            src, dst = q_rows.at[piece], r.q_got.at[kind, c]
            far = pair(src, dst, (chip * 2 + k, f), q_base + kind * nc + chip, q_base + kind * nc + c)
            return chip, far, pltpu.make_async_copy(src, dst, r.local.at[q_local + kind])

        def q_forward(plane):
            r.p_got[k, plane] = r.q_z[plane, :, q_w:]
            for i in range(3):
                piece = r.q_z[plane, :, chip_w * i : chip_w * (i + 1)]
                parts = [piece[third * j : third * (j + 1)] for j in range(3)]
                q_rows[3 * plane + i] = jnp.concatenate(parts, axis=1)
                chip, far, near = q_copies(plane, i)
                when(chip != c, far.start)
                when(chip == c, near.start)

        f1_base = reserve(nc)
        f1_local = wires.local_count
        wires.local_count += 1

        def f1_copies(plane):
            src, dst = r.f1_z.at[plane], r.w_1.at[c, k]
            far = pair(src, dst, (plane * 2 + k, f), f1_base + plane, f1_base + c)
            return far, pltpu.make_async_copy(src, dst, r.local.at[f1_local])

        def f1_forward(plane):
            far, near = f1_copies(plane)
            when(plane != c, far.start)
            when(plane == c, near.start)

        m_first.wait()
        m_chip = r.m_chip
        m_chip[c] = r.m_part[k] + r.m_core[...]
        m_second = [wires.far(m_chip.at[c], m_chip.at[c], peer) for _, peer in chip_peers]
        q_forward(f)
        x_share = Share(r.xg, x_in)
        x_share.start()
        wait_all(m_second)
        total = m_chip[0]
        for other in range(1, nc):
            total = total + m_chip[other]
        r.m_z[f, k] = total
        m_third = [wires.far(r.m_z.at[f, k], r.m_z.at[f, k], peer) for _, peer in plane_peers]
        for _, peer in plane_peers:
            first.append(wires.far(r.biasg.at[f], r.biasg.at[f], peer))
        q_line.arrive(0, q_forward)
        q_line.start(1)
        x_share.relay()
        f2_swap.wait()

        def join_even():
            r.w_2[f, k] = jnp.concatenate([r.f2_half[:rows_d], r.f2_got[...]], axis=1)

        def join_odd():
            r.w_2[f, k] = jnp.concatenate([r.f2_got[...], r.f2_half[rows_d:]], axis=1)

        when(k == 0, join_even)
        when(k == 1, join_odd)
        f2_base = reserve(nf)

        def f2_across(plane):
            ref = r.w_2.at[plane, k]
            return pair(ref, ref, core_dev, f2_base + plane, f2_base + plane)

        def f2_forward(plane):
            f2_across(plane).start()

        f2_forward(f)
        wait_all(m_third)
        m_last = wires.far(r.m_z.at[:, k], r.m_z.at[:, k], core_dev)

        wait_all(first)
        m_last.wait()
        m_rows = [r.m_z[plane].reshape(n_rows, ada_w) for plane in range(nf)]
        r.m_tab[...] = jnp.concatenate(m_rows, axis=1)
        lead = lax.broadcasted_iota(jnp.int32, (n_sub, own), 1)
        lead = lead == SUB * lax.broadcasted_iota(jnp.int32, (n_sub, own), 0)
        lead = jnp.where(lead, 1.0, 0.0).astype(BF16)
        places = lax.broadcasted_iota(jnp.int32, (own, n_rows), 1).astype(F32)

        def hot_rows(blk):
            clip = r.idsg[blk].T[:, 1:2]
            return dot(lead, jnp.where(clip == places, 1.0, 0.0).astype(BF16)).astype(BF16)

        hot_all = jnp.concatenate([hot_rows(blk) for blk in range(nc)], axis=0)
        own_hot = hot_rows(c)
        for kind in range(6):
            value = r.m_tab[:, width * kind : width * (kind + 1)]
            if kind in (0, 1, 5):
                r.tab[kind % 3] = dot3(hot_all, value)
            r.own_tab[kind] = dot3(own_hot, value)

        def tab_row(kind, blk, g):
            return r.tab[kind % 3, pl.ds(blk * n_sub + g, 1), :]

        def own_row(kind, g):
            return r.own_tab[kind, pl.ds(g, 1), :]

        def make_a(blk):
            def body(g):
                rows = sub_rows(g)
                normal, _ = ln_parts(r.xg[blk, rows, :].astype(F32))
                value = normal * (1.0 + tab_row(1, blk, g)) + tab_row(0, blk, g)
                r.a_in[blk, rows, :] = value.astype(BF16)

            loop_rows(body)

        make_a(c)
        for step in (1, 2):
            x_share.arrive(step)
            make_a(xor_of(c, step, nc))
        q_line.arrive(1, q_forward)
        q_line.start(2)
        f1_line.start(0, f1_in)
        x_share.arrive(3)
        make_a(chip_d)
        q_line.arrive(2, q_forward)

        for kind in range(3):
            for other, _ in chip_peers:
                ref = r.q_got.at[kind, other]
                at = q_base + kind * nc + other
                pair(ref, ref, core_dev, at, at).wait()
            ref = r.q_got.at[kind, c]
            pltpu.make_async_copy(ref, ref, r.local.at[q_local + kind]).wait()
        q_core = []
        for chip in range(nc):
            for j in range(3):
                at = chip_w * j
                row = [r.q_got[kind, chip, :, at : at + chip_w] for kind in range(3)]
                w_q[chip, k, third * j : third * (j + 1), :] = jnp.concatenate(row, axis=1)
            q_core.append(wires.far(w_q.at[chip, k], w_q.at[chip, k], core_dev))
        p_core = wires.far(r.p_got.at[k], r.p_got.at[k], core_dev)
        f1_near.wait()
        f1_forward(f)
        f1_line.arrive(0, f1_forward)
        f1_line.start(1)
        x_share.sent()
        p_core.wait()
        for side in range(2):
            row = [r.p_got[side, plane] for plane in range(nf)]
            r.w_p[side * rows_d : (side + 1) * rows_d, :] = jnp.concatenate(row, axis=1)
        wait_all(q_core)

        lane = lax.broadcasted_iota(jnp.int32, (1, chip_w), 1)
        head_of = [
            jnp.where((lane >= HEAD_DIM * h) & (lane < HEAD_DIM * (h + 1)), 1.0, 0.0).astype(BF16)
            for h in range(heads)
        ]

        def weight_q():
            return w_q[...].reshape(width, q_w)

        def qv_bias(plane):
            row = r.biasg[plane]
            return jnp.where(c % 2 == 0, row[:, :chip_w], row[:, chip_w : 2 * chip_w])

        bias_q, bias_v = qv_bias(c // 2), qv_bias(nf // 2 + c // 2)
        at_p = 2 * chip_w
        at_1 = at_p + cols_f
        at_2 = at_1 + ff_c
        bias_p = jnp.concatenate([r.biasg[g][:, at_p : at_p + cols_f] for g in range(nf)], axis=1)
        bias_o = jnp.concatenate([r.biasg[g][:, at_2 : at_2 + cols_f] for g in range(nf)], axis=1)
        bias_1 = r.biasg[c][:, at_1 : at_1 + ff_c]
        zero = jnp.zeros_like(bias_q)
        bias_qkv = jnp.concatenate([bias_q, zero, bias_v], axis=1)
        attn_merge = Merge(r.sum_s, r.sum_r, r.sum_st)

        def attend(i):
            step = nc - 1 - i
            blk = xor_of(c, step, nc)
            value = (dot(r.a_in[blk], weight_q()) + bias_qkv).astype(BF16)
            for kind in range(3):
                r.qkv[kind, blk] = value[:, chip_w * kind : chip_w * (kind + 1)]
            q_now, k_now, v_now = r.qkv[0, blk], r.qkv[1, blk], r.qkv[2, blk]
            frames = r.idsg[blk]
            same = frames.T[:, 0:1] == frames[0:1, :]
            mixed = jnp.zeros((own, chip_w), F32)
            for h in range(heads):
                scores = dot_rt(q_now * head_of[h], k_now) * head_scale
                scores = jnp.where(same, scores, NEG_FILL)
                raised = jnp.exp(scores - jnp.max(scores, axis=-1, keepdims=True))
                share = raised / jnp.sum(raised, axis=-1, keepdims=True)
                r.probs[blk * heads + h] = share
                mixed = mixed + dot(share.astype(BF16), v_now * head_of[h])
            mixed = mixed.astype(BF16)
            r.mixed[blk] = mixed
            attn_merge.put(step, blk, dot(mixed, r.w_p[...]).astype(BF16))

            def next_lines():
                f1_line.arrive(1)
                f1_line.start(2)
                f2_line.start(0)

            when(i == 1, next_lines)

        loop(nc, attend)
        attn_merge.combine()
        f1_line.arrive(1, f1_forward, False)
        f1_line.arrive(2, f1_forward)

        attn_merge.finish()

        def after_attention(g):
            rows = sub_rows(g)
            value = attn_merge.rows(rows) + bias_p
            r.attn[rows, :] = value
            after = r.xg[c, rows, :].astype(F32) + own_row(2, g) * value
            r.after[rows, :] = after
            normal, _ = ln_parts(after)
            r.m_all[c, rows, :] = (normal * (1.0 + own_row(4, g)) + own_row(3, g)).astype(BF16)

        loop_rows(after_attention)
        m_all = r.m_all
        m_share = Share(m_all)
        m_share.start()
        c_share = Share(r.cg, c_in)
        c_share.start()
        f2_line.arrive(0, f2_forward)
        f2_line.start(1)
        f1_core = []
        ref = r.w_1.at[c, k]
        pltpu.make_async_copy(ref, ref, r.local.at[f1_local]).wait()
        f1_core.append(wires.far(ref, ref, core_dev))
        for other, _ in chip_peers:
            ref = r.w_1.at[other, k]
            pair(ref, ref, core_dev, f1_base + other, f1_base + other).wait()
            f1_core.append(wires.far(ref, ref, core_dev))
        m_share.relay()
        f1_line.sent(f1_in)
        f2_line.arrive(1, f2_forward)
        f2_line.start(2)
        wait_all(f1_core)

        def weight_1():
            return r.w_1[...].reshape(width, ff_c)

        def weight_2():
            return r.w_2[...].reshape(width, ff_c)

        dm_merge = Merge(r.sum_s, r.sum_r, r.sum_st)
        br_merge = Merge(r.br_s, r.br_r, r.br_st)

        def mixed_order(i):
            return (1 + 2 * i) * (1 - i // 2) + (6 - 2 * i) * (i // 2)

        def feed(step):
            blk = xor_of(c, step, nc)
            for at in range(1, nc):
                when(step == at, functools.partial(m_share.arrive, at))
            r.hid[...] = dot(m_all[blk], weight_1()) + bias_1

            def gelu_rows(g):
                rows = sub_rows(g)
                value, slope = gelu_both(r.hid[rows, :])
                r.act[blk, rows, :] = value.astype(BF16)
                r.d_hid[blk, rows, :] = slope.astype(BF16)

            loop_rows(gelu_rows)
            when(step == 1, c_share.relay)

        def feed_back(i):
            step = mixed_order(i)
            blk = xor_of(c, step, nc)
            for at in range(1, nc):
                when(step == at, functools.partial(c_share.arrive, at))

            def dbr_rows(g):
                rows = sub_rows(g)
                value = r.cg[blk, rows, :].astype(F32) * tab_row(5, blk, g)
                r.dbr[blk, rows, :] = value.astype(BF16)

            loop_rows(dbr_rows)
            r.hid[...] = dot(r.dbr[blk], weight_2())

            def back_rows(g):
                rows = sub_rows(g)
                value = r.hid[rows, :] * r.d_hid[blk, rows, :].astype(F32)
                r.d_hid[blk, rows, :] = value.astype(BF16)

            loop_rows(back_rows)
            dm_merge.put(step, blk, dot_rt(r.d_hid[blk], weight_1()).astype(BF16))

        loop(nc, feed)
        f2_line.arrive(2, f2_forward)
        for plane in range(nf):
            f2_across(plane).wait()
        loop(nc, feed_back)

        def column_cuts(count):
            return [(at, min(at + 256, count)) for at in range(0, count, 256)]

        def all_rows(ref):
            return ref[...].reshape(group, ref.shape[-1])

        dbr_all = all_rows(r.dbr)
        for lo, hi in column_cuts(ff_c):
            value = dot_lt(dbr_all, r.act[:, :, lo:hi].reshape(group, hi - lo))
            r.g_2[:, :, :, lo:hi] = value.astype(BF16).reshape(nf, 2, rows_d, hi - lo)
        g2_core = wires.far(r.g_2.at[:, core_o], r.g_2r, core_dev)

        dm_merge.combine()
        g_1 = r.w_1
        m_rows_all = all_rows(m_all)
        for lo, hi in column_cuts(ff_c):
            value = dot_lt(m_rows_all, r.d_hid[:, :, lo:hi].reshape(group, hi - lo))
            g_1[:, :, :, lo:hi] = value.astype(BF16).reshape(nc, 2, rows_d, hi - lo)
        g1_core = wires.far(g_1.at[:, core_o], r.g_1r, core_dev)
        c_share.sent()
        g2_core.wait()
        for plane in range(nf):
            r.g_2[plane, k] = add_low(r.g_2[plane, k], r.g_2r[plane])
        sum_2 = Sum(lambda t: r.g_2.at[t, k], r.got_2)
        sum_2.start(0)


        dm_merge.finish()
        da_all = r.da_all

        def back_norm2(g):
            rows = sub_rows(g)
            d_m = dm_merge.rows(rows)
            normal, scale = ln_parts(r.after[rows, :])
            cot_now = r.cg[c, rows, :].astype(F32)
            d_after = cot_now + ln_back(normal, scale, d_m * (1.0 + own_row(4, g)))
            r.d_after[rows, :] = d_after
            da_all[c, rows, :] = (own_row(2, g) * d_after).astype(BF16)
            at = pl.ds(g, 1)
            r.sub[3, at, :] = jnp.sum(d_m, axis=0, keepdims=True)
            r.sub[4, at, :] = jnp.sum(d_m * normal, axis=0, keepdims=True)
            r.sub[2, at, :] = jnp.sum(d_after * r.attn[rows, :], axis=0, keepdims=True)

        loop_rows(back_norm2)
        da_share = Share(da_all)
        da_share.start()
        m_share.sent()
        da_share.relay()

        g1_core.wait()
        for chip in range(nc):
            g_1[chip, k] = add_low(g_1[chip, k], r.g_1r[chip])
        y_1 = r.f1_z
        y_1[c] = g_1[c, k]
        y1_far = [wires.far(g_1.at[other, k], y_1.at[c], peer) for other, peer in chip_peers]

        def branch_out(i):
            step = nc - 1 - i
            blk = xor_of(c, step, nc)
            r.hid[...] = dot_rt(r.act[blk], weight_2())
            r.br_s[blk] = r.hid[...].astype(BF16)
            bias_once = bias_o * jnp.where(step == 0, 1.0, 0.0)

            def gate_rows(g):
                rows = sub_rows(g)
                value = (r.hid[rows, :] + bias_once) * r.cg[blk, rows, :].astype(F32)
                r.sub_gate[pl.ds(blk * n_sub + g, 1), :] = jnp.sum(value, axis=0, keepdims=True)

            loop_rows(gate_rows)

        loop(nc, branch_out)
        sum_2.start(1)

        def gray_order(i):
            return i + i // 2 - 2 * (i // 3)

        back_merge = Merge(r.sum_s, r.sum_r, r.sum_st)

        def attend_back(i):
            step = gray_order(i)
            blk = xor_of(c, step, nc)
            for at in range(1, nc):
                when(step == at, functools.partial(da_share.arrive, at))
            d_mix = dot_rt(da_all[blk], r.w_p[...]).astype(BF16)
            q_now, k_now, v_now = r.qkv[0, blk], r.qkv[1, blk], r.qkv[2, blk]
            d_q = jnp.zeros((own, chip_w), F32)
            d_k = jnp.zeros((own, chip_w), F32)
            d_v = jnp.zeros((own, chip_w), F32)
            for h in range(heads):
                d_mix_h = d_mix * head_of[h]
                share = r.probs[blk * heads + h]
                d_share = dot_rt(d_mix_h, v_now)
                d_score = share * (d_share - jnp.sum(share * d_share, axis=-1, keepdims=True))
                d_score = d_score.astype(BF16)
                d_q = d_q + dot(d_score, k_now * head_of[h])
                d_k = d_k + dot_lt(d_score, q_now * head_of[h])
                d_v = d_v + dot_lt(share.astype(BF16), d_mix_h)
            all_three = jnp.concatenate([d_q * head_scale, d_k * head_scale, d_v], axis=1).astype(BF16)
            r.d_qkv[blk] = all_three
            back_merge.put(step, blk, dot_rt(all_three, weight_q()).astype(BF16))
            when(i == 3, lambda: sum_2.start(2))

        loop(nc, attend_back)
        da_share.sent()

        g_q, g_p = w_q, r.w_p
        a_rows = all_rows(r.a_in)
        for lo, hi in column_cuts(q_w):
            value = dot_lt(a_rows, r.d_qkv[:, :, lo:hi].reshape(group, hi - lo))
            g_q[:, :, :, lo:hi] = value.astype(BF16).reshape(nc, 2, rows_d, hi - lo)
        q_core_back = wires.far(g_q.at[:, core_o], r.g_qr, core_dev)
        wait_all(y1_far)
        sum_1 = Sum(lambda t: y_1.at[t], r.got_1)
        sum_1.start(0)
        g_p[...] = dot_lt(all_rows(r.mixed), all_rows(da_all)).astype(BF16)
        p_core_back = wires.far(own_side(g_p, core_o), r.g_pr, core_dev)
        q_core_back.wait()
        for chip in range(nc):
            g_q[chip, k] = add_low(g_q[chip, k], r.g_qr[chip])
        r.y_got[c] = g_q[c, k]
        yq_far = [wires.far(g_q.at[other, k], r.y_got.at[c], peer) for other, peer in chip_peers]

        def own_terms(step):
            blk = xor_of(c, step, nc)

            def body(g):
                rows = sub_rows(g)
                part = r.sum_s[blk, rows, :].astype(F32)
                normal, _ = ln_parts(r.xg[blk, rows, :].astype(F32))
                at = pl.ds(blk * n_sub + g, 1)
                r.sub_lin[0, at, :] = jnp.sum(part, axis=0, keepdims=True)
                r.sub_lin[1, at, :] = jnp.sum(part * normal, axis=0, keepdims=True)

            loop_rows(body)

        loop(nc, own_terms)
        back_merge.combine()
        all_turned = hot_all.astype(F32).T.astype(BF16)
        hot_turned = own_hot.astype(F32).T.astype(BF16)
        for kind in range(6):
            if kind < 2:
                value = dot3(all_turned, r.sub_lin[kind])
            elif kind < 5:
                value = dot3(hot_turned, r.sub[kind])
            else:
                value = dot3(all_turned, r.sub_gate[...])
            r.d_part[:, :, width * kind : width * (kind + 1)] = value.reshape(2, half, width)
        d_core = wires.far(r.d_part.at[core_o], r.d_core, core_dev)
        d_core.wait()
        r.d_core[...] = r.d_core[...] + r.d_part[k]
        for plane in range(nf):
            r.d_cut[plane] = r.d_core[:, ada_w * plane : ada_w * (plane + 1)].astype(BF16)
        small = []
        for other, peer in plane_peers:
            small.append(wires.far(r.d_cut.at[other], r.dz.at[f], peer))
        r.dz[f] = r.d_cut[f]
        sum_1.start(1)
        p_core_back.wait()
        own_side(g_p, k)[...] = add_low(own_side(g_p, k)[...], r.g_pr[...])
        ones_own = jnp.ones((8, own), BF16)
        ones_all = jnp.ones((8, group), BF16)
        r.d_bias[...] = jnp.zeros((8, width), F32)
        r.d_bias[0:1, :] = dot(ones_own, da_all[c])[0:1]
        r.d_bias[1:2, :] = dot(ones_own, r.dbr[c])[0:1]
        qkv_sums = dot(ones_all, all_rows(r.d_qkv))[0:1]
        r.d_bias[2:3, 0:chip_w] = qkv_sums[:, :chip_w]
        r.d_bias[3:4, 0:chip_w] = qkv_sums[:, 2 * chip_w :]
        ones_ff = dot(ones_all, all_rows(r.d_hid))[0:1]
        r.d_bias[4:5, :] = ones_ff[:, :width]
        for part in range(1, ff_c // width):
            r.d_bias[4 + part : 5 + part, :] = ones_ff[:, part * width : (part + 1) * width]
        r.d_low[...] = r.d_bias[...].astype(BF16)
        bias_far = [wires.far(r.d_low, r.dzb.at[f], peer) for _, peer in plane_peers]
        r.dzb[f] = r.d_low[...]
        wait_all(small)
        value = r.dz[0].astype(F32)
        for plane in range(1, nf):
            value = value + r.dz[plane].astype(F32)
        m_chip[c] = value
        small = [wires.far(m_chip.at[c], m_chip.at[c], peer) for _, peer in chip_peers]
        wait_all(yq_far)
        q_line.sent()
        y_q = r.q_z
        for plane in range(nf):
            row = []
            for i in range(3):
                kind, chip = (3 * plane + i) // nc, (3 * plane + i) % nc
                row.append(r.y_got[chip, :, chip_w * kind : chip_w * (kind + 1)])
            row.append(own_side(g_p, k)[:, plane * cols_f : (plane + 1) * cols_f])
            y_q[plane] = jnp.concatenate(row, axis=1)
        sum_q = Sum(lambda t: y_q.at[t], r.got_q)
        sum_q.start(0)
        sum_1.start(2)
        wait_all(bias_far)
        value = r.dzb[0].astype(F32)
        for plane in range(1, nf):
            value = value + r.dzb[plane].astype(F32)
        r.d_bsum[...] = value
        b_swap = wires.far(r.d_bsum, r.d_coreb, core_dev)

        back_merge.finish()

        def back_norm1(g):
            rows = sub_rows(g)
            d_a = back_merge.rows(rows)
            normal, scale = ln_parts(r.xg[c, rows, :].astype(F32))
            value = r.d_after[rows, :] + ln_back(normal, scale, d_a * (1.0 + own_row(1, g)))
            x_grad[rows, :] = value.astype(BF16)

        loop_rows(back_norm1)
        land(x_grad)
        wait_all(small)
        value = m_chip[0]
        for chip in range(1, nc):
            value = value + m_chip[chip]
        r.d_tot[k] = value
        d_swap = wires.far(r.d_tot.at[k], r.d_tot.at[k], core_dev)
        b_swap.wait()
        r.d_chipb[c] = r.d_bsum[...] + r.d_coreb[...]
        bias_far = [wires.far(r.d_chipb.at[c], r.d_chipb.at[c], peer) for _, peer in chip_peers]
        br_merge.launch()
        sum_q.start(1)
        d_swap.wait()
        d_cols = r.d_tot[...].reshape(n_rows, ada_w)
        silu_turned = r.silu[...].astype(F32).T.astype(BF16)
        o_bada[...] = jnp.sum(d_cols, axis=0)
        value, total = d_cols, None
        for _ in range(3):
            term = value.astype(BF16)
            value = value - term.astype(F32)
            part = dot_rt(term, r.ada[...])
            total = part if total is None else total + part
        r.c_part[f] = total
        c_far = [wires.far(r.c_part.at[f], r.c_part.at[f], peer) for _, peer in plane_peers]
        sum_q.start(2)
        for lo, hi in column_cuts(ada_w):
            o_ada[:, lo:hi] = dot3(silu_turned, d_cols[:, lo:hi])
        land(o_ada, o_bada)
        sum_2.finish(r.all_2.at[k])
        o2_swap = wires.far(r.all_2.at[k], r.all_2.at[k], core_dev)
        br_merge.combine()
        wait_all(c_far)
        value = r.c_part[0]
        for plane in range(1, nf):
            value = value + r.c_part[plane]
        r.c_all[c, k] = value
        c_chip = [wires.far(r.c_all.at[c, k], r.c_all.at[c, k], peer) for _, peer in chip_peers]


        br_merge.finish()

        def finish_out(g):
            rows = sub_rows(g)
            branch = br_merge.rows(rows) + bias_o
            out[rows, :] = (r.after[rows, :] + own_row(5, g) * branch).astype(BF16)

        loop_rows(finish_out)
        land(out)
        wait_all(c_chip)
        c_swap = wires.far(r.c_all.at[:, k], r.c_all.at[:, k], core_dev)
        o2_swap.wait()

        def own_columns(lo):
            def body():
                o_2[...] = r.all_2[:, :, lo : lo + ff_d].reshape(cols_f, ff_d)

            return body

        when(k == 0, own_columns(0))
        when(k == 1, own_columns(ff_d))
        land(o_2)
        wait_all(bias_far)
        own_sums = r.d_chipb[0]
        for chip in range(1, nc):
            own_sums = own_sums + r.d_chipb[chip]
        for plane in range(nf):

            def bias_columns(plane=plane):
                at = plane * cols_f
                o_bp[...] = own_sums[0, at : at + cols_f]
                o_b2[...] = own_sums[1, at : at + cols_f]
                kind, chip = 2 * plane // nc, 2 * plane % nc
                pieces = [r.d_chipb[chip + i, 2 + kind : 3 + kind, 0:chip_w] for i in range(2)]
                o_bqv[...] = jnp.concatenate(pieces, axis=1)[0]
                o_b1[...] = r.d_chipb[plane, 4, :]

            when(f == plane, bias_columns)
        land(o_bqv, o_bp, o_b1, o_b2)
        c_swap.wait()
        d_silu = jnp.concatenate([r.c_all[f, 0], r.c_all[f, 1]], axis=1)
        cond_now = r.cond_own[...]
        gate = 1.0 / (1.0 + jnp.exp(-cond_now))
        o_cond[...] = d_silu * (gate * (1.0 + cond_now * (1.0 - gate)))
        land(o_cond)
        f2_line.sent()
        sum_1.finish(o_1)
        land(o_1)
        sum_q.finish(r.all_q)
        o_q[...] = r.all_q[:, :q_w]
        o_p[...] = r.all_q[:, q_w:]
        land(o_q, o_p)
        wait_all(landed)
        assert wires.remote_count <= n_sem and wires.local_count <= 40

    return pl.pallas_call(
        kernel,
        out_shape=outs,
        in_specs=[ANYWHERE] * 2 + [ON_CHIP] * 8 + [ANYWHERE] * 5,
        out_specs=tuple([ANYWHERE] * len(outs)),
        scratch_shapes=[pltpu.VMEM(item.shape, item.dtype) for item in outs] + list(scratch.values()),
        compiler_params=pltpu.CompilerParams(
            collective_id=0, has_side_effects=True, vmem_limit_bytes=63 * 2**20
        ),
        name="block",
    )(x, cot, frames, clips, *biases, cond, w_ada, wq, wp, w1, w2)


def land_kernel(arrays):
    count = len(arrays)

    def kernel(*refs):
        ins, results, held = refs[:count], refs[count : 2 * count], refs[2 * count : 3 * count]
        arrive, leave = refs[3 * count :]
        steps = [pltpu.make_async_copy(a, b, arrive.at[i]) for i, (a, b) in enumerate(zip(ins, held))]
        copies = [pltpu.make_async_copy(a, b, leave.at[i]) for i, (a, b) in enumerate(zip(held, results))]
        for step in steps:
            step.start()
        for step, copy in zip(steps, copies):
            step.wait()
            copy.start()
        wait_all(copies)

    return pl.pallas_call(
        kernel,
        out_shape=tuple(jax.ShapeDtypeStruct(a.shape, a.dtype) for a in arrays),
        in_specs=[ANYWHERE] * count,
        out_specs=tuple([ANYWHERE] * count),
        scratch_shapes=[pltpu.VMEM(a.shape, a.dtype) for a in arrays]
        + [pltpu.SemaphoreType.DMA((count,))] * 2,
        name="land",
    )(*arrays)


def fits_block(n_dp, nf, width, ff, own, micro):
    nc = n_dp // 2
    return (
        nc == nf
        and nf == 4
        and width % (128 * nf) == 128
        and ff == 4 * width
        and (width // n_dp) % 16 == 0
        and (width // nc) % HEAD_DIM == 0
        and own % (2 * SUB) == 0
    )


def per_device(
    n_dp, nf, patches, cotangent, conditioning, frame_of_slot, clip_of_slot,
    w_ada, b_ada, w_qkv, b_qv, w_proj, b_proj, w_fc1, b_fc1, w_fc2, b_fc2,
):
    nc = n_dp // 2
    sizes = (nc, nf)
    micro, block, width = patches.shape
    own = micro * block
    clips = conditioning.shape[1]
    rows_d = width // n_dp
    cols_f = width // nf
    ff = w_fc1.shape[1] * nf
    ff_d = ff // n_dp
    chip_w = width // nc
    piece_q = math.gcd(3 * width // nf, chip_w)
    piece_1 = math.gcd(ff // nf, ff_d)
    dims = types.SimpleNamespace(
        nc=nc,
        nf=nf,
        per_q=3 * width // nf // piece_q,
        per_1=ff // nf // piece_1,
        chip_q=chip_w // piece_q,
        chip_1=ff // nc // piece_1,
    )
    dp = lax.axis_index("dp")
    f = lax.axis_index("fsdp")
    c, k = dp // 2, dp % 2

    q_send = w_qkv.reshape(rows_d, dims.per_q, piece_q).transpose(1, 0, 2)
    f1_send = w_fc1.reshape(rows_d, dims.per_1, piece_1).transpose(1, 0, 2)
    f2_send = w_fc2.T
    cond = conditioning.reshape(micro * clips, width)
    silu_cond = jax.nn.silu(cond)
    silu_low = silu_cond.astype(BF16)
    ada_w = w_ada.shape[1]
    silu_part = lax.dynamic_slice_in_dim(silu_low, dp * rows_d, rows_d, 1)
    mod_part = dot(silu_part, w_ada) + jnp.where(dp == 0, b_ada.astype(F32), 0.0)[None]
    mod_send = mod_part.reshape(-1, 2, ada_w // 2).transpose(1, 0, 2)
    cut = [0, 2 * cols_f, 3 * cols_f, 3 * cols_f + ff // nf, 4 * cols_f + ff // nf]
    cond_own = lax.dynamic_slice_in_dim(cond, f * cols_f, cols_f, 1)

    def ada_outputs(d_cols):
        grad_w_ada = precise(silu_part.astype(F32), d_cols, ((0,), (0,)))
        d_silu_part = precise(d_cols, w_ada.astype(F32), ((1,), (1,)))
        d_silu = cond_kernel(dims, d_silu_part).transpose(1, 0, 2).reshape(micro * clips, width)
        d_silu_own = lax.dynamic_slice_in_dim(d_silu, f * cols_f, cols_f, 1)
        _, silu_back = jax.vjp(jax.nn.silu, cond_own)
        cond_grad = silu_back(d_silu_own)[0].reshape(micro, clips, cols_f)
        return cond_grad, grad_w_ada, jnp.sum(d_cols, axis=0)

    if fits_block(n_dp, nf, width, ff, own, micro):
        results = block_kernel(
            dims, patches.reshape(own, width), cotangent.reshape(own, width), frame_of_slot,
            clip_of_slot, (b_qv, b_proj, b_fc1, b_fc2, b_ada), conditioning, w_ada, w_qkv, w_proj,
            w_fc1, w_fc2.T,
        )
        (
            output, input_grad, cond_grad, grad_ada, grad_b_ada, grad_qkv, grad_b_qv,
            grad_proj, grad_b_proj, grad_fc1, grad_b_fc1, grad_fc2, grad_b_fc2,
        ) = land_kernel(results)
        return (
            output.reshape(patches.shape),
            input_grad.reshape(patches.shape),
            cond_grad.reshape(micro, clips, cols_f),
            grad_ada,
            grad_b_ada,
            grad_qkv,
            grad_b_qv,
            grad_proj,
            grad_b_proj,
            grad_fc1,
            grad_b_fc1,
            grad_fc2.T,
            grad_b_fc2,
        )

    ids = jnp.stack([frame_of_slot.reshape(own), clip_of_slot.reshape(own)])
    ids = jnp.concatenate([ids, jnp.zeros((6, own), jnp.int32)])
    bias_send = jnp.concatenate([b_qv, b_proj, b_fc1, b_fc2]).astype(F32)[None]

    (x_all, c_all, ids_all, bias_all, mod_all, q_chip, f1_chip, p_chip, f2_chip, _, _) = start_kernel(
        dims, patches.reshape(own, width), cotangent.reshape(own, width), ids, bias_send, mod_send,
        q_send, f1_send, w_proj, f2_send,
    )
    group = nc * own
    modulation = mod_all.transpose(2, 0, 1, 3).reshape(micro * clips, 6 * width)
    q_parts = [
        q_chip[i].reshape(nc, 2, dims.chip_q, rows_d, piece_q).transpose(0, 1, 3, 2, 4).reshape(width, chip_w)
        for i in range(3)
    ]
    w1 = f1_chip.transpose(1, 2, 3, 0, 4).reshape(width, ff // nc)
    wp = p_chip.transpose(0, 2, 1, 3).reshape(chip_w, width)
    w2t = f2_chip.reshape(2, width, ff_d).transpose(1, 0, 2).reshape(width, 2 * ff_d)
    b_parts = [bias_all[:, 0, a:b].reshape(-1) for a, b in zip(cut[:-1], cut[1:])]
    bq = lax.dynamic_slice_in_dim(b_parts[0], c * chip_w, chip_w, 0)
    bv = lax.dynamic_slice_in_dim(b_parts[0], width + c * chip_w, chip_w, 0)
    b1 = lax.dynamic_slice_in_dim(b_parts[2], c * (ff // nc), ff // nc, 0)

    def hot_of(clip_ids):
        count = clip_ids.shape[0]
        row = (jnp.arange(count, dtype=jnp.int32) // block) % micro * clips + clip_ids
        return (row[:, None] == jnp.arange(micro * clips, dtype=jnp.int32)[None]).astype(F32)

    hot_group = hot_of(ids_all[:, 1].reshape(group))
    hot_own = hot_of(clip_of_slot.reshape(own))
    mod_group = precise(hot_group, modulation, ((1,), (0,)))
    mod_own = precise(hot_own, modulation, ((1,), (0,)))
    shift1, scale1 = mod_group[:, :width], mod_group[:, width : 2 * width]
    gate1 = mod_own[:, 2 * width : 3 * width]
    shift2, scale2 = mod_own[:, 3 * width : 4 * width], mod_own[:, 4 * width : 5 * width]
    gate2_group, gate2 = mod_group[:, 5 * width :], mod_own[:, 5 * width :]

    x_group = x_all.reshape(group, width).astype(F32)
    norm1, rstd1 = ln_parts(x_group)
    a_in = (norm1 * (1.0 + scale1) + shift1).astype(BF16)
    zero = jnp.zeros_like(bq)
    q, kk, v = [
        (dot(a_in, w) + b[None]).astype(BF16) for w, b in zip(q_parts, (bq, zero, bv))
    ]
    heads = chip_w // HEAD_DIM
    blocks = group // block
    q4, k4, v4 = [t.reshape(blocks, block, heads, HEAD_DIM) for t in (q, kk, v)]
    frames = ids_all[:, 0].reshape(blocks, block)
    same = (frames[:, :, None] == frames[:, None, :])[:, None]
    scores = jnp.einsum("bqhd,bkhd->bhqk", q4, k4, preferred_element_type=F32) * HEAD_DIM ** (-0.5)
    scores = jnp.where(same, scores, NEG_FILL)
    top = jnp.max(scores, axis=-1, keepdims=True)
    raised = jnp.exp(scores - top)
    probs = raised / jnp.sum(raised, axis=-1, keepdims=True)
    probs_low = probs.astype(BF16)
    mixed = jnp.einsum("bhqk,bkhd->bqhd", probs_low, v4, preferred_element_type=F32)
    mixed = mixed.reshape(group, chip_w).astype(BF16)
    attn_part = dot(mixed, wp)
    (attn_got,) = exchange(
        "attn_sum", 3, sizes, [(CHIP, SPREAD, attn_part.astype(BF16).reshape(nc, own, width))]
    )
    attn = jnp.sum(attn_got.astype(F32), axis=0) + b_parts[1][None]
    x_own = patches.reshape(own, width).astype(F32)
    after = x_own + gate1 * attn
    norm2, rstd2 = ln_parts(after)
    m_own = (norm2 * (1.0 + scale2) + shift2).astype(BF16)
    (m_all,) = exchange("m_gather", 4, sizes, [(CHIP, GATHER, m_own)])
    m_in = m_all.reshape(group, width)

    hidden = dot(m_in, w1) + b1[None]
    act, slope = gelu_both(hidden)
    act = act.astype(BF16)
    branch_part = dot_rt(act, w2t)
    cot_group = c_all.reshape(group, width).astype(F32)
    d_branch = (gate2_group * cot_group).astype(BF16)
    grad_2t = dot_lt(d_branch, act)
    d_hidden = (dot(d_branch, w2t) * slope).astype(BF16)
    grad_1 = dot_lt(m_in, d_hidden)
    d_m_part = dot_rt(d_hidden, w1)
    branch_got, d_m_got = exchange(
        "ff_sum",
        5,
        sizes,
        [
            (CHIP, SPREAD, d_m_part.astype(BF16).reshape(nc, own, width)),
            (CHIP, SPREAD, branch_part.astype(BF16).reshape(nc, own, width)),
        ],
    )[::-1]
    branch = jnp.sum(branch_got.astype(F32), axis=0) + b_parts[3][None]
    output = (after + gate2 * branch).astype(BF16)
    d_m = jnp.sum(d_m_got.astype(F32), axis=0)
    cot_own = cotangent.reshape(own, width).astype(F32)
    d_after = cot_own + ln_back(norm2, rstd2, d_m * (1.0 + scale2))
    d_attn = (gate1 * d_after).astype(BF16)
    (d_attn_all,) = exchange("d_attn_gather", 6, sizes, [(CHIP, GATHER, d_attn)])
    d_attn_group = d_attn_all.reshape(group, width)
    grad_p = dot_lt(mixed, d_attn_group)
    d_mix = dot_rt(d_attn_group, wp).astype(BF16).reshape(blocks, block, heads, HEAD_DIM)
    d_probs = jnp.einsum("bqhd,bkhd->bhqk", d_mix, v4, preferred_element_type=F32)
    d_scores = probs * (d_probs - jnp.sum(probs * d_probs, axis=-1, keepdims=True))
    d_scores = d_scores.astype(BF16)
    dq = jnp.einsum("bhqk,bkhd->bqhd", d_scores, k4, preferred_element_type=F32) * HEAD_DIM ** (-0.5)
    dk = jnp.einsum("bhqk,bqhd->bkhd", d_scores, q4, preferred_element_type=F32) * HEAD_DIM ** (-0.5)
    dv = jnp.einsum("bhqk,bqhd->bkhd", probs_low, d_mix, preferred_element_type=F32)
    dqkv = [t.reshape(group, chip_w).astype(BF16) for t in (dq, dk, dv)]
    d_a_part = sum(dot_rt(t, w) for t, w in zip(dqkv, q_parts))
    grad_q = jnp.stack([dot_lt(a_in, t) for t in dqkv])
    (d_a_got,) = exchange(
        "d_a_sum", 7, sizes, [(CHIP, SPREAD, d_a_part.astype(BF16).reshape(nc, own, width))]
    )
    d_a = jnp.sum(d_a_got.astype(F32), axis=0)
    norm1_own, rstd1_own = ln_parts(x_own)
    scale1_own = mod_own[:, width : 2 * width]
    input_grad = (d_after + ln_back(norm1_own, rstd1_own, d_a * (1.0 + scale1_own))).astype(BF16)

    g_q = grad_q.reshape(3, nc, 2, rows_d, dims.chip_q, piece_q).transpose(2, 1, 0, 4, 3, 5)
    g_1 = grad_1.reshape(nc, 2, rows_d, dims.chip_1, piece_1).transpose(1, 0, 3, 2, 4)
    g_p = grad_p.reshape(2, rows_d, nf, cols_f).transpose(0, 2, 1, 3)
    g_2 = grad_2t.reshape(nf, cols_f, 2, ff_d).transpose(2, 0, 1, 3)
    got = exchange("grad_core", 8, sizes, [(CORE, SPREAD, g.astype(BF16)) for g in (g_q, g_1, g_p, g_2)])
    s_q, s_1, s_p, s_2 = [jnp.sum(g.astype(F32), axis=0).astype(BF16) for g in got]
    r_q, r_1 = exchange("grad_chip", 9, sizes, [(CHIP, SPREAD, s_q), (CHIP, SPREAD, s_1)])
    z_q = r_q.transpose(1, 0, 2, 3, 4).reshape(nf, dims.per_q, rows_d, piece_q)
    z_1 = r_1.reshape(nf, dims.per_1, rows_d, piece_1)
    got = exchange("grad_plane", 10, sizes, [(PLANE, SPREAD, g) for g in (z_q, z_1, s_p, s_2)])
    o_q, o_1, o_p, o_2 = [jnp.sum(g.astype(F32), axis=0) for g in got]
    grad_w_qkv = o_q.transpose(1, 0, 2).reshape(rows_d, 3 * width // nf)
    grad_w_fc1 = o_1.transpose(1, 0, 2).reshape(rows_d, ff // nf)
    grad_w_fc2 = o_2.T

    d_token = jnp.concatenate(
        [d_a, d_a * norm1_own, d_after * attn, d_m, d_m * norm2, cot_own * branch], axis=1
    )
    d_mod = precise(hot_own, d_token, ((0,), (0,)))
    d_branch_own = (gate2 * cot_own).astype(BF16).astype(F32)

    def columns(value):
        return jnp.sum(value.astype(F32), axis=0)

    def spread(value, count):
        return lax.dynamic_update_slice_in_dim(
            jnp.zeros((count,), F32), value, c * value.shape[0], 0
        )

    g_bqv = jnp.concatenate([spread(columns(dqkv[0]), width), spread(columns(dqkv[2]), width)])
    g_b1 = spread(columns(d_hidden), ff)
    bias_terms = jnp.concatenate(
        [
            g_bqv.reshape(nf, -1),
            columns(d_attn).reshape(nf, -1),
            g_b1.reshape(nf, -1),
            columns(d_branch_own).reshape(nf, -1),
        ],
        axis=1,
    )
    n_bias = bias_terms.shape[1]
    bias_rows = -(-n_bias // ada_w)
    bias_terms = jnp.pad(bias_terms, ((0, 0), (0, bias_rows * ada_w - n_bias)))
    terms = jnp.concatenate(
        [d_mod.reshape(micro * clips, nf, ada_w).transpose(1, 0, 2), bias_terms.reshape(nf, bias_rows, ada_w)],
        axis=1,
    )
    pad_rows = -terms.shape[1] % 8
    terms = jnp.pad(terms, ((0, 0), (0, pad_rows), (0, 0)))
    terms = terms.reshape(nf, -1, 2, ada_w // 2).transpose(0, 2, 1, 3)
    total = sum_small_kernel(dims, terms).transpose(1, 0, 2).reshape(-1, ada_w)
    d_cols = total[: micro * clips]
    bias_sums = total[micro * clips : micro * clips + bias_rows].reshape(-1)[:n_bias]
    g_parts = [bias_sums[a:b] for a, b in zip(cut[:-1], cut[1:])]
    cond_grad, grad_w_ada, grad_b_ada = ada_outputs(d_cols)
    return (
        output.reshape(patches.shape),
        input_grad.reshape(patches.shape),
        cond_grad,
        grad_w_ada,
        grad_b_ada,
        grad_w_qkv,
        g_parts[0],
        o_p,
        g_parts[1],
        grad_w_fc1,
        g_parts[2],
        grad_w_fc2,
        g_parts[3],
    )


def solution(mesh):
    tokens = P(None, ("dp", "fsdp"), None)
    ids = P(None, ("dp", "fsdp"))
    both, cols = P("dp", "fsdp"), P("fsdp")
    in_specs = (tokens, tokens, P(), ids, ids) + (both, cols) * 5
    out_specs = (tokens, tokens, P(None, None, "fsdp")) + (both, cols) * 5
    return jax.shard_map(
        functools.partial(per_device, mesh.shape["dp"], mesh.shape["fsdp"]),
        mesh=mesh,
        in_specs=in_specs,
        out_specs=out_specs,
        check_vma=False,
    )
```

```python
import functools
import math
import types

import jax
import jax.numpy as jnp
from jax import lax
from jax.experimental import pallas as pl
from jax.experimental.pallas import tpu as pltpu
from jax.sharding import PartitionSpec as P

HEAD_DIM = 72
EPS = 1e-06
GELU_C = math.sqrt(2.0 / math.pi)
PRECISE = lax.Precision.HIGHEST
NEG_FILL = -1e30
SUB = 16
CORE, CHIP, PLANE, ALL = range(4)
GATHER, SPREAD = range(2)
MESH_ID = pl.DeviceIdType.MESH
F32 = jnp.float32
BF16 = jnp.bfloat16


def xor_of(index, step, size):
    result, bit = 0, 1
    while bit < size:
        mine = (index // bit) % 2
        result = result + ((mine + (step // bit) % 2) % 2) * bit
        bit *= 2
    return result


class Place:
    def __init__(self, n_chip, n_plane):
        self.n = {CORE: 2, CHIP: n_chip, PLANE: n_plane, ALL: 2 * n_chip}
        self.dp = lax.axis_index("dp")
        self.f = lax.axis_index("fsdp")
        self.c = self.dp // 2
        self.k = self.dp % 2

    def index(self, axis):
        return {CORE: self.k, CHIP: self.c, PLANE: self.f, ALL: self.dp}[axis]

    def peer(self, axis, step):
        other = xor_of(self.index(axis), step, self.n[axis])
        if axis == CORE:
            return other, (self.c * 2 + other, self.f)
        if axis == CHIP:
            return other, (other * 2 + self.k, self.f)
        if axis == PLANE:
            return other, (self.dp, other)
        return other, (other, self.f)


def greet(place, axes):
    barrier = pltpu.get_barrier_semaphore()
    count = 0
    for axis in axes:
        for step in range(1, place.n[axis]):
            pl.semaphore_signal(
                barrier, inc=1, device_id=place.peer(axis, step)[1], device_id_type=MESH_ID
            )
            count += 1
    pl.semaphore_wait(barrier, count)


class Wires:
    def __init__(self, send, recv, local):
        self.send, self.recv, self.local = send, recv, local
        self.remote_count = 0
        self.local_count = 0

    def far(self, src, dst, device):
        at = self.remote_count
        self.remote_count += 1
        copy = pltpu.make_async_remote_copy(
            src_ref=src,
            dst_ref=dst,
            send_sem=self.send.at[at],
            recv_sem=self.recv.at[at],
            device_id=device,
            device_id_type=MESH_ID,
        )
        copy.start()
        return copy

    def near(self, src, dst):
        at = self.local_count
        self.local_count += 1
        copy = pltpu.make_async_copy(src, dst, self.local.at[at])
        copy.start()
        return copy


def wait_all(copies):
    for copy in copies:
        copy.wait()


ANYWHERE = pl.BlockSpec(memory_space=pl.ANY)
ON_CHIP = pl.BlockSpec(memory_space=pltpu.VMEM)


def exchange(name, collective_id, sizes, items):
    n_chip, n_plane = sizes
    n_of = {CORE: 2, CHIP: n_chip, PLANE: n_plane, ALL: 2 * n_chip}
    axes = sorted({item[0] for item in items})
    outs = []
    n_far = 0
    for axis, kind, array in items:
        n_far += n_of[axis] - 1
        shape = array.shape if kind == SPREAD else (n_of[axis],) + array.shape
        outs.append(jax.ShapeDtypeStruct(shape, array.dtype))

    def kernel(*refs):
        ins = refs[: len(items)]
        results = refs[len(items) : 2 * len(items)]
        place = Place(n_chip, n_plane)
        wires = Wires(*refs[2 * len(items) :])
        greet(place, axes)
        copies = []
        for (axis, kind, _), src, dst in zip(items, ins, results):
            mine = place.index(axis)
            for step in range(1, n_of[axis]):
                other, device = place.peer(axis, step)
                piece = src if kind == GATHER else src.at[other]
                copies.append(wires.far(piece, dst.at[mine], device))
        for (axis, kind, _), src, dst in zip(items, ins, results):
            mine = place.index(axis)
            copies.append(wires.near(src if kind == GATHER else src.at[mine], dst.at[mine]))
        wait_all(copies)

    return pl.pallas_call(
        kernel,
        out_shape=tuple(outs),
        in_specs=[ANYWHERE] * len(items),
        out_specs=tuple([ANYWHERE] * len(items)),
        scratch_shapes=[
            pltpu.SemaphoreType.DMA((n_far,)),
            pltpu.SemaphoreType.DMA((n_far,)),
            pltpu.SemaphoreType.DMA((len(items),)),
        ],
        compiler_params=pltpu.CompilerParams(collective_id=collective_id, has_side_effects=True),
        name=name,
    )(*[item[2] for item in items])


def start_kernel(dims, x, cot, ids, bias, mod, wq, w1, wp, w2):
    nc, nf = dims.nc, dims.nf
    per_q, per_1 = dims.per_q, dims.per_1
    chip_q, chip_1 = dims.chip_q, dims.chip_1
    part_q = nc * chip_q
    rows, half = mod.shape[1], mod.shape[2]
    n_far = 5 * (nf - 1) + 3 * (nc - 1) + 4 * (nc - 1) + 4 + 1 + (nc - 1) + (nf - 1) + 1
    outs = (
        jax.ShapeDtypeStruct((nc,) + x.shape, x.dtype),
        jax.ShapeDtypeStruct((nc,) + cot.shape, cot.dtype),
        jax.ShapeDtypeStruct((nc,) + ids.shape, ids.dtype),
        jax.ShapeDtypeStruct((nf,) + bias.shape, bias.dtype),
        jax.ShapeDtypeStruct((nf, 2, rows, half), F32),
        jax.ShapeDtypeStruct((3, nc, 2, chip_q) + wq.shape[1:], BF16),
        jax.ShapeDtypeStruct((chip_1, nc, 2) + w1.shape[1:], BF16),
        jax.ShapeDtypeStruct((2, nf) + wp.shape, BF16),
        jax.ShapeDtypeStruct((2, nf) + w2.shape, BF16),
        jax.ShapeDtypeStruct((nf * per_q,) + wq.shape[1:], BF16),
        jax.ShapeDtypeStruct((nf * per_1,) + w1.shape[1:], BF16),
    )

    def kernel(
        x_in, c_in, i_in, b_in, m_in, q_in, f1_in, p_in, f2_in,
        x_all, c_all, i_all, b_all, m_all, q_chip, f1_chip, p_chip, f2_chip, q_rows, f1_rows,
        m_core, m_sum, m_chip, send, recv, local,
    ):
        place = Place(nc, nf)
        wires = Wires(send, recv, local)
        c, k, f = place.c, place.k, place.f
        greet(place, (CORE, CHIP, PLANE))
        core_other, core_peer = place.peer(CORE, 1)
        chip_peers = [place.peer(CHIP, step) for step in range(1, nc)]
        plane_peers = [place.peer(PLANE, step) for step in range(1, nf)]

        m_first = wires.far(m_in.at[core_other], m_core, core_peer)
        q_got, f1_got, p_got, f2_got, small = [], [], [], [], []
        for _, peer in plane_peers:
            q_got.append(wires.far(q_in, q_rows.at[pl.ds(f * per_q, per_q)], peer))
            small.append(wires.far(b_in, b_all.at[f], peer))
        q_got.append(wires.near(q_in, q_rows.at[pl.ds(f * per_q, per_q)]))
        small.append(wires.near(b_in, b_all.at[f]))
        for _, peer in chip_peers:
            small.append(wires.far(i_in, i_all.at[c], peer))
            small.append(wires.far(x_in, x_all.at[c], peer))
        m_first.wait()
        m_sum[...] = m_in[k] + m_core[...]
        m_chip[c] = m_sum[...]
        m_second = [wires.far(m_sum, m_chip.at[c], peer) for _, peer in chip_peers]
        for _, peer in plane_peers:
            p_got.append(wires.far(p_in, p_chip.at[k, f], peer))
        for _, peer in plane_peers:
            f1_got.append(wires.far(f1_in, f1_rows.at[pl.ds(f * per_1, per_1)], peer))
        for _, peer in plane_peers:
            f2_got.append(wires.far(f2_in, f2_chip.at[k, f], peer))
        p_got.append(wires.near(p_in, p_chip.at[k, f]))
        f1_got.append(wires.near(f1_in, f1_rows.at[pl.ds(f * per_1, per_1)]))
        f2_got.append(wires.near(f2_in, f2_chip.at[k, f]))
        small.append(wires.near(i_in, i_all.at[c]))
        small.append(wires.near(x_in, x_all.at[c]))
        for _, peer in chip_peers:
            small.append(wires.far(c_in, c_all.at[c], peer))
        small.append(wires.near(c_in, c_all.at[c]))
        wait_all(m_second)
        total = m_chip[0]
        for other in range(1, nc):
            total = total + m_chip[other]
        m_all[f, k] = total
        wait_all([wires.far(m_all.at[f, k], m_all.at[f, k], peer) for _, peer in plane_peers])
        m_last = wires.far(m_all.at[:, k], m_all.at[:, k], core_peer)

        wait_all(q_got)
        q_moved = []
        for kind in range(3):
            for other, peer in chip_peers:
                q_moved.append(
                    wires.far(
                        q_rows.at[pl.ds(kind * part_q + other * chip_q, chip_q)],
                        q_chip.at[kind, c, k],
                        peer,
                    )
                )
            q_moved.append(
                wires.near(
                    q_rows.at[pl.ds(kind * part_q + c * chip_q, chip_q)], q_chip.at[kind, c, k]
                )
            )
        wait_all(p_got)
        last = [m_last, wires.far(p_chip.at[k], p_chip.at[k], core_peer)]
        wait_all(q_moved)
        last.append(wires.far(q_chip.at[:, :, k], q_chip.at[:, :, k], core_peer))
        wait_all(f1_got)
        f1_moved = []
        for other, peer in chip_peers:
            f1_moved.append(
                wires.far(f1_rows.at[pl.ds(other * chip_1, chip_1)], f1_chip.at[:, c, k], peer)
            )
        f1_moved.append(
            wires.near(f1_rows.at[pl.ds(c * chip_1, chip_1)], f1_chip.at[:, c, k])
        )
        wait_all(f2_got)
        last.append(wires.far(f2_chip.at[k], f2_chip.at[k], core_peer))
        wait_all(f1_moved)
        last.append(wires.far(f1_chip.at[:, :, k], f1_chip.at[:, :, k], core_peer))
        wait_all(small)
        wait_all(last)

    return pl.pallas_call(
        kernel,
        out_shape=outs,
        in_specs=[ANYWHERE] * 4 + [ON_CHIP] + [ANYWHERE] * 4,
        out_specs=tuple([ANYWHERE] * 4 + [ON_CHIP] + [ANYWHERE] * 6),
        scratch_shapes=[
            pltpu.VMEM((rows, half), F32),
            pltpu.VMEM((rows, half), F32),
            pltpu.VMEM((nc, rows, half), F32),
            pltpu.SemaphoreType.DMA((n_far,)),
            pltpu.SemaphoreType.DMA((n_far,)),
            pltpu.SemaphoreType.DMA((12,)),
        ],
        compiler_params=pltpu.CompilerParams(collective_id=0, has_side_effects=True),
        name="start",
    )(x, cot, ids, bias, mod, wq, w1, wp, w2)


def sum_small_kernel(dims, terms):
    nc, nf = dims.nc, dims.nf
    _, _, rows, half = terms.shape
    n_far = (nf - 1) + 1 + (nc - 1) + 1

    def kernel(t_in, total, z_got, both, core_got, chip_got, send, recv, local):
        place = Place(nc, nf)
        wires = Wires(send, recv, local)
        c, k, f = place.c, place.k, place.f
        greet(place, (CORE, CHIP, PLANE))
        core_other, core_peer = place.peer(CORE, 1)
        copies = []
        for step in range(1, nf):
            other, peer = place.peer(PLANE, step)
            copies.append(wires.far(t_in.at[other], z_got.at[f], peer))
        z_got[f] = t_in[f]
        wait_all(copies)
        value = z_got[0]
        for other in range(1, nf):
            value = value + z_got[other]
        both[...] = value
        wires.far(both.at[core_other], core_got, core_peer).wait()
        chip_got[c] = both[k] + core_got[...]
        copies = []
        for step in range(1, nc):
            _, peer = place.peer(CHIP, step)
            copies.append(wires.far(chip_got.at[c], chip_got.at[c], peer))
        wait_all(copies)
        value = chip_got[0]
        for other in range(1, nc):
            value = value + chip_got[other]
        total[k] = value
        wires.far(total.at[k], total.at[k], core_peer).wait()

    return pl.pallas_call(
        kernel,
        out_shape=jax.ShapeDtypeStruct((2, rows, half), F32),
        in_specs=[ON_CHIP],
        out_specs=ON_CHIP,
        scratch_shapes=[
            pltpu.VMEM((nf, 2, rows, half), F32),
            pltpu.VMEM((2, rows, half), F32),
            pltpu.VMEM((rows, half), F32),
            pltpu.VMEM((nc, rows, half), F32),
            pltpu.SemaphoreType.DMA((n_far,)),
            pltpu.SemaphoreType.DMA((n_far,)),
            pltpu.SemaphoreType.DMA((1,)),
        ],
        compiler_params=pltpu.CompilerParams(collective_id=1, has_side_effects=True),
        name="sum_small",
    )(terms)


def cond_kernel(dims, part):
    nc, nf = dims.nc, dims.nf
    nd = 2 * nc
    rows, width = part.shape
    n_far = (nf - 1) + (nd - 1)

    def kernel(p_in, out, got, send, recv, local):
        place = Place(nc, nf)
        wires = Wires(send, recv, local)
        greet(place, (PLANE, ALL))
        copies = []
        for step in range(1, nf):
            copies.append(wires.far(p_in, got.at[place.f], place.peer(PLANE, step)[1]))
        got[place.f] = p_in[...]
        wait_all(copies)
        value = got[0]
        for other in range(1, nf):
            value = value + got[other]
        out[place.dp] = value
        copies = []
        for step in range(1, nd):
            copies.append(
                wires.far(out.at[place.dp], out.at[place.dp], place.peer(ALL, step)[1])
            )
        wait_all(copies)

    return pl.pallas_call(
        kernel,
        out_shape=jax.ShapeDtypeStruct((nd, rows, width), F32),
        in_specs=[ON_CHIP],
        out_specs=ON_CHIP,
        scratch_shapes=[
            pltpu.VMEM((nf, rows, width), F32),
            pltpu.SemaphoreType.DMA((n_far,)),
            pltpu.SemaphoreType.DMA((n_far,)),
            pltpu.SemaphoreType.DMA((1,)),
        ],
        compiler_params=pltpu.CompilerParams(collective_id=2, has_side_effects=True),
        name="cond_sum",
    )(part)


def dot(left, right):
    return jnp.dot(left, right, preferred_element_type=F32)


def dot_rt(left, right):
    return lax.dot_general(left, right, (((1,), (1,)), ((), ())), preferred_element_type=F32)


def dot_lt(left, right):
    return lax.dot_general(left, right, (((0,), (0,)), ((), ())), preferred_element_type=F32)


def precise(left, right, dims):
    return lax.dot_general(
        left, right, (dims, ((), ())), precision=PRECISE, preferred_element_type=F32
    )


def ln_parts(values):
    centre = values - jnp.mean(values, axis=-1, keepdims=True)
    scale = lax.rsqrt(jnp.mean(centre * centre, axis=-1, keepdims=True) + EPS)
    return centre * scale, scale


def ln_back(normal, scale, grad):
    return scale * (
        grad
        - jnp.mean(grad, axis=-1, keepdims=True)
        - normal * jnp.mean(grad * normal, axis=-1, keepdims=True)
    )


def gelu_both(h):
    square = h * h
    t = jnp.tanh(GELU_C * (h + 0.044715 * h * square))
    value = 0.5 * h * (1.0 + t)
    slope = 0.5 * (1.0 + t) + 0.5 * h * (1.0 - t * t) * GELU_C * (1.0 + 3 * 0.044715 * square)
    return value, slope


def dot3(left, right):
    wide_left = left.dtype == F32
    value = left if wide_left else right
    total = None
    for _ in range(3):
        term = value.astype(BF16)
        value = value - term.astype(F32)
        part = dot(term, right) if wide_left else dot(left, term)
        total = part if total is None else total + part
    return total


def add_low(left, right):
    return (left.astype(F32) + right.astype(F32)).astype(BF16)


def block_kernel(dims, x, cot, frames, clips, biases, cond, w_ada, wq, wp, w1, w2):
    nc, nf = dims.nc, dims.nf
    own, width = x.shape
    group = nc * own
    rows_d, q_w = wq.shape
    chip_w = q_w // 3
    cols_f, ff_d = w2.shape
    ff_c = 2 * ff_d
    ada_w = w_ada.shape[1]
    n_bias = sum(item.shape[0] for item in biases)
    heads = chip_w // HEAD_DIM
    micro, n_clips, _ = cond.shape
    n_rows = micro * n_clips
    half = n_rows // 2
    n_sub = own // SUB
    head_scale = HEAD_DIM ** (-0.5)
    last = nf - 2
    third = rows_d // 3

    outs = (
        jax.ShapeDtypeStruct((own, width), BF16),
        jax.ShapeDtypeStruct((own, width), BF16),
        jax.ShapeDtypeStruct((n_rows, cols_f), F32),
        jax.ShapeDtypeStruct((rows_d, ada_w), F32),
        jax.ShapeDtypeStruct((ada_w,), F32),
        jax.ShapeDtypeStruct((rows_d, q_w), F32),
        jax.ShapeDtypeStruct((2 * chip_w,), F32),
        jax.ShapeDtypeStruct((rows_d, cols_f), F32),
        jax.ShapeDtypeStruct((cols_f,), F32),
        jax.ShapeDtypeStruct((rows_d, ff_c), F32),
        jax.ShapeDtypeStruct((ff_c,), F32),
        jax.ShapeDtypeStruct((cols_f, ff_d), F32),
        jax.ShapeDtypeStruct((cols_f,), F32),
    )
    tokens = (nc, own, width)
    n_sem = 240
    scratch = dict(
        xg=pltpu.VMEM(tokens, BF16),
        cg=pltpu.VMEM(tokens, BF16),
        idsg=pltpu.VMEM((nc, 2, own), F32),
        biasg=pltpu.VMEM((nf, 1, n_bias), F32),
        ada=pltpu.VMEM(w_ada.shape, BF16),
        silu=pltpu.VMEM((n_rows, rows_d), BF16),
        cond_own=pltpu.VMEM((n_rows, cols_f), F32),
        m_part=pltpu.VMEM((2, half, ada_w), F32),
        m_core=pltpu.VMEM((half, ada_w), F32),
        m_chip=pltpu.VMEM((nc, half, ada_w), F32),
        m_z=pltpu.VMEM((nf, 2, half, ada_w), BF16),
        m_tab=pltpu.VMEM((n_rows, 6 * width), F32),
        tab=pltpu.VMEM((3, nc * n_sub, width), F32),
        own_tab=pltpu.VMEM((6, n_sub, width), F32),
        q_z=pltpu.VMEM((nf, rows_d, q_w + cols_f), BF16),
        q_rows=pltpu.VMEM((nf * 3, third, q_w), BF16),
        q_got=pltpu.VMEM((3, nc, third, q_w), BF16),
        w_q=pltpu.VMEM((nc, 2, rows_d, q_w), BF16),
        y_got=pltpu.VMEM((nc, rows_d, q_w), BF16),
        f1_z=pltpu.VMEM((nf, rows_d, ff_c), BF16),
        w_1=pltpu.VMEM((nc, 2, rows_d, ff_c), BF16),
        p_got=pltpu.VMEM((2, nf, rows_d, cols_f), BF16),
        w_p=pltpu.VMEM((chip_w, width), BF16),
        f2_half=pltpu.VMEM((cols_f, ff_d), BF16),
        f2_got=pltpu.VMEM((rows_d, ff_d), BF16),
        w_2=pltpu.VMEM((nf, 2, rows_d, ff_c), BF16),
        a_in=pltpu.VMEM(tokens, BF16),
        qkv=pltpu.VMEM((3, nc, own, chip_w), BF16),
        probs=pltpu.VMEM((nc * heads, own, own), F32),
        mixed=pltpu.VMEM((nc, own, chip_w), BF16),
        sum_s=pltpu.VMEM(tokens, BF16),
        sum_r=pltpu.VMEM((2, own, width), BF16),
        sum_st=pltpu.VMEM((2, own // 2, width), BF16),
        br_s=pltpu.VMEM(tokens, BF16),
        br_r=pltpu.VMEM((2, own, width), BF16),
        br_st=pltpu.VMEM((2, own // 2, width), BF16),
        m_all=pltpu.VMEM(tokens, BF16),
        da_all=pltpu.VMEM(tokens, BF16),
        attn=pltpu.VMEM((own, width), F32),
        after=pltpu.VMEM((own, width), F32),
        d_after=pltpu.VMEM((own, width), F32),
        hid=pltpu.VMEM((own, ff_c), F32),
        act=pltpu.VMEM((nc, own, ff_c), BF16),
        d_hid=pltpu.VMEM((nc, own, ff_c), BF16),
        dbr=pltpu.VMEM(tokens, BF16),
        d_qkv=pltpu.VMEM((nc, own, q_w), BF16),
        g_2=pltpu.VMEM((nf, 2, rows_d, ff_c), BF16),
        g_2r=pltpu.VMEM((nf, rows_d, ff_c), BF16),
        g_1r=pltpu.VMEM((nc, rows_d, ff_c), BF16),
        g_qr=pltpu.VMEM((nc, rows_d, q_w), BF16),
        g_pr=pltpu.VMEM((rows_d, width), BF16),
        got_q=pltpu.VMEM((2, nf - 1, rows_d, q_w + cols_f), BF16),
        got_1=pltpu.VMEM((2, nf - 1, rows_d, ff_c), BF16),
        got_2=pltpu.VMEM((2, nf - 1, rows_d, ff_c), BF16),
        all_2=pltpu.VMEM((2, rows_d, ff_c), F32),
        sub=pltpu.VMEM((6, n_sub, width), F32),
        q_nat=pltpu.VMEM((rows_d, q_w), BF16),
        p_nat=pltpu.VMEM((rows_d, cols_f), BF16),
        all_q=pltpu.VMEM((rows_d, q_w + cols_f), F32),
        sub_lin=pltpu.VMEM((2, nc * n_sub, width), F32),
        sub_gate=pltpu.VMEM((nc * n_sub, width), F32),
        d_part=pltpu.VMEM((2, half, 6 * width), F32),
        d_core=pltpu.VMEM((half, 6 * width), F32),
        d_cut=pltpu.VMEM((nf, half, ada_w), BF16),
        d_bias=pltpu.VMEM((8, width), F32),
        dz=pltpu.VMEM((nf, half, ada_w), BF16),
        dzb=pltpu.VMEM((nf, 8, width), BF16),
        d_tot=pltpu.VMEM((2, half, ada_w), F32),
        d_low=pltpu.VMEM((8, width), BF16),
        d_bsum=pltpu.VMEM((8, width), F32),
        d_coreb=pltpu.VMEM((8, width), F32),
        d_chipb=pltpu.VMEM((nc, 8, width), F32),
        c_part=pltpu.VMEM((nf, n_rows, rows_d), F32),
        c_all=pltpu.VMEM((nc, 2, n_rows, rows_d), F32),
        send=pltpu.SemaphoreType.DMA((n_sem,)),
        recv=pltpu.SemaphoreType.DMA((n_sem,)),
        local=pltpu.SemaphoreType.DMA((40,)),
    )
    names = list(scratch)

    def kernel(
        x_in, c_in, frames_in, clips_in, bq_in, bp_in, b1_in, b2_in, ba_in, cond_in, ada_in,
        q_in, p_in, f1_in, f2_in,
        *rest,
    ):
        homes, rest = rest[: len(outs)], rest[len(outs) :]
        held, rest = rest[: len(outs)], rest[len(outs) :]
        (out, x_grad, o_cond, o_ada, o_bada, o_q, o_bqv, o_p, o_bp, o_1, o_b1, o_2, o_b2) = held
        home_of = {id(ref): home for ref, home in zip(held, homes)}
        landed = []
        r = types.SimpleNamespace(**dict(zip(names, rest)))
        place = Place(nc, nf)
        wires = Wires(r.send, r.recv, r.local)
        c, k, f = place.c, place.k, place.f
        core_o, core_dev = place.peer(CORE, 1)
        chip_peers = [place.peer(CHIP, step) for step in range(1, nc)]
        plane_peers = [place.peer(PLANE, step) for step in range(1, nf)]

        def loop(count, body, unroll=1):
            def run(i, carry):
                body(i)
                return carry

            lax.fori_loop(0, count, run, 0, unroll=unroll)

        def loop_rows(body):
            loop(n_sub, body, 2)

        def when(condition, body):
            pl.when(condition)(body)

        def sub_rows(g):
            return pl.ds(pl.multiple_of(g * SUB, SUB), SUB)

        def reserve(count):
            base = wires.remote_count
            wires.remote_count += count
            return base

        def pair(src, dst, device, send_at, recv_at):
            return pltpu.make_async_remote_copy(
                src_ref=src,
                dst_ref=dst,
                send_sem=r.send.at[send_at],
                recv_sem=r.recv.at[recv_at],
                device_id=device,
                device_id_type=MESH_ID,
            )

        chip_x, dev_x = place.peer(CHIP, 1)
        chip_y, dev_y = place.peer(CHIP, 2)
        chip_d, _ = place.peer(CHIP, 3)
        first_half, second_half = pl.ds(0, own // 2), pl.ds(own // 2, own // 2)

        class Share:
            def __init__(self, ref, src=None):
                def copy(chip, rows, device, at, own_src=None):
                    from_ref = ref.at[chip, rows] if own_src is None else own_src.at[rows]
                    return pair(from_ref, ref.at[chip, rows], device, at, at)

                at = reserve(6)
                self.x_a = copy(c, first_half, dev_x, at, src)
                self.x_b = copy(c, second_half, dev_x, at + 1, src)
                self.y_b = copy(c, second_half, dev_y, at + 2, src)
                self.y_a = copy(c, first_half, dev_y, at + 3, src)
                self.on_y = copy(chip_x, first_half, dev_y, at + 4)
                self.on_x = copy(chip_y, second_half, dev_x, at + 5)

            def start(self):
                for item in (self.x_a, self.y_b, self.x_b, self.y_a):
                    item.start()

            def relay(self):
                self.x_a.wait_recv()
                self.on_y.start()
                self.y_b.wait_recv()
                self.on_x.start()

            def arrive(self, step):
                if step == 1:
                    self.x_b.wait_recv()
                elif step == 2:
                    self.y_a.wait_recv()
                else:
                    self.on_y.wait_recv()
                    self.on_x.wait_recv()

            def sent(self):
                for item in (self.x_a, self.x_b, self.y_b, self.y_a, self.on_y, self.on_x):
                    item.wait_send()

        class Merge:
            def __init__(self, terms, got, stage):
                self.terms, self.got, self.stage = terms, got, stage
                at = reserve(6)
                self.d_x = pair(terms.at[chip_d, first_half], stage.at[0], dev_x, at, at)
                self.d_y = pair(terms.at[chip_d, second_half], stage.at[1], dev_y, at + 1, at + 1)

                def copy(chip, rows, to, device, index):
                    return pair(
                        terms.at[chip, rows], got.at[to, rows], device, at + index, at + index
                    )

                self.x_a = copy(chip_x, first_half, 0, dev_x, 2)
                self.x_b = copy(chip_x, second_half, 0, dev_x, 3)
                self.y_b = copy(chip_y, second_half, 1, dev_y, 4)
                self.y_a = copy(chip_y, first_half, 1, dev_y, 5)

            def put(self, step, blk, part):
                self.terms[blk] = part

                def far():
                    self.d_x.start()
                    self.d_y.start()

                when(step == 3, far)
                when(step == 2, self.y_b.start)
                when(step == 1, self.x_a.start)

            def launch(self):
                for item in (self.d_x, self.d_y, self.y_b, self.x_a):
                    item.start()

            def combine(self):
                self.d_y.wait()
                ref = self.terms.at[chip_x, second_half]
                ref[...] = add_low(ref[...], self.stage[1])
                self.x_b.start()
                self.d_x.wait()
                ref = self.terms.at[chip_y, first_half]
                ref[...] = add_low(ref[...], self.stage[0])
                self.y_a.start()

            def finish(self):
                for item in (self.x_a, self.x_b, self.y_b, self.y_a):
                    item.wait()

            def rows(self, at):
                value = self.terms[c, at, :].astype(F32) + self.got[0, at, :].astype(F32)
                return value + self.got[1, at, :].astype(F32)

        def land(*refs):
            for ref in refs:
                landed.append(wires.near(ref, home_of[id(ref)]))

        up, down = (place.dp, f + 1), (place.dp, f - 1)

        class Gather:
            def __init__(self, slot):
                self.slot = slot
                self.up, self.down = reserve(nf - 1), reserve(nf - 1)

            def both(self, step, src=None):
                above = pair(
                    self.slot(f - step) if src is None else src,
                    self.slot(f - step), up, self.up + step, self.up + step,
                )
                below = pair(
                    self.slot(f + step) if src is None else src,
                    self.slot(f + step), down, self.down + step, self.down + step,
                )
                return (
                    ((f - step >= 0) & (f < nf - 1), above),
                    ((f + step <= nf - 1) & (f > 0), below),
                )

            def start(self, step, src=None):
                for condition, copy in self.both(step, src):
                    when(condition, copy.start)

            def arrive(self, step, then=None, wait=True):
                for condition, got, base in (
                    (f - 1 - step >= 0, f - 1 - step, self.up),
                    (f + 1 + step <= nf - 1, f + 1 + step, self.down),
                ):

                    def body(got=got, base=base):
                        slot = self.slot(got)
                        if wait:
                            pair(slot, slot, core_dev, base + step, base + step).wait_recv()
                        if then is not None:
                            then(got)

                    when(condition, body)

            def sent(self, src=None):
                for step in range(nf - 1):
                    for condition, copy in self.both(step, src if step == 0 else None):
                        when(condition, copy.wait_send)

        class Sum:
            def __init__(self, terms, got):
                self.terms, self.got = terms, got
                self.bases = (reserve(nf - 1), reserve(nf - 1))

            def both(self, step):
                for way in range(2):
                    target = f + (nf - 1) - step if way == 0 else f - (nf - 1) + step
                    condition = (f <= step) & (f < nf - 1) if way == 0 else (target >= 0) & (f > 0)
                    more = condition & (f > 0 if way == 0 else f < nf - 1)
                    at = self.bases[way] + step
                    copy = pair(
                        self.terms(target), self.got.at[way, step], up if way == 0 else down, at, at
                    )
                    yield way, target, condition, more, copy

            def wait(self, way, step):
                at = self.bases[way] + step
                ref = self.got.at[way, step]
                pair(ref, ref, core_dev, at, at).wait_recv()

            def start(self, step):
                for way, target, condition, more, copy in self.both(step):
                    if step > 0:

                        def body(way=way, target=target):
                            self.wait(way, step - 1)
                            ref = self.terms(target)
                            ref[...] = add_low(ref[...], self.got[way, step - 1])

                        when(more, body)
                    when(condition, copy.start)

            def finish(self, result):
                result[...] = self.terms(f)[...].astype(F32)
                for way, condition in ((0, f > 0), (1, f < nf - 1)):

                    def body(way=way):
                        self.wait(way, last)
                        result[...] = result[...] + self.got[way, last].astype(F32)

                    when(condition, body)
                for step in range(nf - 1):
                    for _, _, condition, _, copy in self.both(step):
                        when(condition, copy.wait_send)

        def own_side(ref, side):
            return ref.at[pl.ds(pl.multiple_of(side * rows_d, SUB), rows_d)]

        barrier = pltpu.get_barrier_semaphore()
        peers = [core_dev] + [peer for _, peer in chip_peers + plane_peers]
        for peer in peers:
            pl.semaphore_signal(barrier, inc=1, device_id=peer, device_id_type=MESH_ID)

        q_line = Gather(lambda g: r.q_z.at[g])
        f1_line = Gather(lambda g: r.f1_z.at[g])
        f2_line = Gather(lambda g: r.w_2.at[g, k])
        ada_near = wires.near(ada_in, r.ada)
        q_near = wires.near(q_in, r.q_nat)
        p_near = wires.near(p_in, r.p_nat)
        f2_near = wires.near(f2_in, r.f2_half)
        first = []
        first.append(wires.near(x_in, r.xg.at[c]))
        first.append(wires.near(c_in, r.cg.at[c]))
        f1_near = wires.near(f1_in, r.f1_z.at[f])
        order = lax.broadcasted_iota(jnp.int32, frames_in.shape, 0)
        for at, value in ((0, frames_in[...] + 65536 * order), (1, clips_in[...] + n_clips * order)):
            row = [value[i : i + 1].astype(F32) for i in range(micro)]
            r.idsg[c, at : at + 1, :] = jnp.concatenate(row, axis=1)
        row = [ref[...].astype(F32).reshape(1, ref.shape[0]) for ref in (bq_in, bp_in, b1_in, b2_in, ba_in)]
        r.biasg[f] = jnp.concatenate(row, axis=1)
        cond_rows = cond_in[...].reshape(n_rows, width)

        def own_silu(at):
            part = cond_rows[:, rows_d * at : rows_d * (at + 1)]
            r.silu[...] = (part / (1.0 + jnp.exp(-part))).astype(BF16)

        def own_cond(at):
            r.cond_own[...] = cond_rows[:, cols_f * at : cols_f * (at + 1)]

        for at in range(2 * nc):
            when(place.dp == at, functools.partial(own_silu, at))
        for at in range(nf):
            when(f == at, functools.partial(own_cond, at))
        ada_near.wait()
        ada_bias = jnp.where(place.dp == 0, row[4], 0.0)
        value = dot(r.silu[...], r.ada[...]) + ada_bias
        r.m_part[...] = value.reshape(2, half, ada_w)
        q_near.wait()
        p_near.wait()
        r.q_z[f] = jnp.concatenate([r.q_nat[...], r.p_nat[...]], axis=1)
        f2_near.wait()
        pl.semaphore_wait(barrier, len(peers))
        m_first = wires.far(r.m_part.at[core_o], r.m_core, core_dev)
        q_line.start(0)
        for _, peer in chip_peers:
            first.append(wires.far(r.idsg.at[c], r.idsg.at[c], peer))
        f2_swap = wires.far(own_side(r.f2_half, core_o), r.f2_got, core_dev)

        w_q, q_rows = r.w_q, r.q_rows
        q_base = reserve(3 * nc)
        q_local = wires.local_count
        wires.local_count += 3

        def q_copies(plane, i):
            piece = 3 * plane + i
            kind, chip = piece // nc, piece % nc
            src, dst = q_rows.at[piece], r.q_got.at[kind, c]
            far = pair(src, dst, (chip * 2 + k, f), q_base + kind * nc + chip, q_base + kind * nc + c)
            return chip, far, pltpu.make_async_copy(src, dst, r.local.at[q_local + kind])

        def q_forward(plane):
            r.p_got[k, plane] = r.q_z[plane, :, q_w:]
            for i in range(3):
                piece = r.q_z[plane, :, chip_w * i : chip_w * (i + 1)]
                parts = [piece[third * j : third * (j + 1)] for j in range(3)]
                q_rows[3 * plane + i] = jnp.concatenate(parts, axis=1)
                chip, far, near = q_copies(plane, i)
                when(chip != c, far.start)
                when(chip == c, near.start)

        f1_base = reserve(nc)
        f1_local = wires.local_count
        wires.local_count += 1

        def f1_copies(plane):
            src, dst = r.f1_z.at[plane], r.w_1.at[c, k]
            far = pair(src, dst, (plane * 2 + k, f), f1_base + plane, f1_base + c)
            return far, pltpu.make_async_copy(src, dst, r.local.at[f1_local])

        def f1_forward(plane):
            far, near = f1_copies(plane)
            when(plane != c, far.start)
            when(plane == c, near.start)

        m_first.wait()
        m_chip = r.m_chip
        m_chip[c] = r.m_part[k] + r.m_core[...]
        m_second = [wires.far(m_chip.at[c], m_chip.at[c], peer) for _, peer in chip_peers]
        q_forward(f)
        x_share = Share(r.xg, x_in)
        x_share.start()
        wait_all(m_second)
        total = m_chip[0]
        for other in range(1, nc):
            total = total + m_chip[other]
        r.m_z[f, k] = total.astype(BF16)
        m_third = [wires.far(r.m_z.at[f, k], r.m_z.at[f, k], peer) for _, peer in plane_peers]
        for _, peer in plane_peers:
            first.append(wires.far(r.biasg.at[f], r.biasg.at[f], peer))
        q_line.arrive(0, q_forward)
        q_line.start(1)
        x_share.relay()
        f2_swap.wait()

        def join_even():
            r.w_2[f, k] = jnp.concatenate([r.f2_half[:rows_d], r.f2_got[...]], axis=1)

        def join_odd():
            r.w_2[f, k] = jnp.concatenate([r.f2_got[...], r.f2_half[rows_d:]], axis=1)

        when(k == 0, join_even)
        when(k == 1, join_odd)
        f2_base = reserve(nf)

        def f2_across(plane):
            ref = r.w_2.at[plane, k]
            return pair(ref, ref, core_dev, f2_base + plane, f2_base + plane)

        def f2_forward(plane):
            f2_across(plane).start()

        f2_forward(f)
        wait_all(m_third)
        m_last = wires.far(r.m_z.at[:, k], r.m_z.at[:, k], core_dev)

        wait_all(first)
        m_last.wait()
        m_rows = [r.m_z[plane].astype(F32).reshape(n_rows, ada_w) for plane in range(nf)]
        r.m_tab[...] = jnp.concatenate(m_rows, axis=1)
        lead = lax.broadcasted_iota(jnp.int32, (n_sub, own), 1)
        lead = lead == SUB * lax.broadcasted_iota(jnp.int32, (n_sub, own), 0)
        lead = jnp.where(lead, 1.0, 0.0).astype(BF16)
        places = lax.broadcasted_iota(jnp.int32, (own, n_rows), 1).astype(F32)

        def hot_rows(blk):
            clip = r.idsg[blk].T[:, 1:2]
            return dot(lead, jnp.where(clip == places, 1.0, 0.0).astype(BF16)).astype(BF16)

        hot_all = jnp.concatenate([hot_rows(blk) for blk in range(nc)], axis=0)
        own_hot = hot_rows(c)
        for kind in range(6):
            value = r.m_tab[:, width * kind : width * (kind + 1)]
            if kind in (0, 1, 5):
                r.tab[kind % 3] = dot3(hot_all, value)
            r.own_tab[kind] = dot3(own_hot, value)

        def tab_row(kind, blk, g):
            return r.tab[kind % 3, pl.ds(blk * n_sub + g, 1), :]

        def own_row(kind, g):
            return r.own_tab[kind, pl.ds(g, 1), :]

        def make_a(blk):
            def body(g):
                rows = sub_rows(g)
                normal, _ = ln_parts(r.xg[blk, rows, :].astype(F32))
                value = normal * (1.0 + tab_row(1, blk, g)) + tab_row(0, blk, g)
                r.a_in[blk, rows, :] = value.astype(BF16)

            loop_rows(body)

        make_a(c)
        for step in (1, 2):
            x_share.arrive(step)
            make_a(xor_of(c, step, nc))
        q_line.arrive(1, q_forward)
        q_line.start(2)
        f1_line.start(0, f1_in)
        x_share.arrive(3)
        make_a(chip_d)
        q_line.arrive(2, q_forward)

        for kind in range(3):
            for other, _ in chip_peers:
                ref = r.q_got.at[kind, other]
                at = q_base + kind * nc + other
                pair(ref, ref, core_dev, at, at).wait()
            ref = r.q_got.at[kind, c]
            pltpu.make_async_copy(ref, ref, r.local.at[q_local + kind]).wait()
        q_core = []
        for chip in range(nc):
            for j in range(3):
                at = chip_w * j
                row = [r.q_got[kind, chip, :, at : at + chip_w] for kind in range(3)]
                w_q[chip, k, third * j : third * (j + 1), :] = jnp.concatenate(row, axis=1)
            q_core.append(wires.far(w_q.at[chip, k], w_q.at[chip, k], core_dev))
        p_core = wires.far(r.p_got.at[k], r.p_got.at[k], core_dev)
        f1_near.wait()
        f1_forward(f)
        f1_line.arrive(0, f1_forward)
        f1_line.start(1)
        x_share.sent()
        p_core.wait()
        for side in range(2):
            row = [r.p_got[side, plane] for plane in range(nf)]
            r.w_p[side * rows_d : (side + 1) * rows_d, :] = jnp.concatenate(row, axis=1)
        wait_all(q_core)

        lane = lax.broadcasted_iota(jnp.int32, (1, chip_w), 1)
        head_of = [
            jnp.where((lane >= HEAD_DIM * h) & (lane < HEAD_DIM * (h + 1)), 1.0, 0.0).astype(BF16)
            for h in range(heads)
        ]

        def weight_q():
            return w_q[...].reshape(width, q_w)

        def qv_bias(plane):
            row = r.biasg[plane]
            return jnp.where(c % 2 == 0, row[:, :chip_w], row[:, chip_w : 2 * chip_w])

        bias_q, bias_v = qv_bias(c // 2), qv_bias(nf // 2 + c // 2)
        at_p = 2 * chip_w
        at_1 = at_p + cols_f
        at_2 = at_1 + ff_c
        bias_p = jnp.concatenate([r.biasg[g][:, at_p : at_p + cols_f] for g in range(nf)], axis=1)
        bias_o = jnp.concatenate([r.biasg[g][:, at_2 : at_2 + cols_f] for g in range(nf)], axis=1)
        bias_1 = r.biasg[c][:, at_1 : at_1 + ff_c]
        zero = jnp.zeros_like(bias_q)
        bias_qkv = jnp.concatenate([bias_q, zero, bias_v], axis=1)
        attn_merge = Merge(r.sum_s, r.sum_r, r.sum_st)

        def attend(i):
            step = nc - 1 - i
            blk = xor_of(c, step, nc)
            value = (dot(r.a_in[blk], weight_q()) + bias_qkv).astype(BF16)
            for kind in range(3):
                r.qkv[kind, blk] = value[:, chip_w * kind : chip_w * (kind + 1)]
            q_now, k_now, v_now = r.qkv[0, blk], r.qkv[1, blk], r.qkv[2, blk]
            frames = r.idsg[blk]
            same = frames.T[:, 0:1] == frames[0:1, :]
            mixed = jnp.zeros((own, chip_w), F32)
            for h in range(heads):
                scores = dot_rt(q_now * head_of[h], k_now) * head_scale
                scores = jnp.where(same, scores, NEG_FILL)
                raised = jnp.exp(scores - jnp.max(scores, axis=-1, keepdims=True))
                share = raised / jnp.sum(raised, axis=-1, keepdims=True)
                r.probs[blk * heads + h] = share
                mixed = mixed + dot(share.astype(BF16), v_now * head_of[h])
            mixed = mixed.astype(BF16)
            r.mixed[blk] = mixed
            attn_merge.put(step, blk, dot(mixed, r.w_p[...]).astype(BF16))

            def next_lines():
                f1_line.arrive(1)
                f1_line.start(2)
                f2_line.start(0)

            when(i == 1, next_lines)

        loop(nc, attend)
        attn_merge.combine()
        f1_line.arrive(1, f1_forward, False)
        f1_line.arrive(2, f1_forward)

        attn_merge.finish()

        def after_attention(g):
            rows = sub_rows(g)
            value = attn_merge.rows(rows) + bias_p
            r.attn[rows, :] = value
            after = r.xg[c, rows, :].astype(F32) + own_row(2, g) * value
            r.after[rows, :] = after
            normal, _ = ln_parts(after)
            r.m_all[c, rows, :] = (normal * (1.0 + own_row(4, g)) + own_row(3, g)).astype(BF16)

        loop_rows(after_attention)
        m_all = r.m_all
        m_share = Share(m_all)
        m_share.start()
        c_share = Share(r.cg, c_in)
        c_share.start()
        f2_line.arrive(0, f2_forward)
        f2_line.start(1)
        f1_core = []
        ref = r.w_1.at[c, k]
        pltpu.make_async_copy(ref, ref, r.local.at[f1_local]).wait()
        f1_core.append(wires.far(ref, ref, core_dev))
        for other, _ in chip_peers:
            ref = r.w_1.at[other, k]
            pair(ref, ref, core_dev, f1_base + other, f1_base + other).wait()
            f1_core.append(wires.far(ref, ref, core_dev))
        m_share.relay()
        f1_line.sent(f1_in)
        f2_line.arrive(1, f2_forward)
        f2_line.start(2)
        wait_all(f1_core)

        def weight_1():
            return r.w_1[...].reshape(width, ff_c)

        def weight_2():
            return r.w_2[...].reshape(width, ff_c)

        dm_merge = Merge(r.sum_s, r.sum_r, r.sum_st)
        br_merge = Merge(r.br_s, r.br_r, r.br_st)

        def mixed_order(i):
            return (1 + 2 * i) * (1 - i // 2) + (6 - 2 * i) * (i // 2)

        def feed(step):
            blk = xor_of(c, step, nc)
            for at in range(1, nc):
                when(step == at, functools.partial(m_share.arrive, at))
            r.hid[...] = dot(m_all[blk], weight_1()) + bias_1

            def gelu_rows(g):
                rows = sub_rows(g)
                value, slope = gelu_both(r.hid[rows, :])
                r.act[blk, rows, :] = value.astype(BF16)
                r.d_hid[blk, rows, :] = slope.astype(BF16)

            loop_rows(gelu_rows)
            when(step == 1, c_share.relay)

        def feed_back(i):
            step = mixed_order(i)
            blk = xor_of(c, step, nc)
            for at in range(1, nc):
                when(step == at, functools.partial(c_share.arrive, at))

            def dbr_rows(g):
                rows = sub_rows(g)
                value = r.cg[blk, rows, :].astype(F32) * tab_row(5, blk, g)
                r.dbr[blk, rows, :] = value.astype(BF16)

            loop_rows(dbr_rows)
            r.hid[...] = dot(r.dbr[blk], weight_2())

            def back_rows(g):
                rows = sub_rows(g)
                value = r.hid[rows, :] * r.d_hid[blk, rows, :].astype(F32)
                r.d_hid[blk, rows, :] = value.astype(BF16)

            loop_rows(back_rows)
            dm_merge.put(step, blk, dot_rt(r.d_hid[blk], weight_1()).astype(BF16))

        loop(nc, feed)
        f2_line.arrive(2, f2_forward)
        for plane in range(nf):
            f2_across(plane).wait()
        loop(nc, feed_back)

        def column_cuts(count):
            return [(at, min(at + 256, count)) for at in range(0, count, 256)]

        def all_rows(ref):
            return ref[...].reshape(group, ref.shape[-1])

        dbr_all = all_rows(r.dbr)
        for lo, hi in column_cuts(ff_c):
            value = dot_lt(dbr_all, r.act[:, :, lo:hi].reshape(group, hi - lo))
            r.g_2[:, :, :, lo:hi] = value.astype(BF16).reshape(nf, 2, rows_d, hi - lo)
        g2_core = wires.far(r.g_2.at[:, core_o], r.g_2r, core_dev)

        dm_merge.combine()
        g_1 = r.w_1
        m_rows_all = all_rows(m_all)
        for lo, hi in column_cuts(ff_c):
            value = dot_lt(m_rows_all, r.d_hid[:, :, lo:hi].reshape(group, hi - lo))
            g_1[:, :, :, lo:hi] = value.astype(BF16).reshape(nc, 2, rows_d, hi - lo)
        g1_core = wires.far(g_1.at[:, core_o], r.g_1r, core_dev)
        c_share.sent()
        g2_core.wait()
        for plane in range(nf):
            r.g_2[plane, k] = add_low(r.g_2[plane, k], r.g_2r[plane])
        sum_2 = Sum(lambda t: r.g_2.at[t, k], r.got_2)
        sum_2.start(0)


        dm_merge.finish()
        da_all = r.da_all

        def back_norm2(g):
            rows = sub_rows(g)
            d_m = dm_merge.rows(rows)
            normal, scale = ln_parts(r.after[rows, :])
            cot_now = r.cg[c, rows, :].astype(F32)
            d_after = cot_now + ln_back(normal, scale, d_m * (1.0 + own_row(4, g)))
            r.d_after[rows, :] = d_after
            da_all[c, rows, :] = (own_row(2, g) * d_after).astype(BF16)
            at = pl.ds(g, 1)
            r.sub[3, at, :] = jnp.sum(d_m, axis=0, keepdims=True)
            r.sub[4, at, :] = jnp.sum(d_m * normal, axis=0, keepdims=True)
            r.sub[2, at, :] = jnp.sum(d_after * r.attn[rows, :], axis=0, keepdims=True)

        loop_rows(back_norm2)
        da_share = Share(da_all)
        da_share.start()
        m_share.sent()
        da_share.relay()

        g1_core.wait()
        for chip in range(nc):
            g_1[chip, k] = add_low(g_1[chip, k], r.g_1r[chip])
        y_1 = r.f1_z
        y_1[c] = g_1[c, k]
        y1_far = [wires.far(g_1.at[other, k], y_1.at[c], peer) for other, peer in chip_peers]

        def branch_out(i):
            step = nc - 1 - i
            blk = xor_of(c, step, nc)
            r.hid[...] = dot_rt(r.act[blk], weight_2())
            r.br_s[blk] = r.hid[...].astype(BF16)
            bias_once = bias_o * jnp.where(step == 0, 1.0, 0.0)

            def gate_rows(g):
                rows = sub_rows(g)
                value = (r.hid[rows, :] + bias_once) * r.cg[blk, rows, :].astype(F32)
                r.sub_gate[pl.ds(blk * n_sub + g, 1), :] = jnp.sum(value, axis=0, keepdims=True)

            loop_rows(gate_rows)

        loop(nc, branch_out)
        sum_2.start(1)

        def gray_order(i):
            return i + i // 2 - 2 * (i // 3)

        back_merge = Merge(r.sum_s, r.sum_r, r.sum_st)

        def attend_back(i):
            step = gray_order(i)
            blk = xor_of(c, step, nc)
            for at in range(1, nc):
                when(step == at, functools.partial(da_share.arrive, at))
            d_mix = dot_rt(da_all[blk], r.w_p[...]).astype(BF16)
            q_now, k_now, v_now = r.qkv[0, blk], r.qkv[1, blk], r.qkv[2, blk]
            d_q = jnp.zeros((own, chip_w), F32)
            d_k = jnp.zeros((own, chip_w), F32)
            d_v = jnp.zeros((own, chip_w), F32)
            for h in range(heads):
                d_mix_h = d_mix * head_of[h]
                share = r.probs[blk * heads + h]
                d_share = dot_rt(d_mix_h, v_now)
                d_score = share * (d_share - jnp.sum(share * d_share, axis=-1, keepdims=True))
                d_score = d_score.astype(BF16)
                d_q = d_q + dot(d_score, k_now * head_of[h])
                d_k = d_k + dot_lt(d_score, q_now * head_of[h])
                d_v = d_v + dot_lt(share.astype(BF16), d_mix_h)
            all_three = jnp.concatenate([d_q * head_scale, d_k * head_scale, d_v], axis=1).astype(BF16)
            r.d_qkv[blk] = all_three
            back_merge.put(step, blk, dot_rt(all_three, weight_q()).astype(BF16))
            when(i == 3, lambda: sum_2.start(2))

        loop(nc, attend_back)
        da_share.sent()

        g_q, g_p = w_q, r.w_p
        a_rows = all_rows(r.a_in)
        for lo, hi in column_cuts(q_w):
            value = dot_lt(a_rows, r.d_qkv[:, :, lo:hi].reshape(group, hi - lo))
            g_q[:, :, :, lo:hi] = value.astype(BF16).reshape(nc, 2, rows_d, hi - lo)
        q_core_back = wires.far(g_q.at[:, core_o], r.g_qr, core_dev)
        wait_all(y1_far)
        sum_1 = Sum(lambda t: y_1.at[t], r.got_1)
        sum_1.start(0)
        g_p[...] = dot_lt(all_rows(r.mixed), all_rows(da_all)).astype(BF16)
        p_core_back = wires.far(own_side(g_p, core_o), r.g_pr, core_dev)
        q_core_back.wait()
        for chip in range(nc):
            g_q[chip, k] = add_low(g_q[chip, k], r.g_qr[chip])
        r.y_got[c] = g_q[c, k]
        yq_far = [wires.far(g_q.at[other, k], r.y_got.at[c], peer) for other, peer in chip_peers]

        def own_terms(step):
            blk = xor_of(c, step, nc)

            def body(g):
                rows = sub_rows(g)
                part = r.sum_s[blk, rows, :].astype(F32)
                normal, _ = ln_parts(r.xg[blk, rows, :].astype(F32))
                at = pl.ds(blk * n_sub + g, 1)
                r.sub_lin[0, at, :] = jnp.sum(part, axis=0, keepdims=True)
                r.sub_lin[1, at, :] = jnp.sum(part * normal, axis=0, keepdims=True)

            loop_rows(body)

        loop(nc, own_terms)
        back_merge.combine()
        all_turned = hot_all.astype(F32).T.astype(BF16)
        hot_turned = own_hot.astype(F32).T.astype(BF16)
        for kind in range(6):
            if kind < 2:
                value = dot3(all_turned, r.sub_lin[kind])
            elif kind < 5:
                value = dot3(hot_turned, r.sub[kind])
            else:
                value = dot3(all_turned, r.sub_gate[...])
            r.d_part[:, :, width * kind : width * (kind + 1)] = value.reshape(2, half, width)
        d_core = wires.far(r.d_part.at[core_o], r.d_core, core_dev)
        d_core.wait()
        r.d_core[...] = r.d_core[...] + r.d_part[k]
        for plane in range(nf):
            r.d_cut[plane] = r.d_core[:, ada_w * plane : ada_w * (plane + 1)].astype(BF16)
        small = []
        for other, peer in plane_peers:
            small.append(wires.far(r.d_cut.at[other], r.dz.at[f], peer))
        r.dz[f] = r.d_cut[f]
        sum_1.start(1)
        p_core_back.wait()
        own_side(g_p, k)[...] = add_low(own_side(g_p, k)[...], r.g_pr[...])
        ones_own = jnp.ones((8, own), BF16)
        ones_all = jnp.ones((8, group), BF16)
        r.d_bias[...] = jnp.zeros((8, width), F32)
        r.d_bias[0:1, :] = dot(ones_own, da_all[c])[0:1]
        r.d_bias[1:2, :] = dot(ones_own, r.dbr[c])[0:1]
        qkv_sums = dot(ones_all, all_rows(r.d_qkv))[0:1]
        r.d_bias[2:3, 0:chip_w] = qkv_sums[:, :chip_w]
        r.d_bias[3:4, 0:chip_w] = qkv_sums[:, 2 * chip_w :]
        ones_ff = dot(ones_all, all_rows(r.d_hid))[0:1]
        r.d_bias[4:5, :] = ones_ff[:, :width]
        for part in range(1, ff_c // width):
            r.d_bias[4 + part : 5 + part, :] = ones_ff[:, part * width : (part + 1) * width]
        r.d_low[...] = r.d_bias[...].astype(BF16)
        bias_far = [wires.far(r.d_low, r.dzb.at[f], peer) for _, peer in plane_peers]
        r.dzb[f] = r.d_low[...]
        wait_all(small)
        value = r.dz[0].astype(F32)
        for plane in range(1, nf):
            value = value + r.dz[plane].astype(F32)
        m_chip[c] = value
        small = [wires.far(m_chip.at[c], m_chip.at[c], peer) for _, peer in chip_peers]
        wait_all(yq_far)
        q_line.sent()
        y_q = r.q_z
        for plane in range(nf):
            row = []
            for i in range(3):
                kind, chip = (3 * plane + i) // nc, (3 * plane + i) % nc
                row.append(r.y_got[chip, :, chip_w * kind : chip_w * (kind + 1)])
            row.append(own_side(g_p, k)[:, plane * cols_f : (plane + 1) * cols_f])
            y_q[plane] = jnp.concatenate(row, axis=1)
        sum_q = Sum(lambda t: y_q.at[t], r.got_q)
        sum_q.start(0)
        sum_1.start(2)
        wait_all(bias_far)
        value = r.dzb[0].astype(F32)
        for plane in range(1, nf):
            value = value + r.dzb[plane].astype(F32)
        r.d_bsum[...] = value
        b_swap = wires.far(r.d_bsum, r.d_coreb, core_dev)

        back_merge.finish()

        def back_norm1(g):
            rows = sub_rows(g)
            d_a = back_merge.rows(rows)
            normal, scale = ln_parts(r.xg[c, rows, :].astype(F32))
            value = r.d_after[rows, :] + ln_back(normal, scale, d_a * (1.0 + own_row(1, g)))
            x_grad[rows, :] = value.astype(BF16)

        loop_rows(back_norm1)
        land(x_grad)
        wait_all(small)
        value = m_chip[0]
        for chip in range(1, nc):
            value = value + m_chip[chip]
        r.d_tot[k] = value
        d_swap = wires.far(r.d_tot.at[k], r.d_tot.at[k], core_dev)
        b_swap.wait()
        r.d_chipb[c] = r.d_bsum[...] + r.d_coreb[...]
        bias_far = [wires.far(r.d_chipb.at[c], r.d_chipb.at[c], peer) for _, peer in chip_peers]
        br_merge.launch()
        sum_q.start(1)
        d_swap.wait()
        d_cols = r.d_tot[...].reshape(n_rows, ada_w)
        silu_turned = r.silu[...].astype(F32).T.astype(BF16)
        o_bada[...] = jnp.sum(d_cols, axis=0)
        value, total = d_cols, None
        for _ in range(3):
            term = value.astype(BF16)
            value = value - term.astype(F32)
            part = dot_rt(term, r.ada[...])
            total = part if total is None else total + part
        r.c_part[f] = total
        c_far = [wires.far(r.c_part.at[f], r.c_part.at[f], peer) for _, peer in plane_peers]
        sum_q.start(2)
        for lo, hi in column_cuts(ada_w):
            o_ada[:, lo:hi] = dot3(silu_turned, d_cols[:, lo:hi])
        land(o_ada, o_bada)
        sum_2.finish(r.all_2.at[k])
        o2_swap = wires.far(r.all_2.at[k], r.all_2.at[k], core_dev)
        br_merge.combine()
        wait_all(c_far)
        value = r.c_part[0]
        for plane in range(1, nf):
            value = value + r.c_part[plane]
        r.c_all[c, k] = value
        c_chip = [wires.far(r.c_all.at[c, k], r.c_all.at[c, k], peer) for _, peer in chip_peers]


        br_merge.finish()

        def finish_out(g):
            rows = sub_rows(g)
            branch = br_merge.rows(rows) + bias_o
            out[rows, :] = (r.after[rows, :] + own_row(5, g) * branch).astype(BF16)

        loop_rows(finish_out)
        land(out)
        wait_all(c_chip)
        c_swap = wires.far(r.c_all.at[:, k], r.c_all.at[:, k], core_dev)
        o2_swap.wait()

        def own_columns(lo):
            def body():
                o_2[...] = r.all_2[:, :, lo : lo + ff_d].reshape(cols_f, ff_d)

            return body

        when(k == 0, own_columns(0))
        when(k == 1, own_columns(ff_d))
        land(o_2)
        wait_all(bias_far)
        own_sums = r.d_chipb[0]
        for chip in range(1, nc):
            own_sums = own_sums + r.d_chipb[chip]
        for plane in range(nf):

            def bias_columns(plane=plane):
                at = plane * cols_f
                o_bp[...] = own_sums[0, at : at + cols_f]
                o_b2[...] = own_sums[1, at : at + cols_f]
                kind, chip = 2 * plane // nc, 2 * plane % nc
                pieces = [r.d_chipb[chip + i, 2 + kind : 3 + kind, 0:chip_w] for i in range(2)]
                o_bqv[...] = jnp.concatenate(pieces, axis=1)[0]
                o_b1[...] = r.d_chipb[plane, 4, :]

            when(f == plane, bias_columns)
        land(o_bqv, o_bp, o_b1, o_b2)
        c_swap.wait()
        d_silu = jnp.concatenate([r.c_all[f, 0], r.c_all[f, 1]], axis=1)
        cond_now = r.cond_own[...]
        gate = 1.0 / (1.0 + jnp.exp(-cond_now))
        o_cond[...] = d_silu * (gate * (1.0 + cond_now * (1.0 - gate)))
        land(o_cond)
        f2_line.sent()
        sum_1.finish(o_1)
        land(o_1)
        sum_q.finish(r.all_q)
        o_q[...] = r.all_q[:, :q_w]
        o_p[...] = r.all_q[:, q_w:]
        land(o_q, o_p)
        wait_all(landed)
        assert wires.remote_count <= n_sem and wires.local_count <= 40

    return pl.pallas_call(
        kernel,
        out_shape=outs,
        in_specs=[ANYWHERE] * 2 + [ON_CHIP] * 8 + [ANYWHERE] * 5,
        out_specs=tuple([ANYWHERE] * len(outs)),
        scratch_shapes=[pltpu.VMEM(item.shape, item.dtype) for item in outs] + list(scratch.values()),
        compiler_params=pltpu.CompilerParams(
            collective_id=0, has_side_effects=True, vmem_limit_bytes=63 * 2**20
        ),
        name="block",
    )(x, cot, frames, clips, *biases, cond, w_ada, wq, wp, w1, w2)


def land_kernel(arrays):
    count = len(arrays)

    def kernel(*refs):
        ins, results, held = refs[:count], refs[count : 2 * count], refs[2 * count : 3 * count]
        arrive, leave = refs[3 * count :]
        steps = [pltpu.make_async_copy(a, b, arrive.at[i]) for i, (a, b) in enumerate(zip(ins, held))]
        copies = [pltpu.make_async_copy(a, b, leave.at[i]) for i, (a, b) in enumerate(zip(held, results))]
        for step in steps:
            step.start()
        for step, copy in zip(steps, copies):
            step.wait()
            copy.start()
        wait_all(copies)

    return pl.pallas_call(
        kernel,
        out_shape=tuple(jax.ShapeDtypeStruct(a.shape, a.dtype) for a in arrays),
        in_specs=[ANYWHERE] * count,
        out_specs=tuple([ANYWHERE] * count),
        scratch_shapes=[pltpu.VMEM(a.shape, a.dtype) for a in arrays]
        + [pltpu.SemaphoreType.DMA((count,))] * 2,
        name="land",
    )(*arrays)


def fits_block(n_dp, nf, width, ff, own, micro):
    nc = n_dp // 2
    return (
        nc == nf
        and nf == 4
        and width % (128 * nf) == 128
        and ff == 4 * width
        and (width // n_dp) % 16 == 0
        and (width // nc) % HEAD_DIM == 0
        and own % (2 * SUB) == 0
    )


def per_device(
    n_dp, nf, patches, cotangent, conditioning, frame_of_slot, clip_of_slot,
    w_ada, b_ada, w_qkv, b_qv, w_proj, b_proj, w_fc1, b_fc1, w_fc2, b_fc2,
):
    nc = n_dp // 2
    sizes = (nc, nf)
    micro, block, width = patches.shape
    own = micro * block
    clips = conditioning.shape[1]
    rows_d = width // n_dp
    cols_f = width // nf
    ff = w_fc1.shape[1] * nf
    ff_d = ff // n_dp
    chip_w = width // nc
    piece_q = math.gcd(3 * width // nf, chip_w)
    piece_1 = math.gcd(ff // nf, ff_d)
    dims = types.SimpleNamespace(
        nc=nc,
        nf=nf,
        per_q=3 * width // nf // piece_q,
        per_1=ff // nf // piece_1,
        chip_q=chip_w // piece_q,
        chip_1=ff // nc // piece_1,
    )
    dp = lax.axis_index("dp")
    f = lax.axis_index("fsdp")
    c, k = dp // 2, dp % 2

    q_send = w_qkv.reshape(rows_d, dims.per_q, piece_q).transpose(1, 0, 2)
    f1_send = w_fc1.reshape(rows_d, dims.per_1, piece_1).transpose(1, 0, 2)
    f2_send = w_fc2.T
    cond = conditioning.reshape(micro * clips, width)
    silu_cond = jax.nn.silu(cond)
    silu_low = silu_cond.astype(BF16)
    ada_w = w_ada.shape[1]
    silu_part = lax.dynamic_slice_in_dim(silu_low, dp * rows_d, rows_d, 1)
    mod_part = dot(silu_part, w_ada) + jnp.where(dp == 0, b_ada.astype(F32), 0.0)[None]
    mod_send = mod_part.reshape(-1, 2, ada_w // 2).transpose(1, 0, 2)
    cut = [0, 2 * cols_f, 3 * cols_f, 3 * cols_f + ff // nf, 4 * cols_f + ff // nf]
    cond_own = lax.dynamic_slice_in_dim(cond, f * cols_f, cols_f, 1)

    def ada_outputs(d_cols):
        grad_w_ada = precise(silu_part.astype(F32), d_cols, ((0,), (0,)))
        d_silu_part = precise(d_cols, w_ada.astype(F32), ((1,), (1,)))
        d_silu = cond_kernel(dims, d_silu_part).transpose(1, 0, 2).reshape(micro * clips, width)
        d_silu_own = lax.dynamic_slice_in_dim(d_silu, f * cols_f, cols_f, 1)
        _, silu_back = jax.vjp(jax.nn.silu, cond_own)
        cond_grad = silu_back(d_silu_own)[0].reshape(micro, clips, cols_f)
        return cond_grad, grad_w_ada, jnp.sum(d_cols, axis=0)

    if fits_block(n_dp, nf, width, ff, own, micro):
        results = block_kernel(
            dims, patches.reshape(own, width), cotangent.reshape(own, width), frame_of_slot,
            clip_of_slot, (b_qv, b_proj, b_fc1, b_fc2, b_ada), conditioning, w_ada, w_qkv, w_proj,
            w_fc1, w_fc2.T,
        )
        (
            output, input_grad, cond_grad, grad_ada, grad_b_ada, grad_qkv, grad_b_qv,
            grad_proj, grad_b_proj, grad_fc1, grad_b_fc1, grad_fc2, grad_b_fc2,
        ) = land_kernel(results)
        return (
            output.reshape(patches.shape),
            input_grad.reshape(patches.shape),
            cond_grad.reshape(micro, clips, cols_f),
            grad_ada,
            grad_b_ada,
            grad_qkv,
            grad_b_qv,
            grad_proj,
            grad_b_proj,
            grad_fc1,
            grad_b_fc1,
            grad_fc2.T,
            grad_b_fc2,
        )

    ids = jnp.stack([frame_of_slot.reshape(own), clip_of_slot.reshape(own)])
    ids = jnp.concatenate([ids, jnp.zeros((6, own), jnp.int32)])
    bias_send = jnp.concatenate([b_qv, b_proj, b_fc1, b_fc2]).astype(F32)[None]

    (x_all, c_all, ids_all, bias_all, mod_all, q_chip, f1_chip, p_chip, f2_chip, _, _) = start_kernel(
        dims, patches.reshape(own, width), cotangent.reshape(own, width), ids, bias_send, mod_send,
        q_send, f1_send, w_proj, f2_send,
    )
    group = nc * own
    modulation = mod_all.transpose(2, 0, 1, 3).reshape(micro * clips, 6 * width)
    q_parts = [
        q_chip[i].reshape(nc, 2, dims.chip_q, rows_d, piece_q).transpose(0, 1, 3, 2, 4).reshape(width, chip_w)
        for i in range(3)
    ]
    w1 = f1_chip.transpose(1, 2, 3, 0, 4).reshape(width, ff // nc)
    wp = p_chip.transpose(0, 2, 1, 3).reshape(chip_w, width)
    w2t = f2_chip.reshape(2, width, ff_d).transpose(1, 0, 2).reshape(width, 2 * ff_d)
    b_parts = [bias_all[:, 0, a:b].reshape(-1) for a, b in zip(cut[:-1], cut[1:])]
    bq = lax.dynamic_slice_in_dim(b_parts[0], c * chip_w, chip_w, 0)
    bv = lax.dynamic_slice_in_dim(b_parts[0], width + c * chip_w, chip_w, 0)
    b1 = lax.dynamic_slice_in_dim(b_parts[2], c * (ff // nc), ff // nc, 0)

    def hot_of(clip_ids):
        count = clip_ids.shape[0]
        row = (jnp.arange(count, dtype=jnp.int32) // block) % micro * clips + clip_ids
        return (row[:, None] == jnp.arange(micro * clips, dtype=jnp.int32)[None]).astype(F32)

    hot_group = hot_of(ids_all[:, 1].reshape(group))
    hot_own = hot_of(clip_of_slot.reshape(own))
    mod_group = precise(hot_group, modulation, ((1,), (0,)))
    mod_own = precise(hot_own, modulation, ((1,), (0,)))
    shift1, scale1 = mod_group[:, :width], mod_group[:, width : 2 * width]
    gate1 = mod_own[:, 2 * width : 3 * width]
    shift2, scale2 = mod_own[:, 3 * width : 4 * width], mod_own[:, 4 * width : 5 * width]
    gate2_group, gate2 = mod_group[:, 5 * width :], mod_own[:, 5 * width :]

    x_group = x_all.reshape(group, width).astype(F32)
    norm1, rstd1 = ln_parts(x_group)
    a_in = (norm1 * (1.0 + scale1) + shift1).astype(BF16)
    zero = jnp.zeros_like(bq)
    q, kk, v = [
        (dot(a_in, w) + b[None]).astype(BF16) for w, b in zip(q_parts, (bq, zero, bv))
    ]
    heads = chip_w // HEAD_DIM
    blocks = group // block
    q4, k4, v4 = [t.reshape(blocks, block, heads, HEAD_DIM) for t in (q, kk, v)]
    frames = ids_all[:, 0].reshape(blocks, block)
    same = (frames[:, :, None] == frames[:, None, :])[:, None]
    scores = jnp.einsum("bqhd,bkhd->bhqk", q4, k4, preferred_element_type=F32) * HEAD_DIM ** (-0.5)
    scores = jnp.where(same, scores, NEG_FILL)
    top = jnp.max(scores, axis=-1, keepdims=True)
    raised = jnp.exp(scores - top)
    probs = raised / jnp.sum(raised, axis=-1, keepdims=True)
    probs_low = probs.astype(BF16)
    mixed = jnp.einsum("bhqk,bkhd->bqhd", probs_low, v4, preferred_element_type=F32)
    mixed = mixed.reshape(group, chip_w).astype(BF16)
    attn_part = dot(mixed, wp)
    (attn_got,) = exchange(
        "attn_sum", 3, sizes, [(CHIP, SPREAD, attn_part.astype(BF16).reshape(nc, own, width))]
    )
    attn = jnp.sum(attn_got.astype(F32), axis=0) + b_parts[1][None]
    x_own = patches.reshape(own, width).astype(F32)
    after = x_own + gate1 * attn
    norm2, rstd2 = ln_parts(after)
    m_own = (norm2 * (1.0 + scale2) + shift2).astype(BF16)
    (m_all,) = exchange("m_gather", 4, sizes, [(CHIP, GATHER, m_own)])
    m_in = m_all.reshape(group, width)

    hidden = dot(m_in, w1) + b1[None]
    act, slope = gelu_both(hidden)
    act = act.astype(BF16)
    branch_part = dot_rt(act, w2t)
    cot_group = c_all.reshape(group, width).astype(F32)
    d_branch = (gate2_group * cot_group).astype(BF16)
    grad_2t = dot_lt(d_branch, act)
    d_hidden = (dot(d_branch, w2t) * slope).astype(BF16)
    grad_1 = dot_lt(m_in, d_hidden)
    d_m_part = dot_rt(d_hidden, w1)
    branch_got, d_m_got = exchange(
        "ff_sum",
        5,
        sizes,
        [
            (CHIP, SPREAD, d_m_part.astype(BF16).reshape(nc, own, width)),
            (CHIP, SPREAD, branch_part.astype(BF16).reshape(nc, own, width)),
        ],
    )[::-1]
    branch = jnp.sum(branch_got.astype(F32), axis=0) + b_parts[3][None]
    output = (after + gate2 * branch).astype(BF16)
    d_m = jnp.sum(d_m_got.astype(F32), axis=0)
    cot_own = cotangent.reshape(own, width).astype(F32)
    d_after = cot_own + ln_back(norm2, rstd2, d_m * (1.0 + scale2))
    d_attn = (gate1 * d_after).astype(BF16)
    (d_attn_all,) = exchange("d_attn_gather", 6, sizes, [(CHIP, GATHER, d_attn)])
    d_attn_group = d_attn_all.reshape(group, width)
    grad_p = dot_lt(mixed, d_attn_group)
    d_mix = dot_rt(d_attn_group, wp).astype(BF16).reshape(blocks, block, heads, HEAD_DIM)
    d_probs = jnp.einsum("bqhd,bkhd->bhqk", d_mix, v4, preferred_element_type=F32)
    d_scores = probs * (d_probs - jnp.sum(probs * d_probs, axis=-1, keepdims=True))
    d_scores = d_scores.astype(BF16)
    dq = jnp.einsum("bhqk,bkhd->bqhd", d_scores, k4, preferred_element_type=F32) * HEAD_DIM ** (-0.5)
    dk = jnp.einsum("bhqk,bqhd->bkhd", d_scores, q4, preferred_element_type=F32) * HEAD_DIM ** (-0.5)
    dv = jnp.einsum("bhqk,bqhd->bkhd", probs_low, d_mix, preferred_element_type=F32)
    dqkv = [t.reshape(group, chip_w).astype(BF16) for t in (dq, dk, dv)]
    d_a_part = sum(dot_rt(t, w) for t, w in zip(dqkv, q_parts))
    grad_q = jnp.stack([dot_lt(a_in, t) for t in dqkv])
    (d_a_got,) = exchange(
        "d_a_sum", 7, sizes, [(CHIP, SPREAD, d_a_part.astype(BF16).reshape(nc, own, width))]
    )
    d_a = jnp.sum(d_a_got.astype(F32), axis=0)
    norm1_own, rstd1_own = ln_parts(x_own)
    scale1_own = mod_own[:, width : 2 * width]
    input_grad = (d_after + ln_back(norm1_own, rstd1_own, d_a * (1.0 + scale1_own))).astype(BF16)

    g_q = grad_q.reshape(3, nc, 2, rows_d, dims.chip_q, piece_q).transpose(2, 1, 0, 4, 3, 5)
    g_1 = grad_1.reshape(nc, 2, rows_d, dims.chip_1, piece_1).transpose(1, 0, 3, 2, 4)
    g_p = grad_p.reshape(2, rows_d, nf, cols_f).transpose(0, 2, 1, 3)
    g_2 = grad_2t.reshape(nf, cols_f, 2, ff_d).transpose(2, 0, 1, 3)
    got = exchange("grad_core", 8, sizes, [(CORE, SPREAD, g.astype(BF16)) for g in (g_q, g_1, g_p, g_2)])
    s_q, s_1, s_p, s_2 = [jnp.sum(g.astype(F32), axis=0).astype(BF16) for g in got]
    r_q, r_1 = exchange("grad_chip", 9, sizes, [(CHIP, SPREAD, s_q), (CHIP, SPREAD, s_1)])
    z_q = r_q.transpose(1, 0, 2, 3, 4).reshape(nf, dims.per_q, rows_d, piece_q)
    z_1 = r_1.reshape(nf, dims.per_1, rows_d, piece_1)
    got = exchange("grad_plane", 10, sizes, [(PLANE, SPREAD, g) for g in (z_q, z_1, s_p, s_2)])
    o_q, o_1, o_p, o_2 = [jnp.sum(g.astype(F32), axis=0) for g in got]
    grad_w_qkv = o_q.transpose(1, 0, 2).reshape(rows_d, 3 * width // nf)
    grad_w_fc1 = o_1.transpose(1, 0, 2).reshape(rows_d, ff // nf)
    grad_w_fc2 = o_2.T

    d_token = jnp.concatenate(
        [d_a, d_a * norm1_own, d_after * attn, d_m, d_m * norm2, cot_own * branch], axis=1
    )
    d_mod = precise(hot_own, d_token, ((0,), (0,)))
    d_branch_own = (gate2 * cot_own).astype(BF16).astype(F32)

    def columns(value):
        return jnp.sum(value.astype(F32), axis=0)

    def spread(value, count):
        return lax.dynamic_update_slice_in_dim(
            jnp.zeros((count,), F32), value, c * value.shape[0], 0
        )

    g_bqv = jnp.concatenate([spread(columns(dqkv[0]), width), spread(columns(dqkv[2]), width)])
    g_b1 = spread(columns(d_hidden), ff)
    bias_terms = jnp.concatenate(
        [
            g_bqv.reshape(nf, -1),
            columns(d_attn).reshape(nf, -1),
            g_b1.reshape(nf, -1),
            columns(d_branch_own).reshape(nf, -1),
        ],
        axis=1,
    )
    n_bias = bias_terms.shape[1]
    bias_rows = -(-n_bias // ada_w)
    bias_terms = jnp.pad(bias_terms, ((0, 0), (0, bias_rows * ada_w - n_bias)))
    terms = jnp.concatenate(
        [d_mod.reshape(micro * clips, nf, ada_w).transpose(1, 0, 2), bias_terms.reshape(nf, bias_rows, ada_w)],
        axis=1,
    )
    pad_rows = -terms.shape[1] % 8
    terms = jnp.pad(terms, ((0, 0), (0, pad_rows), (0, 0)))
    terms = terms.reshape(nf, -1, 2, ada_w // 2).transpose(0, 2, 1, 3)
    total = sum_small_kernel(dims, terms).transpose(1, 0, 2).reshape(-1, ada_w)
    d_cols = total[: micro * clips]
    bias_sums = total[micro * clips : micro * clips + bias_rows].reshape(-1)[:n_bias]
    g_parts = [bias_sums[a:b] for a, b in zip(cut[:-1], cut[1:])]
    cond_grad, grad_w_ada, grad_b_ada = ada_outputs(d_cols)
    return (
        output.reshape(patches.shape),
        input_grad.reshape(patches.shape),
        cond_grad,
        grad_w_ada,
        grad_b_ada,
        grad_w_qkv,
        g_parts[0],
        o_p,
        g_parts[1],
        grad_w_fc1,
        g_parts[2],
        grad_w_fc2,
        g_parts[3],
    )


def solution(mesh):
    tokens = P(None, ("dp", "fsdp"), None)
    ids = P(None, ("dp", "fsdp"))
    both, cols = P("dp", "fsdp"), P("fsdp")
    in_specs = (tokens, tokens, P(), ids, ids) + (both, cols) * 5
    out_specs = (tokens, tokens, P(None, None, "fsdp")) + (both, cols) * 5
    return jax.shard_map(
        functools.partial(per_device, mesh.shape["dp"], mesh.shape["fsdp"]),
        mesh=mesh,
        in_specs=in_specs,
        out_specs=out_specs,
        check_vma=False,
    )
```

```python
import functools
import math
import types

import jax
import jax.numpy as jnp
from jax import lax
from jax.experimental import pallas as pl
from jax.experimental.pallas import tpu as pltpu
from jax.sharding import PartitionSpec as P

HEAD_DIM = 72
EPS = 1e-06
GELU_C = math.sqrt(2.0 / math.pi)
PRECISE = lax.Precision.HIGHEST
NEG_FILL = -1e30
SUB = 16
CORE, CHIP, PLANE, ALL = range(4)
GATHER, SPREAD = range(2)
MESH_ID = pl.DeviceIdType.MESH
F32 = jnp.float32
BF16 = jnp.bfloat16


def xor_of(index, step, size):
    result, bit = 0, 1
    while bit < size:
        mine = (index // bit) % 2
        result = result + ((mine + (step // bit) % 2) % 2) * bit
        bit *= 2
    return result


class Place:
    def __init__(self, n_chip, n_plane):
        self.n = {CORE: 2, CHIP: n_chip, PLANE: n_plane, ALL: 2 * n_chip}
        self.dp = lax.axis_index("dp")
        self.f = lax.axis_index("fsdp")
        self.c = self.dp // 2
        self.k = self.dp % 2

    def index(self, axis):
        return {CORE: self.k, CHIP: self.c, PLANE: self.f, ALL: self.dp}[axis]

    def peer(self, axis, step):
        other = xor_of(self.index(axis), step, self.n[axis])
        if axis == CORE:
            return other, (self.c * 2 + other, self.f)
        if axis == CHIP:
            return other, (other * 2 + self.k, self.f)
        if axis == PLANE:
            return other, (self.dp, other)
        return other, (other, self.f)


def greet(place, axes):
    barrier = pltpu.get_barrier_semaphore()
    count = 0
    for axis in axes:
        for step in range(1, place.n[axis]):
            pl.semaphore_signal(
                barrier, inc=1, device_id=place.peer(axis, step)[1], device_id_type=MESH_ID
            )
            count += 1
    pl.semaphore_wait(barrier, count)


class Wires:
    def __init__(self, send, recv, local):
        self.send, self.recv, self.local = send, recv, local
        self.remote_count = 0
        self.local_count = 0

    def far(self, src, dst, device):
        at = self.remote_count
        self.remote_count += 1
        copy = pltpu.make_async_remote_copy(
            src_ref=src,
            dst_ref=dst,
            send_sem=self.send.at[at],
            recv_sem=self.recv.at[at],
            device_id=device,
            device_id_type=MESH_ID,
        )
        copy.start()
        return copy

    def near(self, src, dst):
        at = self.local_count
        self.local_count += 1
        copy = pltpu.make_async_copy(src, dst, self.local.at[at])
        copy.start()
        return copy


def wait_all(copies):
    for copy in copies:
        copy.wait()


ANYWHERE = pl.BlockSpec(memory_space=pl.ANY)
ON_CHIP = pl.BlockSpec(memory_space=pltpu.VMEM)


def exchange(name, collective_id, sizes, items):
    n_chip, n_plane = sizes
    n_of = {CORE: 2, CHIP: n_chip, PLANE: n_plane, ALL: 2 * n_chip}
    axes = sorted({item[0] for item in items})
    outs = []
    n_far = 0
    for axis, kind, array in items:
        n_far += n_of[axis] - 1
        shape = array.shape if kind == SPREAD else (n_of[axis],) + array.shape
        outs.append(jax.ShapeDtypeStruct(shape, array.dtype))

    def kernel(*refs):
        ins = refs[: len(items)]
        results = refs[len(items) : 2 * len(items)]
        place = Place(n_chip, n_plane)
        wires = Wires(*refs[2 * len(items) :])
        greet(place, axes)
        copies = []
        for (axis, kind, _), src, dst in zip(items, ins, results):
            mine = place.index(axis)
            for step in range(1, n_of[axis]):
                other, device = place.peer(axis, step)
                piece = src if kind == GATHER else src.at[other]
                copies.append(wires.far(piece, dst.at[mine], device))
        for (axis, kind, _), src, dst in zip(items, ins, results):
            mine = place.index(axis)
            copies.append(wires.near(src if kind == GATHER else src.at[mine], dst.at[mine]))
        wait_all(copies)

    return pl.pallas_call(
        kernel,
        out_shape=tuple(outs),
        in_specs=[ANYWHERE] * len(items),
        out_specs=tuple([ANYWHERE] * len(items)),
        scratch_shapes=[
            pltpu.SemaphoreType.DMA((n_far,)),
            pltpu.SemaphoreType.DMA((n_far,)),
            pltpu.SemaphoreType.DMA((len(items),)),
        ],
        compiler_params=pltpu.CompilerParams(collective_id=collective_id, has_side_effects=True),
        name=name,
    )(*[item[2] for item in items])


def start_kernel(dims, x, cot, ids, bias, mod, wq, w1, wp, w2):
    nc, nf = dims.nc, dims.nf
    per_q, per_1 = dims.per_q, dims.per_1
    chip_q, chip_1 = dims.chip_q, dims.chip_1
    part_q = nc * chip_q
    rows, half = mod.shape[1], mod.shape[2]
    n_far = 5 * (nf - 1) + 3 * (nc - 1) + 4 * (nc - 1) + 4 + 1 + (nc - 1) + (nf - 1) + 1
    outs = (
        jax.ShapeDtypeStruct((nc,) + x.shape, x.dtype),
        jax.ShapeDtypeStruct((nc,) + cot.shape, cot.dtype),
        jax.ShapeDtypeStruct((nc,) + ids.shape, ids.dtype),
        jax.ShapeDtypeStruct((nf,) + bias.shape, bias.dtype),
        jax.ShapeDtypeStruct((nf, 2, rows, half), F32),
        jax.ShapeDtypeStruct((3, nc, 2, chip_q) + wq.shape[1:], BF16),
        jax.ShapeDtypeStruct((chip_1, nc, 2) + w1.shape[1:], BF16),
        jax.ShapeDtypeStruct((2, nf) + wp.shape, BF16),
        jax.ShapeDtypeStruct((2, nf) + w2.shape, BF16),
        jax.ShapeDtypeStruct((nf * per_q,) + wq.shape[1:], BF16),
        jax.ShapeDtypeStruct((nf * per_1,) + w1.shape[1:], BF16),
    )

    def kernel(
        x_in, c_in, i_in, b_in, m_in, q_in, f1_in, p_in, f2_in,
        x_all, c_all, i_all, b_all, m_all, q_chip, f1_chip, p_chip, f2_chip, q_rows, f1_rows,
        m_core, m_sum, m_chip, send, recv, local,
    ):
        place = Place(nc, nf)
        wires = Wires(send, recv, local)
        c, k, f = place.c, place.k, place.f
        greet(place, (CORE, CHIP, PLANE))
        core_other, core_peer = place.peer(CORE, 1)
        chip_peers = [place.peer(CHIP, step) for step in range(1, nc)]
        plane_peers = [place.peer(PLANE, step) for step in range(1, nf)]

        m_first = wires.far(m_in.at[core_other], m_core, core_peer)
        q_got, f1_got, p_got, f2_got, small = [], [], [], [], []
        for _, peer in plane_peers:
            q_got.append(wires.far(q_in, q_rows.at[pl.ds(f * per_q, per_q)], peer))
            small.append(wires.far(b_in, b_all.at[f], peer))
        q_got.append(wires.near(q_in, q_rows.at[pl.ds(f * per_q, per_q)]))
        small.append(wires.near(b_in, b_all.at[f]))
        for _, peer in chip_peers:
            small.append(wires.far(i_in, i_all.at[c], peer))
            small.append(wires.far(x_in, x_all.at[c], peer))
        m_first.wait()
        m_sum[...] = m_in[k] + m_core[...]
        m_chip[c] = m_sum[...]
        m_second = [wires.far(m_sum, m_chip.at[c], peer) for _, peer in chip_peers]
        for _, peer in plane_peers:
            p_got.append(wires.far(p_in, p_chip.at[k, f], peer))
        for _, peer in plane_peers:
            f1_got.append(wires.far(f1_in, f1_rows.at[pl.ds(f * per_1, per_1)], peer))
        for _, peer in plane_peers:
            f2_got.append(wires.far(f2_in, f2_chip.at[k, f], peer))
        p_got.append(wires.near(p_in, p_chip.at[k, f]))
        f1_got.append(wires.near(f1_in, f1_rows.at[pl.ds(f * per_1, per_1)]))
        f2_got.append(wires.near(f2_in, f2_chip.at[k, f]))
        small.append(wires.near(i_in, i_all.at[c]))
        small.append(wires.near(x_in, x_all.at[c]))
        for _, peer in chip_peers:
            small.append(wires.far(c_in, c_all.at[c], peer))
        small.append(wires.near(c_in, c_all.at[c]))
        wait_all(m_second)
        total = m_chip[0]
        for other in range(1, nc):
            total = total + m_chip[other]
        m_all[f, k] = total
        wait_all([wires.far(m_all.at[f, k], m_all.at[f, k], peer) for _, peer in plane_peers])
        m_last = wires.far(m_all.at[:, k], m_all.at[:, k], core_peer)

        wait_all(q_got)
        q_moved = []
        for kind in range(3):
            for other, peer in chip_peers:
                q_moved.append(
                    wires.far(
                        q_rows.at[pl.ds(kind * part_q + other * chip_q, chip_q)],
                        q_chip.at[kind, c, k],
                        peer,
                    )
                )
            q_moved.append(
                wires.near(
                    q_rows.at[pl.ds(kind * part_q + c * chip_q, chip_q)], q_chip.at[kind, c, k]
                )
            )
        wait_all(p_got)
        last = [m_last, wires.far(p_chip.at[k], p_chip.at[k], core_peer)]
        wait_all(q_moved)
        last.append(wires.far(q_chip.at[:, :, k], q_chip.at[:, :, k], core_peer))
        wait_all(f1_got)
        f1_moved = []
        for other, peer in chip_peers:
            f1_moved.append(
                wires.far(f1_rows.at[pl.ds(other * chip_1, chip_1)], f1_chip.at[:, c, k], peer)
            )
        f1_moved.append(
            wires.near(f1_rows.at[pl.ds(c * chip_1, chip_1)], f1_chip.at[:, c, k])
        )
        wait_all(f2_got)
        last.append(wires.far(f2_chip.at[k], f2_chip.at[k], core_peer))
        wait_all(f1_moved)
        last.append(wires.far(f1_chip.at[:, :, k], f1_chip.at[:, :, k], core_peer))
        wait_all(small)
        wait_all(last)

    return pl.pallas_call(
        kernel,
        out_shape=outs,
        in_specs=[ANYWHERE] * 4 + [ON_CHIP] + [ANYWHERE] * 4,
        out_specs=tuple([ANYWHERE] * 4 + [ON_CHIP] + [ANYWHERE] * 6),
        scratch_shapes=[
            pltpu.VMEM((rows, half), F32),
            pltpu.VMEM((rows, half), F32),
            pltpu.VMEM((nc, rows, half), F32),
            pltpu.SemaphoreType.DMA((n_far,)),
            pltpu.SemaphoreType.DMA((n_far,)),
            pltpu.SemaphoreType.DMA((12,)),
        ],
        compiler_params=pltpu.CompilerParams(collective_id=0, has_side_effects=True),
        name="start",
    )(x, cot, ids, bias, mod, wq, w1, wp, w2)


def sum_small_kernel(dims, terms):
    nc, nf = dims.nc, dims.nf
    _, _, rows, half = terms.shape
    n_far = (nf - 1) + 1 + (nc - 1) + 1

    def kernel(t_in, total, z_got, both, core_got, chip_got, send, recv, local):
        place = Place(nc, nf)
        wires = Wires(send, recv, local)
        c, k, f = place.c, place.k, place.f
        greet(place, (CORE, CHIP, PLANE))
        core_other, core_peer = place.peer(CORE, 1)
        copies = []
        for step in range(1, nf):
            other, peer = place.peer(PLANE, step)
            copies.append(wires.far(t_in.at[other], z_got.at[f], peer))
        z_got[f] = t_in[f]
        wait_all(copies)
        value = z_got[0]
        for other in range(1, nf):
            value = value + z_got[other]
        both[...] = value
        wires.far(both.at[core_other], core_got, core_peer).wait()
        chip_got[c] = both[k] + core_got[...]
        copies = []
        for step in range(1, nc):
            _, peer = place.peer(CHIP, step)
            copies.append(wires.far(chip_got.at[c], chip_got.at[c], peer))
        wait_all(copies)
        value = chip_got[0]
        for other in range(1, nc):
            value = value + chip_got[other]
        total[k] = value
        wires.far(total.at[k], total.at[k], core_peer).wait()

    return pl.pallas_call(
        kernel,
        out_shape=jax.ShapeDtypeStruct((2, rows, half), F32),
        in_specs=[ON_CHIP],
        out_specs=ON_CHIP,
        scratch_shapes=[
            pltpu.VMEM((nf, 2, rows, half), F32),
            pltpu.VMEM((2, rows, half), F32),
            pltpu.VMEM((rows, half), F32),
            pltpu.VMEM((nc, rows, half), F32),
            pltpu.SemaphoreType.DMA((n_far,)),
            pltpu.SemaphoreType.DMA((n_far,)),
            pltpu.SemaphoreType.DMA((1,)),
        ],
        compiler_params=pltpu.CompilerParams(collective_id=1, has_side_effects=True),
        name="sum_small",
    )(terms)


def cond_kernel(dims, part):
    nc, nf = dims.nc, dims.nf
    nd = 2 * nc
    rows, width = part.shape
    n_far = (nf - 1) + (nd - 1)

    def kernel(p_in, out, got, send, recv, local):
        place = Place(nc, nf)
        wires = Wires(send, recv, local)
        greet(place, (PLANE, ALL))
        copies = []
        for step in range(1, nf):
            copies.append(wires.far(p_in, got.at[place.f], place.peer(PLANE, step)[1]))
        got[place.f] = p_in[...]
        wait_all(copies)
        value = got[0]
        for other in range(1, nf):
            value = value + got[other]
        out[place.dp] = value
        copies = []
        for step in range(1, nd):
            copies.append(
                wires.far(out.at[place.dp], out.at[place.dp], place.peer(ALL, step)[1])
            )
        wait_all(copies)

    return pl.pallas_call(
        kernel,
        out_shape=jax.ShapeDtypeStruct((nd, rows, width), F32),
        in_specs=[ON_CHIP],
        out_specs=ON_CHIP,
        scratch_shapes=[
            pltpu.VMEM((nf, rows, width), F32),
            pltpu.SemaphoreType.DMA((n_far,)),
            pltpu.SemaphoreType.DMA((n_far,)),
            pltpu.SemaphoreType.DMA((1,)),
        ],
        compiler_params=pltpu.CompilerParams(collective_id=2, has_side_effects=True),
        name="cond_sum",
    )(part)


def dot(left, right):
    return jnp.dot(left, right, preferred_element_type=F32)


def dot_rt(left, right):
    return lax.dot_general(left, right, (((1,), (1,)), ((), ())), preferred_element_type=F32)


def dot_lt(left, right):
    return lax.dot_general(left, right, (((0,), (0,)), ((), ())), preferred_element_type=F32)


def precise(left, right, dims):
    return lax.dot_general(
        left, right, (dims, ((), ())), precision=PRECISE, preferred_element_type=F32
    )


def ln_parts(values):
    centre = values - jnp.mean(values, axis=-1, keepdims=True)
    scale = lax.rsqrt(jnp.mean(centre * centre, axis=-1, keepdims=True) + EPS)
    return centre * scale, scale


def ln_back(normal, scale, grad):
    return scale * (
        grad
        - jnp.mean(grad, axis=-1, keepdims=True)
        - normal * jnp.mean(grad * normal, axis=-1, keepdims=True)
    )


def gelu_both(h):
    square = h * h
    t = jnp.tanh(GELU_C * (h + 0.044715 * h * square))
    value = 0.5 * h * (1.0 + t)
    slope = 0.5 * (1.0 + t) + 0.5 * h * (1.0 - t * t) * GELU_C * (1.0 + 3 * 0.044715 * square)
    return value, slope


def dot3(left, right):
    wide_left = left.dtype == F32
    value = left if wide_left else right
    total = None
    for _ in range(3):
        term = value.astype(BF16)
        value = value - term.astype(F32)
        part = dot(term, right) if wide_left else dot(left, term)
        total = part if total is None else total + part
    return total


def add_low(left, right):
    return (left.astype(F32) + right.astype(F32)).astype(BF16)


def block_kernel(dims, x, cot, frames, clips, biases, cond, w_ada, wq, wp, w1, w2):
    nc, nf = dims.nc, dims.nf
    own, width = x.shape
    group = nc * own
    rows_d, q_w = wq.shape
    chip_w = q_w // 3
    cols_f, ff_d = w2.shape
    ff_c = 2 * ff_d
    ada_w = w_ada.shape[1]
    n_bias = sum(item.shape[0] for item in biases)
    heads = chip_w // HEAD_DIM
    micro, n_clips, _ = cond.shape
    n_rows = micro * n_clips
    half = n_rows // 2
    n_sub = own // SUB
    head_scale = HEAD_DIM ** (-0.5)
    last = nf - 2
    third = rows_d // 3

    outs = (
        jax.ShapeDtypeStruct((own, width), BF16),
        jax.ShapeDtypeStruct((own, width), BF16),
        jax.ShapeDtypeStruct((n_rows, cols_f), F32),
        jax.ShapeDtypeStruct((rows_d, ada_w), F32),
        jax.ShapeDtypeStruct((ada_w,), F32),
        jax.ShapeDtypeStruct((rows_d, q_w), F32),
        jax.ShapeDtypeStruct((2 * chip_w,), F32),
        jax.ShapeDtypeStruct((rows_d, cols_f), F32),
        jax.ShapeDtypeStruct((cols_f,), F32),
        jax.ShapeDtypeStruct((rows_d, ff_c), F32),
        jax.ShapeDtypeStruct((ff_c,), F32),
        jax.ShapeDtypeStruct((cols_f, ff_d), F32),
        jax.ShapeDtypeStruct((cols_f,), F32),
    )
    tokens = (nc, own, width)
    n_sem = 240
    scratch = dict(
        xg=pltpu.VMEM(tokens, BF16),
        cg=pltpu.VMEM(tokens, BF16),
        idsg=pltpu.VMEM((nc, 2, own), F32),
        biasg=pltpu.VMEM((nf, 1, n_bias), F32),
        ada=pltpu.VMEM(w_ada.shape, BF16),
        silu=pltpu.VMEM((n_rows, rows_d), BF16),
        cond_own=pltpu.VMEM((n_rows, cols_f), F32),
        m_part=pltpu.VMEM((2, half, ada_w), F32),
        m_core=pltpu.VMEM((half, ada_w), F32),
        m_chip=pltpu.VMEM((nc, half, ada_w), F32),
        m_z=pltpu.VMEM((nf, 2, half, ada_w), BF16),
        m_tab=pltpu.VMEM((n_rows, 6 * width), F32),
        tab=pltpu.VMEM((3, nc * n_sub, width), F32),
        own_tab=pltpu.VMEM((6, n_sub, width), F32),
        q_z=pltpu.VMEM((nf, rows_d, q_w + cols_f), BF16),
        q_rows=pltpu.VMEM((nf * 3, third, q_w), BF16),
        q_got=pltpu.VMEM((3, nc, third, q_w), BF16),
        w_q=pltpu.VMEM((nc, 2, rows_d, q_w), BF16),
        y_got=pltpu.VMEM((nc, rows_d, q_w), BF16),
        f1_z=pltpu.VMEM((nf, rows_d, ff_c), BF16),
        w_1=pltpu.VMEM((nc, 2, rows_d, ff_c), BF16),
        p_got=pltpu.VMEM((2, nf, rows_d, cols_f), BF16),
        w_p=pltpu.VMEM((chip_w, width), BF16),
        f2_half=pltpu.VMEM((cols_f, ff_d), BF16),
        f2_got=pltpu.VMEM((rows_d, ff_d), BF16),
        w_2=pltpu.VMEM((nf, 2, rows_d, ff_c), BF16),
        a_in=pltpu.VMEM(tokens, BF16),
        qkv=pltpu.VMEM((3, nc, own, chip_w), BF16),
        probs=pltpu.VMEM((nc * heads, own, own), F32),
        mixed=pltpu.VMEM((nc, own, chip_w), BF16),
        sum_s=pltpu.VMEM(tokens, BF16),
        sum_r=pltpu.VMEM((2, own, width), BF16),
        sum_st=pltpu.VMEM((2, own // 2, width), BF16),
        br_s=pltpu.VMEM(tokens, BF16),
        br_r=pltpu.VMEM((2, own, width), BF16),
        br_st=pltpu.VMEM((2, own // 2, width), BF16),
        m_all=pltpu.VMEM(tokens, BF16),
        da_all=pltpu.VMEM(tokens, BF16),
        attn=pltpu.VMEM((own, width), F32),
        after=pltpu.VMEM((own, width), F32),
        d_after=pltpu.VMEM((own, width), F32),
        hid=pltpu.VMEM((own, ff_c), F32),
        act=pltpu.VMEM((nc, own, ff_c), BF16),
        d_hid=pltpu.VMEM((nc, own, ff_c), BF16),
        dbr=pltpu.VMEM(tokens, BF16),
        d_qkv=pltpu.VMEM((nc, own, q_w), BF16),
        g_2=pltpu.VMEM((nf, 2, rows_d, ff_c), BF16),
        g_2r=pltpu.VMEM((nf, rows_d, ff_c), BF16),
        g_1r=pltpu.VMEM((nc, rows_d, ff_c), BF16),
        g_qr=pltpu.VMEM((nc, rows_d, q_w), BF16),
        g_pr=pltpu.VMEM((rows_d, width), BF16),
        got_q=pltpu.VMEM((2, nf - 1, rows_d, q_w + cols_f), BF16),
        got_1=pltpu.VMEM((2, nf - 1, rows_d, ff_c), BF16),
        got_2=pltpu.VMEM((2, nf - 1, rows_d, ff_c), BF16),
        all_2=pltpu.VMEM((2, rows_d, ff_c), F32),
        sub=pltpu.VMEM((6, n_sub, width), F32),
        q_nat=pltpu.VMEM((rows_d, q_w), BF16),
        p_nat=pltpu.VMEM((rows_d, cols_f), BF16),
        all_q=pltpu.VMEM((rows_d, q_w + cols_f), F32),
        sub_lin=pltpu.VMEM((2, nc * n_sub, width), F32),
        sub_gate=pltpu.VMEM((nc * n_sub, width), F32),
        d_part=pltpu.VMEM((2, half, 6 * width), F32),
        d_core=pltpu.VMEM((half, 6 * width), F32),
        d_cut=pltpu.VMEM((nf, half, ada_w), BF16),
        d_bias=pltpu.VMEM((8, width), F32),
        dz=pltpu.VMEM((nf, half, ada_w), BF16),
        dzb=pltpu.VMEM((nf, 8, width), BF16),
        d_tot=pltpu.VMEM((2, half, ada_w), F32),
        d_low=pltpu.VMEM((8, width), BF16),
        d_bsum=pltpu.VMEM((8, width), F32),
        d_coreb=pltpu.VMEM((8, width), F32),
        d_chipb=pltpu.VMEM((nc, 8, width), F32),
        c_part=pltpu.VMEM((nf, n_rows, rows_d), F32),
        c_all=pltpu.VMEM((nc, 2, n_rows, rows_d), F32),
        send=pltpu.SemaphoreType.DMA((n_sem,)),
        recv=pltpu.SemaphoreType.DMA((n_sem,)),
        local=pltpu.SemaphoreType.DMA((40,)),
    )
    names = list(scratch)

    def kernel(
        x_in, c_in, frames_in, clips_in, bq_in, bp_in, b1_in, b2_in, ba_in, cond_in, ada_in,
        q_in, p_in, f1_in, f2_in,
        *rest,
    ):
        homes, rest = rest[: len(outs)], rest[len(outs) :]
        held, rest = rest[: len(outs)], rest[len(outs) :]
        (out, x_grad, o_cond, o_ada, o_bada, o_q, o_bqv, o_p, o_bp, o_1, o_b1, o_2, o_b2) = held
        home_of = {id(ref): home for ref, home in zip(held, homes)}
        landed = []
        r = types.SimpleNamespace(**dict(zip(names, rest)))
        place = Place(nc, nf)
        wires = Wires(r.send, r.recv, r.local)
        c, k, f = place.c, place.k, place.f
        core_o, core_dev = place.peer(CORE, 1)
        chip_peers = [place.peer(CHIP, step) for step in range(1, nc)]
        plane_peers = [place.peer(PLANE, step) for step in range(1, nf)]

        def loop(count, body, unroll=1):
            def run(i, carry):
                body(i)
                return carry

            lax.fori_loop(0, count, run, 0, unroll=unroll)

        def loop_rows(body):
            loop(n_sub, body, 2)

        def when(condition, body):
            pl.when(condition)(body)

        def sub_rows(g):
            return pl.ds(pl.multiple_of(g * SUB, SUB), SUB)

        def reserve(count):
            base = wires.remote_count
            wires.remote_count += count
            return base

        def pair(src, dst, device, send_at, recv_at):
            return pltpu.make_async_remote_copy(
                src_ref=src,
                dst_ref=dst,
                send_sem=r.send.at[send_at],
                recv_sem=r.recv.at[recv_at],
                device_id=device,
                device_id_type=MESH_ID,
            )

        chip_x, dev_x = place.peer(CHIP, 1)
        chip_y, dev_y = place.peer(CHIP, 2)
        chip_d, _ = place.peer(CHIP, 3)
        first_half, second_half = pl.ds(0, own // 2), pl.ds(own // 2, own // 2)

        class Share:
            def __init__(self, ref, src=None):
                def copy(chip, rows, device, at, own_src=None):
                    from_ref = ref.at[chip, rows] if own_src is None else own_src.at[rows]
                    return pair(from_ref, ref.at[chip, rows], device, at, at)

                at = reserve(6)
                self.x_a = copy(c, first_half, dev_x, at, src)
                self.x_b = copy(c, second_half, dev_x, at + 1, src)
                self.y_b = copy(c, second_half, dev_y, at + 2, src)
                self.y_a = copy(c, first_half, dev_y, at + 3, src)
                self.on_y = copy(chip_x, first_half, dev_y, at + 4)
                self.on_x = copy(chip_y, second_half, dev_x, at + 5)

            def start(self):
                for item in (self.x_a, self.y_b, self.x_b, self.y_a):
                    item.start()

            def relay(self):
                self.x_a.wait_recv()
                self.on_y.start()
                self.y_b.wait_recv()
                self.on_x.start()

            def arrive(self, step):
                if step == 1:
                    self.x_b.wait_recv()
                elif step == 2:
                    self.y_a.wait_recv()
                else:
                    self.on_y.wait_recv()
                    self.on_x.wait_recv()

            def sent(self):
                for item in (self.x_a, self.x_b, self.y_b, self.y_a, self.on_y, self.on_x):
                    item.wait_send()

        class Merge:
            def __init__(self, terms, got, stage):
                self.terms, self.got, self.stage = terms, got, stage
                at = reserve(6)
                self.d_x = pair(terms.at[chip_d, first_half], stage.at[0], dev_x, at, at)
                self.d_y = pair(terms.at[chip_d, second_half], stage.at[1], dev_y, at + 1, at + 1)

                def copy(chip, rows, to, device, index):
                    return pair(
                        terms.at[chip, rows], got.at[to, rows], device, at + index, at + index
                    )

                self.x_a = copy(chip_x, first_half, 0, dev_x, 2)
                self.x_b = copy(chip_x, second_half, 0, dev_x, 3)
                self.y_b = copy(chip_y, second_half, 1, dev_y, 4)
                self.y_a = copy(chip_y, first_half, 1, dev_y, 5)

            def put(self, step, blk, part):
                self.terms[blk] = part

                def far():
                    self.d_x.start()
                    self.d_y.start()

                when(step == 3, far)
                when(step == 2, self.y_b.start)
                when(step == 1, self.x_a.start)

            def launch(self):
                for item in (self.d_x, self.d_y, self.y_b, self.x_a):
                    item.start()

            def combine(self):
                self.d_y.wait()
                ref = self.terms.at[chip_x, second_half]
                ref[...] = add_low(ref[...], self.stage[1])
                self.x_b.start()
                self.d_x.wait()
                ref = self.terms.at[chip_y, first_half]
                ref[...] = add_low(ref[...], self.stage[0])
                self.y_a.start()

            def finish(self):
                for item in (self.x_a, self.x_b, self.y_b, self.y_a):
                    item.wait()

            def rows(self, at):
                value = self.terms[c, at, :].astype(F32) + self.got[0, at, :].astype(F32)
                return value + self.got[1, at, :].astype(F32)

        def land(*refs):
            for ref in refs:
                landed.append(wires.near(ref, home_of[id(ref)]))

        up, down = (place.dp, f + 1), (place.dp, f - 1)

        class Gather:
            def __init__(self, slot):
                self.slot = slot
                self.up, self.down = reserve(nf - 1), reserve(nf - 1)

            def both(self, step, src=None):
                above = pair(
                    self.slot(f - step) if src is None else src,
                    self.slot(f - step), up, self.up + step, self.up + step,
                )
                below = pair(
                    self.slot(f + step) if src is None else src,
                    self.slot(f + step), down, self.down + step, self.down + step,
                )
                return (
                    ((f - step >= 0) & (f < nf - 1), above),
                    ((f + step <= nf - 1) & (f > 0), below),
                )

            def start(self, step, src=None):
                for condition, copy in self.both(step, src):
                    when(condition, copy.start)

            def arrive(self, step, then=None, wait=True):
                for condition, got, base in (
                    (f - 1 - step >= 0, f - 1 - step, self.up),
                    (f + 1 + step <= nf - 1, f + 1 + step, self.down),
                ):

                    def body(got=got, base=base):
                        slot = self.slot(got)
                        if wait:
                            pair(slot, slot, core_dev, base + step, base + step).wait_recv()
                        if then is not None:
                            then(got)

                    when(condition, body)

            def sent(self, src=None):
                for step in range(nf - 1):
                    for condition, copy in self.both(step, src if step == 0 else None):
                        when(condition, copy.wait_send)

        class Sum:
            def __init__(self, terms, got):
                self.terms, self.got = terms, got
                self.bases = (reserve(nf - 1), reserve(nf - 1))

            def both(self, step):
                for way in range(2):
                    target = f + (nf - 1) - step if way == 0 else f - (nf - 1) + step
                    condition = (f <= step) & (f < nf - 1) if way == 0 else (target >= 0) & (f > 0)
                    more = condition & (f > 0 if way == 0 else f < nf - 1)
                    at = self.bases[way] + step
                    copy = pair(
                        self.terms(target), self.got.at[way, step], up if way == 0 else down, at, at
                    )
                    yield way, target, condition, more, copy

            def wait(self, way, step):
                at = self.bases[way] + step
                ref = self.got.at[way, step]
                pair(ref, ref, core_dev, at, at).wait_recv()

            def start(self, step):
                for way, target, condition, more, copy in self.both(step):
                    if step > 0:

                        def body(way=way, target=target):
                            self.wait(way, step - 1)
                            ref = self.terms(target)
                            ref[...] = add_low(ref[...], self.got[way, step - 1])

                        when(more, body)
                    when(condition, copy.start)

            def finish(self, result):
                result[...] = self.terms(f)[...].astype(F32)
                for way, condition in ((0, f > 0), (1, f < nf - 1)):

                    def body(way=way):
                        self.wait(way, last)
                        result[...] = result[...] + self.got[way, last].astype(F32)

                    when(condition, body)
                for step in range(nf - 1):
                    for _, _, condition, _, copy in self.both(step):
                        when(condition, copy.wait_send)

        def own_side(ref, side):
            return ref.at[pl.ds(pl.multiple_of(side * rows_d, SUB), rows_d)]

        barrier = pltpu.get_barrier_semaphore()
        peers = [core_dev] + [peer for _, peer in chip_peers + plane_peers]
        for peer in peers:
            pl.semaphore_signal(barrier, inc=1, device_id=peer, device_id_type=MESH_ID)

        q_line = Gather(lambda g: r.q_z.at[g])
        f1_line = Gather(lambda g: r.f1_z.at[g])
        f2_line = Gather(lambda g: r.w_2.at[g, k])
        ada_near = wires.near(ada_in, r.ada)
        q_near = wires.near(q_in, r.q_nat)
        p_near = wires.near(p_in, r.p_nat)
        f2_near = wires.near(f2_in, r.f2_half)
        first = []
        first.append(wires.near(x_in, r.xg.at[c]))
        first.append(wires.near(c_in, r.cg.at[c]))
        f1_near = wires.near(f1_in, r.f1_z.at[f])
        order = lax.broadcasted_iota(jnp.int32, frames_in.shape, 0)
        for at, value in ((0, frames_in[...] + 65536 * order), (1, clips_in[...] + n_clips * order)):
            row = [value[i : i + 1].astype(F32) for i in range(micro)]
            r.idsg[c, at : at + 1, :] = jnp.concatenate(row, axis=1)
        row = [ref[...].astype(F32).reshape(1, ref.shape[0]) for ref in (bq_in, bp_in, b1_in, b2_in, ba_in)]
        r.biasg[f] = jnp.concatenate(row, axis=1)
        cond_rows = cond_in[...].reshape(n_rows, width)

        def own_silu(at):
            part = cond_rows[:, rows_d * at : rows_d * (at + 1)]
            r.silu[...] = (part / (1.0 + jnp.exp(-part))).astype(BF16)

        def own_cond(at):
            r.cond_own[...] = cond_rows[:, cols_f * at : cols_f * (at + 1)]

        for at in range(2 * nc):
            when(place.dp == at, functools.partial(own_silu, at))
        for at in range(nf):
            when(f == at, functools.partial(own_cond, at))
        ada_near.wait()
        ada_bias = jnp.where(place.dp == 0, row[4], 0.0)
        value = dot(r.silu[...], r.ada[...]) + ada_bias
        r.m_part[...] = value.reshape(2, half, ada_w)
        q_near.wait()
        p_near.wait()
        r.q_z[f] = jnp.concatenate([r.q_nat[...], r.p_nat[...]], axis=1)
        f2_near.wait()
        pl.semaphore_wait(barrier, len(peers))
        m_first = wires.far(r.m_part.at[core_o], r.m_core, core_dev)
        q_line.start(0)
        for _, peer in chip_peers:
            first.append(wires.far(r.idsg.at[c], r.idsg.at[c], peer))
        f2_swap = wires.far(own_side(r.f2_half, core_o), r.f2_got, core_dev)

        w_q, q_rows = r.w_q, r.q_rows
        q_base = reserve(3 * nc)
        q_local = wires.local_count
        wires.local_count += 3

        def q_copies(plane, i):
            piece = 3 * plane + i
            kind, chip = piece // nc, piece % nc
            src, dst = q_rows.at[piece], r.q_got.at[kind, c]
            far = pair(src, dst, (chip * 2 + k, f), q_base + kind * nc + chip, q_base + kind * nc + c)
            return chip, far, pltpu.make_async_copy(src, dst, r.local.at[q_local + kind])

        def q_forward(plane):
            r.p_got[k, plane] = r.q_z[plane, :, q_w:]
            for i in range(3):
                piece = r.q_z[plane, :, chip_w * i : chip_w * (i + 1)]
                parts = [piece[third * j : third * (j + 1)] for j in range(3)]
                q_rows[3 * plane + i] = jnp.concatenate(parts, axis=1)
                chip, far, near = q_copies(plane, i)
                when(chip != c, far.start)
                when(chip == c, near.start)

        f1_base = reserve(nc)
        f1_local = wires.local_count
        wires.local_count += 1

        def f1_copies(plane):
            src, dst = r.f1_z.at[plane], r.w_1.at[c, k]
            far = pair(src, dst, (plane * 2 + k, f), f1_base + plane, f1_base + c)
            return far, pltpu.make_async_copy(src, dst, r.local.at[f1_local])

        def f1_forward(plane):
            far, near = f1_copies(plane)
            when(plane != c, far.start)
            when(plane == c, near.start)

        m_first.wait()
        m_chip = r.m_chip
        m_chip[c] = r.m_part[k] + r.m_core[...]
        m_second = [wires.far(m_chip.at[c], m_chip.at[c], peer) for _, peer in chip_peers]
        q_forward(f)
        x_share = Share(r.xg, x_in)
        x_share.start()
        wait_all(m_second)
        total = m_chip[0]
        for other in range(1, nc):
            total = total + m_chip[other]
        r.m_z[f, k] = total.astype(BF16)
        m_third = [wires.far(r.m_z.at[f, k], r.m_z.at[f, k], peer) for _, peer in plane_peers]
        q_line.arrive(0, q_forward)
        q_line.start(1)
        x_share.relay()
        f2_swap.wait()

        def join_even():
            r.w_2[f, k] = jnp.concatenate([r.f2_half[:rows_d], r.f2_got[...]], axis=1)

        def join_odd():
            r.w_2[f, k] = jnp.concatenate([r.f2_got[...], r.f2_half[rows_d:]], axis=1)

        when(k == 0, join_even)
        when(k == 1, join_odd)
        f2_base = reserve(nf)

        def f2_across(plane):
            ref = r.w_2.at[plane, k]
            return pair(ref, ref, core_dev, f2_base + plane, f2_base + plane)

        def f2_forward(plane):
            f2_across(plane).start()

        f2_forward(f)
        wait_all(m_third)
        m_last = wires.far(r.m_z.at[:, k], r.m_z.at[:, k], core_dev)

        wait_all(first)
        m_last.wait()
        m_rows = [r.m_z[plane].astype(F32).reshape(n_rows, ada_w) for plane in range(nf)]
        r.m_tab[...] = jnp.concatenate(m_rows, axis=1)
        lead = lax.broadcasted_iota(jnp.int32, (n_sub, own), 1)
        lead = lead == SUB * lax.broadcasted_iota(jnp.int32, (n_sub, own), 0)
        lead = jnp.where(lead, 1.0, 0.0).astype(BF16)
        places = lax.broadcasted_iota(jnp.int32, (own, n_rows), 1).astype(F32)

        def hot_rows(blk):
            clip = r.idsg[blk].T[:, 1:2]
            return dot(lead, jnp.where(clip == places, 1.0, 0.0).astype(BF16)).astype(BF16)

        hot_all = jnp.concatenate([hot_rows(blk) for blk in range(nc)], axis=0)
        own_hot = hot_rows(c)
        for kind in range(6):
            value = r.m_tab[:, width * kind : width * (kind + 1)]
            if kind in (0, 1, 5):
                r.tab[kind % 3] = dot3(hot_all, value)
            r.own_tab[kind] = dot3(own_hot, value)

        def tab_row(kind, blk, g):
            return r.tab[kind % 3, pl.ds(blk * n_sub + g, 1), :]

        def own_row(kind, g):
            return r.own_tab[kind, pl.ds(g, 1), :]

        def make_a(blk):
            def body(g):
                rows = sub_rows(g)
                normal, _ = ln_parts(r.xg[blk, rows, :].astype(F32))
                value = normal * (1.0 + tab_row(1, blk, g)) + tab_row(0, blk, g)
                r.a_in[blk, rows, :] = value.astype(BF16)

            loop_rows(body)

        make_a(c)
        for step in (1, 2):
            x_share.arrive(step)
            make_a(xor_of(c, step, nc))
        q_line.arrive(1, q_forward)
        q_line.start(2)
        bias_got = [wires.far(r.biasg.at[f], r.biasg.at[f], peer) for _, peer in plane_peers]
        f1_line.start(0, f1_in)
        x_share.arrive(3)
        make_a(chip_d)
        q_line.arrive(2, q_forward)

        for kind in range(3):
            for other, _ in chip_peers:
                ref = r.q_got.at[kind, other]
                at = q_base + kind * nc + other
                pair(ref, ref, core_dev, at, at).wait()
            ref = r.q_got.at[kind, c]
            pltpu.make_async_copy(ref, ref, r.local.at[q_local + kind]).wait()
        q_core = []
        for chip in range(nc):
            for j in range(3):
                at = chip_w * j
                row = [r.q_got[kind, chip, :, at : at + chip_w] for kind in range(3)]
                w_q[chip, k, third * j : third * (j + 1), :] = jnp.concatenate(row, axis=1)
            q_core.append(wires.far(w_q.at[chip, k], w_q.at[chip, k], core_dev))
        p_core = wires.far(r.p_got.at[k], r.p_got.at[k], core_dev)
        f1_near.wait()
        f1_forward(f)
        f1_line.arrive(0, f1_forward)
        f1_line.start(1)
        x_share.sent()
        p_core.wait()
        for side in range(2):
            row = [r.p_got[side, plane] for plane in range(nf)]
            r.w_p[side * rows_d : (side + 1) * rows_d, :] = jnp.concatenate(row, axis=1)
        wait_all(q_core)

        lane = lax.broadcasted_iota(jnp.int32, (1, chip_w), 1)
        head_of = [
            jnp.where((lane >= HEAD_DIM * h) & (lane < HEAD_DIM * (h + 1)), 1.0, 0.0).astype(BF16)
            for h in range(heads)
        ]

        def weight_q():
            return w_q[...].reshape(width, q_w)

        wait_all(bias_got)

        def qv_bias(plane):
            row = r.biasg[plane]
            return jnp.where(c % 2 == 0, row[:, :chip_w], row[:, chip_w : 2 * chip_w])

        bias_q, bias_v = qv_bias(c // 2), qv_bias(nf // 2 + c // 2)
        at_p = 2 * chip_w
        at_1 = at_p + cols_f
        at_2 = at_1 + ff_c
        bias_p = jnp.concatenate([r.biasg[g][:, at_p : at_p + cols_f] for g in range(nf)], axis=1)
        bias_o = jnp.concatenate([r.biasg[g][:, at_2 : at_2 + cols_f] for g in range(nf)], axis=1)
        bias_1 = r.biasg[c][:, at_1 : at_1 + ff_c]
        zero = jnp.zeros_like(bias_q)
        bias_qkv = jnp.concatenate([bias_q, zero, bias_v], axis=1)
        attn_merge = Merge(r.sum_s, r.sum_r, r.sum_st)

        def attend(i):
            step = nc - 1 - i
            blk = xor_of(c, step, nc)
            value = (dot(r.a_in[blk], weight_q()) + bias_qkv).astype(BF16)
            for kind in range(3):
                r.qkv[kind, blk] = value[:, chip_w * kind : chip_w * (kind + 1)]
            q_now, k_now, v_now = r.qkv[0, blk], r.qkv[1, blk], r.qkv[2, blk]
            frames = r.idsg[blk]
            same = frames.T[:, 0:1] == frames[0:1, :]
            mixed = jnp.zeros((own, chip_w), F32)
            for h in range(heads):
                scores = dot_rt(q_now * head_of[h], k_now) * head_scale
                scores = jnp.where(same, scores, NEG_FILL)
                raised = jnp.exp(scores - jnp.max(scores, axis=-1, keepdims=True))
                share = raised / jnp.sum(raised, axis=-1, keepdims=True)
                r.probs[blk * heads + h] = share
                mixed = mixed + dot(share.astype(BF16), v_now * head_of[h])
            mixed = mixed.astype(BF16)
            r.mixed[blk] = mixed
            attn_merge.put(step, blk, dot(mixed, r.w_p[...]).astype(BF16))

            def next_lines():
                f1_line.arrive(1)
                f1_line.start(2)
                f2_line.start(0)

            when(i == 1, next_lines)

        loop(nc, attend)
        attn_merge.combine()
        f1_line.arrive(1, f1_forward, False)
        f1_line.arrive(2, f1_forward)

        attn_merge.finish()

        def after_attention(g):
            rows = sub_rows(g)
            value = attn_merge.rows(rows) + bias_p
            r.attn[rows, :] = value
            after = r.xg[c, rows, :].astype(F32) + own_row(2, g) * value
            r.after[rows, :] = after
            normal, _ = ln_parts(after)
            r.m_all[c, rows, :] = (normal * (1.0 + own_row(4, g)) + own_row(3, g)).astype(BF16)

        loop_rows(after_attention)
        m_all = r.m_all
        m_share = Share(m_all)
        m_share.start()
        c_share = Share(r.cg, c_in)
        c_share.start()
        f2_line.arrive(0, f2_forward)
        f2_line.start(1)
        f1_core = []
        ref = r.w_1.at[c, k]
        pltpu.make_async_copy(ref, ref, r.local.at[f1_local]).wait()
        f1_core.append(wires.far(ref, ref, core_dev))
        for other, _ in chip_peers:
            ref = r.w_1.at[other, k]
            pair(ref, ref, core_dev, f1_base + other, f1_base + other).wait()
            f1_core.append(wires.far(ref, ref, core_dev))
        m_share.relay()
        f1_line.sent(f1_in)
        f2_line.arrive(1, f2_forward)
        f2_line.start(2)
        wait_all(f1_core)

        def weight_1():
            return r.w_1[...].reshape(width, ff_c)

        def weight_2():
            return r.w_2[...].reshape(width, ff_c)

        dm_merge = Merge(r.sum_s, r.sum_r, r.sum_st)
        br_merge = Merge(r.br_s, r.br_r, r.br_st)

        def mixed_order(i):
            return (1 + 2 * i) * (1 - i // 2) + (6 - 2 * i) * (i // 2)

        def feed(step):
            blk = xor_of(c, step, nc)
            for at in range(1, nc):
                when(step == at, functools.partial(m_share.arrive, at))
            r.hid[...] = dot(m_all[blk], weight_1()) + bias_1

            def gelu_rows(g):
                rows = sub_rows(g)
                value, slope = gelu_both(r.hid[rows, :])
                r.act[blk, rows, :] = value.astype(BF16)
                r.d_hid[blk, rows, :] = slope.astype(BF16)

            loop_rows(gelu_rows)
            when(step == 1, c_share.relay)

        def feed_back(i):
            step = mixed_order(i)
            blk = xor_of(c, step, nc)
            for at in range(1, nc):
                when(step == at, functools.partial(c_share.arrive, at))

            def dbr_rows(g):
                rows = sub_rows(g)
                value = r.cg[blk, rows, :].astype(F32) * tab_row(5, blk, g)
                r.dbr[blk, rows, :] = value.astype(BF16)

            loop_rows(dbr_rows)
            r.hid[...] = dot(r.dbr[blk], weight_2())

            def back_rows(g):
                rows = sub_rows(g)
                value = r.hid[rows, :] * r.d_hid[blk, rows, :].astype(F32)
                r.d_hid[blk, rows, :] = value.astype(BF16)

            loop_rows(back_rows)
            dm_merge.put(step, blk, dot_rt(r.d_hid[blk], weight_1()).astype(BF16))

        loop(nc, feed)
        f2_line.arrive(2, f2_forward)
        for plane in range(nf):
            f2_across(plane).wait()
        loop(nc, feed_back)

        def column_cuts(count):
            return [(at, min(at + 256, count)) for at in range(0, count, 256)]

        def all_rows(ref):
            return ref[...].reshape(group, ref.shape[-1])

        dbr_all = all_rows(r.dbr)
        for lo, hi in column_cuts(ff_c):
            value = dot_lt(dbr_all, r.act[:, :, lo:hi].reshape(group, hi - lo))
            r.g_2[:, :, :, lo:hi] = value.astype(BF16).reshape(nf, 2, rows_d, hi - lo)
        g2_core = wires.far(r.g_2.at[:, core_o], r.g_2r, core_dev)

        dm_merge.combine()
        g_1 = r.w_1
        m_rows_all = all_rows(m_all)
        for lo, hi in column_cuts(ff_c):
            value = dot_lt(m_rows_all, r.d_hid[:, :, lo:hi].reshape(group, hi - lo))
            g_1[:, :, :, lo:hi] = value.astype(BF16).reshape(nc, 2, rows_d, hi - lo)
        g1_core = wires.far(g_1.at[:, core_o], r.g_1r, core_dev)
        c_share.sent()
        g2_core.wait()
        for plane in range(nf):
            r.g_2[plane, k] = add_low(r.g_2[plane, k], r.g_2r[plane])
        sum_2 = Sum(lambda t: r.g_2.at[t, k], r.got_2)
        sum_2.start(0)


        dm_merge.finish()
        da_all = r.da_all

        def back_norm2(g):
            rows = sub_rows(g)
            d_m = dm_merge.rows(rows)
            normal, scale = ln_parts(r.after[rows, :])
            cot_now = r.cg[c, rows, :].astype(F32)
            d_after = cot_now + ln_back(normal, scale, d_m * (1.0 + own_row(4, g)))
            r.d_after[rows, :] = d_after
            da_all[c, rows, :] = (own_row(2, g) * d_after).astype(BF16)
            at = pl.ds(g, 1)
            r.sub[3, at, :] = jnp.sum(d_m, axis=0, keepdims=True)
            r.sub[4, at, :] = jnp.sum(d_m * normal, axis=0, keepdims=True)
            r.sub[2, at, :] = jnp.sum(d_after * r.attn[rows, :], axis=0, keepdims=True)

        loop_rows(back_norm2)
        da_share = Share(da_all)
        da_share.start()
        m_share.sent()
        da_share.relay()

        g1_core.wait()
        for chip in range(nc):
            g_1[chip, k] = add_low(g_1[chip, k], r.g_1r[chip])
        y_1 = r.f1_z
        y_1[c] = g_1[c, k]
        y1_far = [wires.far(g_1.at[other, k], y_1.at[c], peer) for other, peer in chip_peers]

        def branch_out(i):
            step = nc - 1 - i
            blk = xor_of(c, step, nc)
            r.hid[...] = dot_rt(r.act[blk], weight_2())
            r.br_s[blk] = r.hid[...].astype(BF16)
            bias_once = bias_o * jnp.where(step == 0, 1.0, 0.0)

            def gate_rows(g):
                rows = sub_rows(g)
                value = (r.hid[rows, :] + bias_once) * r.cg[blk, rows, :].astype(F32)
                r.sub_gate[pl.ds(blk * n_sub + g, 1), :] = jnp.sum(value, axis=0, keepdims=True)

            loop_rows(gate_rows)

        loop(nc, branch_out)
        sum_2.start(1)

        def gray_order(i):
            return i + i // 2 - 2 * (i // 3)

        back_merge = Merge(r.sum_s, r.sum_r, r.sum_st)

        def attend_back(i):
            step = gray_order(i)
            blk = xor_of(c, step, nc)
            for at in range(1, nc):
                when(step == at, functools.partial(da_share.arrive, at))
            d_mix = dot_rt(da_all[blk], r.w_p[...]).astype(BF16)
            q_now, k_now, v_now = r.qkv[0, blk], r.qkv[1, blk], r.qkv[2, blk]
            d_q = jnp.zeros((own, chip_w), F32)
            d_k = jnp.zeros((own, chip_w), F32)
            d_v = jnp.zeros((own, chip_w), F32)
            for h in range(heads):
                d_mix_h = d_mix * head_of[h]
                share = r.probs[blk * heads + h]
                d_share = dot_rt(d_mix_h, v_now)
                d_score = share * (d_share - jnp.sum(share * d_share, axis=-1, keepdims=True))
                d_score = d_score.astype(BF16)
                d_q = d_q + dot(d_score, k_now * head_of[h])
                d_k = d_k + dot_lt(d_score, q_now * head_of[h])
                d_v = d_v + dot_lt(share.astype(BF16), d_mix_h)
            all_three = jnp.concatenate([d_q * head_scale, d_k * head_scale, d_v], axis=1).astype(BF16)
            r.d_qkv[blk] = all_three
            back_merge.put(step, blk, dot_rt(all_three, weight_q()).astype(BF16))
            when(i == 3, lambda: sum_2.start(2))

        loop(nc, attend_back)
        da_share.sent()

        g_q, g_p = w_q, r.w_p
        a_rows = all_rows(r.a_in)
        for lo, hi in column_cuts(q_w):
            value = dot_lt(a_rows, r.d_qkv[:, :, lo:hi].reshape(group, hi - lo))
            g_q[:, :, :, lo:hi] = value.astype(BF16).reshape(nc, 2, rows_d, hi - lo)
        q_core_back = wires.far(g_q.at[:, core_o], r.g_qr, core_dev)
        wait_all(y1_far)
        sum_1 = Sum(lambda t: y_1.at[t], r.got_1)
        sum_1.start(0)
        g_p[...] = dot_lt(all_rows(r.mixed), all_rows(da_all)).astype(BF16)
        p_core_back = wires.far(own_side(g_p, core_o), r.g_pr, core_dev)
        q_core_back.wait()
        for chip in range(nc):
            g_q[chip, k] = add_low(g_q[chip, k], r.g_qr[chip])
        r.y_got[c] = g_q[c, k]
        yq_far = [wires.far(g_q.at[other, k], r.y_got.at[c], peer) for other, peer in chip_peers]

        def own_terms(step):
            blk = xor_of(c, step, nc)

            def body(g):
                rows = sub_rows(g)
                part = r.sum_s[blk, rows, :].astype(F32)
                normal, _ = ln_parts(r.xg[blk, rows, :].astype(F32))
                at = pl.ds(blk * n_sub + g, 1)
                r.sub_lin[0, at, :] = jnp.sum(part, axis=0, keepdims=True)
                r.sub_lin[1, at, :] = jnp.sum(part * normal, axis=0, keepdims=True)

            loop_rows(body)

        loop(nc, own_terms)
        back_merge.combine()
        all_turned = hot_all.astype(F32).T.astype(BF16)
        hot_turned = own_hot.astype(F32).T.astype(BF16)
        for kind in range(6):
            if kind < 2:
                value = dot3(all_turned, r.sub_lin[kind])
            elif kind < 5:
                value = dot3(hot_turned, r.sub[kind])
            else:
                value = dot3(all_turned, r.sub_gate[...])
            r.d_part[:, :, width * kind : width * (kind + 1)] = value.reshape(2, half, width)
        d_core = wires.far(r.d_part.at[core_o], r.d_core, core_dev)
        d_core.wait()
        r.d_core[...] = r.d_core[...] + r.d_part[k]
        for plane in range(nf):
            r.d_cut[plane] = r.d_core[:, ada_w * plane : ada_w * (plane + 1)].astype(BF16)
        small = []
        for other, peer in plane_peers:
            small.append(wires.far(r.d_cut.at[other], r.dz.at[f], peer))
        r.dz[f] = r.d_cut[f]
        sum_1.start(1)
        p_core_back.wait()
        own_side(g_p, k)[...] = add_low(own_side(g_p, k)[...], r.g_pr[...])
        ones_own = jnp.ones((8, own), BF16)
        ones_all = jnp.ones((8, group), BF16)
        r.d_bias[...] = jnp.zeros((8, width), F32)
        r.d_bias[0:1, :] = dot(ones_own, da_all[c])[0:1]
        r.d_bias[1:2, :] = dot(ones_own, r.dbr[c])[0:1]
        qkv_sums = dot(ones_all, all_rows(r.d_qkv))[0:1]
        r.d_bias[2:3, 0:chip_w] = qkv_sums[:, :chip_w]
        r.d_bias[3:4, 0:chip_w] = qkv_sums[:, 2 * chip_w :]
        ones_ff = dot(ones_all, all_rows(r.d_hid))[0:1]
        r.d_bias[4:5, :] = ones_ff[:, :width]
        for part in range(1, ff_c // width):
            r.d_bias[4 + part : 5 + part, :] = ones_ff[:, part * width : (part + 1) * width]
        r.d_low[...] = r.d_bias[...].astype(BF16)
        bias_far = [wires.far(r.d_low, r.dzb.at[f], peer) for _, peer in plane_peers]
        r.dzb[f] = r.d_low[...]
        wait_all(small)
        value = r.dz[0].astype(F32)
        for plane in range(1, nf):
            value = value + r.dz[plane].astype(F32)
        m_chip[c] = value
        small = [wires.far(m_chip.at[c], m_chip.at[c], peer) for _, peer in chip_peers]
        wait_all(yq_far)
        q_line.sent()
        y_q = r.q_z
        for plane in range(nf):
            row = []
            for i in range(3):
                kind, chip = (3 * plane + i) // nc, (3 * plane + i) % nc
                row.append(r.y_got[chip, :, chip_w * kind : chip_w * (kind + 1)])
            row.append(own_side(g_p, k)[:, plane * cols_f : (plane + 1) * cols_f])
            y_q[plane] = jnp.concatenate(row, axis=1)
        sum_q = Sum(lambda t: y_q.at[t], r.got_q)
        sum_q.start(0)
        sum_1.start(2)
        wait_all(bias_far)
        value = r.dzb[0].astype(F32)
        for plane in range(1, nf):
            value = value + r.dzb[plane].astype(F32)
        r.d_bsum[...] = value
        b_swap = wires.far(r.d_bsum, r.d_coreb, core_dev)

        back_merge.finish()

        def back_norm1(g):
            rows = sub_rows(g)
            d_a = back_merge.rows(rows)
            normal, scale = ln_parts(r.xg[c, rows, :].astype(F32))
            value = r.d_after[rows, :] + ln_back(normal, scale, d_a * (1.0 + own_row(1, g)))
            x_grad[rows, :] = value.astype(BF16)

        loop_rows(back_norm1)
        land(x_grad)
        wait_all(small)
        value = m_chip[0]
        for chip in range(1, nc):
            value = value + m_chip[chip]
        r.d_tot[k] = value
        d_swap = wires.far(r.d_tot.at[k], r.d_tot.at[k], core_dev)
        b_swap.wait()
        r.d_chipb[c] = r.d_bsum[...] + r.d_coreb[...]
        bias_far = [wires.far(r.d_chipb.at[c], r.d_chipb.at[c], peer) for _, peer in chip_peers]
        br_merge.launch()
        sum_q.start(1)
        d_swap.wait()
        d_cols = r.d_tot[...].reshape(n_rows, ada_w)
        silu_turned = r.silu[...].astype(F32).T.astype(BF16)
        o_bada[...] = jnp.sum(d_cols, axis=0)
        value, total = d_cols, None
        for _ in range(3):
            term = value.astype(BF16)
            value = value - term.astype(F32)
            part = dot_rt(term, r.ada[...])
            total = part if total is None else total + part
        r.c_part[f] = total
        c_far = [wires.far(r.c_part.at[f], r.c_part.at[f], peer) for _, peer in plane_peers]
        sum_q.start(2)
        for lo, hi in column_cuts(ada_w):
            o_ada[:, lo:hi] = dot3(silu_turned, d_cols[:, lo:hi])
        land(o_ada, o_bada)
        sum_2.finish(r.all_2.at[k])
        o2_swap = wires.far(r.all_2.at[k], r.all_2.at[k], core_dev)
        br_merge.combine()
        wait_all(c_far)
        value = r.c_part[0]
        for plane in range(1, nf):
            value = value + r.c_part[plane]
        r.c_all[c, k] = value
        c_chip = [wires.far(r.c_all.at[c, k], r.c_all.at[c, k], peer) for _, peer in chip_peers]


        br_merge.finish()

        def finish_out(g):
            rows = sub_rows(g)
            branch = br_merge.rows(rows) + bias_o
            out[rows, :] = (r.after[rows, :] + own_row(5, g) * branch).astype(BF16)

        loop_rows(finish_out)
        land(out)
        wait_all(c_chip)
        c_swap = wires.far(r.c_all.at[:, k], r.c_all.at[:, k], core_dev)
        o2_swap.wait()

        def own_columns(lo):
            def body():
                o_2[...] = r.all_2[:, :, lo : lo + ff_d].reshape(cols_f, ff_d)

            return body

        when(k == 0, own_columns(0))
        when(k == 1, own_columns(ff_d))
        land(o_2)
        wait_all(bias_far)
        own_sums = r.d_chipb[0]
        for chip in range(1, nc):
            own_sums = own_sums + r.d_chipb[chip]
        for plane in range(nf):

            def bias_columns(plane=plane):
                at = plane * cols_f
                o_bp[...] = own_sums[0, at : at + cols_f]
                o_b2[...] = own_sums[1, at : at + cols_f]
                kind, chip = 2 * plane // nc, 2 * plane % nc
                pieces = [r.d_chipb[chip + i, 2 + kind : 3 + kind, 0:chip_w] for i in range(2)]
                o_bqv[...] = jnp.concatenate(pieces, axis=1)[0]
                o_b1[...] = r.d_chipb[plane, 4, :]

            when(f == plane, bias_columns)
        land(o_bqv, o_bp, o_b1, o_b2)
        c_swap.wait()
        d_silu = jnp.concatenate([r.c_all[f, 0], r.c_all[f, 1]], axis=1)
        cond_now = r.cond_own[...]
        gate = 1.0 / (1.0 + jnp.exp(-cond_now))
        o_cond[...] = d_silu * (gate * (1.0 + cond_now * (1.0 - gate)))
        land(o_cond)
        f2_line.sent()
        sum_1.finish(o_1)
        land(o_1)
        sum_q.finish(r.all_q)
        o_q[...] = r.all_q[:, :q_w]
        o_p[...] = r.all_q[:, q_w:]
        land(o_q, o_p)
        wait_all(landed)
        assert wires.remote_count <= n_sem and wires.local_count <= 40

    return pl.pallas_call(
        kernel,
        out_shape=outs,
        in_specs=[ANYWHERE] * 2 + [ON_CHIP] * 8 + [ANYWHERE] * 5,
        out_specs=tuple([ANYWHERE] * len(outs)),
        scratch_shapes=[pltpu.VMEM(item.shape, item.dtype) for item in outs] + list(scratch.values()),
        compiler_params=pltpu.CompilerParams(
            collective_id=0, has_side_effects=True, vmem_limit_bytes=63 * 2**20
        ),
        name="block",
    )(x, cot, frames, clips, *biases, cond, w_ada, wq, wp, w1, w2)


def land_kernel(arrays):
    count = len(arrays)

    def kernel(*refs):
        ins, results, held = refs[:count], refs[count : 2 * count], refs[2 * count : 3 * count]
        arrive, leave = refs[3 * count :]
        steps = [pltpu.make_async_copy(a, b, arrive.at[i]) for i, (a, b) in enumerate(zip(ins, held))]
        copies = [pltpu.make_async_copy(a, b, leave.at[i]) for i, (a, b) in enumerate(zip(held, results))]
        for step in steps:
            step.start()
        for step, copy in zip(steps, copies):
            step.wait()
            copy.start()
        wait_all(copies)

    return pl.pallas_call(
        kernel,
        out_shape=tuple(jax.ShapeDtypeStruct(a.shape, a.dtype) for a in arrays),
        in_specs=[ANYWHERE] * count,
        out_specs=tuple([ANYWHERE] * count),
        scratch_shapes=[pltpu.VMEM(a.shape, a.dtype) for a in arrays]
        + [pltpu.SemaphoreType.DMA((count,))] * 2,
        name="land",
    )(*arrays)


def fits_block(n_dp, nf, width, ff, own, micro):
    nc = n_dp // 2
    return (
        nc == nf
        and nf == 4
        and width % (128 * nf) == 128
        and ff == 4 * width
        and (width // n_dp) % 16 == 0
        and (width // nc) % HEAD_DIM == 0
        and own % (2 * SUB) == 0
    )


def per_device(
    n_dp, nf, patches, cotangent, conditioning, frame_of_slot, clip_of_slot,
    w_ada, b_ada, w_qkv, b_qv, w_proj, b_proj, w_fc1, b_fc1, w_fc2, b_fc2,
):
    nc = n_dp // 2
    sizes = (nc, nf)
    micro, block, width = patches.shape
    own = micro * block
    clips = conditioning.shape[1]
    rows_d = width // n_dp
    cols_f = width // nf
    ff = w_fc1.shape[1] * nf
    ff_d = ff // n_dp
    chip_w = width // nc
    piece_q = math.gcd(3 * width // nf, chip_w)
    piece_1 = math.gcd(ff // nf, ff_d)
    dims = types.SimpleNamespace(
        nc=nc,
        nf=nf,
        per_q=3 * width // nf // piece_q,
        per_1=ff // nf // piece_1,
        chip_q=chip_w // piece_q,
        chip_1=ff // nc // piece_1,
    )
    dp = lax.axis_index("dp")
    f = lax.axis_index("fsdp")
    c, k = dp // 2, dp % 2

    q_send = w_qkv.reshape(rows_d, dims.per_q, piece_q).transpose(1, 0, 2)
    f1_send = w_fc1.reshape(rows_d, dims.per_1, piece_1).transpose(1, 0, 2)
    f2_send = w_fc2.T
    cond = conditioning.reshape(micro * clips, width)
    silu_cond = jax.nn.silu(cond)
    silu_low = silu_cond.astype(BF16)
    ada_w = w_ada.shape[1]
    silu_part = lax.dynamic_slice_in_dim(silu_low, dp * rows_d, rows_d, 1)
    mod_part = dot(silu_part, w_ada) + jnp.where(dp == 0, b_ada.astype(F32), 0.0)[None]
    mod_send = mod_part.reshape(-1, 2, ada_w // 2).transpose(1, 0, 2)
    cut = [0, 2 * cols_f, 3 * cols_f, 3 * cols_f + ff // nf, 4 * cols_f + ff // nf]
    cond_own = lax.dynamic_slice_in_dim(cond, f * cols_f, cols_f, 1)

    def ada_outputs(d_cols):
        grad_w_ada = precise(silu_part.astype(F32), d_cols, ((0,), (0,)))
        d_silu_part = precise(d_cols, w_ada.astype(F32), ((1,), (1,)))
        d_silu = cond_kernel(dims, d_silu_part).transpose(1, 0, 2).reshape(micro * clips, width)
        d_silu_own = lax.dynamic_slice_in_dim(d_silu, f * cols_f, cols_f, 1)
        _, silu_back = jax.vjp(jax.nn.silu, cond_own)
        cond_grad = silu_back(d_silu_own)[0].reshape(micro, clips, cols_f)
        return cond_grad, grad_w_ada, jnp.sum(d_cols, axis=0)

    if fits_block(n_dp, nf, width, ff, own, micro):
        results = block_kernel(
            dims, patches.reshape(own, width), cotangent.reshape(own, width), frame_of_slot,
            clip_of_slot, (b_qv, b_proj, b_fc1, b_fc2, b_ada), conditioning, w_ada, w_qkv, w_proj,
            w_fc1, w_fc2.T,
        )
        (
            output, input_grad, cond_grad, grad_ada, grad_b_ada, grad_qkv, grad_b_qv,
            grad_proj, grad_b_proj, grad_fc1, grad_b_fc1, grad_fc2, grad_b_fc2,
        ) = land_kernel(results)
        return (
            output.reshape(patches.shape),
            input_grad.reshape(patches.shape),
            cond_grad.reshape(micro, clips, cols_f),
            grad_ada,
            grad_b_ada,
            grad_qkv,
            grad_b_qv,
            grad_proj,
            grad_b_proj,
            grad_fc1,
            grad_b_fc1,
            grad_fc2.T,
            grad_b_fc2,
        )

    ids = jnp.stack([frame_of_slot.reshape(own), clip_of_slot.reshape(own)])
    ids = jnp.concatenate([ids, jnp.zeros((6, own), jnp.int32)])
    bias_send = jnp.concatenate([b_qv, b_proj, b_fc1, b_fc2]).astype(F32)[None]

    (x_all, c_all, ids_all, bias_all, mod_all, q_chip, f1_chip, p_chip, f2_chip, _, _) = start_kernel(
        dims, patches.reshape(own, width), cotangent.reshape(own, width), ids, bias_send, mod_send,
        q_send, f1_send, w_proj, f2_send,
    )
    group = nc * own
    modulation = mod_all.transpose(2, 0, 1, 3).reshape(micro * clips, 6 * width)
    q_parts = [
        q_chip[i].reshape(nc, 2, dims.chip_q, rows_d, piece_q).transpose(0, 1, 3, 2, 4).reshape(width, chip_w)
        for i in range(3)
    ]
    w1 = f1_chip.transpose(1, 2, 3, 0, 4).reshape(width, ff // nc)
    wp = p_chip.transpose(0, 2, 1, 3).reshape(chip_w, width)
    w2t = f2_chip.reshape(2, width, ff_d).transpose(1, 0, 2).reshape(width, 2 * ff_d)
    b_parts = [bias_all[:, 0, a:b].reshape(-1) for a, b in zip(cut[:-1], cut[1:])]
    bq = lax.dynamic_slice_in_dim(b_parts[0], c * chip_w, chip_w, 0)
    bv = lax.dynamic_slice_in_dim(b_parts[0], width + c * chip_w, chip_w, 0)
    b1 = lax.dynamic_slice_in_dim(b_parts[2], c * (ff // nc), ff // nc, 0)

    def hot_of(clip_ids):
        count = clip_ids.shape[0]
        row = (jnp.arange(count, dtype=jnp.int32) // block) % micro * clips + clip_ids
        return (row[:, None] == jnp.arange(micro * clips, dtype=jnp.int32)[None]).astype(F32)

    hot_group = hot_of(ids_all[:, 1].reshape(group))
    hot_own = hot_of(clip_of_slot.reshape(own))
    mod_group = precise(hot_group, modulation, ((1,), (0,)))
    mod_own = precise(hot_own, modulation, ((1,), (0,)))
    shift1, scale1 = mod_group[:, :width], mod_group[:, width : 2 * width]
    gate1 = mod_own[:, 2 * width : 3 * width]
    shift2, scale2 = mod_own[:, 3 * width : 4 * width], mod_own[:, 4 * width : 5 * width]
    gate2_group, gate2 = mod_group[:, 5 * width :], mod_own[:, 5 * width :]

    x_group = x_all.reshape(group, width).astype(F32)
    norm1, rstd1 = ln_parts(x_group)
    a_in = (norm1 * (1.0 + scale1) + shift1).astype(BF16)
    zero = jnp.zeros_like(bq)
    q, kk, v = [
        (dot(a_in, w) + b[None]).astype(BF16) for w, b in zip(q_parts, (bq, zero, bv))
    ]
    heads = chip_w // HEAD_DIM
    blocks = group // block
    q4, k4, v4 = [t.reshape(blocks, block, heads, HEAD_DIM) for t in (q, kk, v)]
    frames = ids_all[:, 0].reshape(blocks, block)
    same = (frames[:, :, None] == frames[:, None, :])[:, None]
    scores = jnp.einsum("bqhd,bkhd->bhqk", q4, k4, preferred_element_type=F32) * HEAD_DIM ** (-0.5)
    scores = jnp.where(same, scores, NEG_FILL)
    top = jnp.max(scores, axis=-1, keepdims=True)
    raised = jnp.exp(scores - top)
    probs = raised / jnp.sum(raised, axis=-1, keepdims=True)
    probs_low = probs.astype(BF16)
    mixed = jnp.einsum("bhqk,bkhd->bqhd", probs_low, v4, preferred_element_type=F32)
    mixed = mixed.reshape(group, chip_w).astype(BF16)
    attn_part = dot(mixed, wp)
    (attn_got,) = exchange(
        "attn_sum", 3, sizes, [(CHIP, SPREAD, attn_part.astype(BF16).reshape(nc, own, width))]
    )
    attn = jnp.sum(attn_got.astype(F32), axis=0) + b_parts[1][None]
    x_own = patches.reshape(own, width).astype(F32)
    after = x_own + gate1 * attn
    norm2, rstd2 = ln_parts(after)
    m_own = (norm2 * (1.0 + scale2) + shift2).astype(BF16)
    (m_all,) = exchange("m_gather", 4, sizes, [(CHIP, GATHER, m_own)])
    m_in = m_all.reshape(group, width)

    hidden = dot(m_in, w1) + b1[None]
    act, slope = gelu_both(hidden)
    act = act.astype(BF16)
    branch_part = dot_rt(act, w2t)
    cot_group = c_all.reshape(group, width).astype(F32)
    d_branch = (gate2_group * cot_group).astype(BF16)
    grad_2t = dot_lt(d_branch, act)
    d_hidden = (dot(d_branch, w2t) * slope).astype(BF16)
    grad_1 = dot_lt(m_in, d_hidden)
    d_m_part = dot_rt(d_hidden, w1)
    branch_got, d_m_got = exchange(
        "ff_sum",
        5,
        sizes,
        [
            (CHIP, SPREAD, d_m_part.astype(BF16).reshape(nc, own, width)),
            (CHIP, SPREAD, branch_part.astype(BF16).reshape(nc, own, width)),
        ],
    )[::-1]
    branch = jnp.sum(branch_got.astype(F32), axis=0) + b_parts[3][None]
    output = (after + gate2 * branch).astype(BF16)
    d_m = jnp.sum(d_m_got.astype(F32), axis=0)
    cot_own = cotangent.reshape(own, width).astype(F32)
    d_after = cot_own + ln_back(norm2, rstd2, d_m * (1.0 + scale2))
    d_attn = (gate1 * d_after).astype(BF16)
    (d_attn_all,) = exchange("d_attn_gather", 6, sizes, [(CHIP, GATHER, d_attn)])
    d_attn_group = d_attn_all.reshape(group, width)
    grad_p = dot_lt(mixed, d_attn_group)
    d_mix = dot_rt(d_attn_group, wp).astype(BF16).reshape(blocks, block, heads, HEAD_DIM)
    d_probs = jnp.einsum("bqhd,bkhd->bhqk", d_mix, v4, preferred_element_type=F32)
    d_scores = probs * (d_probs - jnp.sum(probs * d_probs, axis=-1, keepdims=True))
    d_scores = d_scores.astype(BF16)
    dq = jnp.einsum("bhqk,bkhd->bqhd", d_scores, k4, preferred_element_type=F32) * HEAD_DIM ** (-0.5)
    dk = jnp.einsum("bhqk,bqhd->bkhd", d_scores, q4, preferred_element_type=F32) * HEAD_DIM ** (-0.5)
    dv = jnp.einsum("bhqk,bqhd->bkhd", probs_low, d_mix, preferred_element_type=F32)
    dqkv = [t.reshape(group, chip_w).astype(BF16) for t in (dq, dk, dv)]
    d_a_part = sum(dot_rt(t, w) for t, w in zip(dqkv, q_parts))
    grad_q = jnp.stack([dot_lt(a_in, t) for t in dqkv])
    (d_a_got,) = exchange(
        "d_a_sum", 7, sizes, [(CHIP, SPREAD, d_a_part.astype(BF16).reshape(nc, own, width))]
    )
    d_a = jnp.sum(d_a_got.astype(F32), axis=0)
    norm1_own, rstd1_own = ln_parts(x_own)
    scale1_own = mod_own[:, width : 2 * width]
    input_grad = (d_after + ln_back(norm1_own, rstd1_own, d_a * (1.0 + scale1_own))).astype(BF16)

    g_q = grad_q.reshape(3, nc, 2, rows_d, dims.chip_q, piece_q).transpose(2, 1, 0, 4, 3, 5)
    g_1 = grad_1.reshape(nc, 2, rows_d, dims.chip_1, piece_1).transpose(1, 0, 3, 2, 4)
    g_p = grad_p.reshape(2, rows_d, nf, cols_f).transpose(0, 2, 1, 3)
    g_2 = grad_2t.reshape(nf, cols_f, 2, ff_d).transpose(2, 0, 1, 3)
    got = exchange("grad_core", 8, sizes, [(CORE, SPREAD, g.astype(BF16)) for g in (g_q, g_1, g_p, g_2)])
    s_q, s_1, s_p, s_2 = [jnp.sum(g.astype(F32), axis=0).astype(BF16) for g in got]
    r_q, r_1 = exchange("grad_chip", 9, sizes, [(CHIP, SPREAD, s_q), (CHIP, SPREAD, s_1)])
    z_q = r_q.transpose(1, 0, 2, 3, 4).reshape(nf, dims.per_q, rows_d, piece_q)
    z_1 = r_1.reshape(nf, dims.per_1, rows_d, piece_1)
    got = exchange("grad_plane", 10, sizes, [(PLANE, SPREAD, g) for g in (z_q, z_1, s_p, s_2)])
    o_q, o_1, o_p, o_2 = [jnp.sum(g.astype(F32), axis=0) for g in got]
    grad_w_qkv = o_q.transpose(1, 0, 2).reshape(rows_d, 3 * width // nf)
    grad_w_fc1 = o_1.transpose(1, 0, 2).reshape(rows_d, ff // nf)
    grad_w_fc2 = o_2.T

    d_token = jnp.concatenate(
        [d_a, d_a * norm1_own, d_after * attn, d_m, d_m * norm2, cot_own * branch], axis=1
    )
    d_mod = precise(hot_own, d_token, ((0,), (0,)))
    d_branch_own = (gate2 * cot_own).astype(BF16).astype(F32)

    def columns(value):
        return jnp.sum(value.astype(F32), axis=0)

    def spread(value, count):
        return lax.dynamic_update_slice_in_dim(
            jnp.zeros((count,), F32), value, c * value.shape[0], 0
        )

    g_bqv = jnp.concatenate([spread(columns(dqkv[0]), width), spread(columns(dqkv[2]), width)])
    g_b1 = spread(columns(d_hidden), ff)
    bias_terms = jnp.concatenate(
        [
            g_bqv.reshape(nf, -1),
            columns(d_attn).reshape(nf, -1),
            g_b1.reshape(nf, -1),
            columns(d_branch_own).reshape(nf, -1),
        ],
        axis=1,
    )
    n_bias = bias_terms.shape[1]
    bias_rows = -(-n_bias // ada_w)
    bias_terms = jnp.pad(bias_terms, ((0, 0), (0, bias_rows * ada_w - n_bias)))
    terms = jnp.concatenate(
        [d_mod.reshape(micro * clips, nf, ada_w).transpose(1, 0, 2), bias_terms.reshape(nf, bias_rows, ada_w)],
        axis=1,
    )
    pad_rows = -terms.shape[1] % 8
    terms = jnp.pad(terms, ((0, 0), (0, pad_rows), (0, 0)))
    terms = terms.reshape(nf, -1, 2, ada_w // 2).transpose(0, 2, 1, 3)
    total = sum_small_kernel(dims, terms).transpose(1, 0, 2).reshape(-1, ada_w)
    d_cols = total[: micro * clips]
    bias_sums = total[micro * clips : micro * clips + bias_rows].reshape(-1)[:n_bias]
    g_parts = [bias_sums[a:b] for a, b in zip(cut[:-1], cut[1:])]
    cond_grad, grad_w_ada, grad_b_ada = ada_outputs(d_cols)
    return (
        output.reshape(patches.shape),
        input_grad.reshape(patches.shape),
        cond_grad,
        grad_w_ada,
        grad_b_ada,
        grad_w_qkv,
        g_parts[0],
        o_p,
        g_parts[1],
        grad_w_fc1,
        g_parts[2],
        grad_w_fc2,
        g_parts[3],
    )


def solution(mesh):
    tokens = P(None, ("dp", "fsdp"), None)
    ids = P(None, ("dp", "fsdp"))
    both, cols = P("dp", "fsdp"), P("fsdp")
    in_specs = (tokens, tokens, P(), ids, ids) + (both, cols) * 5
    out_specs = (tokens, tokens, P(None, None, "fsdp")) + (both, cols) * 5
    return jax.shard_map(
        functools.partial(per_device, mesh.shape["dp"], mesh.shape["fsdp"]),
        mesh=mesh,
        in_specs=in_specs,
        out_specs=out_specs,
        check_vma=False,
    )
```
